32 devices in a mesh: samp: 8 (over y, x, core), head: 4 (over z).
Axes of the slice: x: 2, y: 2, z: 4, core: 2. Of those that a mesh axis runs over, the one named last changes fastest.
Arguments:
- act: bfloat16 [16, 544, 768], P('samp', 'head'), may hold values from -6 to 6
- cond: bfloat16 [16, 544, 384], P('samp', 'head'), may hold values from -6 to 6
- pair: bfloat16 [3, 544, 544, 128], P(None, 'head', 'samp'), may hold values from -6 to 6
- struct_of: int32 [16], P('samp'), may hold values from 0 to 2
- struct_len: int32 [3], replicated, may hold values from 272 to 544, as said below
- gain_first: bfloat16 [384], P('samp'), may hold values from 0.25 to 1.75
- scale_first: bfloat16 [384, 768], P('samp'), may hold values from -0.3125 to 0.3125
- scale_bias_first: bfloat16 [768], P('samp'), may hold values from -4 to 4
- shift_first: bfloat16 [384, 768], P('samp'), may hold values from -0.3125 to 0.3125
- query_weight: bfloat16 [768, 768], P('samp'), may hold values from -0.21875 to 0.21875
- query_bias: bfloat16 [768], P('samp'), may hold values from -3 to 3
- key_weight: bfloat16 [768, 768], P('samp'), may hold values from -0.21875 to 0.21875
- value_weight: bfloat16 [768, 768], P('samp'), may hold values from -0.21875 to 0.21875
- gate_weight: bfloat16 [768, 768], P('samp'), may hold values from -0.21875 to 0.21875
- output_weight: bfloat16 [768, 768], P('samp'), may hold values from -3.5 to 3.5
- pair_weight: bfloat16 [128, 16], P('samp'), may hold values from -0.5 to 0.5
- zero_first: bfloat16 [384, 768], P('samp'), may hold values from -0.3125 to 0.3125
- zero_bias_first: bfloat16 [768], P('samp'), may hold values from -2 to 1
- gain_second: bfloat16 [384], P('samp'), may hold values from 0.25 to 1.75
- scale_second: bfloat16 [384, 768], P('samp'), may hold values from -0.3125 to 0.3125
- scale_bias_second: bfloat16 [768], P('samp'), may hold values from -4 to 4
- shift_second: bfloat16 [384, 768], P('samp'), may hold values from -0.3125 to 0.3125
- swish_weight: bfloat16 [768, 1536], P('samp'), may hold values from -0.21875 to 0.21875
- linear_weight: bfloat16 [768, 1536], P('samp'), may hold values from -0.21875 to 0.21875
- down_weight: bfloat16 [1536, 768], P('samp'), may hold values from -0.3125 to 0.3125
- zero_second: bfloat16 [384, 768], P('samp'), may hold values from -0.3125 to 0.3125
- zero_bias_second: bfloat16 [768], P('samp'), may hold values from -2 to 1
- cotangent: bfloat16 [16, 544, 768], P('samp', 'head'), may hold values from -6 to 6
Outputs:
- layer_out: bfloat16 [16, 544, 768], P('samp', 'head')
- input_grad: float32 [16, 544, 768], P('samp', 'head')
- cond_grad: float32 [16, 544, 384], P('samp', 'head')
- pair_grad: float32 [3, 544, 544, 128], P(None, 'head', 'samp')
- gain_first_grad: float32 [384], P('samp')
- scale_first_grad: float32 [384, 768], P('samp')
- scale_bias_first_grad: float32 [768], P('samp')
- shift_first_grad: float32 [384, 768], P('samp')
- query_weight_grad: float32 [768, 768], P('samp')
- query_bias_grad: float32 [768], P('samp')
- key_weight_grad: float32 [768, 768], P('samp')
- value_weight_grad: float32 [768, 768], P('samp')
- gate_weight_grad: float32 [768, 768], P('samp')
- output_weight_grad: float32 [768, 768], P('samp')
- pair_weight_grad: float32 [128, 16], P('samp')
- zero_first_grad: float32 [384, 768], P('samp')
- zero_bias_first_grad: float32 [768], P('samp')
- gain_second_grad: float32 [384], P('samp')
- scale_second_grad: float32 [384, 768], P('samp')
- scale_bias_second_grad: float32 [768], P('samp')
- shift_second_grad: float32 [384, 768], P('samp')
- swish_weight_grad: float32 [768, 1536], P('samp')
- linear_weight_grad: float32 [768, 1536], P('samp')
- down_weight_grad: float32 [1536, 768], P('samp')
- zero_second_grad: float32 [384, 768], P('samp')
- zero_bias_second_grad: float32 [768], P('samp')
The draws below stay inside these ranges and needn't reach their ends.
Inputs may be any that keep to these rules, and one draw needn't show every extreme that they name: struct_len gives each structure's token count; one structure has exactly 544 tokens.
All inputs are finite; a program needn't handle non-finite values.
Results may differ from the reference program's by a relative error of at most 0.02.
Values may be sent and summed in bfloat16 or wider, within the bound.
A program may use at most 256 MiB of HBM per device.

```python
import jax
import jax.numpy as jnp
from jax import lax

D = 768
HEADS = 16
HEAD_DIM = 48
COND = 384
PAIR = 128
HIDDEN_SIZE = 1536
SLOTS = 544
STRUCTS = 3
SAMPLES = 16


def draw_struct_len(key, part):
    first_key, second_key = jax.random.split(key)
    lengths = jax.random.randint(first_key, (STRUCTS,), SLOTS // 2, SLOTS + 1)
    longest = jax.random.randint(second_key, (), 0, STRUCTS)
    return jnp.where(jnp.arange(STRUCTS) == longest, SLOTS, lengths).astype(jnp.int32)


def set_ends(values, rng, smallest, largest):
    extent = values.shape
    spot = [jax.random.randint(jax.random.fold_in(rng, axis), (), 0, extent[axis]) for axis in range(len(extent))]
    values = values.at[tuple(spot)].set(smallest)
    longest = extent.index(max(extent))
    spot[longest] = (spot[longest] + 1) % extent[longest]
    return values.at[tuple(spot)].set(largest)


def block_levels(own_key, extent, cuts, low, top_value):
    level, own = 1.0, jax.random.fold_in(own_key, 6)
    for axis_at, blocks in cuts:
        draws = jnp.exp(jax.random.uniform(jax.random.fold_in(own, axis_at), (blocks,), jnp.float32, low / len(cuts), top_value / len(cuts)))
        level = level * jnp.repeat(draws, extent[axis_at] // blocks).reshape([-1 if axis == axis_at else 1 for axis in range(len(extent))])
    return level


def normal_values(stream_key, dims, spread, limit, cuts=(), dtype=jnp.bfloat16):
    level = block_levels(stream_key, dims, cuts, -0.22, 0.18) if cuts else 1.0
    array = jax.random.normal(stream_key, dims, jnp.float32) * spread * level
    return jnp.minimum(jnp.maximum(array, -limit), limit).astype(dtype)


def setup_inputs(seed: int = 0) -> dict:
    key_list = jax.random.split(jax.random.key(seed), 29)
    act = normal_values(key_list[0], (SAMPLES, SLOTS, D), 1.0, 6.0, ((0, 8), (1, 4)))
    cond = normal_values(key_list[1], (SAMPLES, SLOTS, COND), 1.0, 6.0, ((0, 8), (1, 4)))
    pair = normal_values(key_list[2], (STRUCTS, SLOTS, SLOTS, PAIR), 1.0, 6.0, ((1, 4), (2, 8)))
    struct_of = set_ends(jax.random.randint(key_list[3], (SAMPLES,), 0, STRUCTS), jax.random.fold_in(key_list[3], 1), 0, STRUCTS - 1).astype(jnp.int32)
    struct_len = draw_struct_len(jax.random.fold_in(key_list[28], 71), 0)
    gain_first = jnp.clip(1.0 + 0.15 * jax.random.normal(key_list[5], (COND,), jnp.float32), 0.25, 1.75).astype(jnp.bfloat16)
    scale_first = normal_values(key_list[6], (COND, D), COND ** -0.5, 0.3125, ((0, 8),))
    scale_bias_first = normal_values(key_list[7], (D,), 1.0, 4.0, ((0, 8),))
    shift_first = normal_values(key_list[8], (COND, D), COND ** -0.5, 0.3125, ((0, 8),))
    query_weight = normal_values(key_list[9], (D, D), D ** -0.5, 0.21875, ((0, 8),))
    query_bias = normal_values(key_list[10], (D,), 0.5, 3.0, ((0, 8),))
    key_weight = normal_values(key_list[11], (D, D), D ** -0.5, 0.21875, ((0, 8),))
    value_weight = normal_values(key_list[12], (D, D), D ** -0.5, 0.21875, ((0, 8),))
    gate_weight = normal_values(key_list[13], (D, D), D ** -0.5, 0.21875, ((0, 8),))
    output_weight = normal_values(key_list[14], (D, D), (max(1, D // 256)) ** -0.5, 3.5, ((0, 8),))
    pair_weight = normal_values(key_list[15], (PAIR, HEADS), PAIR ** -0.5, 0.5, ((0, 8),))
    zero_first = normal_values(key_list[16], (COND, D), COND ** -0.5, 0.3125, ((0, 8),))
    zero_bias_first = jnp.clip(-2.0 + 3.0 * jax.random.uniform(key_list[17], (D,), jnp.float32) ** block_levels(key_list[17], (D,), ((0, 8),), -0.2, 0.2), -2.0, 1.0).astype(jnp.bfloat16)
    gain_second = jnp.clip(1.0 + 0.15 * jax.random.normal(key_list[18], (COND,), jnp.float32), 0.25, 1.75).astype(jnp.bfloat16)
    scale_second = normal_values(key_list[19], (COND, D), COND ** -0.5, 0.3125, ((0, 8),))
    scale_bias_second = normal_values(key_list[20], (D,), 1.0, 4.0, ((0, 8),))
    shift_second = normal_values(key_list[21], (COND, D), COND ** -0.5, 0.3125, ((0, 8),))
    swish_weight = normal_values(key_list[22], (D, HIDDEN_SIZE), D ** -0.5, 0.21875, ((0, 8),))
    linear_weight = normal_values(key_list[23], (D, HIDDEN_SIZE), D ** -0.5, 0.21875, ((0, 8),))
    down_weight = normal_values(key_list[24], (HIDDEN_SIZE, D), (HIDDEN_SIZE // 4) ** -0.5, 0.3125, ((0, 8),))
    zero_second = normal_values(key_list[25], (COND, D), COND ** -0.5, 0.3125, ((0, 8),))
    zero_bias_second = jnp.clip(-2.0 + 3.0 * jax.random.uniform(key_list[26], (D,), jnp.float32) ** block_levels(key_list[26], (D,), ((0, 8),), -0.2, 0.2), -2.0, 1.0).astype(jnp.bfloat16)
    cotangent = normal_values(key_list[27], (SAMPLES, SLOTS, D), 1.0, 6.0, ((0, 8), (1, 4)))
    return {"act": act, "cond": cond, "pair": pair, "struct_of": struct_of, "struct_len": struct_len, "gain_first": gain_first, "scale_first": scale_first, "scale_bias_first": scale_bias_first, "shift_first": shift_first, "query_weight": query_weight, "query_bias": query_bias, "key_weight": key_weight, "value_weight": value_weight, "gate_weight": gate_weight, "output_weight": output_weight, "pair_weight": pair_weight, "zero_first": zero_first, "zero_bias_first": zero_bias_first, "gain_second": gain_second, "scale_second": scale_second, "scale_bias_second": scale_bias_second, "shift_second": shift_second, "swish_weight": swish_weight, "linear_weight": linear_weight, "down_weight": down_weight, "zero_second": zero_second, "zero_bias_second": zero_bias_second, "cotangent": cotangent}


HIGH = lax.Precision.HIGHEST
EPSILON = 1e-05
NEG_BIG = -1000000000.0

@jax.custom_vjp
def low(v):
    return lax.optimization_barrier(v.astype(jnp.bfloat16)).astype(jnp.float32)

@jax.custom_vjp
def low_back(v):
    return v

def low_keep(v):
    return (low(v), None)

def low_pass(kept, grad):
    return (grad,)

def back_keep(v):
    return (v, None)

def back_low(kept, grad):
    return (low(grad),)
low.defvjp(low_keep, low_pass)
low_back.defvjp(back_keep, back_low)

def norm_rows(values):
    centered = values - lax.optimization_barrier(jnp.mean(values, axis=-1, keepdims=True))
    variance = lax.optimization_barrier(jnp.mean(centered * centered, axis=-1, keepdims=True))
    return centered * lax.rsqrt(variance + EPSILON)

def product(left_side, right_side):
    return jnp.einsum('...i,ij->...j', left_side, right_side, precision=HIGH)

def forward(act, cond, pair, struct_of, struct_len, weights):
    gain_first, scale_first, scale_bias_first, shift_first, query_weight, query_bias, key_weight, value_weight, gate_weight, output_weight, pair_weight, zero_first, zero_bias_first, gain_second, scale_second, scale_bias_second, shift_second, swish_weight, linear_weight, down_weight, zero_second, zero_bias_second = weights
    pair_low = low(norm_rows(pair))
    bias_all = low(low_back(jnp.einsum('sijc,ch->shij', pair_low, pair_weight, precision=HIGH)))
    scale_factor = HEAD_DIM ** (-0.5)
    group_size = 4

    def one_group(pieces):
        act_rows, cond_rows, struct_ids = pieces
        in_group = act_rows.shape[0]
        cond_normed = norm_rows(cond_rows)
        cond_first = low(cond_normed * gain_first)
        pre_first = low_back(product(cond_first, scale_first) + scale_bias_first)
        shift_one = low_back(product(cond_first, shift_first))
        adapted = low(jax.nn.sigmoid(pre_first) * norm_rows(act_rows) + shift_one)
        query_rows = low(low_back(product(adapted, query_weight) + query_bias)).reshape(in_group, SLOTS, HEADS, HEAD_DIM)
        key_rows = low(low_back(product(adapted, key_weight))).reshape(in_group, SLOTS, HEADS, HEAD_DIM)
        value_rows = low(low_back(product(adapted, value_weight))).reshape(in_group, SLOTS, HEADS, HEAD_DIM)
        gate_pre = low_back(product(adapted, gate_weight))
        scores = jnp.einsum('gqhd,gkhd->ghqk', query_rows, key_rows, precision=HIGH) * scale_factor + bias_all[struct_ids]
        scores = low_back(scores)
        lengths = struct_len[struct_ids]
        valid_keys = jnp.arange(SLOTS)[None, :] < lengths[:, None]
        scores = jnp.where(valid_keys[:, None, None, :], scores, NEG_BIG)
        attention = jax.nn.softmax(scores, axis=-1)
        attended = jnp.einsum('ghqk,gkhd->gqhd', low(attention), value_rows, precision=HIGH).reshape(in_group, SLOTS, D)
        attended = low(low_back(attended))
        gated_rows = low(jax.nn.sigmoid(gate_pre) * attended)
        branch = low_back(product(gated_rows, output_weight))
        zero_one = jax.nn.sigmoid(low_back(product(cond_rows, zero_first) + zero_bias_first))
        middle = act_rows + zero_one * branch
        cond_second = low(cond_normed * gain_second)
        pre_second = low_back(product(cond_second, scale_second) + scale_bias_second)
        shift_two = low_back(product(cond_second, shift_second))
        adapted_two = low(jax.nn.sigmoid(pre_second) * norm_rows(middle) + shift_two)
        swish_pre = low_back(product(adapted_two, swish_weight))
        linear_pre = low_back(product(adapted_two, linear_weight))
        hidden = low(jax.nn.silu(swish_pre) * linear_pre)
        down_rows = low_back(product(hidden, down_weight))
        zero_two = jax.nn.sigmoid(low_back(product(cond_rows, zero_second) + zero_bias_second))
        return middle + zero_two * down_rows
    groups = act.shape[0] // group_size
    results = lax.map(jax.checkpoint(one_group), (act.reshape(groups, group_size, SLOTS, D), cond.reshape(groups, group_size, SLOTS, COND), struct_of.reshape(groups, group_size)))
    return results.reshape(act.shape)

def reference(act, cond, pair, struct_of, struct_len, gain_first, scale_first, scale_bias_first, shift_first, query_weight, query_bias, key_weight, value_weight, gate_weight, output_weight, pair_weight, zero_first, zero_bias_first, gain_second, scale_second, scale_bias_second, shift_second, swish_weight, linear_weight, down_weight, zero_second, zero_bias_second, cotangent):
    weights = tuple((weight_arg.astype(jnp.float32) for weight_arg in (gain_first, scale_first, scale_bias_first, shift_first, query_weight, query_bias, key_weight, value_weight, gate_weight, output_weight, pair_weight, zero_first, zero_bias_first, gain_second, scale_second, scale_bias_second, shift_second, swish_weight, linear_weight, down_weight, zero_second, zero_bias_second)))

    def run_layer(act_in, cond_in, pair_in, weight_in):
        return forward(act_in, cond_in, pair_in, struct_of, struct_len, weight_in)
    result, pullback = jax.vjp(run_layer, act.astype(jnp.float32), cond.astype(jnp.float32), pair.astype(jnp.float32), weights)
    input_grad, cond_grad, pair_grad, weight_grads = pullback(cotangent.astype(jnp.float32))
    return (result.astype(jnp.bfloat16), input_grad, cond_grad, pair_grad, weight_grads[0], weight_grads[1], weight_grads[2], weight_grads[3], weight_grads[4], weight_grads[5], weight_grads[6], weight_grads[7], weight_grads[8], weight_grads[9], weight_grads[10], weight_grads[11], weight_grads[12], weight_grads[13], weight_grads[14], weight_grads[15], weight_grads[16], weight_grads[17], weight_grads[18], weight_grads[19], weight_grads[20], weight_grads[21])
```

```python
import functools

import jax
import jax.numpy as jnp
from jax import lax
from jax.experimental import pallas as pl
from jax.experimental.pallas import tpu as pltpu
from jax.sharding import PartitionSpec as P

HEAD_DIM = 48
LANES = 128
EPSILON = 1e-05
NEG_BIG = -1000000000.0
F32 = jnp.float32
BF16 = jnp.bfloat16


def norm_rows(values):
    centered = values - jnp.mean(values, axis=-1, keepdims=True)
    variance = jnp.mean(centered * centered, axis=-1, keepdims=True)
    inverse = lax.rsqrt(variance + EPSILON)
    return (centered * inverse, inverse)


def norm_back(normed, inverse, upstream):
    mean_grad = jnp.mean(upstream, axis=-1, keepdims=True)
    mean_cross = jnp.mean(upstream * normed, axis=-1, keepdims=True)
    return inverse * (upstream - mean_grad - normed * mean_cross)


def product(left_side, right_side):
    return lax.dot_general(
        left_side, right_side, (((1,), (0,)), ((), ())), preferred_element_type=F32
    )


def back_product(upstream, right_side):
    return lax.dot_general(
        upstream, right_side, (((1,), (1,)), ((), ())), preferred_element_type=F32
    )


def outer_sum(left_side, upstream):
    return lax.dot_general(
        left_side, upstream, (((0,), (0,)), ((), ())), preferred_element_type=F32
    )


def column_sum(upstream):
    return jnp.sum(upstream.astype(F32), axis=0)


def sigmoid_slope(gate_sig):
    return gate_sig * (1.0 - gate_sig)


def head_windows(width):
    group = LANES * HEAD_DIM // 16
    group = min(group, width)
    windows = []
    for head in range(group // HEAD_DIM):
        first = head * HEAD_DIM
        last = first + HEAD_DIM - 1
        start = first // LANES * LANES
        stop = (last // LANES + 1) * LANES
        windows.append((start, stop - start, first - start))
    return (group, windows)


def head_mask(width, offset):
    lane = lax.broadcasted_iota(jnp.int32, (1, width), 1)
    return (lane >= offset) & (lane < offset + HEAD_DIM)


def dot_nt(left, right):
    return lax.dot_general(left, right, (((1,), (1,)), ((), ())), preferred_element_type=F32)


def dot_nn(left, right):
    return lax.dot_general(left, right, (((1,), (0,)), ((), ())), preferred_element_type=F32)


def dot_tn(left, right):
    return lax.dot_general(left, right, (((0,), (0,)), ((), ())), preferred_element_type=F32)


def attend_kernel(struct_ref, len_ref, q_ref, k_ref, v_ref, bias_ref, out_ref, prob_ref, acc_ref):
    sample = pl.program_id(0)
    group_at = pl.program_id(1)
    length = len_ref[struct_ref[sample]]
    keys = k_ref.shape[1]
    group, windows = head_windows(q_ref.shape[2])
    valid = lax.broadcasted_iota(jnp.int32, (1, keys), 1) < length
    acc_ref[...] = jnp.zeros_like(acc_ref)
    for at, (start, width, offset) in enumerate(windows):
        lanes = slice(start, start + width)
        mask = head_mask(width, offset)
        query = q_ref[0, :, lanes]
        query = jnp.where(mask, query, jnp.zeros_like(query))
        scores = dot_nt(query, k_ref[0, :, lanes]) * HEAD_DIM ** (-0.5) + bias_ref[
            0, at
        ].astype(F32)
        scores = jnp.where(valid, scores, NEG_BIG)
        weights = jnp.exp(scores - jnp.max(scores, axis=1, keepdims=True))
        weights = weights * (1.0 / jnp.sum(weights, axis=1, keepdims=True))
        weights = weights.astype(BF16)
        prob_ref[0, at] = weights
        mixed = dot_nn(weights, v_ref[0, :, lanes])
        acc_ref[:, lanes] += jnp.where(mask, mixed, 0.0)
    out_ref[0] = acc_ref[...].astype(BF16)


def attend(struct_of, struct_len, query, key, value, bias):
    samples, rows, width = query.shape
    keys = key.shape[1]
    heads = bias.shape[1]
    group, windows = head_windows(width)
    each = len(windows)
    return pl.pallas_call(
        attend_kernel,
        out_shape=(
            jax.ShapeDtypeStruct((samples, rows, width), BF16),
            jax.ShapeDtypeStruct((samples, heads, rows, keys), BF16),
        ),
        grid_spec=pltpu.PrefetchScalarGridSpec(
            num_scalar_prefetch=2,
            grid=(samples, heads // each),
            in_specs=[
                pl.BlockSpec((1, rows, group), lambda b, g, s, n: (b, 0, g)),
                pl.BlockSpec((1, keys, group), lambda b, g, s, n: (b, 0, g)),
                pl.BlockSpec((1, keys, group), lambda b, g, s, n: (b, 0, g)),
                pl.BlockSpec((1, each, rows, keys), lambda b, g, s, n: (s[b], g, 0, 0)),
            ],
            out_specs=[
                pl.BlockSpec((1, rows, group), lambda b, g, s, n: (b, 0, g)),
                pl.BlockSpec((1, each, rows, keys), lambda b, g, s, n: (b, g, 0, 0)),
            ],
            scratch_shapes=[pltpu.VMEM((rows, group), F32)],
        ),
        compiler_params=pltpu.CompilerParams(vmem_limit_bytes=48 << 20),
        name="attend",
    )(struct_of, struct_len, query, key, value, bias)


def attend_back_kernel(
    struct_ref, q_ref, k_ref, v_ref, do_ref, prob_ref, dq_ref, dk_ref, dv_ref, bias_ref,
    dq_acc, dk_acc, dv_acc, bias_acc,
):
    samples = q_ref.shape[0]
    structs = bias_ref.shape[0]
    group, windows = head_windows(q_ref.shape[2])
    scale = HEAD_DIM ** (-0.5)
    for sample in range(samples):
        struct = struct_ref[sample]
        dq_acc[...] = jnp.zeros_like(dq_acc)
        dk_acc[...] = jnp.zeros_like(dk_acc)
        dv_acc[...] = jnp.zeros_like(dv_acc)
        for at, (start, width, offset) in enumerate(windows):
            lanes = slice(start, start + width)
            mask = head_mask(width, offset)
            upstream = do_ref[sample, :, lanes]
            upstream = jnp.where(mask, upstream, jnp.zeros_like(upstream))
            query = q_ref[sample, :, lanes]
            query = jnp.where(mask, query, jnp.zeros_like(query))
            low = prob_ref[sample, at]
            weights = low.astype(F32)
            d_weights = dot_nt(upstream, v_ref[sample, :, lanes])
            dv_acc[:, lanes] += dot_tn(low, upstream)
            cross = weights * d_weights
            delta = jnp.sum(cross, axis=1, keepdims=True)
            d_scores = (cross - weights * delta).astype(BF16)
            dq_acc[:, lanes] += jnp.where(mask, dot_nn(d_scores, k_ref[sample, :, lanes]), 0.0)
            dk_acc[:, lanes] += dot_tn(d_scores, query)
            for slab in range(structs):
                part = jnp.where(struct == slab, 1.0, 0.0) * d_scores.astype(F32)
                if sample == 0:
                    bias_acc[slab, at] = part
                elif sample < samples - 1:
                    bias_acc[slab, at] += part
                else:
                    bias_ref[slab, at] = (bias_acc[slab, at] + part).astype(BF16)
        dq_ref[sample] = (dq_acc[...] * scale).astype(BF16)
        dk_ref[sample] = (dk_acc[...] * scale).astype(BF16)
        dv_ref[sample] = dv_acc[...].astype(BF16)


def attend_back(struct_of, structs, query, key, value, upstream, prob):
    samples, rows, width = query.shape
    keys = key.shape[1]
    heads = prob.shape[1]
    group, windows = head_windows(width)
    each = len(windows)
    return pl.pallas_call(
        attend_back_kernel,
        out_shape=(
            jax.ShapeDtypeStruct((samples, rows, width), BF16),
            jax.ShapeDtypeStruct((samples, keys, width), BF16),
            jax.ShapeDtypeStruct((samples, keys, width), BF16),
            jax.ShapeDtypeStruct((structs, heads, rows, keys), BF16),
        ),
        grid_spec=pltpu.PrefetchScalarGridSpec(
            num_scalar_prefetch=1,
            grid=(heads // each,),
            in_specs=[
                pl.BlockSpec((samples, rows, group), lambda g, s: (0, 0, g)),
                pl.BlockSpec((samples, keys, group), lambda g, s: (0, 0, g)),
                pl.BlockSpec((samples, keys, group), lambda g, s: (0, 0, g)),
                pl.BlockSpec((samples, rows, group), lambda g, s: (0, 0, g)),
                pl.BlockSpec((samples, each, rows, keys), lambda g, s: (0, g, 0, 0)),
            ],
            out_specs=[
                pl.BlockSpec((samples, rows, group), lambda g, s: (0, 0, g)),
                pl.BlockSpec((samples, keys, group), lambda g, s: (0, 0, g)),
                pl.BlockSpec((samples, keys, group), lambda g, s: (0, 0, g)),
                pl.BlockSpec((structs, each, rows, keys), lambda g, s: (0, g, 0, 0)),
            ],
            scratch_shapes=[
                pltpu.VMEM((rows, group), F32),
                pltpu.VMEM((keys, group), F32),
                pltpu.VMEM((keys, group), F32),
                pltpu.VMEM((structs, each, rows, keys), F32),
            ],
        ),
        compiler_params=pltpu.CompilerParams(vmem_limit_bytes=60 << 20),
        name="attend_back",
    )(struct_of, query, key, value, upstream, prob)


def pack_rows(pieces, columns):
    return jnp.concatenate([piece.reshape(-1, columns) for piece in pieces], axis=0)


def pack_small(pieces, columns):
    flat = jnp.concatenate([piece.reshape(-1) for piece in pieces])
    rows = -(-flat.shape[0] // columns)
    rows = -(-rows // 8) * 8
    return jnp.pad(flat, (0, rows * columns - flat.shape[0])).reshape(rows, columns)


def unpack_rows(gathered, shapes):
    whole, at = [], 0
    count, _, columns = gathered.shape
    for rows, cols in shapes:
        held = rows * cols // columns
        whole.append(gathered[:, at : at + held].reshape(count * rows, cols))
        at += held
    return whole


def unpack_small(gathered, shapes):
    whole, at = [], 0
    count = gathered.shape[0]
    flat = gathered.reshape(count, -1)
    for shape in shapes:
        size = 1
        for extent in shape:
            size *= extent
        whole.append(flat[:, at : at + size].reshape((count * shape[0],) + shape[1:]))
        at += size
    return whole


def per_device(
    act, cond, pair, struct_of, struct_len,
    gain_first, scale_first, scale_bias_first, shift_first,
    query_weight, query_bias, key_weight, value_weight, gate_weight, output_weight,
    pair_weight, zero_first, zero_bias_first,
    gain_second, scale_second, scale_bias_second, shift_second,
    swish_weight, linear_weight, down_weight, zero_second, zero_bias_second,
    cotangent,
):
    samples, rows, width = act.shape
    cond_width = cond.shape[2]
    total = samples * rows
    structs = pair.shape[0]
    small = (
        gain_first, scale_bias_first, query_bias, zero_bias_first, gain_second,
        scale_bias_second, zero_bias_second, pair_weight,
    )
    early = (scale_first, shift_first, query_weight, key_weight, value_weight, gate_weight)
    late = (
        output_weight, zero_first, scale_second, shift_second, swish_weight, linear_weight,
        down_weight, zero_second,
    )
    small_all = lax.all_gather(pack_small(small, width), "samp", axis=0)
    early_all = lax.all_gather(pack_rows(early, width), "samp", axis=0)
    late_all = lax.all_gather(pack_rows(late, width), "samp", axis=0)
    (gain_one, bias_one, bias_query, bias_zero_one, gain_two, bias_two, bias_zero_two, pair_proj_w) = (
        unpack_small(small_all, [piece.shape for piece in small])
    )
    (w_scale, w_shift, w_query, w_key, w_value, w_gate) = unpack_rows(
        early_all, [piece.shape for piece in early]
    )
    (w_out, w_zero, w_scale_two, w_shift_two, w_swish, w_linear, w_down, w_zero_two) = unpack_rows(
        late_all, [piece.shape for piece in late]
    )

    pair_normed, pair_inverse = norm_rows(pair.astype(F32))
    pair_low = pair_normed.astype(BF16)
    pair_proj = jnp.einsum("sijc,ch->shij", pair_low, pair_proj_w, preferred_element_type=F32)
    bias_all = lax.all_gather(pair_proj.astype(BF16), "samp", axis=3, tiled=True)

    act_rows = act.reshape(total, width).astype(F32)
    cond_low = cond.reshape(total, cond_width)
    act_normed, act_inverse = norm_rows(act_rows)
    cond_normed, cond_inverse = norm_rows(cond_low.astype(F32))
    cond_first = (cond_normed * gain_one.astype(F32)).astype(BF16)
    sig_first = jax.nn.sigmoid(product(cond_first, w_scale) + bias_one.astype(F32))
    adapted = (sig_first * act_normed + product(cond_first, w_shift)).astype(BF16)
    key_rows = product(adapted, w_key).astype(BF16)
    value_rows = product(adapted, w_value).astype(BF16)
    query_rows = (product(adapted, w_query) + bias_query.astype(F32)).astype(BF16)
    gate_sig = jax.nn.sigmoid(product(adapted, w_gate))
    key_value = jnp.stack((key_rows, value_rows)).reshape(2, samples, rows, width)
    key_value = lax.all_gather(key_value, "head", axis=2, tiled=True)
    query_split = query_rows.reshape(samples, rows, width)
    attended, prob = attend(
        struct_of, struct_len, query_split, key_value[0], key_value[1], bias_all
    )
    attn_float = attended.reshape(total, width).astype(F32)

    gated_rows = (gate_sig * attn_float).astype(BF16)
    branch = product(gated_rows, w_out)
    zero_sig_first = jax.nn.sigmoid(product(cond_low, w_zero) + bias_zero_one.astype(F32))
    middle = act_rows + zero_sig_first * branch
    mid_normed, mid_inverse = norm_rows(middle)
    cond_second = (cond_normed * gain_two.astype(F32)).astype(BF16)
    sig_second = jax.nn.sigmoid(product(cond_second, w_scale_two) + bias_two.astype(F32))
    adapted_two = (sig_second * mid_normed + product(cond_second, w_shift_two)).astype(BF16)
    swish_pre = product(adapted_two, w_swish)
    linear_pre = product(adapted_two, w_linear)
    swish_sig = jax.nn.sigmoid(swish_pre)
    hidden = (swish_pre * swish_sig * linear_pre).astype(BF16)
    down_rows = product(hidden, w_down)
    zero_sig_second = jax.nn.sigmoid(product(cond_low, w_zero_two) + bias_zero_two.astype(F32))
    layer_out = (middle + zero_sig_second * down_rows).astype(BF16)

    upstream = cotangent.reshape(total, width).astype(F32)
    d_down = (upstream * zero_sig_second).astype(BF16)
    d_zero_second = (upstream * down_rows * sigmoid_slope(zero_sig_second)).astype(BF16)
    d_hidden = back_product(d_down, w_down)
    d_swish = (
        d_hidden * linear_pre * swish_sig * (1.0 + swish_pre * (1.0 - swish_sig))
    ).astype(BF16)
    d_linear = (d_hidden * swish_pre * swish_sig).astype(BF16)
    d_adapted_two = back_product(d_swish, w_swish) + back_product(d_linear, w_linear)
    d_shift_second = d_adapted_two.astype(BF16)
    d_pre_second = (d_adapted_two * mid_normed * sigmoid_slope(sig_second)).astype(BF16)
    d_cond_second = back_product(d_shift_second, w_shift_two) + back_product(
        d_pre_second, w_scale_two
    )
    d_middle = upstream + norm_back(mid_normed, mid_inverse, d_adapted_two * sig_second)
    d_branch = (d_middle * zero_sig_first).astype(BF16)
    d_zero_first = (d_middle * branch * sigmoid_slope(zero_sig_first)).astype(BF16)
    d_gated = back_product(d_branch, w_out)
    d_gate = (d_gated * attn_float * sigmoid_slope(gate_sig)).astype(BF16)
    d_attended = (d_gated * gate_sig).astype(BF16)

    late_grads = (
        outer_sum(gated_rows, d_branch),
        outer_sum(cond_low, d_zero_first),
        outer_sum(cond_second, d_pre_second),
        outer_sum(cond_second, d_shift_second),
        outer_sum(adapted_two, d_swish),
        outer_sum(adapted_two, d_linear),
        outer_sum(hidden, d_down),
        outer_sum(cond_low, d_zero_second),
    )

    d_query, d_key, d_value, bias_grad = attend_back(
        struct_of, structs, query_split, key_value[0], key_value[1],
        d_attended.reshape(samples, rows, width), prob,
    )
    d_key_value = lax.psum_scatter(
        jnp.stack((d_key, d_value)), "head", scatter_dimension=2, tiled=True
    )
    d_query = d_query.reshape(total, width)
    d_key = d_key_value[0].reshape(total, width)
    d_value = d_key_value[1].reshape(total, width)
    bias_summed = lax.psum_scatter(bias_grad, "samp", scatter_dimension=3, tiled=True)
    pair_weight_grad = jnp.einsum("sijc,shij->ch", pair_low, bias_summed, preferred_element_type=F32)
    pair_upstream = jnp.einsum(
        "shij,ch->sijc", bias_summed, pair_proj_w, preferred_element_type=F32
    )
    pair_grad = norm_back(pair_normed, pair_inverse, pair_upstream)
    d_adapted = (
        back_product(d_query, w_query)
        + back_product(d_key, w_key)
        + back_product(d_value, w_value)
        + back_product(d_gate, w_gate)
    )
    d_shift_first = d_adapted.astype(BF16)
    d_pre_first = (d_adapted * act_normed * sigmoid_slope(sig_first)).astype(BF16)
    d_cond_first = back_product(d_shift_first, w_shift) + back_product(d_pre_first, w_scale)
    input_grad = d_middle + norm_back(act_normed, act_inverse, d_adapted * sig_first)
    d_cond_normed = d_cond_first * gain_one.astype(F32) + d_cond_second * gain_two.astype(F32)
    cond_grad = (
        norm_back(cond_normed, cond_inverse, d_cond_normed)
        + back_product(d_zero_first, w_zero)
        + back_product(d_zero_second, w_zero_two)
    )
    early_grads = (
        outer_sum(cond_first, d_pre_first),
        outer_sum(cond_first, d_shift_first),
        outer_sum(adapted, d_query),
        outer_sum(adapted, d_key),
        outer_sum(adapted, d_value),
        outer_sum(adapted, d_gate),
    )
    small_grads = (
        jnp.sum(d_cond_first * cond_normed, axis=0),
        column_sum(d_pre_first),
        column_sum(d_query),
        column_sum(d_zero_first),
        jnp.sum(d_cond_second * cond_normed, axis=0),
        column_sum(d_pre_second),
        column_sum(d_zero_second),
        pair_weight_grad,
    )
    count = lax.axis_size("samp")

    def pack_grads(grads, shapes):
        pieces = [
            grad.astype(BF16).reshape(count, shape[0] * shape[1] // width, width)
            for grad, shape in zip(grads, shapes)
        ]
        return jnp.concatenate(pieces, axis=1)

    def reduce(packed):
        summed = lax.psum_scatter(packed, "samp", scatter_dimension=0, tiled=True)
        return lax.psum(summed[0], "head").astype(F32)

    late_sum = reduce(pack_grads(late_grads, [piece.shape for piece in late]))
    early_sum = reduce(pack_grads(early_grads, [piece.shape for piece in early]))
    small_flat = jnp.concatenate(
        [grad.astype(BF16).reshape(count, -1) for grad in small_grads], axis=1
    )
    small_sum = lax.psum(
        lax.psum_scatter(small_flat, "samp", scatter_dimension=0, tiled=True), "head"
    ).astype(F32)
    (g_out, g_zero, g_scale_two, g_shift_two, g_swish, g_linear, g_down, g_zero_two) = unpack_rows(
        late_sum[None], [piece.shape for piece in late]
    )
    (g_scale, g_shift, g_query, g_key, g_value, g_gate) = unpack_rows(
        early_sum[None], [piece.shape for piece in early]
    )
    (g_gain, g_bias, g_bias_query, g_bias_zero, g_gain_two, g_bias_two, g_bias_zero_two, g_pair) = (
        unpack_small(small_sum, [piece.shape for piece in small])
    )
    return (
        layer_out.reshape(act.shape), input_grad.reshape(act.shape), cond_grad.reshape(cond.shape),
        pair_grad, g_gain, g_scale, g_bias, g_shift, g_query, g_bias_query, g_key, g_value, g_gate,
        g_out, g_pair, g_zero, g_bias_zero, g_gain_two, g_scale_two, g_bias_two, g_shift_two,
        g_swish, g_linear, g_down, g_zero_two, g_bias_zero_two,
    )


def solution(mesh):
    tokens = P("samp", "head", None)
    pairs = P(None, "head", "samp", None)
    vector = P("samp")
    matrix = P("samp", None)
    weights = (
        vector, matrix, vector, matrix, matrix, vector, matrix, matrix, matrix, matrix, matrix,
        matrix, vector, vector, matrix, vector, matrix, matrix, matrix, matrix, matrix, vector,
    )
    return jax.shard_map(
        per_device,
        mesh=mesh,
        in_specs=(tokens, tokens, pairs, vector, P()) + weights + (tokens,),
        out_specs=(tokens, tokens, tokens, pairs) + weights,
        check_vma=False,
    )
```

```python
import functools

import jax
import jax.numpy as jnp
from jax import lax
from jax.experimental import pallas as pl
from jax.experimental.pallas import tpu as pltpu
from jax.sharding import PartitionSpec as P

HEAD_DIM = 48
LANES = 128
MAIN = 64
KEY_LANES = 640
MESH = pl.DeviceIdType.MESH
EPSILON = 1e-05
NEG_BIG = -1000000000.0
F32 = jnp.float32
BF16 = jnp.bfloat16


def norm_rows(values):
    centered = values - jnp.mean(values, axis=-1, keepdims=True)
    variance = jnp.mean(centered * centered, axis=-1, keepdims=True)
    inverse = lax.rsqrt(variance + EPSILON)
    return (centered * inverse, inverse)


def norm_back(normed, inverse, upstream):
    mean_grad = jnp.mean(upstream, axis=-1, keepdims=True)
    mean_cross = jnp.mean(upstream * normed, axis=-1, keepdims=True)
    return inverse * (upstream - mean_grad - normed * mean_cross)


def product(left_side, right_side):
    return lax.dot_general(
        left_side, right_side, (((1,), (0,)), ((), ())), preferred_element_type=F32
    )


def back_product(upstream, right_side):
    return lax.dot_general(
        upstream, right_side, (((1,), (1,)), ((), ())), preferred_element_type=F32
    )


def outer_sum(left_side, upstream):
    return lax.dot_general(
        left_side, upstream, (((0,), (0,)), ((), ())), preferred_element_type=F32
    )


def column_sum(upstream):
    return jnp.sum(upstream.astype(F32), axis=0)


def sigmoid_slope(gate_sig):
    return gate_sig * (1.0 - gate_sig)


def head_windows(width):
    group = LANES * HEAD_DIM // 16
    group = min(group, width)
    windows = []
    for head in range(group // HEAD_DIM):
        first = head * HEAD_DIM
        last = first + HEAD_DIM - 1
        start = first // LANES * LANES
        stop = (last // LANES + 1) * LANES
        windows.append((start, stop - start, first - start))
    return (group, windows)


def head_mask(width, offset):
    lane = lax.broadcasted_iota(jnp.int32, (1, width), 1)
    return (lane >= offset) & (lane < offset + HEAD_DIM)


def dot_nt(left, right):
    return lax.dot_general(left, right, (((1,), (1,)), ((), ())), preferred_element_type=F32)


def dot_nn(left, right):
    return lax.dot_general(left, right, (((1,), (0,)), ((), ())), preferred_element_type=F32)


def dot_tn(left, right):
    return lax.dot_general(left, right, (((0,), (0,)), ((), ())), preferred_element_type=F32)


def key_rows_order(rows, block):
    pieces = rows.shape[1] // block
    main = [rows[:, at * block : at * block + MAIN] for at in range(pieces)]
    tail = [rows[:, at * block + MAIN : (at + 1) * block] for at in range(pieces)]
    return jnp.concatenate(main + tail, axis=1)


def key_rows_back(rows, block):
    pieces = rows.shape[1] // block
    tail = block - MAIN
    parts = []
    for at in range(pieces):
        parts.append(rows[:, at * MAIN : (at + 1) * MAIN])
        parts.append(rows[:, pieces * MAIN + at * tail : pieces * MAIN + (at + 1) * tail])
    return jnp.concatenate(parts, axis=1)


def pack_bias(bias):
    structs, heads, rows, block = bias.shape
    main = bias[..., :MAIN].reshape(structs, heads // 2, 2, rows, MAIN)
    main = main.transpose(0, 1, 3, 2, 4).reshape(-1, rows, LANES)
    tail = bias[..., MAIN:].transpose(0, 2, 1, 3).reshape(structs, rows, -1)
    tail = jnp.pad(tail, ((0, 0), (0, 0), (0, LANES - tail.shape[2])))
    return jnp.concatenate((main, tail), axis=0)


def unpack_bias(packed, structs, heads):
    rows = packed.shape[1]
    pairs = structs * heads // 2
    main = packed[:pairs].reshape(structs, heads // 2, rows, 2, MAIN)
    main = main.transpose(0, 1, 3, 2, 4).reshape(structs, heads, rows, MAIN)
    tail = packed[pairs:, :, :MAIN].reshape(structs, rows, heads, -1).transpose(0, 2, 1, 3)
    return jnp.concatenate((main, tail), axis=3)


def tail_switch(count, heads, tail):
    lanes = count * heads * tail
    source = lax.broadcasted_iota(jnp.int32, (lanes, lanes), 0)
    target = lax.broadcasted_iota(jnp.int32, (lanes, lanes), 1)
    owner = source // (heads * tail)
    head = source // tail % heads
    spot = head * (count * tail) + owner * tail + source % tail
    return jnp.where(spot == target, 1.0, 0.0).astype(BF16)


def swap_halves(tile):
    return pltpu.roll(tile, MAIN, 1)


def low_half(tile):
    return lax.broadcasted_iota(jnp.int32, tile.shape, 1) < MAIN


def key_places(count, block):
    lane = lax.broadcasted_iota(jnp.int32, (1, KEY_LANES), 1)
    tail = block - MAIN
    spare = lane - count * MAIN
    main_at = lane + tail * (lane // MAIN)
    tail_at = block * (spare // tail) + MAIN + spare % tail
    past = jnp.where(spare < count * tail, tail_at, count * block)
    return jnp.where(spare < 0, main_at, past)


def attend_kernel(
    struct_ref, len_ref, q_ref, kv_ref, pack_ref, out_ref, prob_ref, key_ref, value_ref, tail_ref, acc_ref
):
    samples, rows, width = q_ref.shape
    count = pack_ref.shape[0]
    spans = kv_ref.shape[0]
    heads = width // HEAD_DIM
    block = rows * spans // count
    tail = block - MAIN
    structs = pack_ref.shape[1] // (heads // 2 + 1)
    main_rows = rows // block * MAIN
    keys = count * block
    group, windows = head_windows(width)
    switch = tail_switch(count, heads, tail)
    places = key_places(count, block)
    key_ref[keys:] = jnp.zeros_like(key_ref[keys:])
    value_ref[keys:] = jnp.zeros_like(value_ref[keys:])

    def one_sample(sample, carry):
        struct = struct_ref[sample]
        valid = places < len_ref[struct]
        for span in range(spans):
            for which, held in ((0, key_ref), (1, value_ref)):
                held[span * main_rows : (span + 1) * main_rows] = kv_ref[span, which, sample, :main_rows]
                spot = count * MAIN + span * (rows - main_rows)
                held[spot : spot + rows - main_rows] = kv_ref[span, which, sample, main_rows:]
        tiles = []
        for pair in range(count // 2):
            even = pack_ref[2 * pair, structs * heads // 2 + struct]
            odd = swap_halves(pack_ref[2 * pair + 1, structs * heads // 2 + struct])
            tiles.append(jnp.where(low_half(even), even, odd))
        mixed = dot_nn(jnp.concatenate(tiles, axis=1), switch).astype(BF16)
        for at in range(count // 2):
            tail_ref[at] = mixed[:, at * LANES : (at + 1) * LANES]

        def one_group(place, carry):
            acc_ref[...] = jnp.zeros_like(acc_ref)
            for at, (start, span, offset) in enumerate(windows):
                lanes = pl.ds(pl.multiple_of(place * group + start, LANES), span)
                mask = head_mask(span, offset)
                tile = struct * (heads // 2) + place * (len(windows) // 2) + at // 2
                bias = []
                for pair in range(count // 2):
                    even = pack_ref[2 * pair, tile]
                    odd = pack_ref[2 * pair + 1, tile]
                    if at % 2 == 0:
                        bias.append(jnp.where(low_half(even), even, swap_halves(odd)))
                    else:
                        bias.append(jnp.where(low_half(even), swap_halves(even), odd))
                per_tile = LANES // (count * tail)
                rest = tail_ref[place * (len(windows) // per_tile) + at // per_tile]
                turn = at % per_tile * count * tail
                bias.append(pltpu.roll(rest, LANES - turn, 1) if turn else rest)
                query = q_ref[sample, :, lanes]
                query = jnp.where(mask, query, jnp.zeros_like(query))
                scores = dot_nt(query, key_ref[:, lanes]) * HEAD_DIM ** (-0.5) + jnp.concatenate(
                    bias, axis=1
                ).astype(F32)
                scores = jnp.where(valid, scores, NEG_BIG)
                weights = jnp.exp(scores - jnp.max(scores, axis=1, keepdims=True))
                weights = weights * (1.0 / jnp.sum(weights, axis=1, keepdims=True))
                weights = weights.astype(BF16)
                prob_ref[sample, place * len(windows) + at] = weights
                mixed = dot_nn(weights, value_ref[:, lanes])
                within = slice(start, start + span)
                acc_ref[:, within] += jnp.where(mask, mixed, 0.0)
            out_ref[sample, :, pl.ds(pl.multiple_of(place * group, LANES), group)] = acc_ref[
                ...
            ].astype(BF16)
            return carry

        return lax.fori_loop(0, width // group, one_group, carry)

    lax.fori_loop(0, samples, one_sample, 0)


def attend(struct_of, struct_len, query, key_value, packed):
    samples, rows, width = query.shape
    group, windows = head_windows(width)
    count = packed.shape[0]
    heads = width // HEAD_DIM
    vmem = pl.BlockSpec(memory_space=pltpu.VMEM)
    smem = pl.BlockSpec(memory_space=pltpu.SMEM)
    return pl.pallas_call(
        attend_kernel,
        out_shape=(
            jax.ShapeDtypeStruct((samples, rows, width), BF16),
            jax.ShapeDtypeStruct((samples, heads, rows, KEY_LANES), BF16),
        ),
        in_specs=[smem, smem, vmem, vmem, vmem],
        out_specs=[vmem, vmem],
        scratch_shapes=[
            pltpu.VMEM((KEY_LANES, width), BF16),
            pltpu.VMEM((KEY_LANES, width), BF16),
            pltpu.VMEM((count // 2, rows, LANES), BF16),
            pltpu.VMEM((rows, group), F32),
        ],
        compiler_params=pltpu.CompilerParams(vmem_limit_bytes=56 << 20),
        name="attend",
    )(struct_of, struct_len, query, key_value, packed)


def flip(index, bit):
    return index + bit - 2 * bit * lax.rem(lax.div(index, bit), 2)


def flips(index, bits):
    spots = [index]
    for bit in bits:
        spots = spots + [flip(spot, bit) for spot in spots]
    return spots


def reduce_orders(count):
    bits = []
    bit = 2
    while bit < count:
        bits.append(bit)
        bit *= 2
    half = len(bits) // 2
    return ([1] + bits, [1] + bits[half:] + bits[:half])


def greet(partners):
    barrier = pltpu.get_barrier_semaphore()
    for partner in partners:
        pl.semaphore_signal(barrier, inc=1, device_id=partner, device_id_type=MESH)
    pl.semaphore_wait(barrier, len(partners))


def send(source, target, send_sem, recv_sem, device):
    return pltpu.make_async_remote_copy(
        src_ref=source, dst_ref=target, send_sem=send_sem, recv_sem=recv_sem,
        device_id=device, device_id_type=MESH,
    )


def attend_back_kernel(
    struct_ref, q_ref, kv_ref, do_ref, prob_ref, dq_ref, dkv_ref, dpb_ref,
    key_ref, value_ref, dq_acc, dk_acc, dv_acc, first_ref, tail_ref, part_ref, span_ref, pack_ref,
    got_zero, got_one, got_two, span_send, span_recv, pack_send, pack_recv,
):
    samples, rows, width = q_ref.shape
    count = pack_ref.shape[0]
    spans = kv_ref.shape[0]
    heads = width // HEAD_DIM
    block = rows * spans // count
    tail = block - MAIN
    structs = pack_ref.shape[1] // (heads // 2 + 1)
    main_rows = rows // block * MAIN
    keys = count * block
    group, windows = head_windows(width)
    scale = HEAD_DIM ** (-0.5)
    me = lax.axis_index("samp")
    my_span = lax.axis_index("head")
    orders = reduce_orders(count)
    others = [lax.rem(my_span + away, spans) for away in range(1, spans)]
    greet(
        [dict(samp=flip(me, bit)) for bit in sorted(orders[0])] + [dict(head=other) for other in others]
    )
    switch = tail_switch(count, heads, tail)
    key_ref[keys:] = jnp.zeros_like(key_ref[keys:])
    value_ref[keys:] = jnp.zeros_like(value_ref[keys:])

    def span_copy(place, sample, away):
        lanes = pl.ds(pl.multiple_of(place * group, LANES), group)
        return send(
            part_ref.at[others[away], :, sample, :, lanes],
            span_ref.at[away, :, sample, :, lanes],
            span_send.at[place, sample, away],
            span_recv.at[place, sample, away],
            dict(head=others[away]),
        )

    def one_group(place, carry):
        for sample in range(samples):
            for span in range(spans):
                for which, held in ((0, key_ref), (1, value_ref)):
                    held[span * main_rows : (span + 1) * main_rows] = kv_ref[
                        span, which, sample, :main_rows, pl.ds(pl.multiple_of(place * group, LANES), group)
                    ]
                    spot = count * MAIN + span * (rows - main_rows)
                    held[spot : spot + rows - main_rows] = kv_ref[
                        span, which, sample, main_rows:, pl.ds(pl.multiple_of(place * group, LANES), group)
                    ]
            dq_acc[...] = jnp.zeros_like(dq_acc)
            dk_acc[...] = jnp.zeros_like(dk_acc)
            dv_acc[...] = jnp.zeros_like(dv_acc)
            kept = [jnp.where(struct_ref[0] == slab, 1.0, 0.0).astype(BF16) for slab in range(structs)]
            added = [jnp.where(struct_ref[1] == slab, 1.0, 0.0).astype(BF16) for slab in range(structs)]
            even_scores = None
            for at, (start, span, offset) in enumerate(windows):
                lanes = pl.ds(pl.multiple_of(place * group + start, LANES), span)
                within = slice(start, start + span)
                mask = head_mask(span, offset)
                upstream = do_ref[sample, :, lanes]
                upstream = jnp.where(mask, upstream, jnp.zeros_like(upstream))
                query = q_ref[sample, :, lanes]
                query = jnp.where(mask, query, jnp.zeros_like(query))
                low = prob_ref[sample, place * len(windows) + at]
                weights = low.astype(F32)
                d_weights = dot_nt(upstream, value_ref[:, within])
                dv_acc[:, within] += dot_tn(low[:, :keys], upstream)
                cross = weights * d_weights
                delta = jnp.sum(cross, axis=1, keepdims=True)
                d_scores = (cross - weights * delta).astype(BF16)
                dq_acc[:, within] += jnp.where(mask, dot_nn(d_scores, key_ref[:, within]), 0.0)
                dk_acc[:, within] += dot_tn(d_scores[:, :keys], query)
                per_tile = LANES // (count * tail)
                turn = at % per_tile * count * tail
                rest = d_scores[:, count * MAIN :]
                rest = pltpu.roll(rest, turn, 1) if turn else rest
                spot = place * (len(windows) // per_tile) + at // per_tile
                if turn:
                    tail_ref[sample, spot] += rest
                else:
                    tail_ref[sample, spot] = rest
                if at % 2 == 0:
                    even_scores = d_scores
                    continue
                for pair in range(count // 2):
                    even = even_scores[:, pair * LANES : (pair + 1) * LANES]
                    odd = d_scores[:, pair * LANES : (pair + 1) * LANES]
                    low_tile = jnp.where(low_half(even), even, swap_halves(odd))
                    high_tile = jnp.where(low_half(even), swap_halves(even), odd)
                    for side, tile in ((0, low_tile), (1, high_tile)):
                        owner = 2 * pair + side
                        if sample == 0:
                            first_ref[at // 2, owner] = tile
                            continue
                        old = first_ref[at // 2, owner]
                        for slab in range(structs):
                            spot = slab * (heads // 2) + place * (len(windows) // 2) + at // 2
                            pack_ref[owner, spot] = old * kept[slab] + tile * added[slab]
            lanes = pl.ds(pl.multiple_of(place * group, LANES), group)
            dq_ref[sample, :, lanes] = (dq_acc[...] * scale).astype(BF16)
            for span in range(spans):
                spot = count * MAIN + span * (rows - main_rows)
                for which, total, factor in ((0, dk_acc, scale), (1, dv_acc, 1.0)):
                    part_ref[span, which, sample, :main_rows, lanes] = (
                        total[span * main_rows : (span + 1) * main_rows] * factor
                    ).astype(BF16)
                    part_ref[span, which, sample, main_rows:, lanes] = (
                        total[spot : spot + rows - main_rows] * factor
                    ).astype(BF16)
            for away in range(spans - 1):
                span_copy(place, sample, away).start()
        return carry

    lax.fori_loop(0, width // group, one_group, 0)

    mixed = []
    for sample in range(samples):
        whole = jnp.concatenate([tail_ref[sample, at] for at in range(count // 2)], axis=1)
        mixed.append(dot_nt(whole, switch))
    for pair in range(count // 2):
        tiles = [part[:, pair * LANES : (pair + 1) * LANES] for part in mixed]
        for slab in range(structs):
            both = jnp.zeros_like(tiles[0])
            for sample in range(samples):
                both = both + jnp.where(struct_ref[sample] == slab, tiles[sample], 0.0)
            spot = structs * heads // 2 + slab
            pack_ref[2 * pair, spot] = jnp.where(low_half(both), both, 0.0).astype(BF16)
            pack_ref[2 * pair + 1, spot] = jnp.where(low_half(both), swap_halves(both), 0.0).astype(BF16)

    tiles = pack_ref.shape[1]
    halves = (pl.ds(0, tiles // 2), pl.ds(tiles // 2, tiles - tiles // 2))
    bounds = ((0, tiles // 2), (tiles // 2, tiles))
    landing = (got_zero, got_one, got_two)

    def stage_copies(step, half):
        order = orders[half]
        kept = flips(me, order[step + 1 :])
        return [
            send(
                pack_ref.at[flip(spot, order[step]), halves[half]],
                landing[step].at[at, halves[half]],
                pack_send.at[step, half, at],
                pack_recv.at[step, half, at],
                dict(samp=flip(me, order[step])),
            )
            for at, spot in enumerate(kept)
        ]

    flights = [[stage_copies(step, half) for half in range(2)] for step in range(len(orders[0]))]
    for half in range(2):
        for copy in flights[0][half]:
            copy.start()
    for step in range(len(orders[0])):
        for half in range(2):
            kept = flips(me, orders[half][step + 1 :])
            for at, spot in enumerate(kept):
                flights[step][half][at].wait_recv()

                def add(tile, carry, spot=spot, at=at, step=step):
                    pack_ref[spot, tile] = (
                        pack_ref[spot, tile].astype(F32) + landing[step][at, tile].astype(F32)
                    ).astype(BF16)
                    return carry

                lax.fori_loop(bounds[half][0], bounds[half][1], add, 0)
            if step + 1 < len(orders[0]):
                for copy in flights[step + 1][half]:
                    copy.start()

    def out(tile, carry):
        dpb_ref[tile] = pack_ref[me, tile]
        return carry

    lax.fori_loop(0, tiles, out, 0)

    for place in range(width // group):
        for sample in range(samples):
            for away in range(spans - 1):
                span_copy(place, sample, away).wait_recv()
    for which in range(2):
        for sample in range(samples):
            total = part_ref[my_span, which, sample].astype(F32)
            for away in range(spans - 1):
                total += span_ref[away, which, sample].astype(F32)
            dkv_ref[which, sample] = total.astype(BF16)
    for place in range(width // group):
        for sample in range(samples):
            for away in range(spans - 1):
                span_copy(place, sample, away).wait_send()
    for stage in flights:
        for half in stage:
            for copy in half:
                copy.wait_send()


def attend_back(struct_of, structs, query, key_value, upstream, prob, count):
    samples, rows, width = query.shape
    spans = key_value.shape[0]
    heads = width // HEAD_DIM
    group, windows = head_windows(width)
    keys = rows * spans
    tiles = structs * (heads // 2 + 1)
    steps = count.bit_length() - 1
    vmem = pl.BlockSpec(memory_space=pltpu.VMEM)
    smem = pl.BlockSpec(memory_space=pltpu.SMEM)
    return pl.pallas_call(
        attend_back_kernel,
        out_shape=(
            jax.ShapeDtypeStruct((samples, rows, width), BF16),
            jax.ShapeDtypeStruct((2, samples, rows, width), BF16),
            jax.ShapeDtypeStruct((tiles, rows, LANES), BF16),
        ),
        in_specs=[smem, vmem, vmem, vmem, vmem],
        out_specs=[vmem, vmem, vmem],
        scratch_shapes=[
            pltpu.VMEM((KEY_LANES, group), BF16),
            pltpu.VMEM((KEY_LANES, group), BF16),
            pltpu.VMEM((rows, group), F32),
            pltpu.VMEM((keys, group), F32),
            pltpu.VMEM((keys, group), F32),
            pltpu.VMEM((len(windows) // 2, count, rows, LANES), BF16),
            pltpu.VMEM((samples, count // 2, rows, LANES), BF16),
            pltpu.VMEM((spans, 2, samples, rows, width), BF16),
            pltpu.VMEM((spans - 1, 2, samples, rows, width), BF16),
            pltpu.VMEM((count, tiles, rows, LANES), BF16),
            pltpu.VMEM((count // 2, tiles, rows, LANES), BF16),
            pltpu.VMEM((count // 4, tiles, rows, LANES), BF16),
            pltpu.VMEM((count // 8, tiles, rows, LANES), BF16),
            pltpu.SemaphoreType.DMA((width // group, samples, spans - 1)),
            pltpu.SemaphoreType.DMA((width // group, samples, spans - 1)),
            pltpu.SemaphoreType.DMA((steps, 2, count // 2)),
            pltpu.SemaphoreType.DMA((steps, 2, count // 2)),
        ],
        compiler_params=pltpu.CompilerParams(
            vmem_limit_bytes=60 << 20, collective_id=1, has_side_effects=True
        ),
        name="attend_back",
    )(struct_of, query, key_value, upstream, prob)


def pack_rows(pieces, columns):
    return jnp.concatenate([piece.reshape(-1, columns) for piece in pieces], axis=0)


def pack_small(pieces, columns):
    flat = jnp.concatenate([piece.reshape(-1) for piece in pieces])
    rows = -(-flat.shape[0] // columns)
    rows = -(-rows // 8) * 8
    return jnp.pad(flat, (0, rows * columns - flat.shape[0])).reshape(rows, columns)


def unpack_rows(gathered, shapes):
    whole, at = [], 0
    count, _, columns = gathered.shape
    for rows, cols in shapes:
        held = rows * cols // columns
        whole.append(gathered[:, at : at + held].reshape(count * rows, cols))
        at += held
    return whole


def unpack_small(gathered, shapes):
    whole, at = [], 0
    count = gathered.shape[0]
    flat = gathered.reshape(count, -1)
    for shape in shapes:
        size = 1
        for extent in shape:
            size *= extent
        whole.append(flat[:, at : at + size].reshape((count * shape[0],) + shape[1:]))
        at += size
    return whole


def plain_kernel(struct_ref, len_ref, q_ref, k_ref, v_ref, bias_ref, out_ref, prob_ref, acc_ref):
    sample = pl.program_id(0)
    group_at = pl.program_id(1)
    length = len_ref[struct_ref[sample]]
    keys = k_ref.shape[1]
    group, windows = head_windows(q_ref.shape[2])
    valid = lax.broadcasted_iota(jnp.int32, (1, keys), 1) < length
    acc_ref[...] = jnp.zeros_like(acc_ref)
    for at, (start, width, offset) in enumerate(windows):
        lanes = slice(start, start + width)
        mask = head_mask(width, offset)
        query = q_ref[0, :, lanes]
        query = jnp.where(mask, query, jnp.zeros_like(query))
        scores = dot_nt(query, k_ref[0, :, lanes]) * HEAD_DIM ** (-0.5) + bias_ref[
            0, at
        ].astype(F32)
        scores = jnp.where(valid, scores, NEG_BIG)
        weights = jnp.exp(scores - jnp.max(scores, axis=1, keepdims=True))
        weights = weights * (1.0 / jnp.sum(weights, axis=1, keepdims=True))
        weights = weights.astype(BF16)
        prob_ref[0, at] = weights
        mixed = dot_nn(weights, v_ref[0, :, lanes])
        acc_ref[:, lanes] += jnp.where(mask, mixed, 0.0)
    out_ref[0] = acc_ref[...].astype(BF16)


def plain(struct_of, struct_len, query, key, value, bias):
    samples, rows, width = query.shape
    keys = key.shape[1]
    heads = bias.shape[1]
    group, windows = head_windows(width)
    each = len(windows)
    return pl.pallas_call(
        plain_kernel,
        out_shape=(
            jax.ShapeDtypeStruct((samples, rows, width), BF16),
            jax.ShapeDtypeStruct((samples, heads, rows, keys), BF16),
        ),
        grid_spec=pltpu.PrefetchScalarGridSpec(
            num_scalar_prefetch=2,
            grid=(samples, heads // each),
            in_specs=[
                pl.BlockSpec((1, rows, group), lambda b, g, s, n: (b, 0, g)),
                pl.BlockSpec((1, keys, group), lambda b, g, s, n: (b, 0, g)),
                pl.BlockSpec((1, keys, group), lambda b, g, s, n: (b, 0, g)),
                pl.BlockSpec((1, each, rows, keys), lambda b, g, s, n: (s[b], g, 0, 0)),
            ],
            out_specs=[
                pl.BlockSpec((1, rows, group), lambda b, g, s, n: (b, 0, g)),
                pl.BlockSpec((1, each, rows, keys), lambda b, g, s, n: (b, g, 0, 0)),
            ],
            scratch_shapes=[pltpu.VMEM((rows, group), F32)],
        ),
        compiler_params=pltpu.CompilerParams(vmem_limit_bytes=48 << 20),
        name="plain",
    )(struct_of, struct_len, query, key, value, bias)


def plain_back_kernel(
    struct_ref, q_ref, k_ref, v_ref, do_ref, prob_ref, dq_ref, dk_ref, dv_ref, bias_ref,
    dq_acc, dk_acc, dv_acc, bias_acc,
):
    samples = q_ref.shape[0]
    structs = bias_ref.shape[0]
    group, windows = head_windows(q_ref.shape[2])
    scale = HEAD_DIM ** (-0.5)
    for sample in range(samples):
        struct = struct_ref[sample]
        dq_acc[...] = jnp.zeros_like(dq_acc)
        dk_acc[...] = jnp.zeros_like(dk_acc)
        dv_acc[...] = jnp.zeros_like(dv_acc)
        for at, (start, width, offset) in enumerate(windows):
            lanes = slice(start, start + width)
            mask = head_mask(width, offset)
            upstream = do_ref[sample, :, lanes]
            upstream = jnp.where(mask, upstream, jnp.zeros_like(upstream))
            query = q_ref[sample, :, lanes]
            query = jnp.where(mask, query, jnp.zeros_like(query))
            low = prob_ref[sample, at]
            weights = low.astype(F32)
            d_weights = dot_nt(upstream, v_ref[sample, :, lanes])
            dv_acc[:, lanes] += dot_tn(low, upstream)
            cross = weights * d_weights
            delta = jnp.sum(cross, axis=1, keepdims=True)
            d_scores = (cross - weights * delta).astype(BF16)
            dq_acc[:, lanes] += jnp.where(mask, dot_nn(d_scores, k_ref[sample, :, lanes]), 0.0)
            dk_acc[:, lanes] += dot_tn(d_scores, query)
            for slab in range(structs):
                part = jnp.where(struct == slab, 1.0, 0.0) * d_scores.astype(F32)
                if sample == 0:
                    bias_acc[slab, at] = part
                elif sample < samples - 1:
                    bias_acc[slab, at] += part
                else:
                    bias_ref[slab, at] = (bias_acc[slab, at] + part).astype(BF16)
        dq_ref[sample] = (dq_acc[...] * scale).astype(BF16)
        dk_ref[sample] = (dk_acc[...] * scale).astype(BF16)
        dv_ref[sample] = dv_acc[...].astype(BF16)


def plain_back(struct_of, structs, query, key, value, upstream, prob):
    samples, rows, width = query.shape
    keys = key.shape[1]
    heads = prob.shape[1]
    group, windows = head_windows(width)
    each = len(windows)
    return pl.pallas_call(
        plain_back_kernel,
        out_shape=(
            jax.ShapeDtypeStruct((samples, rows, width), BF16),
            jax.ShapeDtypeStruct((samples, keys, width), BF16),
            jax.ShapeDtypeStruct((samples, keys, width), BF16),
            jax.ShapeDtypeStruct((structs, heads, rows, keys), BF16),
        ),
        grid_spec=pltpu.PrefetchScalarGridSpec(
            num_scalar_prefetch=1,
            grid=(heads // each,),
            in_specs=[
                pl.BlockSpec((samples, rows, group), lambda g, s: (0, 0, g)),
                pl.BlockSpec((samples, keys, group), lambda g, s: (0, 0, g)),
                pl.BlockSpec((samples, keys, group), lambda g, s: (0, 0, g)),
                pl.BlockSpec((samples, rows, group), lambda g, s: (0, 0, g)),
                pl.BlockSpec((samples, each, rows, keys), lambda g, s: (0, g, 0, 0)),
            ],
            out_specs=[
                pl.BlockSpec((samples, rows, group), lambda g, s: (0, 0, g)),
                pl.BlockSpec((samples, keys, group), lambda g, s: (0, 0, g)),
                pl.BlockSpec((samples, keys, group), lambda g, s: (0, 0, g)),
                pl.BlockSpec((structs, each, rows, keys), lambda g, s: (0, g, 0, 0)),
            ],
            scratch_shapes=[
                pltpu.VMEM((rows, group), F32),
                pltpu.VMEM((keys, group), F32),
                pltpu.VMEM((keys, group), F32),
                pltpu.VMEM((structs, each, rows, keys), F32),
            ],
        ),
        compiler_params=pltpu.CompilerParams(vmem_limit_bytes=60 << 20),
        name="plain_back",
    )(struct_of, query, key, value, upstream, prob)


def plain_device(
    act, cond, pair, struct_of, struct_len,
    gain_first, scale_first, scale_bias_first, shift_first,
    query_weight, query_bias, key_weight, value_weight, gate_weight, output_weight,
    pair_weight, zero_first, zero_bias_first,
    gain_second, scale_second, scale_bias_second, shift_second,
    swish_weight, linear_weight, down_weight, zero_second, zero_bias_second,
    cotangent,
):
    samples, rows, width = act.shape
    cond_width = cond.shape[2]
    total = samples * rows
    structs = pair.shape[0]
    small = (
        gain_first, scale_bias_first, query_bias, zero_bias_first, gain_second,
        scale_bias_second, zero_bias_second, pair_weight,
    )
    early = (scale_first, shift_first, query_weight, key_weight, value_weight, gate_weight)
    late = (
        output_weight, zero_first, scale_second, shift_second, swish_weight, linear_weight,
        down_weight, zero_second,
    )
    small_all = lax.all_gather(pack_small(small, width), "samp", axis=0)
    early_all = lax.all_gather(pack_rows(early, width), "samp", axis=0)
    late_all = lax.all_gather(pack_rows(late, width), "samp", axis=0)
    (gain_one, bias_one, bias_query, bias_zero_one, gain_two, bias_two, bias_zero_two, pair_proj_w) = (
        unpack_small(small_all, [piece.shape for piece in small])
    )
    (w_scale, w_shift, w_query, w_key, w_value, w_gate) = unpack_rows(
        early_all, [piece.shape for piece in early]
    )
    (w_out, w_zero, w_scale_two, w_shift_two, w_swish, w_linear, w_down, w_zero_two) = unpack_rows(
        late_all, [piece.shape for piece in late]
    )

    pair_normed, pair_inverse = norm_rows(pair.astype(F32))
    pair_low = pair_normed.astype(BF16)
    pair_proj = jnp.einsum("sijc,ch->shij", pair_low, pair_proj_w, preferred_element_type=F32)
    bias_all = lax.all_gather(pair_proj.astype(BF16), "samp", axis=3, tiled=True)

    act_rows = act.reshape(total, width).astype(F32)
    cond_low = cond.reshape(total, cond_width)
    act_normed, act_inverse = norm_rows(act_rows)
    cond_normed, cond_inverse = norm_rows(cond_low.astype(F32))
    cond_first = (cond_normed * gain_one.astype(F32)).astype(BF16)
    sig_first = jax.nn.sigmoid(product(cond_first, w_scale) + bias_one.astype(F32))
    adapted = (sig_first * act_normed + product(cond_first, w_shift)).astype(BF16)
    key_rows = product(adapted, w_key).astype(BF16)
    value_rows = product(adapted, w_value).astype(BF16)
    query_rows = (product(adapted, w_query) + bias_query.astype(F32)).astype(BF16)
    gate_sig = jax.nn.sigmoid(product(adapted, w_gate))
    key_value = jnp.stack((key_rows, value_rows)).reshape(2, samples, rows, width)
    key_value = lax.all_gather(key_value, "head", axis=2, tiled=True)
    query_split = query_rows.reshape(samples, rows, width)
    attended, prob = plain(
        struct_of, struct_len, query_split, key_value[0], key_value[1], bias_all
    )
    attn_float = attended.reshape(total, width).astype(F32)

    gated_rows = (gate_sig * attn_float).astype(BF16)
    branch = product(gated_rows, w_out)
    zero_sig_first = jax.nn.sigmoid(product(cond_low, w_zero) + bias_zero_one.astype(F32))
    middle = act_rows + zero_sig_first * branch
    mid_normed, mid_inverse = norm_rows(middle)
    cond_second = (cond_normed * gain_two.astype(F32)).astype(BF16)
    sig_second = jax.nn.sigmoid(product(cond_second, w_scale_two) + bias_two.astype(F32))
    adapted_two = (sig_second * mid_normed + product(cond_second, w_shift_two)).astype(BF16)
    swish_pre = product(adapted_two, w_swish)
    linear_pre = product(adapted_two, w_linear)
    swish_sig = jax.nn.sigmoid(swish_pre)
    hidden = (swish_pre * swish_sig * linear_pre).astype(BF16)
    down_rows = product(hidden, w_down)
    zero_sig_second = jax.nn.sigmoid(product(cond_low, w_zero_two) + bias_zero_two.astype(F32))
    layer_out = (middle + zero_sig_second * down_rows).astype(BF16)

    upstream = cotangent.reshape(total, width).astype(F32)
    d_down = (upstream * zero_sig_second).astype(BF16)
    d_zero_second = (upstream * down_rows * sigmoid_slope(zero_sig_second)).astype(BF16)
    d_hidden = back_product(d_down, w_down)
    d_swish = (
        d_hidden * linear_pre * swish_sig * (1.0 + swish_pre * (1.0 - swish_sig))
    ).astype(BF16)
    d_linear = (d_hidden * swish_pre * swish_sig).astype(BF16)
    d_adapted_two = back_product(d_swish, w_swish) + back_product(d_linear, w_linear)
    d_shift_second = d_adapted_two.astype(BF16)
    d_pre_second = (d_adapted_two * mid_normed * sigmoid_slope(sig_second)).astype(BF16)
    d_cond_second = back_product(d_shift_second, w_shift_two) + back_product(
        d_pre_second, w_scale_two
    )
    d_middle = upstream + norm_back(mid_normed, mid_inverse, d_adapted_two * sig_second)
    d_branch = (d_middle * zero_sig_first).astype(BF16)
    d_zero_first = (d_middle * branch * sigmoid_slope(zero_sig_first)).astype(BF16)
    d_gated = back_product(d_branch, w_out)
    d_gate = (d_gated * attn_float * sigmoid_slope(gate_sig)).astype(BF16)
    d_attended = (d_gated * gate_sig).astype(BF16)

    late_grads = (
        outer_sum(gated_rows, d_branch),
        outer_sum(cond_low, d_zero_first),
        outer_sum(cond_second, d_pre_second),
        outer_sum(cond_second, d_shift_second),
        outer_sum(adapted_two, d_swish),
        outer_sum(adapted_two, d_linear),
        outer_sum(hidden, d_down),
        outer_sum(cond_low, d_zero_second),
    )

    d_query, d_key, d_value, bias_grad = plain_back(
        struct_of, structs, query_split, key_value[0], key_value[1],
        d_attended.reshape(samples, rows, width), prob,
    )
    d_key_value = lax.psum_scatter(
        jnp.stack((d_key, d_value)), "head", scatter_dimension=2, tiled=True
    )
    d_query = d_query.reshape(total, width)
    d_key = d_key_value[0].reshape(total, width)
    d_value = d_key_value[1].reshape(total, width)
    bias_summed = lax.psum_scatter(bias_grad, "samp", scatter_dimension=3, tiled=True)
    pair_weight_grad = jnp.einsum("sijc,shij->ch", pair_low, bias_summed, preferred_element_type=F32)
    pair_upstream = jnp.einsum(
        "shij,ch->sijc", bias_summed, pair_proj_w, preferred_element_type=F32
    )
    pair_grad = norm_back(pair_normed, pair_inverse, pair_upstream)
    d_adapted = (
        back_product(d_query, w_query)
        + back_product(d_key, w_key)
        + back_product(d_value, w_value)
        + back_product(d_gate, w_gate)
    )
    d_shift_first = d_adapted.astype(BF16)
    d_pre_first = (d_adapted * act_normed * sigmoid_slope(sig_first)).astype(BF16)
    d_cond_first = back_product(d_shift_first, w_shift) + back_product(d_pre_first, w_scale)
    input_grad = d_middle + norm_back(act_normed, act_inverse, d_adapted * sig_first)
    d_cond_normed = d_cond_first * gain_one.astype(F32) + d_cond_second * gain_two.astype(F32)
    cond_grad = (
        norm_back(cond_normed, cond_inverse, d_cond_normed)
        + back_product(d_zero_first, w_zero)
        + back_product(d_zero_second, w_zero_two)
    )
    early_grads = (
        outer_sum(cond_first, d_pre_first),
        outer_sum(cond_first, d_shift_first),
        outer_sum(adapted, d_query),
        outer_sum(adapted, d_key),
        outer_sum(adapted, d_value),
        outer_sum(adapted, d_gate),
    )
    small_grads = (
        jnp.sum(d_cond_first * cond_normed, axis=0),
        column_sum(d_pre_first),
        column_sum(d_query),
        column_sum(d_zero_first),
        jnp.sum(d_cond_second * cond_normed, axis=0),
        column_sum(d_pre_second),
        column_sum(d_zero_second),
        pair_weight_grad,
    )
    count = lax.axis_size("samp")

    def pack_grads(grads, shapes):
        pieces = [
            grad.astype(BF16).reshape(count, shape[0] * shape[1] // width, width)
            for grad, shape in zip(grads, shapes)
        ]
        return jnp.concatenate(pieces, axis=1)

    def reduce(packed):
        summed = lax.psum_scatter(packed, "samp", scatter_dimension=0, tiled=True)
        return lax.psum(summed[0], "head").astype(F32)

    late_sum = reduce(pack_grads(late_grads, [piece.shape for piece in late]))
    early_sum = reduce(pack_grads(early_grads, [piece.shape for piece in early]))
    small_flat = jnp.concatenate(
        [grad.astype(BF16).reshape(count, -1) for grad in small_grads], axis=1
    )
    small_sum = lax.psum(
        lax.psum_scatter(small_flat, "samp", scatter_dimension=0, tiled=True), "head"
    ).astype(F32)
    (g_out, g_zero, g_scale_two, g_shift_two, g_swish, g_linear, g_down, g_zero_two) = unpack_rows(
        late_sum[None], [piece.shape for piece in late]
    )
    (g_scale, g_shift, g_query, g_key, g_value, g_gate) = unpack_rows(
        early_sum[None], [piece.shape for piece in early]
    )
    (g_gain, g_bias, g_bias_query, g_bias_zero, g_gain_two, g_bias_two, g_bias_zero_two, g_pair) = (
        unpack_small(small_sum, [piece.shape for piece in small])
    )
    return (
        layer_out.reshape(act.shape), input_grad.reshape(act.shape), cond_grad.reshape(cond.shape),
        pair_grad, g_gain, g_scale, g_bias, g_shift, g_query, g_bias_query, g_key, g_value, g_gate,
        g_out, g_pair, g_zero, g_bias_zero, g_gain_two, g_scale_two, g_bias_two, g_shift_two,
        g_swish, g_linear, g_down, g_zero_two, g_bias_zero_two,
    )


def per_device(
    act, cond, pair, struct_of, struct_len,
    gain_first, scale_first, scale_bias_first, shift_first,
    query_weight, query_bias, key_weight, value_weight, gate_weight, output_weight,
    pair_weight, zero_first, zero_bias_first,
    gain_second, scale_second, scale_bias_second, shift_second,
    swish_weight, linear_weight, down_weight, zero_second, zero_bias_second,
    cotangent,
):
    samples, rows, width = act.shape
    cond_width = cond.shape[2]
    total = samples * rows
    structs = pair.shape[0]
    block = pair.shape[2]
    count = lax.axis_size("samp")
    small = (
        gain_first, scale_bias_first, query_bias, zero_bias_first, gain_second,
        scale_bias_second, zero_bias_second, pair_weight,
    )
    early = (scale_first, shift_first, query_weight, key_weight, value_weight, gate_weight)
    late = (
        output_weight, zero_first, scale_second, shift_second, swish_weight, linear_weight,
        down_weight, zero_second,
    )
    small_all = lax.all_gather(pack_small(small, width), "samp", axis=0)
    early_all = lax.all_gather(pack_rows(early, width), "samp", axis=0)
    late_all = lax.all_gather(pack_rows(late, width), "samp", axis=0)
    (gain_one, bias_one, bias_query, bias_zero_one, gain_two, bias_two, bias_zero_two, pair_proj_w) = (
        unpack_small(small_all, [piece.shape for piece in small])
    )
    (w_scale, w_shift, w_query, w_key, w_value, w_gate) = unpack_rows(
        early_all, [piece.shape for piece in early]
    )
    (w_out, w_zero, w_scale_two, w_shift_two, w_swish, w_linear, w_down, w_zero_two) = unpack_rows(
        late_all, [piece.shape for piece in late]
    )

    pair_normed, pair_inverse = norm_rows(pair.astype(F32))
    pair_low = pair_normed.astype(BF16)
    pair_proj = jnp.einsum("sijc,ch->shij", pair_low, pair_proj_w, preferred_element_type=F32)
    packed = lax.all_gather(pack_bias(pair_proj.astype(BF16)), "samp", axis=0)

    act_rows = act.reshape(total, width).astype(F32)
    cond_low = cond.reshape(total, cond_width)
    act_normed, act_inverse = norm_rows(act_rows)
    cond_normed, cond_inverse = norm_rows(cond_low.astype(F32))
    cond_first = (cond_normed * gain_one.astype(F32)).astype(BF16)
    sig_first = jax.nn.sigmoid(product(cond_first, w_scale) + bias_one.astype(F32))
    adapted = (sig_first * act_normed + product(cond_first, w_shift)).astype(BF16)
    key_rows = product(adapted, w_key).astype(BF16)
    value_rows = product(adapted, w_value).astype(BF16)
    query_rows = (product(adapted, w_query) + bias_query.astype(F32)).astype(BF16)
    gate_sig = jax.nn.sigmoid(product(adapted, w_gate))
    key_value = jnp.stack(
        [key_rows_order(half.reshape(samples, rows, width), block) for half in (key_rows, value_rows)]
    )
    key_value = lax.all_gather(key_value, "head", axis=0)
    query_split = query_rows.reshape(samples, rows, width)
    attended, prob = attend(struct_of, struct_len, query_split, key_value, packed)
    attn_float = attended.reshape(total, width).astype(F32)

    gated_rows = (gate_sig * attn_float).astype(BF16)
    branch = product(gated_rows, w_out)
    zero_sig_first = jax.nn.sigmoid(product(cond_low, w_zero) + bias_zero_one.astype(F32))
    middle = act_rows + zero_sig_first * branch
    mid_normed, mid_inverse = norm_rows(middle)
    cond_second = (cond_normed * gain_two.astype(F32)).astype(BF16)
    sig_second = jax.nn.sigmoid(product(cond_second, w_scale_two) + bias_two.astype(F32))
    adapted_two = (sig_second * mid_normed + product(cond_second, w_shift_two)).astype(BF16)
    swish_pre = product(adapted_two, w_swish)
    linear_pre = product(adapted_two, w_linear)
    swish_sig = jax.nn.sigmoid(swish_pre)
    hidden = (swish_pre * swish_sig * linear_pre).astype(BF16)
    down_rows = product(hidden, w_down)
    zero_sig_second = jax.nn.sigmoid(product(cond_low, w_zero_two) + bias_zero_two.astype(F32))
    layer_out = (middle + zero_sig_second * down_rows).astype(BF16)

    upstream = cotangent.reshape(total, width).astype(F32)
    d_down = (upstream * zero_sig_second).astype(BF16)
    d_zero_second = (upstream * down_rows * sigmoid_slope(zero_sig_second)).astype(BF16)
    d_hidden = back_product(d_down, w_down)
    d_swish = (
        d_hidden * linear_pre * swish_sig * (1.0 + swish_pre * (1.0 - swish_sig))
    ).astype(BF16)
    d_linear = (d_hidden * swish_pre * swish_sig).astype(BF16)
    d_adapted_two = back_product(d_swish, w_swish) + back_product(d_linear, w_linear)
    d_shift_second = d_adapted_two.astype(BF16)
    d_pre_second = (d_adapted_two * mid_normed * sigmoid_slope(sig_second)).astype(BF16)
    d_cond_second = back_product(d_shift_second, w_shift_two) + back_product(
        d_pre_second, w_scale_two
    )
    d_middle = upstream + norm_back(mid_normed, mid_inverse, d_adapted_two * sig_second)
    d_branch = (d_middle * zero_sig_first).astype(BF16)
    d_zero_first = (d_middle * branch * sigmoid_slope(zero_sig_first)).astype(BF16)
    d_gated = back_product(d_branch, w_out)
    d_gate = (d_gated * attn_float * sigmoid_slope(gate_sig)).astype(BF16)
    d_attended = (d_gated * gate_sig).astype(BF16)

    late_grads = (
        outer_sum(gated_rows, d_branch),
        outer_sum(cond_low, d_zero_first),
        outer_sum(cond_second, d_pre_second),
        outer_sum(cond_second, d_shift_second),
        outer_sum(adapted_two, d_swish),
        outer_sum(adapted_two, d_linear),
        outer_sum(hidden, d_down),
        outer_sum(cond_low, d_zero_second),
    )

    d_query, d_key_value, bias_packed = attend_back(
        struct_of, structs, query_split, key_value, d_attended.reshape(samples, rows, width), prob, count
    )
    d_query = d_query.reshape(total, width)
    d_key = key_rows_back(d_key_value[0], block).reshape(total, width)
    d_value = key_rows_back(d_key_value[1], block).reshape(total, width)
    bias_summed = unpack_bias(bias_packed, structs, width // HEAD_DIM)
    pair_weight_grad = jnp.einsum("sijc,shij->ch", pair_low, bias_summed, preferred_element_type=F32)
    pair_upstream = jnp.einsum(
        "shij,ch->sijc", bias_summed, pair_proj_w, preferred_element_type=F32
    )
    pair_grad = norm_back(pair_normed, pair_inverse, pair_upstream)
    d_adapted = (
        back_product(d_query, w_query)
        + back_product(d_key, w_key)
        + back_product(d_value, w_value)
        + back_product(d_gate, w_gate)
    )
    d_shift_first = d_adapted.astype(BF16)
    d_pre_first = (d_adapted * act_normed * sigmoid_slope(sig_first)).astype(BF16)
    d_cond_first = back_product(d_shift_first, w_shift) + back_product(d_pre_first, w_scale)
    input_grad = d_middle + norm_back(act_normed, act_inverse, d_adapted * sig_first)
    d_cond_normed = d_cond_first * gain_one.astype(F32) + d_cond_second * gain_two.astype(F32)
    cond_grad = (
        norm_back(cond_normed, cond_inverse, d_cond_normed)
        + back_product(d_zero_first, w_zero)
        + back_product(d_zero_second, w_zero_two)
    )
    early_grads = (
        outer_sum(cond_first, d_pre_first),
        outer_sum(cond_first, d_shift_first),
        outer_sum(adapted, d_query),
        outer_sum(adapted, d_key),
        outer_sum(adapted, d_value),
        outer_sum(adapted, d_gate),
    )
    small_grads = (
        jnp.sum(d_cond_first * cond_normed, axis=0),
        column_sum(d_pre_first),
        column_sum(d_query),
        column_sum(d_zero_first),
        jnp.sum(d_cond_second * cond_normed, axis=0),
        column_sum(d_pre_second),
        column_sum(d_zero_second),
        pair_weight_grad,
    )

    def pack_grads(grads, shapes):
        pieces = [
            grad.astype(BF16).reshape(count, shape[0] * shape[1] // width, width)
            for grad, shape in zip(grads, shapes)
        ]
        return jnp.concatenate(pieces, axis=1)

    def reduce(packed):
        summed = lax.psum_scatter(packed, "samp", scatter_dimension=0, tiled=True)
        return lax.psum(summed[0], "head").astype(F32)

    late_sum = reduce(pack_grads(late_grads, [piece.shape for piece in late]))
    early_sum = reduce(pack_grads(early_grads, [piece.shape for piece in early]))
    small_flat = jnp.concatenate(
        [grad.astype(BF16).reshape(count, -1) for grad in small_grads], axis=1
    )
    small_sum = lax.psum(
        lax.psum_scatter(small_flat, "samp", scatter_dimension=0, tiled=True), "head"
    ).astype(F32)
    (g_out, g_zero, g_scale_two, g_shift_two, g_swish, g_linear, g_down, g_zero_two) = unpack_rows(
        late_sum[None], [piece.shape for piece in late]
    )
    (g_scale, g_shift, g_query, g_key, g_value, g_gate) = unpack_rows(
        early_sum[None], [piece.shape for piece in early]
    )
    (g_gain, g_bias, g_bias_query, g_bias_zero, g_gain_two, g_bias_two, g_bias_zero_two, g_pair) = (
        unpack_small(small_sum, [piece.shape for piece in small])
    )
    return (
        layer_out.reshape(act.shape), input_grad.reshape(act.shape), cond_grad.reshape(cond.shape),
        pair_grad, g_gain, g_scale, g_bias, g_shift, g_query, g_bias_query, g_key, g_value, g_gate,
        g_out, g_pair, g_zero, g_bias_zero, g_gain_two, g_scale_two, g_bias_two, g_shift_two,
        g_swish, g_linear, g_down, g_zero_two, g_bias_zero_two,
    )


def fits(mesh, act, pair):
    samples, rows, width = act.shape
    count, spans = mesh.shape["samp"], mesh.shape["head"]
    block = pair.shape[2]
    tail = block - MAIN
    heads = width // HEAD_DIM
    return (
        count == 8
        and samples == 2
        and tail > 0
        and heads * tail == MAIN
        and rows % block == 0
        and rows * spans == block * count
        and rows % 8 == 0
        and block * count <= KEY_LANES
    )


def solution(mesh):
    tokens = P("samp", "head", None)
    pairs = P(None, "head", "samp", None)
    vector = P("samp")
    matrix = P("samp", None)
    weights = (
        vector, matrix, vector, matrix, matrix, vector, matrix, matrix, matrix, matrix, matrix,
        matrix, vector, vector, matrix, vector, matrix, matrix, matrix, matrix, matrix, vector,
    )
    def choose(*arrays):
        body = per_device if fits(mesh, arrays[0], arrays[2]) else plain_device
        return body(*arrays)

    return jax.shard_map(
        choose,
        mesh=mesh,
        in_specs=(tokens, tokens, pairs, vector, P()) + weights + (tokens,),
        out_specs=(tokens, tokens, tokens, pairs) + weights,
        check_vma=False,
    )
```

```python
import functools

import jax
import jax.numpy as jnp
from jax import lax
from jax.experimental import pallas as pl
from jax.experimental.pallas import tpu as pltpu
from jax.sharding import PartitionSpec as P

HEAD_DIM = 48
LANES = 128
MAIN = 64
KEY_LANES = 640
MESH = pl.DeviceIdType.MESH
EPSILON = 1e-05
NEG_BIG = -1000000000.0
F32 = jnp.float32
BF16 = jnp.bfloat16


def norm_rows(values):
    centered = values - jnp.mean(values, axis=-1, keepdims=True)
    variance = jnp.mean(centered * centered, axis=-1, keepdims=True)
    inverse = lax.rsqrt(variance + EPSILON)
    return (centered * inverse, inverse)


def norm_back(normed, inverse, upstream):
    mean_grad = jnp.mean(upstream, axis=-1, keepdims=True)
    mean_cross = jnp.mean(upstream * normed, axis=-1, keepdims=True)
    return inverse * (upstream - mean_grad - normed * mean_cross)


def product(left_side, right_side):
    return lax.dot_general(
        left_side, right_side, (((1,), (0,)), ((), ())), preferred_element_type=F32
    )


def back_product(upstream, right_side):
    return lax.dot_general(
        upstream, right_side, (((1,), (1,)), ((), ())), preferred_element_type=F32
    )


def outer_sum(left_side, upstream):
    return lax.dot_general(
        left_side, upstream, (((0,), (0,)), ((), ())), preferred_element_type=F32
    )


def column_sum(upstream):
    return jnp.sum(upstream.astype(F32), axis=0)


def sigmoid_slope(gate_sig):
    return gate_sig * (1.0 - gate_sig)


def head_windows(width):
    group = LANES * HEAD_DIM // 16
    group = min(group, width)
    windows = []
    for head in range(group // HEAD_DIM):
        first = head * HEAD_DIM
        last = first + HEAD_DIM - 1
        start = first // LANES * LANES
        stop = (last // LANES + 1) * LANES
        windows.append((start, stop - start, first - start))
    return (group, windows)


def head_mask(width, offset):
    lane = lax.broadcasted_iota(jnp.int32, (1, width), 1)
    return (lane >= offset) & (lane < offset + HEAD_DIM)


def dot_nt(left, right):
    return lax.dot_general(left, right, (((1,), (1,)), ((), ())), preferred_element_type=F32)


def dot_nn(left, right):
    return lax.dot_general(left, right, (((1,), (0,)), ((), ())), preferred_element_type=F32)


def dot_tn(left, right):
    return lax.dot_general(left, right, (((0,), (0,)), ((), ())), preferred_element_type=F32)


def key_rows_order(rows, block):
    pieces = rows.shape[1] // block
    main = [rows[:, at * block : at * block + MAIN] for at in range(pieces)]
    tail = [rows[:, at * block + MAIN : (at + 1) * block] for at in range(pieces)]
    return jnp.concatenate(main + tail, axis=1)


def key_rows_back(rows, block):
    pieces = rows.shape[1] // block
    tail = block - MAIN
    parts = []
    for at in range(pieces):
        parts.append(rows[:, at * MAIN : (at + 1) * MAIN])
        parts.append(rows[:, pieces * MAIN + at * tail : pieces * MAIN + (at + 1) * tail])
    return jnp.concatenate(parts, axis=1)


def unpack_bias(packed, structs, heads):
    rows = packed.shape[1]
    pairs = structs * heads // 2
    main = packed[:pairs].reshape(structs, heads // 2, rows, 2, MAIN)
    main = main.transpose(0, 1, 3, 2, 4).reshape(structs, heads, rows, MAIN)
    tail = packed[pairs:, :, :MAIN].reshape(structs, rows, -1, heads).transpose(0, 3, 1, 2)
    return jnp.concatenate((main, tail), axis=3)


def tail_switch(count, heads, tail):
    lanes = count * heads * tail
    source = lax.broadcasted_iota(jnp.int32, (lanes, lanes), 0)
    target = lax.broadcasted_iota(jnp.int32, (lanes, lanes), 1)
    owner = source // (heads * tail)
    head = source % heads
    spot = head * (count * tail) + owner * tail + source // heads % tail
    return jnp.where(spot == target, 1.0, 0.0).astype(BF16)


def swap_halves(tile):
    return pltpu.roll(tile, MAIN, 1)


def low_half(tile):
    return lax.broadcasted_iota(jnp.int32, tile.shape, 1) < MAIN


def key_places(count, block):
    lane = lax.broadcasted_iota(jnp.int32, (1, KEY_LANES), 1)
    tail = block - MAIN
    spare = lane - count * MAIN
    main_at = lane + tail * (lane // MAIN)
    tail_at = block * (spare // tail) + MAIN + spare % tail
    past = jnp.where(spare < count * tail, tail_at, count * block)
    return jnp.where(spare < 0, main_at, past)


def flip(index, bit):
    return index + bit - 2 * bit * lax.rem(lax.div(index, bit), 2)


def flips(index, bits):
    spots = [index]
    for bit in bits:
        spots = spots + [flip(spot, bit) for spot in spots]
    return spots


def reduce_orders(count):
    bits = []
    bit = 2
    while bit < count:
        bits.append(bit)
        bit *= 2
    half = len(bits) // 2
    return ([1] + bits, [1] + bits[half:] + bits[:half])


def greet(partners):
    barrier = pltpu.get_barrier_semaphore()
    for partner in partners:
        pl.semaphore_signal(barrier, inc=1, device_id=partner, device_id_type=MESH)
    pl.semaphore_wait(barrier, len(partners))


def send(source, target, send_sem, recv_sem, device):
    return pltpu.make_async_remote_copy(
        src_ref=source, dst_ref=target, send_sem=send_sem, recv_sem=recv_sem,
        device_id=device, device_id_type=MESH,
    )


def sigmoid(values):
    return 1.0 / (1.0 + jnp.exp(-values))


def one_hot(shape, source_of):
    target = lax.broadcasted_iota(jnp.int32, shape, 0)
    source = lax.broadcasted_iota(jnp.int32, shape, 1)
    return jnp.where(source == source_of(target), 1.0, 0.0).astype(BF16)


def key_row_of(place, block, pieces):
    tail = block - MAIN
    main_at = place // MAIN * block + place % MAIN
    spare = place - pieces * MAIN
    tail_at = spare // tail * block + MAIN + spare % tail
    return jnp.where(place < pieces * MAIN, main_at, tail_at)


def front_kernel(
    struct_ref, len_ref, act_ref, cond_ref, small_ref, pair_ref,
    scale_in, shift_in, key_in, value_in, query_in, gate_in,
    out_ref, prob_ref, adapted_ref, sig_ref, gate_ref, query_ref, kv_ref, full_ref,
    scale_w, shift_w, key_w, value_w, query_w, gate_w,
    small_all, pack_ref, pair_buf, tails_ref, keys_ref, values_ref, tail_ref, acc_ref,
    pair_sem, own_sem, small_send, small_recv, gather_send, gather_recv, pack_send, pack_recv,
    span_send, span_recv,
):
    total, width = act_ref.shape
    samples, rows = prob_ref.shape[0], prob_ref.shape[2]
    count = pack_ref.shape[0]
    spans = kv_ref.shape[0]
    heads = width // HEAD_DIM
    structs = pair_ref.shape[0]
    block = pair_ref.shape[2]
    tail = block - MAIN
    pieces = rows // block
    main_rows = pieces * MAIN
    keys = count * block
    pairs = heads // 2
    group, windows = head_windows(width)
    me = lax.axis_index("samp")
    my_span = lax.axis_index("head")
    reduce_pair = reduce_orders(count)
    orders = [order[1:] + order[:1] for order in reduce_pair]
    bits = sorted(reduce_pair[0])
    steps = len(bits)
    peers = flips(me, bits)

    shards = (scale_in, shift_in, key_in, value_in, query_in, gate_in)
    wholes = (scale_w, shift_w, key_w, value_w, query_w, gate_w)
    owns = [
        pltpu.make_async_copy(shard, whole.at[me], own_sem.at[at])
        for at, (shard, whole) in enumerate(zip(shards, wholes))
    ]
    for copy in owns:
        copy.start()

    def pair_copy(place):
        slot = lax.rem(place, 2)
        struct = lax.div(place, rows // 8)
        first = pl.multiple_of(lax.rem(place, rows // 8) * 8, 8)
        return pltpu.make_async_copy(
            pair_ref.at[struct, pl.ds(first, 8)], pair_buf.at[slot], pair_sem.at[slot]
        )

    pair_copy(0).start()
    small_all[me] = small_ref[...]
    greet(
        [dict(samp=peer) for peer in peers[1:]]
        + [dict(head=lax.rem(my_span + away, spans)) for away in range(1, spans)]
    )
    for at in range(1, count):
        send(
            small_ref, small_all.at[me], small_send.at[at], small_recv.at[at], dict(samp=peers[at])
        ).start()

    def gather_copies(which, step, sending):
        order = orders[which % 2]
        held = flips(me, order[:step])
        copies = []
        for at, spot in enumerate(held):
            slot = spot if sending else flip(spot, order[step])
            copies.append(
                send(
                    wholes[which].at[slot], wholes[which].at[slot],
                    gather_send.at[which, step, at], gather_recv.at[which, step, at],
                    dict(samp=flip(me, order[step])),
                )
            )
        return copies

    def gather_start(pair_at, step):
        for which in (2 * pair_at, 2 * pair_at + 1):
            for copy in gather_copies(which, step, True):
                copy.start()

    def gather_wait(pair_at, step):
        for which in (2 * pair_at, 2 * pair_at + 1):
            for copy in gather_copies(which, step, False):
                copy.wait_recv()

    tiles = pack_ref.shape[1]
    halves = (pl.ds(0, tiles // 2), pl.ds(tiles // 2, tiles - tiles // 2))

    def pack_copies(half, step, sending):
        order = orders[half]
        copies = []
        for at, spot in enumerate(flips(me, order[:step])):
            slot = spot if sending else flip(spot, order[step])
            copies.append(
                send(
                    pack_ref.at[slot, halves[half]], pack_ref.at[slot, halves[half]],
                    pack_send.at[half, step, at], pack_recv.at[half, step, at],
                    dict(samp=flip(me, order[step])),
                )
            )
        return copies

    def pack_start(step):
        for half in range(2):
            for copy in pack_copies(half, step, True):
                copy.start()

    def pack_wait(step):
        for half in range(2):
            for copy in pack_copies(half, step, False):
                copy.wait_recv()

    for copy in owns:
        copy.wait()
    gather_start(0, 0)
    gather_start(1, 0)

    for at in range(1, count):
        send(
            small_ref, small_all.at[peers[at]], small_send.at[at], small_recv.at[at], dict(samp=peers[at])
        ).wait_recv()
    full = small_all[0].astype(F32)
    for at in range(1, count):
        full = full + small_all[at].astype(F32)
    full_ref[...] = full
    project = full[8:, :LANES].astype(BF16)
    swap_rows = one_hot((8 * pairs, 8 * pairs), lambda row: row % 8 * pairs + row // 8)

    def pair_block(place, carry):
        slot = lax.rem(place, 2)
        struct = lax.div(place, rows // 8)
        first = pl.multiple_of(lax.rem(place, rows // 8) * 8, 8)

        @pl.when(place + 1 < structs * (rows // 8))
        def _():
            pair_copy(place + 1).start()

        pair_copy(place).wait()
        values = pair_buf[slot].astype(F32)
        centered = values - jnp.mean(values, axis=2, keepdims=True)
        variance = jnp.mean(centered * centered, axis=2, keepdims=True)
        normed = centered * lax.rsqrt(variance + EPSILON)
        low = normed.astype(BF16)
        rows_of = []
        for at in range(8):
            both = dot_nt(project, low[at, :MAIN])
            wide = jnp.concatenate((both[:pairs], both[pairs:]), axis=1)
            rows_of.append(wide)
        mixed = dot_nn(swap_rows, jnp.concatenate(rows_of, axis=0).astype(BF16))
        for at in range(pairs):
            pack_ref[me, struct * pairs + at, pl.ds(first, 8)] = mixed[at * 8 : (at + 1) * 8].astype(BF16)
        for at in range(tail):
            tails_ref[struct, at, pl.ds(first, 8)] = normed[:, MAIN + at]
        return carry

    blocks = structs * (rows // 8)
    cuts = [blocks * at // 8 for at in range(9)]
    lax.fori_loop(cuts[0], cuts[1], pair_block, 0)
    gather_wait(0, 0)
    gather_start(0, 1)
    lax.fori_loop(cuts[1], cuts[3], pair_block, 0)
    gather_wait(1, 0)
    gather_start(1, 1)
    gather_start(2, 0)
    lax.fori_loop(cuts[3], cuts[5], pair_block, 0)
    gather_wait(0, 1)
    gather_start(0, 2)
    lax.fori_loop(cuts[5], cuts[7], pair_block, 0)
    gather_wait(1, 1)
    gather_start(1, 2)
    lax.fori_loop(cuts[7], cuts[8], pair_block, 0)
    gather_wait(2, 0)
    gather_start(2, 1)

    lane = lax.broadcasted_iota(jnp.int32, (heads, heads), 0)
    other = lax.broadcasted_iota(jnp.int32, (heads, heads), 1)
    natural = jnp.where(other == lane // 2 + lane % 2 * pairs, 1.0, 0.0).astype(BF16)
    in_order = dot_nn(natural, project).astype(BF16)
    for struct in range(structs):
        parts = []
        for at in range(tail):
            parts.append(dot_nt(tails_ref[struct, at].astype(BF16), in_order))
        parts.append(jnp.zeros((rows, LANES - tail * heads), F32))
        pack_ref[me, structs * pairs + struct] = jnp.concatenate(parts, axis=1).astype(BF16)
    pack_start(0)

    gain_one = full[0:1, : cond_ref.shape[1]]
    act_normed, _ = norm_rows(act_ref[...].astype(F32))
    cond_normed, _ = norm_rows(cond_ref[...].astype(F32))
    cond_first = (cond_normed * gain_one).astype(BF16)
    gather_wait(0, 2)
    scale = scale_w[...].reshape(-1, width)
    shift = shift_w[...].reshape(-1, width)
    sig_first = sigmoid(dot_nn(cond_first, scale) + full[1:2])
    adapted = sig_first * act_normed + dot_nn(cond_first, shift)
    sig_ref[...] = sig_first
    adapted_ref[...] = adapted.astype(BF16)
    reorder = one_hot((rows, rows), lambda row: key_row_of(row, block, pieces))
    gather_wait(1, 2)
    for which, whole in ((0, key_w), (1, value_w)):
        for sample in range(samples):
            ordered = dot_nn(
                reorder, adapted[sample * rows : (sample + 1) * rows].astype(BF16)
            ).astype(BF16)
            kv_ref[my_span, which, sample] = dot_nn(ordered, whole[...].reshape(-1, width)).astype(BF16)

    def span_move(way, step, which, sending):
        delta = 1 - 2 * way
        shard = my_span - delta * step if sending else my_span - delta * (step + 1)
        target = my_span + delta
        there = (shard >= 0) & (shard < spans)
        if sending:
            there = there & (target >= 0) & (target < spans)
        copy = send(
            kv_ref.at[shard, which], kv_ref.at[shard, which],
            span_send.at[way, step, which], span_recv.at[way, step, which],
            dict(head=target if sending else my_span - delta),
        )
        return there, copy

    def span_start(step, which):
        for way in range(2):
            there, copy = span_move(way, step, which, True)
            pl.when(there)(copy.start)

    def span_wait(step, which):
        for way in range(2):
            there, copy = span_move(way, step, which, False)
            pl.when(there)(copy.wait_recv)

    span_start(0, 0)
    span_start(0, 1)
    gather_wait(2, 1)
    gather_start(2, 2)
    pack_wait(0)
    pack_start(1)
    gather_wait(2, 2)
    low = adapted.astype(BF16)
    query = dot_nn(low, query_w[...].reshape(-1, width)) + full[2:3]
    for sample in range(samples):
        query_ref[sample] = query[sample * rows : (sample + 1) * rows].astype(BF16)
    span_wait(0, 0)
    span_start(1, 0)
    gate_ref[...] = sigmoid(dot_nn(low, gate_w[...].reshape(-1, width)))
    span_wait(0, 1)
    span_start(1, 1)
    for step in range(1, spans - 1):
        for which in range(2):
            if step == 1 and which == 1:
                pack_wait(1)
                pack_start(2)
            span_wait(step, which)
            if step + 1 < spans - 1:
                span_start(step + 1, which)
    pack_wait(2)

    switch = tail_switch(count, heads, tail)
    places = key_places(count, block)
    keys_ref[keys:] = jnp.zeros_like(keys_ref[keys:])
    values_ref[keys:] = jnp.zeros_like(values_ref[keys:])

    def one_sample(sample, carry):
        struct = struct_ref[sample]
        valid = places < len_ref[struct]
        for span in range(spans):
            for which, held in ((0, keys_ref), (1, values_ref)):
                held[span * main_rows : (span + 1) * main_rows] = kv_ref[span, which, sample, :main_rows]
                spot = count * MAIN + span * (rows - main_rows)
                held[spot : spot + rows - main_rows] = kv_ref[span, which, sample, main_rows:]
        tiles_of = []
        for pair in range(count // 2):
            even = pack_ref[2 * pair, structs * pairs + struct]
            odd = swap_halves(pack_ref[2 * pair + 1, structs * pairs + struct])
            tiles_of.append(jnp.where(low_half(even), even, odd))
        mixed = dot_nn(jnp.concatenate(tiles_of, axis=1), switch).astype(BF16)
        for at in range(count // 2):
            tail_ref[at] = mixed[:, at * LANES : (at + 1) * LANES]

        def one_group(place, carry):
            acc_ref[...] = jnp.zeros_like(acc_ref)
            for at, (start, span, offset) in enumerate(windows):
                lanes = pl.ds(pl.multiple_of(place * group + start, LANES), span)
                mask = head_mask(span, offset)
                tile = struct * pairs + place * (len(windows) // 2) + at // 2
                bias = []
                for pair in range(count // 2):
                    even = pack_ref[2 * pair, tile]
                    odd = pack_ref[2 * pair + 1, tile]
                    if at % 2 == 0:
                        bias.append(jnp.where(low_half(even), even, swap_halves(odd)))
                    else:
                        bias.append(jnp.where(low_half(even), swap_halves(even), odd))
                per_tile = LANES // (count * tail)
                rest = tail_ref[place * (len(windows) // per_tile) + at // per_tile]
                turn = at % per_tile * count * tail
                bias.append(pltpu.roll(rest, LANES - turn, 1) if turn else rest)
                query = query_ref[sample, :, lanes]
                query = jnp.where(mask, query, jnp.zeros_like(query))
                scores = dot_nt(query, keys_ref[:, lanes]) * HEAD_DIM ** (-0.5) + jnp.concatenate(
                    bias, axis=1
                ).astype(F32)
                scores = jnp.where(valid, scores, NEG_BIG)
                weights = jnp.exp(scores - jnp.max(scores, axis=1, keepdims=True))
                weights = weights * (1.0 / jnp.sum(weights, axis=1, keepdims=True))
                weights = weights.astype(BF16)
                prob_ref[sample, place * len(windows) + at] = weights
                mixed = dot_nn(weights, values_ref[:, lanes])
                within = slice(start, start + span)
                acc_ref[:, within] += jnp.where(mask, mixed, 0.0)
            out_ref[sample, :, pl.ds(pl.multiple_of(place * group, LANES), group)] = acc_ref[
                ...
            ].astype(BF16)
            return carry

        return lax.fori_loop(0, width // group, one_group, carry)

    lax.fori_loop(0, samples, one_sample, 0)

    for at in range(1, count):
        send(
            small_ref, small_all.at[me], small_send.at[at], small_recv.at[at], dict(samp=peers[at])
        ).wait_send()
    for which in range(len(wholes)):
        for step in range(steps):
            for copy in gather_copies(which, step, True):
                copy.wait_send()
    for half in range(2):
        for step in range(steps):
            for copy in pack_copies(half, step, True):
                copy.wait_send()
    for step in range(spans - 1):
        for which in range(2):
            for way in range(2):
                there, copy = span_move(way, step, which, True)
                pl.when(there)(copy.wait_send)


def front(struct_of, struct_len, act, cond, small, pair, shards, samples, count, spans):
    total, width = act.shape
    rows = total // samples
    structs, block = pair.shape[0], pair.shape[2]
    heads = width // HEAD_DIM
    group, windows = head_windows(width)
    tail = block - MAIN
    tiles = structs * (heads // 2 + 1)
    steps = count.bit_length() - 1
    vmem = pl.BlockSpec(memory_space=pltpu.VMEM)
    smem = pl.BlockSpec(memory_space=pltpu.SMEM)
    far = pl.BlockSpec(memory_space=pl.ANY)
    dma = pltpu.SemaphoreType.DMA
    return pl.pallas_call(
        front_kernel,
        out_shape=(
            jax.ShapeDtypeStruct((samples, rows, width), BF16),
            jax.ShapeDtypeStruct((samples, heads, rows, KEY_LANES), BF16),
            jax.ShapeDtypeStruct((total, width), BF16),
            jax.ShapeDtypeStruct((total, width), F32),
            jax.ShapeDtypeStruct((total, width), F32),
            jax.ShapeDtypeStruct((samples, rows, width), BF16),
            jax.ShapeDtypeStruct((spans, 2, samples, rows, width), BF16),
            jax.ShapeDtypeStruct(small.shape, F32),
        )
        + tuple(jax.ShapeDtypeStruct((count,) + shard.shape, BF16) for shard in shards),
        in_specs=[smem, smem, vmem, vmem, vmem] + [far] * 7,
        out_specs=[vmem] * 14,
        scratch_shapes=[
            pltpu.VMEM((count,) + small.shape, BF16),
            pltpu.VMEM((count, tiles, rows, LANES), BF16),
            pltpu.VMEM((2, 8, block, LANES), BF16),
            pltpu.VMEM((structs, tail, rows, LANES), F32),
            pltpu.VMEM((KEY_LANES, width), BF16),
            pltpu.VMEM((KEY_LANES, width), BF16),
            pltpu.VMEM((count // 2, rows, LANES), BF16),
            pltpu.VMEM((rows, group), F32),
            dma((2,)),
            dma((len(shards),)),
            dma((count,)),
            dma((count,)),
            dma((len(shards), steps, count // 2)),
            dma((len(shards), steps, count // 2)),
            dma((2, steps, count // 2)),
            dma((2, steps, count // 2)),
            dma((2, spans - 1, 2)),
            dma((2, spans - 1, 2)),
        ],
        compiler_params=pltpu.CompilerParams(
            vmem_limit_bytes=60 << 20, collective_id=2, has_side_effects=True
        ),
        name="front",
    )(struct_of, struct_len, act, cond, small, pair, *shards)


def attend_back_kernel(
    struct_ref, q_ref, kv_ref, do_ref, prob_ref, dq_ref, dkv_ref, dpb_ref,
    key_ref, value_ref, dq_acc, dk_acc, dv_acc, first_ref, tail_ref, part_ref, span_ref, pack_ref,
    got_zero, got_one, got_two, span_send, span_recv, pack_send, pack_recv,
):
    samples, rows, width = q_ref.shape
    count = pack_ref.shape[0]
    spans = kv_ref.shape[0]
    heads = width // HEAD_DIM
    block = rows * spans // count
    tail = block - MAIN
    structs = pack_ref.shape[1] // (heads // 2 + 1)
    main_rows = rows // block * MAIN
    keys = count * block
    group, windows = head_windows(width)
    scale = HEAD_DIM ** (-0.5)
    me = lax.axis_index("samp")
    my_span = lax.axis_index("head")
    orders = reduce_orders(count)
    others = [lax.rem(my_span + away, spans) for away in range(1, spans)]
    greet(
        [dict(samp=flip(me, bit)) for bit in sorted(orders[0])] + [dict(head=other) for other in others]
    )
    switch = tail_switch(count, heads, tail)
    key_ref[keys:] = jnp.zeros_like(key_ref[keys:])
    value_ref[keys:] = jnp.zeros_like(value_ref[keys:])

    def span_copy(place, sample, away):
        lanes = pl.ds(pl.multiple_of(place * group, LANES), group)
        return send(
            part_ref.at[others[away], :, sample, :, lanes],
            span_ref.at[away, :, sample, :, lanes],
            span_send.at[place, sample, away],
            span_recv.at[place, sample, away],
            dict(head=others[away]),
        )

    def one_group(place, carry):
        for sample in range(samples):
            for span in range(spans):
                for which, held in ((0, key_ref), (1, value_ref)):
                    held[span * main_rows : (span + 1) * main_rows] = kv_ref[
                        span, which, sample, :main_rows, pl.ds(pl.multiple_of(place * group, LANES), group)
                    ]
                    spot = count * MAIN + span * (rows - main_rows)
                    held[spot : spot + rows - main_rows] = kv_ref[
                        span, which, sample, main_rows:, pl.ds(pl.multiple_of(place * group, LANES), group)
                    ]
            dq_acc[...] = jnp.zeros_like(dq_acc)
            dk_acc[...] = jnp.zeros_like(dk_acc)
            dv_acc[...] = jnp.zeros_like(dv_acc)
            kept = [jnp.where(struct_ref[0] == slab, 1.0, 0.0).astype(BF16) for slab in range(structs)]
            added = [jnp.where(struct_ref[1] == slab, 1.0, 0.0).astype(BF16) for slab in range(structs)]
            even_scores = None
            for at, (start, span, offset) in enumerate(windows):
                lanes = pl.ds(pl.multiple_of(place * group + start, LANES), span)
                within = slice(start, start + span)
                mask = head_mask(span, offset)
                upstream = do_ref[sample, :, lanes]
                upstream = jnp.where(mask, upstream, jnp.zeros_like(upstream))
                query = q_ref[sample, :, lanes]
                query = jnp.where(mask, query, jnp.zeros_like(query))
                low = prob_ref[sample, place * len(windows) + at]
                weights = low.astype(F32)
                d_weights = dot_nt(upstream, value_ref[:, within])
                dv_acc[:, within] += dot_tn(low[:, :keys], upstream)
                cross = weights * d_weights
                delta = jnp.sum(cross, axis=1, keepdims=True)
                d_scores = (cross - weights * delta).astype(BF16)
                dq_acc[:, within] += jnp.where(mask, dot_nn(d_scores, key_ref[:, within]), 0.0)
                dk_acc[:, within] += dot_tn(d_scores[:, :keys], query)
                per_tile = LANES // (count * tail)
                turn = at % per_tile * count * tail
                rest = d_scores[:, count * MAIN :]
                rest = pltpu.roll(rest, turn, 1) if turn else rest
                spot = place * (len(windows) // per_tile) + at // per_tile
                if turn:
                    tail_ref[sample, spot] += rest
                else:
                    tail_ref[sample, spot] = rest
                if at % 2 == 0:
                    even_scores = d_scores
                    continue
                for pair in range(count // 2):
                    even = even_scores[:, pair * LANES : (pair + 1) * LANES]
                    odd = d_scores[:, pair * LANES : (pair + 1) * LANES]
                    low_tile = jnp.where(low_half(even), even, swap_halves(odd))
                    high_tile = jnp.where(low_half(even), swap_halves(even), odd)
                    for side, tile in ((0, low_tile), (1, high_tile)):
                        owner = 2 * pair + side
                        if sample == 0:
                            first_ref[at // 2, owner] = tile
                            continue
                        old = first_ref[at // 2, owner]
                        for slab in range(structs):
                            spot = slab * (heads // 2) + place * (len(windows) // 2) + at // 2
                            pack_ref[owner, spot] = old * kept[slab] + tile * added[slab]
            lanes = pl.ds(pl.multiple_of(place * group, LANES), group)
            dq_ref[sample, :, lanes] = (dq_acc[...] * scale).astype(BF16)
            for span in range(spans):
                spot = count * MAIN + span * (rows - main_rows)
                for which, total, factor in ((0, dk_acc, scale), (1, dv_acc, 1.0)):
                    part_ref[span, which, sample, :main_rows, lanes] = (
                        total[span * main_rows : (span + 1) * main_rows] * factor
                    ).astype(BF16)
                    part_ref[span, which, sample, main_rows:, lanes] = (
                        total[spot : spot + rows - main_rows] * factor
                    ).astype(BF16)
            for away in range(spans - 1):
                span_copy(place, sample, away).start()
        return carry

    lax.fori_loop(0, width // group, one_group, 0)

    mixed = []
    for sample in range(samples):
        whole = jnp.concatenate([tail_ref[sample, at] for at in range(count // 2)], axis=1)
        mixed.append(dot_nt(whole, switch))
    for pair in range(count // 2):
        tiles = [part[:, pair * LANES : (pair + 1) * LANES] for part in mixed]
        for slab in range(structs):
            both = jnp.zeros_like(tiles[0])
            for sample in range(samples):
                both = both + jnp.where(struct_ref[sample] == slab, tiles[sample], 0.0)
            spot = structs * heads // 2 + slab
            pack_ref[2 * pair, spot] = jnp.where(low_half(both), both, 0.0).astype(BF16)
            pack_ref[2 * pair + 1, spot] = jnp.where(low_half(both), swap_halves(both), 0.0).astype(BF16)

    tiles = pack_ref.shape[1]
    halves = (pl.ds(0, tiles // 2), pl.ds(tiles // 2, tiles - tiles // 2))
    bounds = ((0, tiles // 2), (tiles // 2, tiles))
    landing = (got_zero, got_one, got_two)

    def stage_copies(step, half):
        order = orders[half]
        kept = flips(me, order[step + 1 :])
        return [
            send(
                pack_ref.at[flip(spot, order[step]), halves[half]],
                landing[step].at[at, halves[half]],
                pack_send.at[step, half, at],
                pack_recv.at[step, half, at],
                dict(samp=flip(me, order[step])),
            )
            for at, spot in enumerate(kept)
        ]

    flights = [[stage_copies(step, half) for half in range(2)] for step in range(len(orders[0]))]
    for half in range(2):
        for copy in flights[0][half]:
            copy.start()
    for step in range(len(orders[0])):
        for half in range(2):
            kept = flips(me, orders[half][step + 1 :])
            for at, spot in enumerate(kept):
                flights[step][half][at].wait_recv()

                def add(tile, carry, spot=spot, at=at, step=step):
                    pack_ref[spot, tile] = (
                        pack_ref[spot, tile].astype(F32) + landing[step][at, tile].astype(F32)
                    ).astype(BF16)
                    return carry

                lax.fori_loop(bounds[half][0], bounds[half][1], add, 0)
            if step + 1 < len(orders[0]):
                for copy in flights[step + 1][half]:
                    copy.start()

    def out(tile, carry):
        dpb_ref[tile] = pack_ref[me, tile]
        return carry

    lax.fori_loop(0, tiles, out, 0)

    for place in range(width // group):
        for sample in range(samples):
            for away in range(spans - 1):
                span_copy(place, sample, away).wait_recv()
    for which in range(2):
        for sample in range(samples):
            total = part_ref[my_span, which, sample].astype(F32)
            for away in range(spans - 1):
                total += span_ref[away, which, sample].astype(F32)
            dkv_ref[which, sample] = total.astype(BF16)
    for place in range(width // group):
        for sample in range(samples):
            for away in range(spans - 1):
                span_copy(place, sample, away).wait_send()
    for stage in flights:
        for half in stage:
            for copy in half:
                copy.wait_send()


def attend_back(struct_of, structs, query, key_value, upstream, prob, count):
    samples, rows, width = query.shape
    spans = key_value.shape[0]
    heads = width // HEAD_DIM
    group, windows = head_windows(width)
    keys = rows * spans
    tiles = structs * (heads // 2 + 1)
    steps = count.bit_length() - 1
    vmem = pl.BlockSpec(memory_space=pltpu.VMEM)
    smem = pl.BlockSpec(memory_space=pltpu.SMEM)
    return pl.pallas_call(
        attend_back_kernel,
        out_shape=(
            jax.ShapeDtypeStruct((samples, rows, width), BF16),
            jax.ShapeDtypeStruct((2, samples, rows, width), BF16),
            jax.ShapeDtypeStruct((tiles, rows, LANES), BF16),
        ),
        in_specs=[smem, vmem, vmem, vmem, vmem],
        out_specs=[vmem, vmem, vmem],
        scratch_shapes=[
            pltpu.VMEM((KEY_LANES, group), BF16),
            pltpu.VMEM((KEY_LANES, group), BF16),
            pltpu.VMEM((rows, group), F32),
            pltpu.VMEM((keys, group), F32),
            pltpu.VMEM((keys, group), F32),
            pltpu.VMEM((len(windows) // 2, count, rows, LANES), BF16),
            pltpu.VMEM((samples, count // 2, rows, LANES), BF16),
            pltpu.VMEM((spans, 2, samples, rows, width), BF16),
            pltpu.VMEM((spans - 1, 2, samples, rows, width), BF16),
            pltpu.VMEM((count, tiles, rows, LANES), BF16),
            pltpu.VMEM((count // 2, tiles, rows, LANES), BF16),
            pltpu.VMEM((count // 4, tiles, rows, LANES), BF16),
            pltpu.VMEM((count // 8, tiles, rows, LANES), BF16),
            pltpu.SemaphoreType.DMA((width // group, samples, spans - 1)),
            pltpu.SemaphoreType.DMA((width // group, samples, spans - 1)),
            pltpu.SemaphoreType.DMA((steps, 2, count // 2)),
            pltpu.SemaphoreType.DMA((steps, 2, count // 2)),
        ],
        compiler_params=pltpu.CompilerParams(
            vmem_limit_bytes=60 << 20, collective_id=1, has_side_effects=True
        ),
        name="attend_back",
    )(struct_of, query, key_value, upstream, prob)


def pack_rows(pieces, columns):
    return jnp.concatenate([piece.reshape(-1, columns) for piece in pieces], axis=0)


def pack_small(pieces, columns):
    flat = jnp.concatenate([piece.reshape(-1) for piece in pieces])
    rows = -(-flat.shape[0] // columns)
    rows = -(-rows // 8) * 8
    return jnp.pad(flat, (0, rows * columns - flat.shape[0])).reshape(rows, columns)


def unpack_rows(gathered, shapes):
    whole, at = [], 0
    count, _, columns = gathered.shape
    for rows, cols in shapes:
        held = rows * cols // columns
        whole.append(gathered[:, at : at + held].reshape(count * rows, cols))
        at += held
    return whole


def unpack_small(gathered, shapes):
    whole, at = [], 0
    count = gathered.shape[0]
    flat = gathered.reshape(count, -1)
    for shape in shapes:
        size = 1
        for extent in shape:
            size *= extent
        whole.append(flat[:, at : at + size].reshape((count * shape[0],) + shape[1:]))
        at += size
    return whole


def plain_kernel(struct_ref, len_ref, q_ref, k_ref, v_ref, bias_ref, out_ref, prob_ref, acc_ref):
    sample = pl.program_id(0)
    group_at = pl.program_id(1)
    length = len_ref[struct_ref[sample]]
    keys = k_ref.shape[1]
    group, windows = head_windows(q_ref.shape[2])
    valid = lax.broadcasted_iota(jnp.int32, (1, keys), 1) < length
    acc_ref[...] = jnp.zeros_like(acc_ref)
    for at, (start, width, offset) in enumerate(windows):
        lanes = slice(start, start + width)
        mask = head_mask(width, offset)
        query = q_ref[0, :, lanes]
        query = jnp.where(mask, query, jnp.zeros_like(query))
        scores = dot_nt(query, k_ref[0, :, lanes]) * HEAD_DIM ** (-0.5) + bias_ref[
            0, at
        ].astype(F32)
        scores = jnp.where(valid, scores, NEG_BIG)
        weights = jnp.exp(scores - jnp.max(scores, axis=1, keepdims=True))
        weights = weights * (1.0 / jnp.sum(weights, axis=1, keepdims=True))
        weights = weights.astype(BF16)
        prob_ref[0, at] = weights
        mixed = dot_nn(weights, v_ref[0, :, lanes])
        acc_ref[:, lanes] += jnp.where(mask, mixed, 0.0)
    out_ref[0] = acc_ref[...].astype(BF16)


def plain(struct_of, struct_len, query, key, value, bias):
    samples, rows, width = query.shape
    keys = key.shape[1]
    heads = bias.shape[1]
    group, windows = head_windows(width)
    each = len(windows)
    return pl.pallas_call(
        plain_kernel,
        out_shape=(
            jax.ShapeDtypeStruct((samples, rows, width), BF16),
            jax.ShapeDtypeStruct((samples, heads, rows, keys), BF16),
        ),
        grid_spec=pltpu.PrefetchScalarGridSpec(
            num_scalar_prefetch=2,
            grid=(samples, heads // each),
            in_specs=[
                pl.BlockSpec((1, rows, group), lambda b, g, s, n: (b, 0, g)),
                pl.BlockSpec((1, keys, group), lambda b, g, s, n: (b, 0, g)),
                pl.BlockSpec((1, keys, group), lambda b, g, s, n: (b, 0, g)),
                pl.BlockSpec((1, each, rows, keys), lambda b, g, s, n: (s[b], g, 0, 0)),
            ],
            out_specs=[
                pl.BlockSpec((1, rows, group), lambda b, g, s, n: (b, 0, g)),
                pl.BlockSpec((1, each, rows, keys), lambda b, g, s, n: (b, g, 0, 0)),
            ],
            scratch_shapes=[pltpu.VMEM((rows, group), F32)],
        ),
        compiler_params=pltpu.CompilerParams(vmem_limit_bytes=48 << 20),
        name="plain",
    )(struct_of, struct_len, query, key, value, bias)


def plain_back_kernel(
    struct_ref, q_ref, k_ref, v_ref, do_ref, prob_ref, dq_ref, dk_ref, dv_ref, bias_ref,
    dq_acc, dk_acc, dv_acc, bias_acc,
):
    samples = q_ref.shape[0]
    structs = bias_ref.shape[0]
    group, windows = head_windows(q_ref.shape[2])
    scale = HEAD_DIM ** (-0.5)
    for sample in range(samples):
        struct = struct_ref[sample]
        dq_acc[...] = jnp.zeros_like(dq_acc)
        dk_acc[...] = jnp.zeros_like(dk_acc)
        dv_acc[...] = jnp.zeros_like(dv_acc)
        for at, (start, width, offset) in enumerate(windows):
            lanes = slice(start, start + width)
            mask = head_mask(width, offset)
            upstream = do_ref[sample, :, lanes]
            upstream = jnp.where(mask, upstream, jnp.zeros_like(upstream))
            query = q_ref[sample, :, lanes]
            query = jnp.where(mask, query, jnp.zeros_like(query))
            low = prob_ref[sample, at]
            weights = low.astype(F32)
            d_weights = dot_nt(upstream, v_ref[sample, :, lanes])
            dv_acc[:, lanes] += dot_tn(low, upstream)
            cross = weights * d_weights
            delta = jnp.sum(cross, axis=1, keepdims=True)
            d_scores = (cross - weights * delta).astype(BF16)
            dq_acc[:, lanes] += jnp.where(mask, dot_nn(d_scores, k_ref[sample, :, lanes]), 0.0)
            dk_acc[:, lanes] += dot_tn(d_scores, query)
            for slab in range(structs):
                part = jnp.where(struct == slab, 1.0, 0.0) * d_scores.astype(F32)
                if sample == 0:
                    bias_acc[slab, at] = part
                elif sample < samples - 1:
                    bias_acc[slab, at] += part
                else:
                    bias_ref[slab, at] = (bias_acc[slab, at] + part).astype(BF16)
        dq_ref[sample] = (dq_acc[...] * scale).astype(BF16)
        dk_ref[sample] = (dk_acc[...] * scale).astype(BF16)
        dv_ref[sample] = dv_acc[...].astype(BF16)


def plain_back(struct_of, structs, query, key, value, upstream, prob):
    samples, rows, width = query.shape
    keys = key.shape[1]
    heads = prob.shape[1]
    group, windows = head_windows(width)
    each = len(windows)
    return pl.pallas_call(
        plain_back_kernel,
        out_shape=(
            jax.ShapeDtypeStruct((samples, rows, width), BF16),
            jax.ShapeDtypeStruct((samples, keys, width), BF16),
            jax.ShapeDtypeStruct((samples, keys, width), BF16),
            jax.ShapeDtypeStruct((structs, heads, rows, keys), BF16),
        ),
        grid_spec=pltpu.PrefetchScalarGridSpec(
            num_scalar_prefetch=1,
            grid=(heads // each,),
            in_specs=[
                pl.BlockSpec((samples, rows, group), lambda g, s: (0, 0, g)),
                pl.BlockSpec((samples, keys, group), lambda g, s: (0, 0, g)),
                pl.BlockSpec((samples, keys, group), lambda g, s: (0, 0, g)),
                pl.BlockSpec((samples, rows, group), lambda g, s: (0, 0, g)),
                pl.BlockSpec((samples, each, rows, keys), lambda g, s: (0, g, 0, 0)),
            ],
            out_specs=[
                pl.BlockSpec((samples, rows, group), lambda g, s: (0, 0, g)),
                pl.BlockSpec((samples, keys, group), lambda g, s: (0, 0, g)),
                pl.BlockSpec((samples, keys, group), lambda g, s: (0, 0, g)),
                pl.BlockSpec((structs, each, rows, keys), lambda g, s: (0, g, 0, 0)),
            ],
            scratch_shapes=[
                pltpu.VMEM((rows, group), F32),
                pltpu.VMEM((keys, group), F32),
                pltpu.VMEM((keys, group), F32),
                pltpu.VMEM((structs, each, rows, keys), F32),
            ],
        ),
        compiler_params=pltpu.CompilerParams(vmem_limit_bytes=60 << 20),
        name="plain_back",
    )(struct_of, query, key, value, upstream, prob)


def plain_device(
    act, cond, pair, struct_of, struct_len,
    gain_first, scale_first, scale_bias_first, shift_first,
    query_weight, query_bias, key_weight, value_weight, gate_weight, output_weight,
    pair_weight, zero_first, zero_bias_first,
    gain_second, scale_second, scale_bias_second, shift_second,
    swish_weight, linear_weight, down_weight, zero_second, zero_bias_second,
    cotangent,
):
    samples, rows, width = act.shape
    cond_width = cond.shape[2]
    total = samples * rows
    structs = pair.shape[0]
    small = (
        gain_first, scale_bias_first, query_bias, zero_bias_first, gain_second,
        scale_bias_second, zero_bias_second, pair_weight,
    )
    early = (scale_first, shift_first, query_weight, key_weight, value_weight, gate_weight)
    late = (
        output_weight, zero_first, scale_second, shift_second, swish_weight, linear_weight,
        down_weight, zero_second,
    )
    small_all = lax.all_gather(pack_small(small, width), "samp", axis=0)
    early_all = lax.all_gather(pack_rows(early, width), "samp", axis=0)
    late_all = lax.all_gather(pack_rows(late, width), "samp", axis=0)
    (gain_one, bias_one, bias_query, bias_zero_one, gain_two, bias_two, bias_zero_two, pair_proj_w) = (
        unpack_small(small_all, [piece.shape for piece in small])
    )
    (w_scale, w_shift, w_query, w_key, w_value, w_gate) = unpack_rows(
        early_all, [piece.shape for piece in early]
    )
    (w_out, w_zero, w_scale_two, w_shift_two, w_swish, w_linear, w_down, w_zero_two) = unpack_rows(
        late_all, [piece.shape for piece in late]
    )

    pair_normed, pair_inverse = norm_rows(pair.astype(F32))
    pair_low = pair_normed.astype(BF16)
    pair_proj = jnp.einsum("sijc,ch->shij", pair_low, pair_proj_w, preferred_element_type=F32)
    bias_all = lax.all_gather(pair_proj.astype(BF16), "samp", axis=3, tiled=True)

    act_rows = act.reshape(total, width).astype(F32)
    cond_low = cond.reshape(total, cond_width)
    act_normed, act_inverse = norm_rows(act_rows)
    cond_normed, cond_inverse = norm_rows(cond_low.astype(F32))
    cond_first = (cond_normed * gain_one.astype(F32)).astype(BF16)
    sig_first = jax.nn.sigmoid(product(cond_first, w_scale) + bias_one.astype(F32))
    adapted = (sig_first * act_normed + product(cond_first, w_shift)).astype(BF16)
    key_rows = product(adapted, w_key).astype(BF16)
    value_rows = product(adapted, w_value).astype(BF16)
    query_rows = (product(adapted, w_query) + bias_query.astype(F32)).astype(BF16)
    gate_sig = jax.nn.sigmoid(product(adapted, w_gate))
    key_value = jnp.stack((key_rows, value_rows)).reshape(2, samples, rows, width)
    key_value = lax.all_gather(key_value, "head", axis=2, tiled=True)
    query_split = query_rows.reshape(samples, rows, width)
    attended, prob = plain(
        struct_of, struct_len, query_split, key_value[0], key_value[1], bias_all
    )
    attn_float = attended.reshape(total, width).astype(F32)

    gated_rows = (gate_sig * attn_float).astype(BF16)
    branch = product(gated_rows, w_out)
    zero_sig_first = jax.nn.sigmoid(product(cond_low, w_zero) + bias_zero_one.astype(F32))
    middle = act_rows + zero_sig_first * branch
    mid_normed, mid_inverse = norm_rows(middle)
    cond_second = (cond_normed * gain_two.astype(F32)).astype(BF16)
    sig_second = jax.nn.sigmoid(product(cond_second, w_scale_two) + bias_two.astype(F32))
    adapted_two = (sig_second * mid_normed + product(cond_second, w_shift_two)).astype(BF16)
    swish_pre = product(adapted_two, w_swish)
    linear_pre = product(adapted_two, w_linear)
    swish_sig = jax.nn.sigmoid(swish_pre)
    hidden = (swish_pre * swish_sig * linear_pre).astype(BF16)
    down_rows = product(hidden, w_down)
    zero_sig_second = jax.nn.sigmoid(product(cond_low, w_zero_two) + bias_zero_two.astype(F32))
    layer_out = (middle + zero_sig_second * down_rows).astype(BF16)

    upstream = cotangent.reshape(total, width).astype(F32)
    d_down = (upstream * zero_sig_second).astype(BF16)
    d_zero_second = (upstream * down_rows * sigmoid_slope(zero_sig_second)).astype(BF16)
    d_hidden = back_product(d_down, w_down)
    d_swish = (
        d_hidden * linear_pre * swish_sig * (1.0 + swish_pre * (1.0 - swish_sig))
    ).astype(BF16)
    d_linear = (d_hidden * swish_pre * swish_sig).astype(BF16)
    d_adapted_two = back_product(d_swish, w_swish) + back_product(d_linear, w_linear)
    d_shift_second = d_adapted_two.astype(BF16)
    d_pre_second = (d_adapted_two * mid_normed * sigmoid_slope(sig_second)).astype(BF16)
    d_cond_second = back_product(d_shift_second, w_shift_two) + back_product(
        d_pre_second, w_scale_two
    )
    d_middle = upstream + norm_back(mid_normed, mid_inverse, d_adapted_two * sig_second)
    d_branch = (d_middle * zero_sig_first).astype(BF16)
    d_zero_first = (d_middle * branch * sigmoid_slope(zero_sig_first)).astype(BF16)
    d_gated = back_product(d_branch, w_out)
    d_gate = (d_gated * attn_float * sigmoid_slope(gate_sig)).astype(BF16)
    d_attended = (d_gated * gate_sig).astype(BF16)

    late_grads = (
        outer_sum(gated_rows, d_branch),
        outer_sum(cond_low, d_zero_first),
        outer_sum(cond_second, d_pre_second),
        outer_sum(cond_second, d_shift_second),
        outer_sum(adapted_two, d_swish),
        outer_sum(adapted_two, d_linear),
        outer_sum(hidden, d_down),
        outer_sum(cond_low, d_zero_second),
    )

    d_query, d_key, d_value, bias_grad = plain_back(
        struct_of, structs, query_split, key_value[0], key_value[1],
        d_attended.reshape(samples, rows, width), prob,
    )
    d_key_value = lax.psum_scatter(
        jnp.stack((d_key, d_value)), "head", scatter_dimension=2, tiled=True
    )
    d_query = d_query.reshape(total, width)
    d_key = d_key_value[0].reshape(total, width)
    d_value = d_key_value[1].reshape(total, width)
    bias_summed = lax.psum_scatter(bias_grad, "samp", scatter_dimension=3, tiled=True)
    pair_weight_grad = jnp.einsum("sijc,shij->ch", pair_low, bias_summed, preferred_element_type=F32)
    pair_upstream = jnp.einsum(
        "shij,ch->sijc", bias_summed, pair_proj_w, preferred_element_type=F32
    )
    pair_grad = norm_back(pair_normed, pair_inverse, pair_upstream)
    d_adapted = (
        back_product(d_query, w_query)
        + back_product(d_key, w_key)
        + back_product(d_value, w_value)
        + back_product(d_gate, w_gate)
    )
    d_shift_first = d_adapted.astype(BF16)
    d_pre_first = (d_adapted * act_normed * sigmoid_slope(sig_first)).astype(BF16)
    d_cond_first = back_product(d_shift_first, w_shift) + back_product(d_pre_first, w_scale)
    input_grad = d_middle + norm_back(act_normed, act_inverse, d_adapted * sig_first)
    d_cond_normed = d_cond_first * gain_one.astype(F32) + d_cond_second * gain_two.astype(F32)
    cond_grad = (
        norm_back(cond_normed, cond_inverse, d_cond_normed)
        + back_product(d_zero_first, w_zero)
        + back_product(d_zero_second, w_zero_two)
    )
    early_grads = (
        outer_sum(cond_first, d_pre_first),
        outer_sum(cond_first, d_shift_first),
        outer_sum(adapted, d_query),
        outer_sum(adapted, d_key),
        outer_sum(adapted, d_value),
        outer_sum(adapted, d_gate),
    )
    small_grads = (
        jnp.sum(d_cond_first * cond_normed, axis=0),
        column_sum(d_pre_first),
        column_sum(d_query),
        column_sum(d_zero_first),
        jnp.sum(d_cond_second * cond_normed, axis=0),
        column_sum(d_pre_second),
        column_sum(d_zero_second),
        pair_weight_grad,
    )
    count = lax.axis_size("samp")

    def pack_grads(grads, shapes):
        pieces = [
            grad.astype(BF16).reshape(count, shape[0] * shape[1] // width, width)
            for grad, shape in zip(grads, shapes)
        ]
        return jnp.concatenate(pieces, axis=1)

    def reduce(packed):
        summed = lax.psum_scatter(packed, "samp", scatter_dimension=0, tiled=True)
        return lax.psum(summed[0], "head").astype(F32)

    late_sum = reduce(pack_grads(late_grads, [piece.shape for piece in late]))
    early_sum = reduce(pack_grads(early_grads, [piece.shape for piece in early]))
    small_flat = jnp.concatenate(
        [grad.astype(BF16).reshape(count, -1) for grad in small_grads], axis=1
    )
    small_sum = lax.psum(
        lax.psum_scatter(small_flat, "samp", scatter_dimension=0, tiled=True), "head"
    ).astype(F32)
    (g_out, g_zero, g_scale_two, g_shift_two, g_swish, g_linear, g_down, g_zero_two) = unpack_rows(
        late_sum[None], [piece.shape for piece in late]
    )
    (g_scale, g_shift, g_query, g_key, g_value, g_gate) = unpack_rows(
        early_sum[None], [piece.shape for piece in early]
    )
    (g_gain, g_bias, g_bias_query, g_bias_zero, g_gain_two, g_bias_two, g_bias_zero_two, g_pair) = (
        unpack_small(small_sum, [piece.shape for piece in small])
    )
    return (
        layer_out.reshape(act.shape), input_grad.reshape(act.shape), cond_grad.reshape(cond.shape),
        pair_grad, g_gain, g_scale, g_bias, g_shift, g_query, g_bias_query, g_key, g_value, g_gate,
        g_out, g_pair, g_zero, g_bias_zero, g_gain_two, g_scale_two, g_bias_two, g_shift_two,
        g_swish, g_linear, g_down, g_zero_two, g_bias_zero_two,
    )


def per_device(
    act, cond, pair, struct_of, struct_len,
    gain_first, scale_first, scale_bias_first, shift_first,
    query_weight, query_bias, key_weight, value_weight, gate_weight, output_weight,
    pair_weight, zero_first, zero_bias_first,
    gain_second, scale_second, scale_bias_second, shift_second,
    swish_weight, linear_weight, down_weight, zero_second, zero_bias_second,
    cotangent,
):
    samples, rows, width = act.shape
    cond_width = cond.shape[2]
    total = samples * rows
    structs = pair.shape[0]
    block = pair.shape[2]
    count = lax.axis_size("samp")
    small = (
        gain_first, scale_bias_first, query_bias, zero_bias_first, gain_second,
        scale_bias_second, zero_bias_second,
    )
    early = (scale_first, shift_first, key_weight, value_weight, query_weight, gate_weight)
    late = (
        output_weight, zero_first, scale_second, shift_second, swish_weight, linear_weight,
        down_weight, zero_second,
    )
    spans = lax.axis_size("head")
    late_all = lax.all_gather(pack_rows(late, width), "samp", axis=0)
    mine = lax.broadcasted_iota(jnp.int32, (count, 1), 0) == lax.axis_index("samp")

    def spread(piece, columns):
        held = jnp.where(mine, piece[None], jnp.zeros_like(piece[None])).reshape(1, -1)
        return jnp.pad(held, ((0, 0), (0, columns - held.shape[1])))

    even_odd = jnp.concatenate((pair_weight[:, 0::2], pair_weight[:, 1::2]), axis=1).T
    held = jnp.where(mine.reshape(1, count, 1), even_odd[:, None], jnp.zeros_like(even_odd[:, None]))
    held = jnp.pad(held.reshape(even_odd.shape[0], -1), ((0, 0), (0, width - LANES)))
    packed_small = jnp.concatenate(
        [spread(piece, width) for piece in small] + [jnp.zeros((1, width), BF16), held], axis=0
    )
    (attended, prob, adapted, sig_first, gate_sig, query_split, key_value, full, *early_whole) = front(
        struct_of, struct_len, act.reshape(total, width), cond.reshape(total, cond_width), packed_small,
        pair, early, samples, count, spans,
    )
    (w_scale, w_shift, w_key, w_value, w_query, w_gate) = [
        whole.reshape(-1, width) for whole in early_whole
    ]
    gain_one, bias_zero_one, gain_two = full[0, :cond_width], full[3], full[4, :cond_width]
    bias_two, bias_zero_two = full[5], full[6]
    heads = width // HEAD_DIM
    pair_proj_w = full[8:, :LANES].reshape(2, heads // 2, -1).transpose(2, 1, 0).reshape(-1, heads).astype(BF16)
    (w_out, w_zero, w_scale_two, w_shift_two, w_swish, w_linear, w_down, w_zero_two) = unpack_rows(
        late_all, [piece.shape for piece in late]
    )

    pair_normed, pair_inverse = norm_rows(pair.astype(F32))
    pair_low = pair_normed.astype(BF16)
    act_rows = act.reshape(total, width).astype(F32)
    cond_low = cond.reshape(total, cond_width)
    act_normed, act_inverse = norm_rows(act_rows)
    cond_normed, cond_inverse = norm_rows(cond_low.astype(F32))
    cond_first = (cond_normed * gain_one.astype(F32)).astype(BF16)
    attn_float = attended.reshape(total, width).astype(F32)

    gated_rows = (gate_sig * attn_float).astype(BF16)
    branch = product(gated_rows, w_out)
    zero_sig_first = jax.nn.sigmoid(product(cond_low, w_zero) + bias_zero_one.astype(F32))
    middle = act_rows + zero_sig_first * branch
    mid_normed, mid_inverse = norm_rows(middle)
    cond_second = (cond_normed * gain_two.astype(F32)).astype(BF16)
    sig_second = jax.nn.sigmoid(product(cond_second, w_scale_two) + bias_two.astype(F32))
    adapted_two = (sig_second * mid_normed + product(cond_second, w_shift_two)).astype(BF16)
    swish_pre = product(adapted_two, w_swish)
    linear_pre = product(adapted_two, w_linear)
    swish_sig = jax.nn.sigmoid(swish_pre)
    hidden = (swish_pre * swish_sig * linear_pre).astype(BF16)
    down_rows = product(hidden, w_down)
    zero_sig_second = jax.nn.sigmoid(product(cond_low, w_zero_two) + bias_zero_two.astype(F32))
    layer_out = (middle + zero_sig_second * down_rows).astype(BF16)

    upstream = cotangent.reshape(total, width).astype(F32)
    d_down = (upstream * zero_sig_second).astype(BF16)
    d_zero_second = (upstream * down_rows * sigmoid_slope(zero_sig_second)).astype(BF16)
    d_hidden = back_product(d_down, w_down)
    d_swish = (
        d_hidden * linear_pre * swish_sig * (1.0 + swish_pre * (1.0 - swish_sig))
    ).astype(BF16)
    d_linear = (d_hidden * swish_pre * swish_sig).astype(BF16)
    d_adapted_two = back_product(d_swish, w_swish) + back_product(d_linear, w_linear)
    d_shift_second = d_adapted_two.astype(BF16)
    d_pre_second = (d_adapted_two * mid_normed * sigmoid_slope(sig_second)).astype(BF16)
    d_cond_second = back_product(d_shift_second, w_shift_two) + back_product(
        d_pre_second, w_scale_two
    )
    d_middle = upstream + norm_back(mid_normed, mid_inverse, d_adapted_two * sig_second)
    d_branch = (d_middle * zero_sig_first).astype(BF16)
    d_zero_first = (d_middle * branch * sigmoid_slope(zero_sig_first)).astype(BF16)
    d_gated = back_product(d_branch, w_out)
    d_gate = (d_gated * attn_float * sigmoid_slope(gate_sig)).astype(BF16)
    d_attended = (d_gated * gate_sig).astype(BF16)

    late_grads = (
        outer_sum(gated_rows, d_branch),
        outer_sum(cond_low, d_zero_first),
        outer_sum(cond_second, d_pre_second),
        outer_sum(cond_second, d_shift_second),
        outer_sum(adapted_two, d_swish),
        outer_sum(adapted_two, d_linear),
        outer_sum(hidden, d_down),
        outer_sum(cond_low, d_zero_second),
    )

    d_query, d_key_value, bias_packed = attend_back(
        struct_of, structs, query_split, key_value, d_attended.reshape(samples, rows, width), prob, count
    )
    d_query = d_query.reshape(total, width)
    d_key = key_rows_back(d_key_value[0], block).reshape(total, width)
    d_value = key_rows_back(d_key_value[1], block).reshape(total, width)
    bias_summed = unpack_bias(bias_packed, structs, width // HEAD_DIM)
    pair_weight_grad = jnp.einsum("sijc,shij->ch", pair_low, bias_summed, preferred_element_type=F32)
    pair_upstream = jnp.einsum(
        "shij,ch->sijc", bias_summed, pair_proj_w, preferred_element_type=F32
    )
    pair_grad = norm_back(pair_normed, pair_inverse, pair_upstream)
    d_adapted = (
        back_product(d_query, w_query)
        + back_product(d_key, w_key)
        + back_product(d_value, w_value)
        + back_product(d_gate, w_gate)
    )
    d_shift_first = d_adapted.astype(BF16)
    d_pre_first = (d_adapted * act_normed * sigmoid_slope(sig_first)).astype(BF16)
    d_cond_first = back_product(d_shift_first, w_shift) + back_product(d_pre_first, w_scale)
    input_grad = d_middle + norm_back(act_normed, act_inverse, d_adapted * sig_first)
    d_cond_normed = d_cond_first * gain_one.astype(F32) + d_cond_second * gain_two.astype(F32)
    cond_grad = (
        norm_back(cond_normed, cond_inverse, d_cond_normed)
        + back_product(d_zero_first, w_zero)
        + back_product(d_zero_second, w_zero_two)
    )
    early_grads = (
        outer_sum(cond_first, d_pre_first),
        outer_sum(cond_first, d_shift_first),
        outer_sum(adapted, d_key),
        outer_sum(adapted, d_value),
        outer_sum(adapted, d_query),
        outer_sum(adapted, d_gate),
    )
    small_grads = (
        jnp.sum(d_cond_first * cond_normed, axis=0),
        column_sum(d_pre_first),
        column_sum(d_query),
        column_sum(d_zero_first),
        jnp.sum(d_cond_second * cond_normed, axis=0),
        column_sum(d_pre_second),
        column_sum(d_zero_second),
        pair_weight_grad,
    )

    def pack_grads(grads, shapes):
        pieces = [
            grad.astype(BF16).reshape(count, shape[0] * shape[1] // width, width)
            for grad, shape in zip(grads, shapes)
        ]
        return jnp.concatenate(pieces, axis=1)

    def reduce(packed):
        summed = lax.psum_scatter(packed, "samp", scatter_dimension=0, tiled=True)
        return lax.psum(summed[0], "head").astype(F32)

    late_sum = reduce(pack_grads(late_grads, [piece.shape for piece in late]))
    early_sum = reduce(pack_grads(early_grads, [piece.shape for piece in early]))
    small_flat = jnp.concatenate(
        [grad.astype(BF16).reshape(count, -1) for grad in small_grads], axis=1
    )
    small_sum = lax.psum(
        lax.psum_scatter(small_flat, "samp", scatter_dimension=0, tiled=True), "head"
    ).astype(F32)
    (g_out, g_zero, g_scale_two, g_shift_two, g_swish, g_linear, g_down, g_zero_two) = unpack_rows(
        late_sum[None], [piece.shape for piece in late]
    )
    (g_scale, g_shift, g_key, g_value, g_query, g_gate) = unpack_rows(
        early_sum[None], [piece.shape for piece in early]
    )
    (g_gain, g_bias, g_bias_query, g_bias_zero, g_gain_two, g_bias_two, g_bias_zero_two, g_pair) = (
        unpack_small(small_sum, [piece.shape for piece in small + (pair_weight,)])
    )
    return (
        layer_out.reshape(act.shape), input_grad.reshape(act.shape), cond_grad.reshape(cond.shape),
        pair_grad, g_gain, g_scale, g_bias, g_shift, g_query, g_bias_query, g_key, g_value, g_gate,
        g_out, g_pair, g_zero, g_bias_zero, g_gain_two, g_scale_two, g_bias_two, g_shift_two,
        g_swish, g_linear, g_down, g_zero_two, g_bias_zero_two,
    )


def fits(mesh, act, pair):
    samples, rows, width = act.shape
    count, spans = mesh.shape["samp"], mesh.shape["head"]
    block = pair.shape[2]
    tail = block - MAIN
    heads = width // HEAD_DIM
    return (
        count == 8
        and samples == 2
        and tail > 0
        and heads * tail == MAIN
        and rows % block == 0
        and rows * spans == block * count
        and rows % 8 == 0
        and block * count <= KEY_LANES
    )


def solution(mesh):
    tokens = P("samp", "head", None)
    pairs = P(None, "head", "samp", None)
    vector = P("samp")
    matrix = P("samp", None)
    weights = (
        vector, matrix, vector, matrix, matrix, vector, matrix, matrix, matrix, matrix, matrix,
        matrix, vector, vector, matrix, vector, matrix, matrix, matrix, matrix, matrix, vector,
    )
    def choose(*arrays):
        body = per_device if fits(mesh, arrays[0], arrays[2]) else plain_device
        return body(*arrays)

    return jax.shard_map(
        choose,
        mesh=mesh,
        in_specs=(tokens, tokens, pairs, vector, P()) + weights + (tokens,),
        out_specs=(tokens, tokens, tokens, pairs) + weights,
        check_vma=False,
    )
```

```python
import functools

import jax
import jax.numpy as jnp
from jax import lax
from jax.experimental import pallas as pl
from jax.experimental.pallas import tpu as pltpu
from jax.sharding import PartitionSpec as P

HEAD_DIM = 48
LANES = 128
MAIN = 64
KEY_LANES = 640
MESH = pl.DeviceIdType.MESH
EPSILON = 1e-05
NEG_BIG = -1000000000.0
F32 = jnp.float32
BF16 = jnp.bfloat16


def norm_rows(values):
    centered = values - jnp.mean(values, axis=-1, keepdims=True)
    variance = jnp.mean(centered * centered, axis=-1, keepdims=True)
    inverse = lax.rsqrt(variance + EPSILON)
    return (centered * inverse, inverse)


def norm_back(normed, inverse, upstream):
    mean_grad = jnp.mean(upstream, axis=-1, keepdims=True)
    mean_cross = jnp.mean(upstream * normed, axis=-1, keepdims=True)
    return inverse * (upstream - mean_grad - normed * mean_cross)


def product(left_side, right_side):
    return lax.dot_general(
        left_side, right_side, (((1,), (0,)), ((), ())), preferred_element_type=F32
    )


def back_product(upstream, right_side):
    return lax.dot_general(
        upstream, right_side, (((1,), (1,)), ((), ())), preferred_element_type=F32
    )


def outer_sum(left_side, upstream):
    return lax.dot_general(
        left_side, upstream, (((0,), (0,)), ((), ())), preferred_element_type=F32
    )


def column_sum(upstream):
    return jnp.sum(upstream.astype(F32), axis=0)


def sigmoid_slope(gate_sig):
    return gate_sig * (1.0 - gate_sig)


def head_windows(width):
    group = LANES * HEAD_DIM // 16
    group = min(group, width)
    windows = []
    for head in range(group // HEAD_DIM):
        first = head * HEAD_DIM
        last = first + HEAD_DIM - 1
        start = first // LANES * LANES
        stop = (last // LANES + 1) * LANES
        windows.append((start, stop - start, first - start))
    return (group, windows)


def head_mask(width, offset):
    lane = lax.broadcasted_iota(jnp.int32, (1, width), 1)
    return (lane >= offset) & (lane < offset + HEAD_DIM)


def dot_nt(left, right):
    return lax.dot_general(left, right, (((1,), (1,)), ((), ())), preferred_element_type=F32)


def dot_nn(left, right):
    return lax.dot_general(left, right, (((1,), (0,)), ((), ())), preferred_element_type=F32)


def dot_tn(left, right):
    return lax.dot_general(left, right, (((0,), (0,)), ((), ())), preferred_element_type=F32)


def tail_switch(count, heads, tail):
    lanes = count * heads * tail
    source = lax.broadcasted_iota(jnp.int32, (lanes, lanes), 0)
    target = lax.broadcasted_iota(jnp.int32, (lanes, lanes), 1)
    owner = source // (heads * tail)
    head = source % heads
    spot = head * (count * tail) + owner * tail + source // heads % tail
    return jnp.where(spot == target, 1.0, 0.0).astype(BF16)


def swap_halves(tile):
    return pltpu.roll(tile, MAIN, 1)


def low_half(tile):
    return lax.broadcasted_iota(jnp.int32, tile.shape, 1) < MAIN


def key_places(count, block):
    lane = lax.broadcasted_iota(jnp.int32, (1, KEY_LANES), 1)
    tail = block - MAIN
    spare = lane - count * MAIN
    main_at = lane + tail * (lane // MAIN)
    tail_at = block * (spare // tail) + MAIN + spare % tail
    past = jnp.where(spare < count * tail, tail_at, count * block)
    return jnp.where(spare < 0, main_at, past)


def flip(index, bit):
    return index + bit - 2 * bit * lax.rem(lax.div(index, bit), 2)


def flips(index, bits):
    spots = [index]
    for bit in bits:
        spots = spots + [flip(spot, bit) for spot in spots]
    return spots


def reduce_orders(count):
    bits = []
    bit = 2
    while bit < count:
        bits.append(bit)
        bit *= 2
    half = len(bits) // 2
    return ([1] + bits, [1] + bits[half:] + bits[:half])


def greet(partners):
    barrier = pltpu.get_barrier_semaphore()
    for partner in partners:
        pl.semaphore_signal(barrier, inc=1, device_id=partner, device_id_type=MESH)
    pl.semaphore_wait(barrier, len(partners))


def send(source, target, send_sem, recv_sem, device):
    return pltpu.make_async_remote_copy(
        src_ref=source, dst_ref=target, send_sem=send_sem, recv_sem=recv_sem,
        device_id=device, device_id_type=MESH,
    )


def sigmoid(values):
    return 1.0 / (1.0 + jnp.exp(-values))


def one_hot(shape, source_of):
    target = lax.broadcasted_iota(jnp.int32, shape, 0)
    source = lax.broadcasted_iota(jnp.int32, shape, 1)
    return jnp.where(source == source_of(target), 1.0, 0.0).astype(BF16)


def key_row_of(place, block, pieces):
    tail = block - MAIN
    main_at = place // MAIN * block + place % MAIN
    spare = place - pieces * MAIN
    tail_at = spare // tail * block + MAIN + spare % tail
    return jnp.where(place < pieces * MAIN, main_at, tail_at)


def front_kernel(
    struct_ref, len_ref, act_ref, cond_ref, small_ref, pair_ref,
    scale_in, shift_in, key_in, value_in, query_in, gate_in,
    out_ref, prob_ref, adapted_ref, sig_ref, gate_ref, query_ref, kv_ref, full_ref,
    scale_w, shift_w, key_w, value_w, query_w, gate_w,
    small_all, pack_ref, pair_buf, tails_ref, keys_ref, values_ref, tail_ref, acc_ref,
    pair_sem, own_sem, small_send, small_recv, gather_send, gather_recv, pack_send, pack_recv,
    span_send, span_recv,
):
    total, width = act_ref.shape
    samples, rows = prob_ref.shape[0], prob_ref.shape[2]
    count = pack_ref.shape[0]
    spans = kv_ref.shape[0]
    heads = width // HEAD_DIM
    structs = pair_ref.shape[0]
    block = pair_ref.shape[2]
    tail = block - MAIN
    pieces = rows // block
    main_rows = pieces * MAIN
    keys = count * block
    pairs = heads // 2
    group, windows = head_windows(width)
    me = lax.axis_index("samp")
    my_span = lax.axis_index("head")
    reduce_pair = reduce_orders(count)
    orders = [order[1:] + order[:1] for order in reduce_pair]
    bits = sorted(reduce_pair[0])
    steps = len(bits)
    peers = flips(me, bits)

    shards = (scale_in, shift_in, key_in, value_in, query_in, gate_in)
    wholes = (scale_w, shift_w, key_w, value_w, query_w, gate_w)
    owns = [
        pltpu.make_async_copy(shard, whole.at[me], own_sem.at[at])
        for at, (shard, whole) in enumerate(zip(shards, wholes))
    ]
    for copy in owns:
        copy.start()

    def pair_copy(place):
        slot = lax.rem(place, 2)
        struct = lax.div(place, rows // 8)
        first = pl.multiple_of(lax.rem(place, rows // 8) * 8, 8)
        return pltpu.make_async_copy(
            pair_ref.at[struct, pl.ds(first, 8)], pair_buf.at[slot], pair_sem.at[slot]
        )

    pair_copy(0).start()
    small_all[me] = small_ref[...]
    greet(
        [dict(samp=peer) for peer in peers[1:]]
        + [dict(head=lax.rem(my_span + away, spans)) for away in range(1, spans)]
    )
    for at in range(1, count):
        send(
            small_ref, small_all.at[me], small_send.at[at], small_recv.at[at], dict(samp=peers[at])
        ).start()

    def gather_copies(which, step, sending):
        order = orders[which % 2]
        held = flips(me, order[:step])
        copies = []
        for at, spot in enumerate(held):
            slot = spot if sending else flip(spot, order[step])
            copies.append(
                send(
                    wholes[which].at[slot], wholes[which].at[slot],
                    gather_send.at[which, step, at], gather_recv.at[which, step, at],
                    dict(samp=flip(me, order[step])),
                )
            )
        return copies

    def gather_start(pair_at, step):
        for which in (2 * pair_at, 2 * pair_at + 1):
            for copy in gather_copies(which, step, True):
                copy.start()

    def gather_wait(pair_at, step):
        for which in (2 * pair_at, 2 * pair_at + 1):
            for copy in gather_copies(which, step, False):
                copy.wait_recv()

    tiles = pack_ref.shape[1]
    halves = (pl.ds(0, tiles // 2), pl.ds(tiles // 2, tiles - tiles // 2))

    def pack_copies(half, step, sending):
        order = orders[half]
        copies = []
        for at, spot in enumerate(flips(me, order[:step])):
            slot = spot if sending else flip(spot, order[step])
            copies.append(
                send(
                    pack_ref.at[slot, halves[half]], pack_ref.at[slot, halves[half]],
                    pack_send.at[half, step, at], pack_recv.at[half, step, at],
                    dict(samp=flip(me, order[step])),
                )
            )
        return copies

    def pack_start(step):
        for half in range(2):
            for copy in pack_copies(half, step, True):
                copy.start()

    def pack_wait(step):
        for half in range(2):
            for copy in pack_copies(half, step, False):
                copy.wait_recv()

    for copy in owns:
        copy.wait()
    gather_start(0, 0)
    gather_start(1, 0)

    for at in range(1, count):
        send(
            small_ref, small_all.at[peers[at]], small_send.at[at], small_recv.at[at], dict(samp=peers[at])
        ).wait_recv()
    full = small_all[0].astype(F32)
    for at in range(1, count):
        full = full + small_all[at].astype(F32)
    full_ref[...] = full
    project = full[8:, :LANES].astype(BF16)
    swap_rows = one_hot((8 * pairs, 8 * pairs), lambda row: row % 8 * pairs + row // 8)

    def pair_block(place, carry):
        slot = lax.rem(place, 2)
        struct = lax.div(place, rows // 8)
        first = pl.multiple_of(lax.rem(place, rows // 8) * 8, 8)

        @pl.when(place + 1 < structs * (rows // 8))
        def _():
            pair_copy(place + 1).start()

        pair_copy(place).wait()
        values = pair_buf[slot].astype(F32)
        centered = values - jnp.mean(values, axis=2, keepdims=True)
        variance = jnp.mean(centered * centered, axis=2, keepdims=True)
        normed = centered * lax.rsqrt(variance + EPSILON)
        low = normed.astype(BF16)
        rows_of = []
        for at in range(8):
            both = dot_nt(project, low[at, :MAIN])
            wide = jnp.concatenate((both[:pairs], both[pairs:]), axis=1)
            rows_of.append(wide)
        mixed = dot_nn(swap_rows, jnp.concatenate(rows_of, axis=0).astype(BF16))
        for at in range(pairs):
            pack_ref[me, struct * pairs + at, pl.ds(first, 8)] = mixed[at * 8 : (at + 1) * 8].astype(BF16)
        for at in range(tail):
            tails_ref[struct, at, pl.ds(first, 8)] = normed[:, MAIN + at]
        return carry

    blocks = structs * (rows // 8)
    cuts = [blocks * at // 8 for at in range(9)]
    lax.fori_loop(cuts[0], cuts[1], pair_block, 0)
    gather_wait(0, 0)
    gather_start(0, 1)
    lax.fori_loop(cuts[1], cuts[3], pair_block, 0)
    gather_wait(1, 0)
    gather_start(1, 1)
    gather_start(2, 0)
    lax.fori_loop(cuts[3], cuts[5], pair_block, 0)
    gather_wait(0, 1)
    gather_start(0, 2)
    lax.fori_loop(cuts[5], cuts[7], pair_block, 0)
    gather_wait(1, 1)
    gather_start(1, 2)
    lax.fori_loop(cuts[7], cuts[8], pair_block, 0)
    gather_wait(2, 0)
    gather_start(2, 1)

    lane = lax.broadcasted_iota(jnp.int32, (heads, heads), 0)
    other = lax.broadcasted_iota(jnp.int32, (heads, heads), 1)
    natural = jnp.where(other == lane // 2 + lane % 2 * pairs, 1.0, 0.0).astype(BF16)
    in_order = dot_nn(natural, project).astype(BF16)
    for struct in range(structs):
        parts = []
        for at in range(tail):
            parts.append(dot_nt(tails_ref[struct, at].astype(BF16), in_order))
        parts.append(jnp.zeros((rows, LANES - tail * heads), F32))
        pack_ref[me, structs * pairs + struct] = jnp.concatenate(parts, axis=1).astype(BF16)
    pack_start(0)

    gain_one = full[0:1, : cond_ref.shape[1]]
    act_normed, _ = norm_rows(act_ref[...].astype(F32))
    cond_normed, _ = norm_rows(cond_ref[...].astype(F32))
    cond_first = (cond_normed * gain_one).astype(BF16)
    gather_wait(0, 2)
    scale = scale_w[...].reshape(-1, width)
    shift = shift_w[...].reshape(-1, width)
    sig_first = sigmoid(dot_nn(cond_first, scale) + full[1:2])
    adapted = sig_first * act_normed + dot_nn(cond_first, shift)
    sig_ref[...] = sig_first
    adapted_ref[...] = adapted.astype(BF16)
    reorder = one_hot((rows, rows), lambda row: key_row_of(row, block, pieces))
    gather_wait(1, 2)
    for which, whole in ((0, key_w), (1, value_w)):
        for sample in range(samples):
            ordered = dot_nn(
                reorder, adapted[sample * rows : (sample + 1) * rows].astype(BF16)
            ).astype(BF16)
            kv_ref[my_span, which, sample] = dot_nn(ordered, whole[...].reshape(-1, width)).astype(BF16)

    def span_move(way, step, which, sending):
        delta = 1 - 2 * way
        shard = my_span - delta * step if sending else my_span - delta * (step + 1)
        target = my_span + delta
        there = (shard >= 0) & (shard < spans)
        if sending:
            there = there & (target >= 0) & (target < spans)
        copy = send(
            kv_ref.at[shard, which], kv_ref.at[shard, which],
            span_send.at[way, step, which], span_recv.at[way, step, which],
            dict(head=target if sending else my_span - delta),
        )
        return there, copy

    def span_start(step, which):
        for way in range(2):
            there, copy = span_move(way, step, which, True)
            pl.when(there)(copy.start)

    def span_wait(step, which):
        for way in range(2):
            there, copy = span_move(way, step, which, False)
            pl.when(there)(copy.wait_recv)

    span_start(0, 0)
    span_start(0, 1)
    gather_wait(2, 1)
    gather_start(2, 2)
    pack_wait(0)
    pack_start(1)
    gather_wait(2, 2)
    low = adapted.astype(BF16)
    query = dot_nn(low, query_w[...].reshape(-1, width)) + full[2:3]
    for sample in range(samples):
        query_ref[sample] = query[sample * rows : (sample + 1) * rows].astype(BF16)
    span_wait(0, 0)
    span_start(1, 0)
    gate_ref[...] = sigmoid(dot_nn(low, gate_w[...].reshape(-1, width)))
    span_wait(0, 1)
    span_start(1, 1)
    for step in range(1, spans - 1):
        for which in range(2):
            if step == 1 and which == 1:
                pack_wait(1)
                pack_start(2)
            span_wait(step, which)
            if step + 1 < spans - 1:
                span_start(step + 1, which)
    pack_wait(2)

    switch = tail_switch(count, heads, tail)
    places = key_places(count, block)
    keys_ref[keys:] = jnp.zeros_like(keys_ref[keys:])
    values_ref[keys:] = jnp.zeros_like(values_ref[keys:])

    def one_sample(sample, carry):
        struct = struct_ref[sample]
        valid = places < len_ref[struct]
        for span in range(spans):
            for which, held in ((0, keys_ref), (1, values_ref)):
                held[span * main_rows : (span + 1) * main_rows] = kv_ref[span, which, sample, :main_rows]
                spot = count * MAIN + span * (rows - main_rows)
                held[spot : spot + rows - main_rows] = kv_ref[span, which, sample, main_rows:]
        tiles_of = []
        for pair in range(count // 2):
            even = pack_ref[2 * pair, structs * pairs + struct]
            odd = swap_halves(pack_ref[2 * pair + 1, structs * pairs + struct])
            tiles_of.append(jnp.where(low_half(even), even, odd))
        mixed = dot_nn(jnp.concatenate(tiles_of, axis=1), switch).astype(BF16)
        for at in range(count // 2):
            tail_ref[at] = mixed[:, at * LANES : (at + 1) * LANES]

        def one_group(place, carry):
            acc_ref[...] = jnp.zeros_like(acc_ref)
            for at, (start, span, offset) in enumerate(windows):
                lanes = pl.ds(pl.multiple_of(place * group + start, LANES), span)
                mask = head_mask(span, offset)
                tile = struct * pairs + place * (len(windows) // 2) + at // 2
                bias = []
                for pair in range(count // 2):
                    even = pack_ref[2 * pair, tile]
                    odd = pack_ref[2 * pair + 1, tile]
                    if at % 2 == 0:
                        bias.append(jnp.where(low_half(even), even, swap_halves(odd)))
                    else:
                        bias.append(jnp.where(low_half(even), swap_halves(even), odd))
                per_tile = LANES // (count * tail)
                rest = tail_ref[place * (len(windows) // per_tile) + at // per_tile]
                turn = at % per_tile * count * tail
                bias.append(pltpu.roll(rest, LANES - turn, 1) if turn else rest)
                query = query_ref[sample, :, lanes]
                query = jnp.where(mask, query, jnp.zeros_like(query))
                scores = dot_nt(query, keys_ref[:, lanes]) * HEAD_DIM ** (-0.5) + jnp.concatenate(
                    bias, axis=1
                ).astype(F32)
                scores = jnp.where(valid, scores, NEG_BIG)
                weights = jnp.exp(scores - jnp.max(scores, axis=1, keepdims=True))
                weights = weights * (1.0 / jnp.sum(weights, axis=1, keepdims=True))
                weights = weights.astype(BF16)
                prob_ref[sample, place * len(windows) + at] = weights
                mixed = dot_nn(weights, values_ref[:, lanes])
                within = slice(start, start + span)
                acc_ref[:, within] += jnp.where(mask, mixed, 0.0)
            out_ref[sample, :, pl.ds(pl.multiple_of(place * group, LANES), group)] = acc_ref[
                ...
            ].astype(BF16)
            return carry

        return lax.fori_loop(0, width // group, one_group, carry)

    lax.fori_loop(0, samples, one_sample, 0)

    for at in range(1, count):
        send(
            small_ref, small_all.at[me], small_send.at[at], small_recv.at[at], dict(samp=peers[at])
        ).wait_send()
    for which in range(len(wholes)):
        for step in range(steps):
            for copy in gather_copies(which, step, True):
                copy.wait_send()
    for half in range(2):
        for step in range(steps):
            for copy in pack_copies(half, step, True):
                copy.wait_send()
    for step in range(spans - 1):
        for which in range(2):
            for way in range(2):
                there, copy = span_move(way, step, which, True)
                pl.when(there)(copy.wait_send)


def front(struct_of, struct_len, act, cond, small, pair, shards, samples, count, spans):
    total, width = act.shape
    rows = total // samples
    structs, block = pair.shape[0], pair.shape[2]
    heads = width // HEAD_DIM
    group, windows = head_windows(width)
    tail = block - MAIN
    tiles = structs * (heads // 2 + 1)
    steps = count.bit_length() - 1
    vmem = pl.BlockSpec(memory_space=pltpu.VMEM)
    smem = pl.BlockSpec(memory_space=pltpu.SMEM)
    far = pl.BlockSpec(memory_space=pl.ANY)
    dma = pltpu.SemaphoreType.DMA
    return pl.pallas_call(
        front_kernel,
        out_shape=(
            jax.ShapeDtypeStruct((samples, rows, width), BF16),
            jax.ShapeDtypeStruct((samples, heads, rows, KEY_LANES), BF16),
            jax.ShapeDtypeStruct((total, width), BF16),
            jax.ShapeDtypeStruct((total, width), F32),
            jax.ShapeDtypeStruct((total, width), F32),
            jax.ShapeDtypeStruct((samples, rows, width), BF16),
            jax.ShapeDtypeStruct((spans, 2, samples, rows, width), BF16),
            jax.ShapeDtypeStruct(small.shape, F32),
        )
        + tuple(jax.ShapeDtypeStruct((count,) + shard.shape, BF16) for shard in shards),
        in_specs=[smem, smem, vmem, vmem, vmem] + [far] * 7,
        out_specs=[vmem] * 14,
        scratch_shapes=[
            pltpu.VMEM((count,) + small.shape, BF16),
            pltpu.VMEM((count, tiles, rows, LANES), BF16),
            pltpu.VMEM((2, 8, block, LANES), BF16),
            pltpu.VMEM((structs, tail, rows, LANES), F32),
            pltpu.VMEM((KEY_LANES, width), BF16),
            pltpu.VMEM((KEY_LANES, width), BF16),
            pltpu.VMEM((count // 2, rows, LANES), BF16),
            pltpu.VMEM((rows, group), F32),
            dma((2,)),
            dma((len(shards),)),
            dma((count,)),
            dma((count,)),
            dma((len(shards), steps, count // 2)),
            dma((len(shards), steps, count // 2)),
            dma((2, steps, count // 2)),
            dma((2, steps, count // 2)),
            dma((2, spans - 1, 2)),
            dma((2, spans - 1, 2)),
        ],
        compiler_params=pltpu.CompilerParams(
            vmem_limit_bytes=60 << 20, collective_id=2, has_side_effects=True
        ),
        name="front",
    )(struct_of, struct_len, act, cond, small, pair, *shards)


class Halving:
    def __init__(self, me, order, source, zones, send_sem, recv_sem):
        self.me, self.order, self.source, self.zones = me, order, source, zones
        self.send_sem, self.recv_sem = send_sem, recv_sem

    def copies(self, step):
        kept = flips(self.me, self.order[step + 1 :])
        found = []
        for at, spot in enumerate(kept):
            if step == 0:
                leaving = self.source.at[flip(spot, self.order[0])]
            else:
                leaving = self.zones[step - 1].at[2 * at + 1]
            found.append(
                send(
                    leaving, self.zones[step].at[at], self.send_sem.at[step, at],
                    self.recv_sem.at[step, at], dict(samp=flip(self.me, self.order[step])),
                )
            )
        return found

    def start(self, step):
        for copy in self.copies(step):
            copy.start()

    def finish(self, step):
        kept = flips(self.me, self.order[step + 1 :])
        zone = self.zones[step]
        for at, copy in enumerate(self.copies(step)):
            copy.wait_recv()

            def add(turn, carry, at=at):
                lines = pl.ds(pl.multiple_of(turn * 16, 16), 16)
                mine = self.source[kept[at], lines] if step == 0 else self.zones[step - 1][2 * at, lines]
                zone[at, lines] = (zone[at, lines].astype(F32) + mine.astype(F32)).astype(BF16)
                return carry

            lax.fori_loop(0, zone.shape[1] // 16, add, 0)

    def settle(self):
        for step in range(len(self.order)):
            for copy in self.copies(step):
                copy.wait_send()


def zone_shapes(shapes, count):
    zones = []
    for rows, columns in shapes:
        size = count // 2
        while size:
            zones.append(pltpu.VMEM((size, rows, columns), BF16))
            size //= 2
    return zones


def spans_of(shapes, columns, spans):
    lines = []
    for at, (rows, wide) in enumerate(shapes):
        for half in range(wide // columns):
            lines += [(at, row, half * columns) for row in range(0, rows, 8)]
    each = len(lines) // spans
    moves = []
    for piece in range(spans):
        row = 0
        for at, start, lane in lines[piece * each : (piece + 1) * each]:
            last = moves[-1] if moves else None
            if last and last[0] == piece and last[2] == at and last[4] == lane and last[3] + last[5] == start:
                moves[-1] = last[:5] + (last[5] + 8,)
            else:
                moves.append((piece, row, at, start, lane, 8))
            row += 8
    return (each * 8, moves)


def attend_back_kernel(
    late_shapes, struct_ref, q_ref, kv_ref, do_ref, prob_ref, *refs
):
    lates, refs = refs[: len(late_shapes)], refs[len(late_shapes) :]
    (dq_ref, dkv_ref, dpb_ref, late_out, *refs) = refs
    steps = 3
    late_zones, refs = refs[: steps * len(late_shapes)], refs[steps * len(late_shapes) :]
    (late_send, late_recv, *refs) = refs
    attend_back_body(
        late_shapes, struct_ref, q_ref, kv_ref, do_ref, prob_ref, lates, dq_ref, dkv_ref, dpb_ref, late_out,
        late_zones, late_send, late_recv, *refs
    )


def attend_back_body(
    late_shapes, struct_ref, q_ref, kv_ref, do_ref, prob_ref, lates, dq_ref, dkv_ref, dpb_ref, late_out,
    late_zones, late_send, late_recv,
    key_ref, value_ref, dq_acc, dk_acc, dv_acc, first_ref, tail_ref, part_ref, span_ref, pack_ref,
    got_zero, got_one, got_two, span_send, span_recv, pack_send, pack_recv,
):
    samples, rows, width = q_ref.shape
    count = pack_ref.shape[0]
    spans = kv_ref.shape[0]
    heads = width // HEAD_DIM
    block = rows * spans // count
    tail = block - MAIN
    structs = pack_ref.shape[1] // (heads // 2 + 1)
    main_rows = rows // block * MAIN
    keys = count * block
    group, windows = head_windows(width)
    scale = HEAD_DIM ** (-0.5)
    me = lax.axis_index("samp")
    my_span = lax.axis_index("head")
    orders = reduce_orders(count)
    others = [lax.rem(my_span + away, spans) for away in range(1, spans)]
    greet(
        [dict(samp=flip(me, bit)) for bit in sorted(orders[0])] + [dict(head=other) for other in others]
    )
    movers = [
        Halving(
            me, orders[at % 2], lates[at], late_zones[3 * at : 3 * at + 3], late_send.at[at], late_recv.at[at]
        )
        for at in range(len(lates))
    ]
    for mover in movers:
        mover.start(0)
    switch = tail_switch(count, heads, tail)
    key_ref[keys:] = jnp.zeros_like(key_ref[keys:])
    value_ref[keys:] = jnp.zeros_like(value_ref[keys:])

    def span_copy(place, sample, away):
        lanes = pl.ds(pl.multiple_of(place * group, LANES), group)
        return send(
            part_ref.at[others[away], :, sample, :, lanes],
            span_ref.at[away, :, sample, :, lanes],
            span_send.at[place, sample, away],
            span_recv.at[place, sample, away],
            dict(head=others[away]),
        )

    def one_group(place, carry):
        for sample in range(samples):
            for span in range(spans):
                for which, held in ((0, key_ref), (1, value_ref)):
                    held[span * main_rows : (span + 1) * main_rows] = kv_ref[
                        span, which, sample, :main_rows, pl.ds(pl.multiple_of(place * group, LANES), group)
                    ]
                    spot = count * MAIN + span * (rows - main_rows)
                    held[spot : spot + rows - main_rows] = kv_ref[
                        span, which, sample, main_rows:, pl.ds(pl.multiple_of(place * group, LANES), group)
                    ]
            dq_acc[...] = jnp.zeros_like(dq_acc)
            dk_acc[...] = jnp.zeros_like(dk_acc)
            dv_acc[...] = jnp.zeros_like(dv_acc)
            kept = [jnp.where(struct_ref[0] == slab, 1.0, 0.0).astype(BF16) for slab in range(structs)]
            added = [jnp.where(struct_ref[1] == slab, 1.0, 0.0).astype(BF16) for slab in range(structs)]
            even_scores = None
            for at, (start, span, offset) in enumerate(windows):
                lanes = pl.ds(pl.multiple_of(place * group + start, LANES), span)
                within = slice(start, start + span)
                mask = head_mask(span, offset)
                upstream = do_ref[sample, :, lanes]
                upstream = jnp.where(mask, upstream, jnp.zeros_like(upstream))
                query = q_ref[sample, :, lanes]
                query = jnp.where(mask, query, jnp.zeros_like(query))
                low = prob_ref[sample, place * len(windows) + at]
                weights = low.astype(F32)
                d_weights = dot_nt(upstream, value_ref[:, within])
                dv_acc[:, within] += dot_tn(low[:, :keys], upstream)
                cross = weights * d_weights
                delta = jnp.sum(cross, axis=1, keepdims=True)
                d_scores = (cross - weights * delta).astype(BF16)
                dq_acc[:, within] += jnp.where(mask, dot_nn(d_scores, key_ref[:, within]), 0.0)
                dk_acc[:, within] += dot_tn(d_scores[:, :keys], query)
                per_tile = LANES // (count * tail)
                turn = at % per_tile * count * tail
                rest = d_scores[:, count * MAIN :]
                rest = pltpu.roll(rest, turn, 1) if turn else rest
                spot = place * (len(windows) // per_tile) + at // per_tile
                if turn:
                    tail_ref[sample, spot] += rest
                else:
                    tail_ref[sample, spot] = rest
                if at % 2 == 0:
                    even_scores = d_scores
                    continue
                for pair in range(count // 2):
                    even = even_scores[:, pair * LANES : (pair + 1) * LANES]
                    odd = d_scores[:, pair * LANES : (pair + 1) * LANES]
                    low_tile = jnp.where(low_half(even), even, swap_halves(odd))
                    high_tile = jnp.where(low_half(even), swap_halves(even), odd)
                    for side, tile in ((0, low_tile), (1, high_tile)):
                        owner = 2 * pair + side
                        if sample == 0:
                            first_ref[at // 2, owner] = tile
                            continue
                        old = first_ref[at // 2, owner]
                        for slab in range(structs):
                            spot = slab * (heads // 2) + place * (len(windows) // 2) + at // 2
                            pack_ref[owner, spot] = old * kept[slab] + tile * added[slab]
            lanes = pl.ds(pl.multiple_of(place * group, LANES), group)
            dq_ref[sample, :, lanes] = (dq_acc[...] * scale).astype(BF16)
            for span in range(spans):
                spot = count * MAIN + span * (rows - main_rows)
                for which, total, factor in ((0, dk_acc, scale), (1, dv_acc, 1.0)):
                    part_ref[span, which, sample, :main_rows, lanes] = (
                        total[span * main_rows : (span + 1) * main_rows] * factor
                    ).astype(BF16)
                    part_ref[span, which, sample, main_rows:, lanes] = (
                        total[spot : spot + rows - main_rows] * factor
                    ).astype(BF16)
            for away in range(spans - 1):
                span_copy(place, sample, away).start()
        return carry

    for place in range(width // group):
        one_group(place, 0)
        for mover in movers:
            mover.finish(place)
            mover.start(place + 1)

    mixed = []
    for sample in range(samples):
        whole = jnp.concatenate([tail_ref[sample, at] for at in range(count // 2)], axis=1)
        mixed.append(dot_nt(whole, switch))
    for pair in range(count // 2):
        tiles = [part[:, pair * LANES : (pair + 1) * LANES] for part in mixed]
        for slab in range(structs):
            both = jnp.zeros_like(tiles[0])
            for sample in range(samples):
                both = both + jnp.where(struct_ref[sample] == slab, tiles[sample], 0.0)
            spot = structs * heads // 2 + slab
            pack_ref[2 * pair, spot] = jnp.where(low_half(both), both, 0.0).astype(BF16)
            pack_ref[2 * pair + 1, spot] = jnp.where(low_half(both), swap_halves(both), 0.0).astype(BF16)

    tiles = pack_ref.shape[1]
    halves = (pl.ds(0, tiles // 2), pl.ds(tiles // 2, tiles - tiles // 2))
    bounds = ((0, tiles // 2), (tiles // 2, tiles))
    landing = (got_zero, got_one, got_two)

    def stage_copies(step, half):
        order = orders[half]
        kept = flips(me, order[step + 1 :])
        return [
            send(
                pack_ref.at[flip(spot, order[step]), halves[half]],
                landing[step].at[at, halves[half]],
                pack_send.at[step, half, at],
                pack_recv.at[step, half, at],
                dict(samp=flip(me, order[step])),
            )
            for at, spot in enumerate(kept)
        ]

    flights = [[stage_copies(step, half) for half in range(2)] for step in range(len(orders[0]))]
    for half in range(2):
        for copy in flights[0][half]:
            copy.start()
    for step in range(len(orders[0])):
        for half in range(2):
            kept = flips(me, orders[half][step + 1 :])
            for at, spot in enumerate(kept):
                flights[step][half][at].wait_recv()

                def add(tile, carry, spot=spot, at=at, step=step):
                    pack_ref[spot, tile] = (
                        pack_ref[spot, tile].astype(F32) + landing[step][at, tile].astype(F32)
                    ).astype(BF16)
                    return carry

                lax.fori_loop(bounds[half][0], bounds[half][1], add, 0)
            if step + 1 < len(orders[0]):
                for copy in flights[step + 1][half]:
                    copy.start()
        if step == 0:
            for mover in movers:
                mover.finish(2)
            _, moves = spans_of(late_shapes, width, spans)
            for piece, row, at, start, lane, size in moves:
                late_out[piece, row : row + size] = movers[at].zones[2][
                    0, start : start + size, lane : lane + width
                ]

    def out(tile, carry):
        dpb_ref[tile] = pack_ref[me, tile]
        return carry

    lax.fori_loop(0, tiles, out, 0)

    for place in range(width // group):
        for sample in range(samples):
            for away in range(spans - 1):
                span_copy(place, sample, away).wait_recv()
    for which in range(2):
        for sample in range(samples):
            total = part_ref[my_span, which, sample].astype(F32)
            for away in range(spans - 1):
                total += span_ref[away, which, sample].astype(F32)
            dkv_ref[which, sample] = total.astype(BF16)
    for place in range(width // group):
        for sample in range(samples):
            for away in range(spans - 1):
                span_copy(place, sample, away).wait_send()
    for stage in flights:
        for half in stage:
            for copy in half:
                copy.wait_send()
    for mover in movers:
        mover.settle()


def attend_back(struct_of, structs, query, key_value, upstream, prob, lates, count):
    samples, rows, width = query.shape
    spans = key_value.shape[0]
    heads = width // HEAD_DIM
    group, windows = head_windows(width)
    keys = rows * spans
    tiles = structs * (heads // 2 + 1)
    steps = count.bit_length() - 1
    vmem = pl.BlockSpec(memory_space=pltpu.VMEM)
    smem = pl.BlockSpec(memory_space=pltpu.SMEM)
    late_shapes = [late.shape[1:] for late in lates]
    each, _ = spans_of(late_shapes, width, spans)
    dma = pltpu.SemaphoreType.DMA
    return pl.pallas_call(
        functools.partial(attend_back_kernel, late_shapes),
        out_shape=(
            jax.ShapeDtypeStruct((samples, rows, width), BF16),
            jax.ShapeDtypeStruct((2, samples, rows, width), BF16),
            jax.ShapeDtypeStruct((tiles, rows, LANES), BF16),
            jax.ShapeDtypeStruct((spans, each, width), BF16),
        ),
        in_specs=[smem] + [vmem] * (4 + len(lates)),
        out_specs=[vmem] * 4,
        scratch_shapes=zone_shapes(late_shapes, count)
        + [
            dma((len(lates), steps, count // 2)),
            dma((len(lates), steps, count // 2)),
            pltpu.VMEM((KEY_LANES, group), BF16),
            pltpu.VMEM((KEY_LANES, group), BF16),
            pltpu.VMEM((rows, group), F32),
            pltpu.VMEM((keys, group), F32),
            pltpu.VMEM((keys, group), F32),
            pltpu.VMEM((len(windows) // 2, count, rows, LANES), BF16),
            pltpu.VMEM((samples, count // 2, rows, LANES), BF16),
            pltpu.VMEM((spans, 2, samples, rows, width), BF16),
            pltpu.VMEM((spans - 1, 2, samples, rows, width), BF16),
            pltpu.VMEM((count, tiles, rows, LANES), BF16),
            pltpu.VMEM((count // 2, tiles, rows, LANES), BF16),
            pltpu.VMEM((count // 4, tiles, rows, LANES), BF16),
            pltpu.VMEM((count // 8, tiles, rows, LANES), BF16),
            pltpu.SemaphoreType.DMA((width // group, samples, spans - 1)),
            pltpu.SemaphoreType.DMA((width // group, samples, spans - 1)),
            pltpu.SemaphoreType.DMA((steps, 2, count // 2)),
            pltpu.SemaphoreType.DMA((steps, 2, count // 2)),
        ],
        compiler_params=pltpu.CompilerParams(
            vmem_limit_bytes=60 << 20, collective_id=1, has_side_effects=True
        ),
        name="attend_back",
    )(struct_of, query, key_value, upstream, prob, *lates)


def pair_switch(heads):
    lanes = heads * MAIN
    source = lax.broadcasted_iota(jnp.int32, (lanes, lanes), 0)
    target = lax.broadcasted_iota(jnp.int32, (lanes, lanes), 1)
    return jnp.where(source % heads * MAIN + source // heads == target, 1.0, 0.0).astype(BF16)


def spread_heads(matrix, keys):
    channels, heads = matrix.shape
    one = lax.broadcasted_iota(jnp.int32, (heads, keys * heads), 0)
    two = lax.broadcasted_iota(jnp.int32, (heads, keys * heads), 1)
    repeat = dot_nn(matrix, jnp.where(two % heads == one, 1.0, 0.0).astype(BF16))
    owner = lax.broadcasted_iota(jnp.int32, (1, keys * heads), 1) // heads
    return [jnp.where(owner == key, repeat, 0.0).astype(BF16) for key in range(keys)]


def mean_pair():
    one = lax.broadcasted_iota(jnp.int32, (2 * LANES, 2 * LANES), 0) // LANES
    two = lax.broadcasted_iota(jnp.int32, (2 * LANES, 2 * LANES), 1) // LANES
    return jnp.where(one == two, 1.0 / LANES, 0.0).astype(BF16)


def norm_pair(low, means):
    centered = low.astype(F32) - dot_nn(low, means)
    variance = dot_nn((centered * centered).astype(BF16), means)
    inverse = lax.rsqrt(variance + EPSILON)
    return (centered * inverse, inverse)


GROUP = 16


def finish_kernel(
    early_shapes, late_shapes,
    act_ref, cond_ref, adapted_ref, sig_ref, full_ref, dq_ref, dkv_ref, dgate_ref, dmid_ref, dcond_ref,
    extra_ref, vector_ref, dpb_ref, late_ref, pair_ref, scale_w, shift_w, key_w, value_w, query_w, gate_w,
    *refs
):
    (ig_ref, cg_ref, pg_ref, small_out, *refs) = refs
    early_out, refs = refs[: len(early_shapes)], refs[len(early_shapes) :]
    late_out, refs = refs[: len(late_shapes)], refs[len(late_shapes) :]
    grads, refs = refs[: len(early_shapes)], refs[len(early_shapes) :]
    zones, refs = refs[: 3 * len(early_shapes)], refs[3 * len(early_shapes) :]
    (
        early_ref, early_got, late_got, early_all, late_all, small_ref, small_got, sum_ref, sum_got,
        pair_buf, lead_ref, lead_turned, spread_ref, block_ref, tail_block, weight_acc,
        pair_sem, block_sem, grad_send, grad_recv, late_send, late_recv, early_send, early_recv,
        small_send, small_recv, sum_send, sum_recv,
    ) = refs
    total, width = act_ref.shape
    count = grads[0].shape[0]
    spans = late_ref.shape[0]
    structs, block, rows, _ = pair_buf.shape
    samples = total // rows
    heads = width // HEAD_DIM
    tail = block - MAIN
    pieces = rows // block
    pairs = heads // 2
    me = lax.axis_index("samp")
    my_span = lax.axis_index("head")
    orders = reduce_orders(count)
    peers = flips(me, sorted(orders[0]))
    others = [lax.rem(my_span + away, spans) for away in range(1, spans)]

    loads = [
        pltpu.make_async_copy(pair_ref.at[struct], pair_buf.at[struct], pair_sem.at[struct])
        for struct in range(structs)
    ]
    for load in loads:
        load.start()
    greet([dict(samp=peer) for peer in peers[1:]] + [dict(head=other) for other in others])

    def span_scatter(source, got, sems):
        return [
            send(source.at[other], got.at[at], sems[0].at[0, at], sems[1].at[0, at], dict(head=other))
            for at, other in enumerate(others)
        ]

    def span_spread(whole, sems):
        return [
            send(whole.at[my_span], whole.at[my_span], sems[0].at[1, at], sems[1].at[1, at], dict(head=other))
            for at, other in enumerate(others)
        ]

    def span_add(source, got, whole):
        def add(turn, carry):
            lines = pl.ds(pl.multiple_of(turn * 8, 8), 8)
            summed = source[my_span, lines].astype(F32)
            for at in range(spans - 1):
                summed = summed + got[at, lines].astype(F32)
            whole[my_span, lines] = summed.astype(BF16)
            return carry

        lax.fori_loop(0, source.shape[1] // 8, add, 0)

    late_sems = (late_send, late_recv)
    early_sems = (early_send, early_recv)
    for copy in span_scatter(late_ref, late_got, late_sems):
        copy.start()

    adapted = adapted_ref[...]
    back = one_hot((rows, rows), lambda row: row)
    place = lax.broadcasted_iota(jnp.int32, (rows, rows), 1)
    row = lax.broadcasted_iota(jnp.int32, (rows, rows), 0)
    back = jnp.where(row == key_row_of(place, block, pieces), 1.0, 0.0).astype(BF16)
    d_query = jnp.concatenate([dq_ref[at].astype(F32) for at in range(samples)], axis=0).astype(BF16)
    d_key, d_value = [
        jnp.concatenate([dot_nn(back, dkv_ref[which, at]) for at in range(samples)], axis=0).astype(BF16)
        for which in range(2)
    ]
    d_gate = dgate_ref[...]

    def store_grad(at, left, right):
        size = grads[at].shape[1]
        value = dot_tn(left, right).astype(BF16)
        for owner in range(count):
            grads[at][owner] = value[owner * size : (owner + 1) * size]

    movers = [
        Halving(
            me, orders[at % 2], grads[at], zones[3 * at : 3 * at + 3], grad_send.at[at], grad_recv.at[at]
        )
        for at in range(len(grads))
    ]
    for at, upstream in ((2, d_key), (3, d_value), (4, d_query), (5, d_gate)):
        store_grad(at, adapted, upstream)
        movers[at].start(0)

    d_adapted = dot_nt(d_query, query_w[...].reshape(-1, width))
    d_adapted += dot_nt(d_key, key_w[...].reshape(-1, width))
    d_adapted += dot_nt(d_value, value_w[...].reshape(-1, width))
    d_adapted += dot_nt(d_gate, gate_w[...].reshape(-1, width))
    gain_one = full_ref[0:1, : cond_ref.shape[1]]
    act_normed, act_inverse = norm_rows(act_ref[...].astype(F32))
    cond_normed, cond_inverse = norm_rows(cond_ref[...].astype(F32))
    cond_first = (cond_normed * gain_one).astype(BF16)
    sig_first = sig_ref[...]
    d_shift = d_adapted.astype(BF16)
    d_pre = (d_adapted * act_normed * sigmoid_slope(sig_first)).astype(BF16)
    store_grad(0, cond_first, d_pre)
    store_grad(1, cond_first, d_shift)
    movers[0].start(0)
    movers[1].start(0)
    ig_ref[...] = dmid_ref[...] + norm_back(act_normed, act_inverse, d_adapted * sig_first)
    d_cond = dot_nt(d_shift, shift_w[...].reshape(-1, width)) + dot_nt(d_pre, scale_w[...].reshape(-1, width))
    cg_ref[...] = norm_back(cond_normed, cond_inverse, d_cond * gain_one + dcond_ref[...]) + extra_ref[...]
    small_ref[...] = vector_ref[...]
    small_ref[0:1, : cond_ref.shape[1]] = jnp.sum(d_cond * cond_normed, axis=0, keepdims=True)
    small_ref[1:2] = jnp.sum(d_pre.astype(F32), axis=0, keepdims=True)
    small_ref[2:3] = jnp.sum(d_query.astype(F32), axis=0, keepdims=True)

    even_odd = full_ref[8:, :LANES]
    one = lax.broadcasted_iota(jnp.int32, (heads, heads), 0)
    two = lax.broadcasted_iota(jnp.int32, (heads, heads), 1)
    natural = jnp.where(two == one // 2 + one % 2 * pairs, 1.0, 0.0).astype(BF16)
    project = dot_nn(natural, even_odd.astype(BF16))
    project = (project - jnp.mean(project, axis=1, keepdims=True)).astype(BF16)
    eye = jnp.where(
        lax.broadcasted_iota(jnp.int32, (LANES, LANES), 0) == lax.broadcasted_iota(jnp.int32, (LANES, LANES), 1),
        1.0, 0.0,
    ).astype(BF16)
    columns = dot_nt(eye, project).astype(BF16)
    for at, part in enumerate(spread_heads(columns, GROUP)):
        spread_ref[at * LANES : (at + 1) * LANES] = part
    switch = pair_switch(heads)
    means = mean_pair()
    groups = MAIN // GROUP
    for struct in range(structs):
        whole = jnp.concatenate([dpb_ref[struct * pairs + at] for at in range(pairs)], axis=1)
        mixed = dot_nt(whole, switch).astype(BF16)
        for at in range(groups):
            lead_ref[struct * groups + at] = mixed[:, at * GROUP * heads : (at + 1) * GROUP * heads]
    turn_eye = one_hot((rows, rows), lambda line: line)
    weight_acc[...] = jnp.zeros_like(weight_acc)
    for load in loads:
        load.wait()

    def back_keys(struct, first, keys, lead, target):
        for at in range(keys // 2):
            key = first + 2 * at
            low = jnp.concatenate((pair_buf[struct, key], pair_buf[struct, key + 1]), axis=1)
            normed, inverse = norm_pair(low, means)
            upstream = dot_nt(lead, spread_ref[2 * at * LANES : (2 * at + 2) * LANES, : lead.shape[1]])
            cross = dot_nn((upstream * normed).astype(BF16), means)
            result = inverse * (upstream - normed * cross)
            target(2 * at, result[:, :LANES])
            target(2 * at + 1, result[:, LANES:])
            kept = normed.astype(BF16)
            for side in range(2):
                turned = lead_turned[(2 * at + side) * heads : (2 * at + side + 1) * heads]
                weight_acc[...] += dot_nn(turned, kept[:, side * LANES : (side + 1) * LANES])

    def block_copy(turn):
        slot = lax.rem(turn, 2)
        return pltpu.make_async_copy(
            block_ref.at[slot],
            pg_ref.at[lax.div(turn, groups), pl.ds(lax.rem(turn, groups) * GROUP, GROUP)],
            block_sem.at[slot],
        )

    def pair_group(turn, carry):
        @pl.when(turn >= 2)
        def _():
            block_copy(turn - 2).wait()

        slot = lax.rem(turn, 2)
        lead = lead_ref[turn]
        lead_turned[...] = dot_tn(lead, turn_eye).astype(BF16)

        def target(at, value):
            block_ref[slot, at] = value

        back_keys(lax.div(turn, groups), lax.rem(turn, groups) * GROUP, GROUP, lead, target)
        block_copy(turn).start()
        return carry

    turns = structs * groups
    cuts = [turns * at // 6 for at in range(7)]
    lax.fori_loop(cuts[0], cuts[1], pair_group, 0)
    for at in range(len(movers)):
        movers[at].finish(0)
        movers[at].start(1)
    for copy in span_scatter(late_ref, late_got, late_sems):
        copy.wait_recv()
    span_add(late_ref, late_got, late_all)
    for copy in span_spread(late_all, late_sems):
        copy.start()
    lax.fori_loop(cuts[1], cuts[3], pair_group, 0)
    for at in range(len(movers)):
        movers[at].finish(1)
        movers[at].start(2)
    lax.fori_loop(cuts[3], cuts[5], pair_group, 0)
    for at in range(len(movers)):
        movers[at].finish(2)
    _, moves = spans_of(early_shapes, width, spans)
    for piece, line, at, start, lane, size in moves:
        early_ref[piece, line : line + size] = movers[at].zones[2][0, start : start + size, lane : lane + width]
    for copy in span_scatter(early_ref, early_got, early_sems):
        copy.start()
    lax.fori_loop(cuts[5], cuts[6], pair_group, 0)
    for struct in range(structs):
        lead = dpb_ref[structs * pairs + struct]
        lead = lead[:, : tail * heads]
        lead_turned[: tail * heads] = dot_tn(lead, turn_eye).astype(BF16)

        def tail_target(at, value, struct=struct):
            tail_block[struct, at] = value

        back_keys(struct, MAIN, tail, lead, tail_target)
    tail_copies = [
        pltpu.make_async_copy(
            tail_block.at[struct], pg_ref.at[struct, pl.ds(MAIN, tail)], pair_sem.at[struct]
        )
        for struct in range(structs)
    ]
    for copy in tail_copies:
        copy.start()
    small_ref[8:, :LANES] = weight_acc[...]

    def small_copies(sending):
        return [
            send(
                small_ref, small_got.at[me if sending else peers[at]], small_send.at[at], small_recv.at[at],
                dict(samp=peers[at]),
            )
            for at in range(1, count)
        ]

    def sum_copies(sending):
        return [
            send(
                sum_ref, sum_got.at[my_span if sending else lax.rem(my_span + spans - 1 - at, spans)],
                sum_send.at[at], sum_recv.at[at], dict(head=other),
            )
            for at, other in enumerate(others)
        ]

    for copy in small_copies(True):
        copy.start()
    small_got[me] = small_ref[...]
    for copy in small_copies(False):
        copy.wait_recv()
    summed = small_got[0]
    for at in range(1, count):
        summed = summed + small_got[at]
    sum_ref[...] = summed
    for copy in sum_copies(True):
        copy.start()
    sum_got[my_span] = summed
    for copy in span_scatter(early_ref, early_got, early_sems):
        copy.wait_recv()
    span_add(early_ref, early_got, early_all)
    for copy in span_spread(early_all, early_sems):
        copy.start()
    for copy in span_spread(late_all, late_sems):
        copy.wait_recv()
    _, late_moves = spans_of(late_shapes, width, spans)
    for piece, line, at, start, lane, size in late_moves:
        late_out[at][start : start + size, lane : lane + width] = late_all[piece, line : line + size].astype(F32)
    for copy in sum_copies(False):
        copy.wait_recv()
    summed = sum_got[0]
    for at in range(1, spans):
        summed = summed + sum_got[at]
    small_out[...] = summed
    for copy in span_spread(early_all, early_sems):
        copy.wait_recv()
    for piece, line, at, start, lane, size in moves:
        early_out[at][start : start + size, lane : lane + width] = early_all[piece, line : line + size].astype(F32)

    block_copy(turns - 2).wait()
    block_copy(turns - 1).wait()
    for copy in tail_copies:
        copy.wait()
    for mover in movers:
        mover.settle()
    for copies in (
        span_scatter(late_ref, late_got, late_sems), span_scatter(early_ref, early_got, early_sems),
        span_spread(late_all, late_sems), span_spread(early_all, early_sems),
        small_copies(True), sum_copies(True),
    ):
        for copy in copies:
            copy.wait_send()


def finish(
    act, cond, adapted, sig, full, d_query, d_key_value, d_gate, d_middle, d_cond, extra, vectors, packed,
    late, pair, weights, late_shapes,
):
    total, width = act.shape
    cond_width = cond.shape[1]
    spans, late_each, _ = late.shape
    count = weights[0].shape[0]
    structs, block, rows, _ = pair.shape
    heads = width // HEAD_DIM
    tail = block - MAIN
    early_shapes = [weight.shape[1:] for weight in weights]
    early_each, _ = spans_of(early_shapes, width, spans)
    steps = count.bit_length() - 1
    vmem = pl.BlockSpec(memory_space=pltpu.VMEM)
    far = pl.BlockSpec(memory_space=pl.ANY)
    dma = pltpu.SemaphoreType.DMA
    turns = structs * (MAIN // GROUP)
    return pl.pallas_call(
        functools.partial(finish_kernel, early_shapes, late_shapes),
        out_shape=(
            jax.ShapeDtypeStruct((total, width), F32),
            jax.ShapeDtypeStruct((total, cond_width), F32),
            jax.ShapeDtypeStruct(pair.shape, F32),
            jax.ShapeDtypeStruct(full.shape, F32),
        )
        + tuple(jax.ShapeDtypeStruct(shape, F32) for shape in list(early_shapes) + list(late_shapes)),
        in_specs=[vmem] * 14 + [far] + [vmem] * 6,
        out_specs=[vmem, vmem, far, vmem] + [vmem] * (len(early_shapes) + len(late_shapes)),
        scratch_shapes=[pltpu.VMEM(weight.shape, BF16) for weight in weights]
        + zone_shapes(early_shapes, count)
        + [
            pltpu.VMEM((spans, early_each, width), BF16),
            pltpu.VMEM((spans - 1, early_each, width), BF16),
            pltpu.VMEM((spans - 1, late_each, width), BF16),
            pltpu.VMEM((spans, early_each, width), BF16),
            pltpu.VMEM((spans, late_each, width), BF16),
            pltpu.VMEM(full.shape, F32),
            pltpu.VMEM((count,) + full.shape, F32),
            pltpu.VMEM(full.shape, F32),
            pltpu.VMEM((spans,) + full.shape, F32),
            pltpu.VMEM(pair.shape, BF16),
            pltpu.VMEM((turns, rows, GROUP * heads), BF16),
            pltpu.VMEM((GROUP * heads, rows), BF16),
            pltpu.VMEM((GROUP * LANES, GROUP * heads), BF16),
            pltpu.VMEM((2, GROUP, rows, LANES), F32),
            pltpu.VMEM((structs, tail, rows, LANES), F32),
            pltpu.VMEM((heads, LANES), F32),
            dma((structs,)),
            dma((2,)),
            dma((len(weights), steps, count // 2)),
            dma((len(weights), steps, count // 2)),
            dma((2, spans - 1)),
            dma((2, spans - 1)),
            dma((2, spans - 1)),
            dma((2, spans - 1)),
            dma((count,)),
            dma((count,)),
            dma((spans,)),
            dma((spans,)),
        ],
        compiler_params=pltpu.CompilerParams(
            vmem_limit_bytes=60 << 20, collective_id=3, has_side_effects=True
        ),
        name="finish",
    )(
        act, cond, adapted, sig, full, d_query, d_key_value, d_gate, d_middle, d_cond, extra, vectors, packed,
        late, pair, *weights
    )


def pack_rows(pieces, columns):
    return jnp.concatenate([piece.reshape(-1, columns) for piece in pieces], axis=0)


def pack_small(pieces, columns):
    flat = jnp.concatenate([piece.reshape(-1) for piece in pieces])
    rows = -(-flat.shape[0] // columns)
    rows = -(-rows // 8) * 8
    return jnp.pad(flat, (0, rows * columns - flat.shape[0])).reshape(rows, columns)


def unpack_rows(gathered, shapes):
    whole, at = [], 0
    count, _, columns = gathered.shape
    for rows, cols in shapes:
        held = rows * cols // columns
        whole.append(gathered[:, at : at + held].reshape(count * rows, cols))
        at += held
    return whole


def unpack_small(gathered, shapes):
    whole, at = [], 0
    count = gathered.shape[0]
    flat = gathered.reshape(count, -1)
    for shape in shapes:
        size = 1
        for extent in shape:
            size *= extent
        whole.append(flat[:, at : at + size].reshape((count * shape[0],) + shape[1:]))
        at += size
    return whole


def plain_kernel(struct_ref, len_ref, q_ref, k_ref, v_ref, bias_ref, out_ref, prob_ref, acc_ref):
    sample = pl.program_id(0)
    group_at = pl.program_id(1)
    length = len_ref[struct_ref[sample]]
    keys = k_ref.shape[1]
    group, windows = head_windows(q_ref.shape[2])
    valid = lax.broadcasted_iota(jnp.int32, (1, keys), 1) < length
    acc_ref[...] = jnp.zeros_like(acc_ref)
    for at, (start, width, offset) in enumerate(windows):
        lanes = slice(start, start + width)
        mask = head_mask(width, offset)
        query = q_ref[0, :, lanes]
        query = jnp.where(mask, query, jnp.zeros_like(query))
        scores = dot_nt(query, k_ref[0, :, lanes]) * HEAD_DIM ** (-0.5) + bias_ref[
            0, at
        ].astype(F32)
        scores = jnp.where(valid, scores, NEG_BIG)
        weights = jnp.exp(scores - jnp.max(scores, axis=1, keepdims=True))
        weights = weights * (1.0 / jnp.sum(weights, axis=1, keepdims=True))
        weights = weights.astype(BF16)
        prob_ref[0, at] = weights
        mixed = dot_nn(weights, v_ref[0, :, lanes])
        acc_ref[:, lanes] += jnp.where(mask, mixed, 0.0)
    out_ref[0] = acc_ref[...].astype(BF16)


def plain(struct_of, struct_len, query, key, value, bias):
    samples, rows, width = query.shape
    keys = key.shape[1]
    heads = bias.shape[1]
    group, windows = head_windows(width)
    each = len(windows)
    return pl.pallas_call(
        plain_kernel,
        out_shape=(
            jax.ShapeDtypeStruct((samples, rows, width), BF16),
            jax.ShapeDtypeStruct((samples, heads, rows, keys), BF16),
        ),
        grid_spec=pltpu.PrefetchScalarGridSpec(
            num_scalar_prefetch=2,
            grid=(samples, heads // each),
            in_specs=[
                pl.BlockSpec((1, rows, group), lambda b, g, s, n: (b, 0, g)),
                pl.BlockSpec((1, keys, group), lambda b, g, s, n: (b, 0, g)),
                pl.BlockSpec((1, keys, group), lambda b, g, s, n: (b, 0, g)),
                pl.BlockSpec((1, each, rows, keys), lambda b, g, s, n: (s[b], g, 0, 0)),
            ],
            out_specs=[
                pl.BlockSpec((1, rows, group), lambda b, g, s, n: (b, 0, g)),
                pl.BlockSpec((1, each, rows, keys), lambda b, g, s, n: (b, g, 0, 0)),
            ],
            scratch_shapes=[pltpu.VMEM((rows, group), F32)],
        ),
        compiler_params=pltpu.CompilerParams(vmem_limit_bytes=48 << 20),
        name="plain",
    )(struct_of, struct_len, query, key, value, bias)


def plain_back_kernel(
    struct_ref, q_ref, k_ref, v_ref, do_ref, prob_ref, dq_ref, dk_ref, dv_ref, bias_ref,
    dq_acc, dk_acc, dv_acc, bias_acc,
):
    samples = q_ref.shape[0]
    structs = bias_ref.shape[0]
    group, windows = head_windows(q_ref.shape[2])
    scale = HEAD_DIM ** (-0.5)
    for sample in range(samples):
        struct = struct_ref[sample]
        dq_acc[...] = jnp.zeros_like(dq_acc)
        dk_acc[...] = jnp.zeros_like(dk_acc)
        dv_acc[...] = jnp.zeros_like(dv_acc)
        for at, (start, width, offset) in enumerate(windows):
            lanes = slice(start, start + width)
            mask = head_mask(width, offset)
            upstream = do_ref[sample, :, lanes]
            upstream = jnp.where(mask, upstream, jnp.zeros_like(upstream))
            query = q_ref[sample, :, lanes]
            query = jnp.where(mask, query, jnp.zeros_like(query))
            low = prob_ref[sample, at]
            weights = low.astype(F32)
            d_weights = dot_nt(upstream, v_ref[sample, :, lanes])
            dv_acc[:, lanes] += dot_tn(low, upstream)
            cross = weights * d_weights
            delta = jnp.sum(cross, axis=1, keepdims=True)
            d_scores = (cross - weights * delta).astype(BF16)
            dq_acc[:, lanes] += jnp.where(mask, dot_nn(d_scores, k_ref[sample, :, lanes]), 0.0)
            dk_acc[:, lanes] += dot_tn(d_scores, query)
            for slab in range(structs):
                part = jnp.where(struct == slab, 1.0, 0.0) * d_scores.astype(F32)
                if sample == 0:
                    bias_acc[slab, at] = part
                elif sample < samples - 1:
                    bias_acc[slab, at] += part
                else:
                    bias_ref[slab, at] = (bias_acc[slab, at] + part).astype(BF16)
        dq_ref[sample] = (dq_acc[...] * scale).astype(BF16)
        dk_ref[sample] = (dk_acc[...] * scale).astype(BF16)
        dv_ref[sample] = dv_acc[...].astype(BF16)


def plain_back(struct_of, structs, query, key, value, upstream, prob):
    samples, rows, width = query.shape
    keys = key.shape[1]
    heads = prob.shape[1]
    group, windows = head_windows(width)
    each = len(windows)
    return pl.pallas_call(
        plain_back_kernel,
        out_shape=(
            jax.ShapeDtypeStruct((samples, rows, width), BF16),
            jax.ShapeDtypeStruct((samples, keys, width), BF16),
            jax.ShapeDtypeStruct((samples, keys, width), BF16),
            jax.ShapeDtypeStruct((structs, heads, rows, keys), BF16),
        ),
        grid_spec=pltpu.PrefetchScalarGridSpec(
            num_scalar_prefetch=1,
            grid=(heads // each,),
            in_specs=[
                pl.BlockSpec((samples, rows, group), lambda g, s: (0, 0, g)),
                pl.BlockSpec((samples, keys, group), lambda g, s: (0, 0, g)),
                pl.BlockSpec((samples, keys, group), lambda g, s: (0, 0, g)),
                pl.BlockSpec((samples, rows, group), lambda g, s: (0, 0, g)),
                pl.BlockSpec((samples, each, rows, keys), lambda g, s: (0, g, 0, 0)),
            ],
            out_specs=[
                pl.BlockSpec((samples, rows, group), lambda g, s: (0, 0, g)),
                pl.BlockSpec((samples, keys, group), lambda g, s: (0, 0, g)),
                pl.BlockSpec((samples, keys, group), lambda g, s: (0, 0, g)),
                pl.BlockSpec((structs, each, rows, keys), lambda g, s: (0, g, 0, 0)),
            ],
            scratch_shapes=[
                pltpu.VMEM((rows, group), F32),
                pltpu.VMEM((keys, group), F32),
                pltpu.VMEM((keys, group), F32),
                pltpu.VMEM((structs, each, rows, keys), F32),
            ],
        ),
        compiler_params=pltpu.CompilerParams(vmem_limit_bytes=60 << 20),
        name="plain_back",
    )(struct_of, query, key, value, upstream, prob)


def plain_device(
    act, cond, pair, struct_of, struct_len,
    gain_first, scale_first, scale_bias_first, shift_first,
    query_weight, query_bias, key_weight, value_weight, gate_weight, output_weight,
    pair_weight, zero_first, zero_bias_first,
    gain_second, scale_second, scale_bias_second, shift_second,
    swish_weight, linear_weight, down_weight, zero_second, zero_bias_second,
    cotangent,
):
    samples, rows, width = act.shape
    cond_width = cond.shape[2]
    total = samples * rows
    structs = pair.shape[0]
    small = (
        gain_first, scale_bias_first, query_bias, zero_bias_first, gain_second,
        scale_bias_second, zero_bias_second, pair_weight,
    )
    early = (scale_first, shift_first, query_weight, key_weight, value_weight, gate_weight)
    late = (
        output_weight, zero_first, scale_second, shift_second, swish_weight, linear_weight,
        down_weight, zero_second,
    )
    small_all = lax.all_gather(pack_small(small, width), "samp", axis=0)
    early_all = lax.all_gather(pack_rows(early, width), "samp", axis=0)
    late_all = lax.all_gather(pack_rows(late, width), "samp", axis=0)
    (gain_one, bias_one, bias_query, bias_zero_one, gain_two, bias_two, bias_zero_two, pair_proj_w) = (
        unpack_small(small_all, [piece.shape for piece in small])
    )
    (w_scale, w_shift, w_query, w_key, w_value, w_gate) = unpack_rows(
        early_all, [piece.shape for piece in early]
    )
    (w_out, w_zero, w_scale_two, w_shift_two, w_swish, w_linear, w_down, w_zero_two) = unpack_rows(
        late_all, [piece.shape for piece in late]
    )

    pair_normed, pair_inverse = norm_rows(pair.astype(F32))
    pair_low = pair_normed.astype(BF16)
    pair_proj = jnp.einsum("sijc,ch->shij", pair_low, pair_proj_w, preferred_element_type=F32)
    bias_all = lax.all_gather(pair_proj.astype(BF16), "samp", axis=3, tiled=True)

    act_rows = act.reshape(total, width).astype(F32)
    cond_low = cond.reshape(total, cond_width)
    act_normed, act_inverse = norm_rows(act_rows)
    cond_normed, cond_inverse = norm_rows(cond_low.astype(F32))
    cond_first = (cond_normed * gain_one.astype(F32)).astype(BF16)
    sig_first = jax.nn.sigmoid(product(cond_first, w_scale) + bias_one.astype(F32))
    adapted = (sig_first * act_normed + product(cond_first, w_shift)).astype(BF16)
    key_rows = product(adapted, w_key).astype(BF16)
    value_rows = product(adapted, w_value).astype(BF16)
    query_rows = (product(adapted, w_query) + bias_query.astype(F32)).astype(BF16)
    gate_sig = jax.nn.sigmoid(product(adapted, w_gate))
    key_value = jnp.stack((key_rows, value_rows)).reshape(2, samples, rows, width)
    key_value = lax.all_gather(key_value, "head", axis=2, tiled=True)
    query_split = query_rows.reshape(samples, rows, width)
    attended, prob = plain(
        struct_of, struct_len, query_split, key_value[0], key_value[1], bias_all
    )
    attn_float = attended.reshape(total, width).astype(F32)

    gated_rows = (gate_sig * attn_float).astype(BF16)
    branch = product(gated_rows, w_out)
    zero_sig_first = jax.nn.sigmoid(product(cond_low, w_zero) + bias_zero_one.astype(F32))
    middle = act_rows + zero_sig_first * branch
    mid_normed, mid_inverse = norm_rows(middle)
    cond_second = (cond_normed * gain_two.astype(F32)).astype(BF16)
    sig_second = jax.nn.sigmoid(product(cond_second, w_scale_two) + bias_two.astype(F32))
    adapted_two = (sig_second * mid_normed + product(cond_second, w_shift_two)).astype(BF16)
    swish_pre = product(adapted_two, w_swish)
    linear_pre = product(adapted_two, w_linear)
    swish_sig = jax.nn.sigmoid(swish_pre)
    hidden = (swish_pre * swish_sig * linear_pre).astype(BF16)
    down_rows = product(hidden, w_down)
    zero_sig_second = jax.nn.sigmoid(product(cond_low, w_zero_two) + bias_zero_two.astype(F32))
    layer_out = (middle + zero_sig_second * down_rows).astype(BF16)

    upstream = cotangent.reshape(total, width).astype(F32)
    d_down = (upstream * zero_sig_second).astype(BF16)
    d_zero_second = (upstream * down_rows * sigmoid_slope(zero_sig_second)).astype(BF16)
    d_hidden = back_product(d_down, w_down)
    d_swish = (
        d_hidden * linear_pre * swish_sig * (1.0 + swish_pre * (1.0 - swish_sig))
    ).astype(BF16)
    d_linear = (d_hidden * swish_pre * swish_sig).astype(BF16)
    d_adapted_two = back_product(d_swish, w_swish) + back_product(d_linear, w_linear)
    d_shift_second = d_adapted_two.astype(BF16)
    d_pre_second = (d_adapted_two * mid_normed * sigmoid_slope(sig_second)).astype(BF16)
    d_cond_second = back_product(d_shift_second, w_shift_two) + back_product(
        d_pre_second, w_scale_two
    )
    d_middle = upstream + norm_back(mid_normed, mid_inverse, d_adapted_two * sig_second)
    d_branch = (d_middle * zero_sig_first).astype(BF16)
    d_zero_first = (d_middle * branch * sigmoid_slope(zero_sig_first)).astype(BF16)
    d_gated = back_product(d_branch, w_out)
    d_gate = (d_gated * attn_float * sigmoid_slope(gate_sig)).astype(BF16)
    d_attended = (d_gated * gate_sig).astype(BF16)

    late_grads = (
        outer_sum(gated_rows, d_branch),
        outer_sum(cond_low, d_zero_first),
        outer_sum(cond_second, d_pre_second),
        outer_sum(cond_second, d_shift_second),
        outer_sum(adapted_two, d_swish),
        outer_sum(adapted_two, d_linear),
        outer_sum(hidden, d_down),
        outer_sum(cond_low, d_zero_second),
    )

    d_query, d_key, d_value, bias_grad = plain_back(
        struct_of, structs, query_split, key_value[0], key_value[1],
        d_attended.reshape(samples, rows, width), prob,
    )
    d_key_value = lax.psum_scatter(
        jnp.stack((d_key, d_value)), "head", scatter_dimension=2, tiled=True
    )
    d_query = d_query.reshape(total, width)
    d_key = d_key_value[0].reshape(total, width)
    d_value = d_key_value[1].reshape(total, width)
    bias_summed = lax.psum_scatter(bias_grad, "samp", scatter_dimension=3, tiled=True)
    pair_weight_grad = jnp.einsum("sijc,shij->ch", pair_low, bias_summed, preferred_element_type=F32)
    pair_upstream = jnp.einsum(
        "shij,ch->sijc", bias_summed, pair_proj_w, preferred_element_type=F32
    )
    pair_grad = norm_back(pair_normed, pair_inverse, pair_upstream)
    d_adapted = (
        back_product(d_query, w_query)
        + back_product(d_key, w_key)
        + back_product(d_value, w_value)
        + back_product(d_gate, w_gate)
    )
    d_shift_first = d_adapted.astype(BF16)
    d_pre_first = (d_adapted * act_normed * sigmoid_slope(sig_first)).astype(BF16)
    d_cond_first = back_product(d_shift_first, w_shift) + back_product(d_pre_first, w_scale)
    input_grad = d_middle + norm_back(act_normed, act_inverse, d_adapted * sig_first)
    d_cond_normed = d_cond_first * gain_one.astype(F32) + d_cond_second * gain_two.astype(F32)
    cond_grad = (
        norm_back(cond_normed, cond_inverse, d_cond_normed)
        + back_product(d_zero_first, w_zero)
        + back_product(d_zero_second, w_zero_two)
    )
    early_grads = (
        outer_sum(cond_first, d_pre_first),
        outer_sum(cond_first, d_shift_first),
        outer_sum(adapted, d_query),
        outer_sum(adapted, d_key),
        outer_sum(adapted, d_value),
        outer_sum(adapted, d_gate),
    )
    small_grads = (
        jnp.sum(d_cond_first * cond_normed, axis=0),
        column_sum(d_pre_first),
        column_sum(d_query),
        column_sum(d_zero_first),
        jnp.sum(d_cond_second * cond_normed, axis=0),
        column_sum(d_pre_second),
        column_sum(d_zero_second),
        pair_weight_grad,
    )
    count = lax.axis_size("samp")

    def pack_grads(grads, shapes):
        pieces = [
            grad.astype(BF16).reshape(count, shape[0] * shape[1] // width, width)
            for grad, shape in zip(grads, shapes)
        ]
        return jnp.concatenate(pieces, axis=1)

    def reduce(packed):
        summed = lax.psum_scatter(packed, "samp", scatter_dimension=0, tiled=True)
        return lax.psum(summed[0], "head").astype(F32)

    late_sum = reduce(pack_grads(late_grads, [piece.shape for piece in late]))
    early_sum = reduce(pack_grads(early_grads, [piece.shape for piece in early]))
    small_flat = jnp.concatenate(
        [grad.astype(BF16).reshape(count, -1) for grad in small_grads], axis=1
    )
    small_sum = lax.psum(
        lax.psum_scatter(small_flat, "samp", scatter_dimension=0, tiled=True), "head"
    ).astype(F32)
    (g_out, g_zero, g_scale_two, g_shift_two, g_swish, g_linear, g_down, g_zero_two) = unpack_rows(
        late_sum[None], [piece.shape for piece in late]
    )
    (g_scale, g_shift, g_query, g_key, g_value, g_gate) = unpack_rows(
        early_sum[None], [piece.shape for piece in early]
    )
    (g_gain, g_bias, g_bias_query, g_bias_zero, g_gain_two, g_bias_two, g_bias_zero_two, g_pair) = (
        unpack_small(small_sum, [piece.shape for piece in small])
    )
    return (
        layer_out.reshape(act.shape), input_grad.reshape(act.shape), cond_grad.reshape(cond.shape),
        pair_grad, g_gain, g_scale, g_bias, g_shift, g_query, g_bias_query, g_key, g_value, g_gate,
        g_out, g_pair, g_zero, g_bias_zero, g_gain_two, g_scale_two, g_bias_two, g_shift_two,
        g_swish, g_linear, g_down, g_zero_two, g_bias_zero_two,
    )


def per_device(
    act, cond, pair, struct_of, struct_len,
    gain_first, scale_first, scale_bias_first, shift_first,
    query_weight, query_bias, key_weight, value_weight, gate_weight, output_weight,
    pair_weight, zero_first, zero_bias_first,
    gain_second, scale_second, scale_bias_second, shift_second,
    swish_weight, linear_weight, down_weight, zero_second, zero_bias_second,
    cotangent,
):
    samples, rows, width = act.shape
    cond_width = cond.shape[2]
    total = samples * rows
    structs = pair.shape[0]
    block = pair.shape[2]
    count = lax.axis_size("samp")
    small = (
        gain_first, scale_bias_first, query_bias, zero_bias_first, gain_second,
        scale_bias_second, zero_bias_second,
    )
    early = (scale_first, shift_first, key_weight, value_weight, query_weight, gate_weight)
    late = (
        output_weight, zero_first, scale_second, shift_second, swish_weight, linear_weight,
        down_weight, zero_second,
    )
    spans = lax.axis_size("head")
    late_all = lax.all_gather(pack_rows(late, width), "samp", axis=0)
    mine = lax.broadcasted_iota(jnp.int32, (count, 1), 0) == lax.axis_index("samp")

    def spread(piece, columns):
        held = jnp.where(mine, piece[None], jnp.zeros_like(piece[None])).reshape(1, -1)
        return jnp.pad(held, ((0, 0), (0, columns - held.shape[1])))

    even_odd = jnp.concatenate((pair_weight[:, 0::2], pair_weight[:, 1::2]), axis=1).T
    held = jnp.where(mine.reshape(1, count, 1), even_odd[:, None], jnp.zeros_like(even_odd[:, None]))
    held = jnp.pad(held.reshape(even_odd.shape[0], -1), ((0, 0), (0, width - LANES)))
    packed_small = jnp.concatenate(
        [spread(piece, width) for piece in small] + [jnp.zeros((1, width), BF16), held], axis=0
    )
    (attended, prob, adapted, sig_first, gate_sig, query_split, key_value, full, *early_whole) = front(
        struct_of, struct_len, act.reshape(total, width), cond.reshape(total, cond_width), packed_small,
        pair, early, samples, count, spans,
    )
    (w_scale, w_shift, w_key, w_value, w_query, w_gate) = [
        whole.reshape(-1, width) for whole in early_whole
    ]
    gain_one, bias_zero_one, gain_two = full[0, :cond_width], full[3], full[4, :cond_width]
    bias_two, bias_zero_two = full[5], full[6]
    heads = width // HEAD_DIM
    (w_out, w_zero, w_scale_two, w_shift_two, w_swish, w_linear, w_down, w_zero_two) = unpack_rows(
        late_all, [piece.shape for piece in late]
    )

    act_rows = act.reshape(total, width).astype(F32)
    cond_low = cond.reshape(total, cond_width)
    act_normed, act_inverse = norm_rows(act_rows)
    cond_normed, cond_inverse = norm_rows(cond_low.astype(F32))
    cond_first = (cond_normed * gain_one.astype(F32)).astype(BF16)
    attn_float = attended.reshape(total, width).astype(F32)

    gated_rows = (gate_sig * attn_float).astype(BF16)
    branch = product(gated_rows, w_out)
    zero_sig_first = jax.nn.sigmoid(product(cond_low, w_zero) + bias_zero_one.astype(F32))
    middle = act_rows + zero_sig_first * branch
    mid_normed, mid_inverse = norm_rows(middle)
    cond_second = (cond_normed * gain_two.astype(F32)).astype(BF16)
    sig_second = jax.nn.sigmoid(product(cond_second, w_scale_two) + bias_two.astype(F32))
    adapted_two = (sig_second * mid_normed + product(cond_second, w_shift_two)).astype(BF16)
    swish_pre = product(adapted_two, w_swish)
    linear_pre = product(adapted_two, w_linear)
    swish_sig = jax.nn.sigmoid(swish_pre)
    hidden = (swish_pre * swish_sig * linear_pre).astype(BF16)
    down_rows = product(hidden, w_down)
    zero_sig_second = jax.nn.sigmoid(product(cond_low, w_zero_two) + bias_zero_two.astype(F32))
    layer_out = (middle + zero_sig_second * down_rows).astype(BF16)

    upstream = cotangent.reshape(total, width).astype(F32)
    d_down = (upstream * zero_sig_second).astype(BF16)
    d_zero_second = (upstream * down_rows * sigmoid_slope(zero_sig_second)).astype(BF16)
    d_hidden = back_product(d_down, w_down)
    d_swish = (
        d_hidden * linear_pre * swish_sig * (1.0 + swish_pre * (1.0 - swish_sig))
    ).astype(BF16)
    d_linear = (d_hidden * swish_pre * swish_sig).astype(BF16)
    d_adapted_two = back_product(d_swish, w_swish) + back_product(d_linear, w_linear)
    d_shift_second = d_adapted_two.astype(BF16)
    d_pre_second = (d_adapted_two * mid_normed * sigmoid_slope(sig_second)).astype(BF16)
    d_cond_second = back_product(d_shift_second, w_shift_two) + back_product(
        d_pre_second, w_scale_two
    )
    d_middle = upstream + norm_back(mid_normed, mid_inverse, d_adapted_two * sig_second)
    d_branch = (d_middle * zero_sig_first).astype(BF16)
    d_zero_first = (d_middle * branch * sigmoid_slope(zero_sig_first)).astype(BF16)
    d_gated = back_product(d_branch, w_out)
    d_gate = (d_gated * attn_float * sigmoid_slope(gate_sig)).astype(BF16)
    d_attended = (d_gated * gate_sig).astype(BF16)

    def shares(grad, shape):
        return grad.astype(BF16).reshape((count,) + shape)

    order = (4, 5, 6, 0, 1, 2, 7, 3)
    late_grads = (
        outer_sum(gated_rows, d_branch),
        outer_sum(cond_low, d_zero_first),
        outer_sum(cond_second, d_pre_second),
        outer_sum(cond_second, d_shift_second),
        outer_sum(adapted_two, d_swish),
        outer_sum(adapted_two, d_linear),
        outer_sum(hidden, d_down),
        outer_sum(cond_low, d_zero_second),
    )
    late_parts = [shares(late_grads[at], late[at].shape) for at in order]
    d_query, d_key_value, bias_packed, late_sum = attend_back(
        struct_of, structs, query_split, key_value, d_attended.reshape(samples, rows, width), prob,
        late_parts, count,
    )
    d_cond_two = d_cond_second * gain_two
    extra = back_product(d_zero_first, w_zero) + back_product(d_zero_second, w_zero_two)
    vectors = jnp.stack(
        [
            column_sum(d_zero_first),
            jnp.pad(jnp.sum(d_cond_second * cond_normed, axis=0), (0, width - cond_width)),
            column_sum(d_pre_second),
            column_sum(d_zero_second),
        ]
    )
    vectors = jnp.pad(vectors, ((3, full.shape[0] - 7), (0, 0)))
    (input_grad, cond_grad, pair_grad, small_sum, *weight_grads) = finish(
        act.reshape(total, width), cond_low, adapted, sig_first, full, d_query, d_key_value, d_gate,
        d_middle, d_cond_two, extra, vectors, bias_packed, late_sum, pair.transpose(0, 2, 1, 3),
        early_whole, [late[at].shape for at in order],
    )
    (g_scale, g_shift, g_key, g_value, g_query, g_gate) = weight_grads[:6]
    late_found = [None] * len(order)
    for at, grad in zip(order, weight_grads[6:]):
        late_found[at] = grad
    (g_out, g_zero, g_scale_two, g_shift_two, g_swish, g_linear, g_down, g_zero_two) = late_found
    mine_at = lax.axis_index("samp")

    def own(row, size):
        return lax.dynamic_slice(small_sum, (row, mine_at * size), (1, size))[0]

    cond_share, share = cond_width // count, width // count
    channels = pair.shape[3] // count
    g_pair = lax.dynamic_slice(small_sum, (8, mine_at * channels), (heads, channels)).T
    return (
        layer_out.reshape(act.shape), input_grad.reshape(act.shape), cond_grad.reshape(cond.shape),
        pair_grad.transpose(0, 2, 1, 3), own(0, cond_share), g_scale, own(1, share), g_shift, g_query,
        own(2, share), g_key, g_value, g_gate, g_out, g_pair, g_zero, own(3, share), own(4, cond_share),
        g_scale_two, own(5, share), g_shift_two, g_swish, g_linear, g_down, g_zero_two, own(6, share),
    )


def fits(mesh, act, pair):
    samples, rows, width = act.shape
    count, spans = mesh.shape["samp"], mesh.shape["head"]
    block = pair.shape[2]
    tail = block - MAIN
    heads = width // HEAD_DIM
    return (
        count == 8
        and samples == 2
        and tail > 0
        and heads * tail == MAIN
        and rows % block == 0
        and rows * spans == block * count
        and rows % 8 == 0
        and block * count <= KEY_LANES
    )


def solution(mesh):
    tokens = P("samp", "head", None)
    pairs = P(None, "head", "samp", None)
    vector = P("samp")
    matrix = P("samp", None)
    weights = (
        vector, matrix, vector, matrix, matrix, vector, matrix, matrix, matrix, matrix, matrix,
        matrix, vector, vector, matrix, vector, matrix, matrix, matrix, matrix, matrix, vector,
    )
    def choose(*arrays):
        body = per_device if fits(mesh, arrays[0], arrays[2]) else plain_device
        return body(*arrays)

    return jax.shard_map(
        choose,
        mesh=mesh,
        in_specs=(tokens, tokens, pairs, vector, P()) + weights + (tokens,),
        out_specs=(tokens, tokens, tokens, pairs) + weights,
        check_vma=False,
    )
```

```python
import functools

import jax
import jax.numpy as jnp
from jax import lax
from jax.experimental import pallas as pl
from jax.experimental.pallas import tpu as pltpu
from jax.sharding import PartitionSpec as P

HEAD_DIM = 48
LANES = 128
MAIN = 64
KEY_LANES = 640
MESH = pl.DeviceIdType.MESH
EPSILON = 1e-05
NEG_BIG = -1000000000.0
F32 = jnp.float32
BF16 = jnp.bfloat16


def norm_rows(values):
    centered = values - jnp.mean(values, axis=-1, keepdims=True)
    variance = jnp.mean(centered * centered, axis=-1, keepdims=True)
    inverse = lax.rsqrt(variance + EPSILON)
    return (centered * inverse, inverse)


def norm_back(normed, inverse, upstream):
    mean_grad = jnp.mean(upstream, axis=-1, keepdims=True)
    mean_cross = jnp.mean(upstream * normed, axis=-1, keepdims=True)
    return inverse * (upstream - mean_grad - normed * mean_cross)


def product(left_side, right_side):
    return lax.dot_general(
        left_side, right_side, (((1,), (0,)), ((), ())), preferred_element_type=F32
    )


def back_product(upstream, right_side):
    return lax.dot_general(
        upstream, right_side, (((1,), (1,)), ((), ())), preferred_element_type=F32
    )


def outer_sum(left_side, upstream):
    return lax.dot_general(
        left_side, upstream, (((0,), (0,)), ((), ())), preferred_element_type=F32
    )


def column_sum(upstream):
    return jnp.sum(upstream.astype(F32), axis=0)


def sigmoid_slope(gate_sig):
    return gate_sig * (1.0 - gate_sig)


def head_windows(width):
    group = LANES * HEAD_DIM // 16
    group = min(group, width)
    windows = []
    for head in range(group // HEAD_DIM):
        first = head * HEAD_DIM
        last = first + HEAD_DIM - 1
        start = first // LANES * LANES
        stop = (last // LANES + 1) * LANES
        windows.append((start, stop - start, first - start))
    return (group, windows)


def head_mask(width, offset):
    lane = lax.broadcasted_iota(jnp.int32, (1, width), 1)
    return (lane >= offset) & (lane < offset + HEAD_DIM)


def dot_nt(left, right):
    return lax.dot_general(left, right, (((1,), (1,)), ((), ())), preferred_element_type=F32)


def dot_nn(left, right):
    return lax.dot_general(left, right, (((1,), (0,)), ((), ())), preferred_element_type=F32)


def dot_tn(left, right):
    return lax.dot_general(left, right, (((0,), (0,)), ((), ())), preferred_element_type=F32)


def tail_switch(count, heads, tail):
    lanes = count * heads * tail
    source = lax.broadcasted_iota(jnp.int32, (lanes, lanes), 0)
    target = lax.broadcasted_iota(jnp.int32, (lanes, lanes), 1)
    owner = source // (heads * tail)
    head = source % heads
    spot = head * (count * tail) + owner * tail + source // heads % tail
    return jnp.where(spot == target, 1.0, 0.0).astype(BF16)


def swap_halves(tile):
    return pltpu.roll(tile, MAIN, 1)


def low_half(tile):
    return lax.broadcasted_iota(jnp.int32, tile.shape, 1) < MAIN


def key_places(count, block):
    lane = lax.broadcasted_iota(jnp.int32, (1, KEY_LANES), 1)
    tail = block - MAIN
    spare = lane - count * MAIN
    main_at = lane + tail * (lane // MAIN)
    tail_at = block * (spare // tail) + MAIN + spare % tail
    past = jnp.where(spare < count * tail, tail_at, count * block)
    return jnp.where(spare < 0, main_at, past)


def flip(index, bit):
    return index + bit - 2 * bit * lax.rem(lax.div(index, bit), 2)


def flips(index, bits):
    spots = [index]
    for bit in bits:
        spots = spots + [flip(spot, bit) for spot in spots]
    return spots


def reduce_orders(count):
    bits = []
    bit = 2
    while bit < count:
        bits.append(bit)
        bit *= 2
    half = len(bits) // 2
    return ([1] + bits, [1] + bits[half:] + bits[:half])


def greet(partners):
    barrier = pltpu.get_barrier_semaphore()
    for partner in partners:
        pl.semaphore_signal(barrier, inc=1, device_id=partner, device_id_type=MESH)
    pl.semaphore_wait(barrier, len(partners))


def send(source, target, send_sem, recv_sem, device):
    return pltpu.make_async_remote_copy(
        src_ref=source, dst_ref=target, send_sem=send_sem, recv_sem=recv_sem,
        device_id=device, device_id_type=MESH,
    )


def sigmoid(values):
    return 1.0 / (1.0 + jnp.exp(-values))


def one_hot(shape, source_of):
    target = lax.broadcasted_iota(jnp.int32, shape, 0)
    source = lax.broadcasted_iota(jnp.int32, shape, 1)
    return jnp.where(source == source_of(target), 1.0, 0.0).astype(BF16)


def key_row_of(place, block, pieces):
    tail = block - MAIN
    main_at = place // MAIN * block + place % MAIN
    spare = place - pieces * MAIN
    tail_at = spare // tail * block + MAIN + spare % tail
    return jnp.where(place < pieces * MAIN, main_at, tail_at)


def pair_switch(heads):
    lanes = heads * MAIN
    source = lax.broadcasted_iota(jnp.int32, (lanes, lanes), 0)
    target = lax.broadcasted_iota(jnp.int32, (lanes, lanes), 1)
    return jnp.where(source % heads * MAIN + source // heads == target, 1.0, 0.0).astype(BF16)


def spread_heads(matrix, keys):
    channels, heads = matrix.shape
    one = lax.broadcasted_iota(jnp.int32, (heads, keys * heads), 0)
    two = lax.broadcasted_iota(jnp.int32, (heads, keys * heads), 1)
    repeat = dot_nn(matrix, jnp.where(two % heads == one, 1.0, 0.0).astype(BF16))
    owner = lax.broadcasted_iota(jnp.int32, (1, keys * heads), 1) // heads
    return [jnp.where(owner == key, repeat, 0.0).astype(BF16) for key in range(keys)]


def mean_pair():
    one = lax.broadcasted_iota(jnp.int32, (2 * LANES, 2 * LANES), 0) // LANES
    two = lax.broadcasted_iota(jnp.int32, (2 * LANES, 2 * LANES), 1) // LANES
    return jnp.where(one == two, 1.0 / LANES, 0.0).astype(BF16)


def norm_pair(low, means):
    centered = low.astype(F32) - dot_nn(low, means)
    variance = dot_nn((centered * centered).astype(BF16), means)
    inverse = lax.rsqrt(variance + EPSILON)
    return (centered * inverse, inverse)


GROUP = 16


def columns_of(project):
    size = project.shape[1]
    eye = one_hot((size, size), lambda row: row)
    return dot_nt(eye, project).astype(BF16)


def front_kernel(
    struct_ref, len_ref, act_ref, cond_ref, small_ref, pair_ref,
    *refs
):
    shards, refs = refs[:14], refs[14:]
    (out_ref, prob_out, adapted_ref, sig_ref, gate_ref, query_ref, kv_out, full_ref, *refs) = refs
    whole_outs, refs = refs[:14], refs[14:]
    (prob_ref, kv_ref, *refs) = refs
    wholes, refs = refs[:14], refs[14:]
    (scale_w, shift_w, key_w, value_w, query_w, gate_w) = wholes[:6]
    (
        small_all, pack_ref, pair_buf, lead_ref, spread_ref, keys_ref, values_ref, tail_ref, acc_ref,
        pair_sem, own_sem, small_send, small_recv, gather_send, gather_recv, pack_send, pack_recv,
        span_send, span_recv, whole_sem, prob_sem, kv_sem,
    ) = refs
    total, width = act_ref.shape
    samples, rows = out_ref.shape[0], out_ref.shape[1]
    count = pack_ref.shape[0]
    spans = kv_ref.shape[0]
    heads = width // HEAD_DIM
    structs = pair_ref.shape[0]
    block = pair_ref.shape[1]
    tail = block - MAIN
    pieces = rows // block
    main_rows = pieces * MAIN
    keys = count * block
    pairs = heads // 2
    group, windows = head_windows(width)
    me = lax.axis_index("samp")
    my_span = lax.axis_index("head")
    reduce_pair = reduce_orders(count)
    orders = [order[1:] + order[:1] for order in reduce_pair]
    bits = sorted(reduce_pair[0])
    steps = len(bits)
    peers = flips(me, bits)

    owns = [
        pltpu.make_async_copy(shard, whole.at[me], own_sem.at[at])
        for at, (shard, whole) in enumerate(zip(shards, wholes))
    ]
    for copy in owns:
        copy.start()

    loads = [
        pltpu.make_async_copy(pair_ref.at[struct], pair_buf.at[struct], pair_sem.at[struct])
        for struct in range(structs)
    ]
    for load in loads:
        load.start()
    whole_moves = [
        pltpu.make_async_copy(whole, out, whole_sem.at[at])
        for at, (whole, out) in enumerate(zip(wholes, whole_outs))
    ]
    prob_moves = [
        pltpu.make_async_copy(prob_ref.at[at], prob_out.at[at], prob_sem.at[at]) for at in range(samples)
    ]
    kv_move = pltpu.make_async_copy(kv_ref, kv_out, kv_sem.at[0])
    small_all[me] = small_ref[...]
    greet(
        [dict(samp=peer) for peer in peers[1:]]
        + [dict(head=lax.rem(my_span + away, spans)) for away in range(1, spans)]
    )
    for at in range(1, count):
        send(
            small_ref, small_all.at[me], small_send.at[at], small_recv.at[at], dict(samp=peers[at])
        ).start()

    def gather_copies(which, step, sending):
        order = orders[which % 2]
        held = flips(me, order[:step])
        copies = []
        for at, spot in enumerate(held):
            slot = spot if sending else flip(spot, order[step])
            copies.append(
                send(
                    shards[which] if at == 0 else wholes[which].at[slot], wholes[which].at[slot],
                    gather_send.at[which, step, at], gather_recv.at[which, step, at],
                    dict(samp=flip(me, order[step])),
                )
            )
        return copies

    def gather_start(pair_at, step):
        for which in (2 * pair_at, 2 * pair_at + 1):
            for copy in gather_copies(which, step, True):
                copy.start()

    def gather_wait(pair_at, step):
        for which in (2 * pair_at, 2 * pair_at + 1):
            for copy in gather_copies(which, step, False):
                copy.wait_recv()

    def late_start(step):
        for pair_at in range(3, 7):
            gather_start(pair_at, step)

    def late_out(pair_at):
        gather_wait(pair_at, 2)
        for which in (2 * pair_at, 2 * pair_at + 1):
            whole_moves[which].start()

    def late_wait(step):
        for pair_at in range(3, 7):
            gather_wait(pair_at, step)

    tiles = pack_ref.shape[1]
    halves = (pl.ds(0, tiles // 2), pl.ds(tiles // 2, tiles - tiles // 2))

    def pack_copies(half, step, sending):
        order = orders[half]
        copies = []
        for at, spot in enumerate(flips(me, order[:step])):
            slot = spot if sending else flip(spot, order[step])
            copies.append(
                send(
                    pack_ref.at[slot, halves[half]], pack_ref.at[slot, halves[half]],
                    pack_send.at[half, step, at], pack_recv.at[half, step, at],
                    dict(samp=flip(me, order[step])),
                )
            )
        return copies

    def pack_start(step):
        for half in range(2):
            for copy in pack_copies(half, step, True):
                copy.start()

    def pack_wait(step):
        for half in range(2):
            for copy in pack_copies(half, step, False):
                copy.wait_recv()

    gather_start(0, 0)
    gather_start(1, 0)

    for at in range(1, count):
        send(
            small_ref, small_all.at[peers[at]], small_send.at[at], small_recv.at[at], dict(samp=peers[at])
        ).wait_recv()
    full = small_all[0].astype(F32)
    for at in range(1, count):
        full = full + small_all[at].astype(F32)
    full_ref[...] = full
    for at, part in enumerate(spread_heads(columns_of(full[8:, :LANES].astype(BF16)), GROUP)):
        spread_ref[at * LANES : (at + 1) * LANES] = part
    means = mean_pair()
    order_switch = pair_switch(heads)
    groups = MAIN // GROUP
    for load in loads:
        load.wait()

    def project_keys(struct, first, number):
        total_lead = None
        for at in range(number // 2):
            key = first + 2 * at
            low = jnp.concatenate((pair_buf[struct, key], pair_buf[struct, key + 1]), axis=1)
            normed, _ = norm_pair(low, means)
            lead = dot_nn(
                normed.astype(BF16),
                spread_ref[2 * at * LANES : (2 * at + 2) * LANES, : number * heads],
            )
            total_lead = lead if total_lead is None else total_lead + lead
        return total_lead.astype(BF16)

    def pair_group(turn, carry):
        lead_ref[turn] = project_keys(lax.div(turn, groups), lax.rem(turn, groups) * GROUP, GROUP)
        return carry

    turns = structs * groups
    cuts = [turns * at // 6 for at in range(7)]
    gather_wait(0, 0)
    gather_start(0, 1)
    gather_wait(1, 0)
    gather_start(1, 1)
    gather_start(2, 0)
    lax.fori_loop(cuts[0], cuts[1], pair_group, 0)
    gather_wait(0, 1)
    gather_start(0, 2)
    lax.fori_loop(cuts[1], cuts[2], pair_group, 0)
    gather_wait(2, 0)
    gather_start(2, 1)
    late_start(0)
    lax.fori_loop(cuts[2], cuts[3], pair_group, 0)
    gather_wait(1, 1)
    gather_start(1, 2)

    gain_one = full[0:1, : cond_ref.shape[1]]
    act_normed, _ = norm_rows(act_ref[...].astype(F32))
    cond_normed, _ = norm_rows(cond_ref[...].astype(F32))
    cond_first = (cond_normed * gain_one).astype(BF16)
    for copy in owns[:6]:
        copy.wait()
    gather_wait(0, 2)
    scale = scale_w[...].reshape(-1, width)
    shift = shift_w[...].reshape(-1, width)
    sig_first = sigmoid(dot_nn(cond_first, scale) + full[1:2])
    adapted = sig_first * act_normed + dot_nn(cond_first, shift)
    sig_ref[...] = sig_first
    adapted_ref[...] = adapted.astype(BF16)
    reorder = one_hot((rows, rows), lambda row: key_row_of(row, block, pieces))
    gather_wait(1, 2)
    for which, whole in ((0, key_w), (1, value_w)):
        for sample in range(samples):
            ordered = dot_nn(
                reorder, adapted[sample * rows : (sample + 1) * rows].astype(BF16)
            ).astype(BF16)
            kv_ref[my_span, which, sample] = dot_nn(ordered, whole[...].reshape(-1, width)).astype(BF16)

    def span_move(way, step, which, sending):
        delta = 1 - 2 * way
        shard = my_span - delta * step if sending else my_span - delta * (step + 1)
        target = my_span + delta
        there = (shard >= 0) & (shard < spans)
        if sending:
            there = there & (target >= 0) & (target < spans)
        copy = send(
            kv_ref.at[shard, which], kv_ref.at[shard, which],
            span_send.at[way, step, which], span_recv.at[way, step, which],
            dict(head=target if sending else my_span - delta),
        )
        return there, copy

    def span_start(step, which):
        for way in range(2):
            there, copy = span_move(way, step, which, True)
            pl.when(there)(copy.start)

    def span_wait(step, which):
        for way in range(2):
            there, copy = span_move(way, step, which, False)
            pl.when(there)(copy.wait_recv)

    span_start(0, 0)
    lax.fori_loop(cuts[3], cuts[6], pair_group, 0)
    for struct in range(structs):
        whole = jnp.concatenate([lead_ref[struct * groups + at] for at in range(groups)], axis=1)
        mixed = dot_nn(whole, order_switch).astype(BF16)
        for at in range(pairs):
            pack_ref[me, struct * pairs + at] = mixed[:, at * LANES : (at + 1) * LANES]
        rest = project_keys(struct, MAIN, tail)
        blank = jnp.zeros((rows, LANES - tail * heads), BF16)
        pack_ref[me, structs * pairs + struct] = jnp.concatenate((rest, blank), axis=1)
    pack_start(0)
    span_wait(0, 0)
    span_start(1, 0)
    span_start(0, 1)
    gather_wait(2, 1)
    gather_start(2, 2)
    low = adapted.astype(BF16)
    gather_wait(2, 2)
    for move in whole_moves[:6]:
        move.start()
    query = dot_nn(low, query_w[...].reshape(-1, width)) + full[2:3]
    for sample in range(samples):
        query_ref[sample] = query[sample * rows : (sample + 1) * rows].astype(BF16)
    pack_wait(0)
    pack_start(1)
    gate_ref[...] = sigmoid(dot_nn(low, gate_w[...].reshape(-1, width)))
    late_wait(0)
    late_start(1)
    for step in range(1, spans - 1):
        span_wait(step, 0)
        if step + 1 < spans - 1:
            span_start(step + 1, 0)
        span_wait(step - 1, 1)
        span_start(step, 1)
    pack_wait(1)
    pack_start(2)

    switch = tail_switch(count, heads, tail)
    places = key_places(count, block)
    keys_ref[keys:] = jnp.zeros_like(keys_ref[keys:])
    values_ref[keys:] = jnp.zeros_like(values_ref[keys:])

    def gather_keys(sample, which, held):
        for span in range(spans):
            held[span * main_rows : (span + 1) * main_rows] = kv_ref[span, which, sample, :main_rows]
            spot = count * MAIN + span * (rows - main_rows)
            held[spot : spot + rows - main_rows] = kv_ref[span, which, sample, main_rows:]

    def one_sample(sample, carry):
        struct = struct_ref[sample]
        valid = places < len_ref[struct]
        gather_keys(sample, 0, keys_ref)
        tiles_of = []
        for pair in range(count // 2):
            even = pack_ref[2 * pair, structs * pairs + struct]
            odd = swap_halves(pack_ref[2 * pair + 1, structs * pairs + struct])
            tiles_of.append(jnp.where(low_half(even), even, odd))
        mixed = dot_nn(jnp.concatenate(tiles_of, axis=1), switch).astype(BF16)
        for at in range(count // 2):
            tail_ref[at] = mixed[:, at * LANES : (at + 1) * LANES]

        def one_group(place, carry):
            for at, (start, span, offset) in enumerate(windows):
                lanes = pl.ds(pl.multiple_of(place * group + start, LANES), span)
                mask = head_mask(span, offset)
                tile = struct * pairs + place * (len(windows) // 2) + at // 2
                bias = []
                for pair in range(count // 2):
                    even = pack_ref[2 * pair, tile]
                    odd = pack_ref[2 * pair + 1, tile]
                    if at % 2 == 0:
                        bias.append(jnp.where(low_half(even), even, swap_halves(odd)))
                    else:
                        bias.append(jnp.where(low_half(even), swap_halves(even), odd))
                per_tile = LANES // (count * tail)
                rest = tail_ref[place * (len(windows) // per_tile) + at // per_tile]
                turn = at % per_tile * count * tail
                bias.append(pltpu.roll(rest, LANES - turn, 1) if turn else rest)
                query = query_ref[sample, :, lanes]
                query = jnp.where(mask, query, jnp.zeros_like(query))
                scores = dot_nt(query, keys_ref[:, lanes]) * HEAD_DIM ** (-0.5) + jnp.concatenate(
                    bias, axis=1
                ).astype(F32)
                scores = jnp.where(valid, scores, NEG_BIG)
                weights = jnp.exp(scores - jnp.max(scores, axis=1, keepdims=True))
                weights = weights * (1.0 / jnp.sum(weights, axis=1, keepdims=True))
                prob_ref[sample, place * len(windows) + at] = weights.astype(BF16)
            return carry

        return lax.fori_loop(0, width // group, one_group, carry)

    def mix_sample(sample, carry):
        gather_keys(sample, 1, values_ref)

        def mix_group(place, carry):
            acc_ref[...] = jnp.zeros_like(acc_ref)
            for at, (start, span, offset) in enumerate(windows):
                lanes = pl.ds(pl.multiple_of(place * group + start, LANES), span)
                weights = prob_ref[sample, place * len(windows) + at]
                mixed = dot_nn(weights, values_ref[:, lanes])
                within = slice(start, start + span)
                acc_ref[:, within] += jnp.where(head_mask(span, offset), mixed, 0.0)
            out_ref[sample, :, pl.ds(pl.multiple_of(place * group, LANES), group)] = acc_ref[
                ...
            ].astype(BF16)
            return carry

        return lax.fori_loop(0, width // group, mix_group, carry)

    pack_wait(2)
    lax.fori_loop(0, samples // 2, one_sample, 0)
    for move in prob_moves[: samples // 2]:
        move.start()
    span_wait(spans - 2, 1)
    kv_move.start()
    lax.fori_loop(samples // 2, samples, one_sample, 0)
    for move in prob_moves[samples // 2 :]:
        move.start()
    for copy in owns[6:]:
        copy.wait()
    for pair_at in range(3, 7):
        gather_wait(pair_at, 1)
        gather_start(pair_at, 2)
        if pair_at == 3:
            lax.fori_loop(0, samples, mix_sample, 0)
        else:
            late_out(pair_at - 1)
    late_out(6)
    for move in whole_moves + prob_moves + [kv_move]:
        move.wait()

    for at in range(1, count):
        send(
            small_ref, small_all.at[me], small_send.at[at], small_recv.at[at], dict(samp=peers[at])
        ).wait_send()
    for which in range(len(wholes)):
        for step in range(steps):
            for copy in gather_copies(which, step, True):
                copy.wait_send()
    for half in range(2):
        for step in range(steps):
            for copy in pack_copies(half, step, True):
                copy.wait_send()
    for step in range(spans - 1):
        for which in range(2):
            for way in range(2):
                there, copy = span_move(way, step, which, True)
                pl.when(there)(copy.wait_send)


def front(struct_of, struct_len, act, cond, small, pair, shards, samples, count, spans):
    total, width = act.shape
    rows = total // samples
    structs, block = pair.shape[0], pair.shape[1]
    heads = width // HEAD_DIM
    group, windows = head_windows(width)
    tail = block - MAIN
    tiles = structs * (heads // 2 + 1)
    steps = count.bit_length() - 1
    vmem = pl.BlockSpec(memory_space=pltpu.VMEM)
    smem = pl.BlockSpec(memory_space=pltpu.SMEM)
    far = pl.BlockSpec(memory_space=pl.ANY)
    dma = pltpu.SemaphoreType.DMA
    return pl.pallas_call(
        front_kernel,
        out_shape=(
            jax.ShapeDtypeStruct((samples, rows, width), BF16),
            jax.ShapeDtypeStruct((samples, heads, rows, KEY_LANES), BF16),
            jax.ShapeDtypeStruct((total, width), BF16),
            jax.ShapeDtypeStruct((total, width), F32),
            jax.ShapeDtypeStruct((total, width), F32),
            jax.ShapeDtypeStruct((samples, rows, width), BF16),
            jax.ShapeDtypeStruct((spans, 2, samples, rows, width), BF16),
            jax.ShapeDtypeStruct(small.shape, F32),
        )
        + tuple(jax.ShapeDtypeStruct((count,) + shard.shape, BF16) for shard in shards),
        in_specs=[smem, smem, vmem, vmem, vmem] + [far] * 15,
        out_specs=[vmem, far] + [vmem] * 4 + [far, vmem] + [far] * 14,
        scratch_shapes=[
            pltpu.VMEM((samples, heads, rows, KEY_LANES), BF16),
            pltpu.VMEM((spans, 2, samples, rows, width), BF16),
        ]
        + [pltpu.VMEM((count,) + shard.shape, BF16) for shard in shards]
        + [
            pltpu.VMEM((count,) + small.shape, BF16),
            pltpu.VMEM((count, tiles, rows, LANES), BF16),
            pltpu.VMEM(pair.shape, BF16),
            pltpu.VMEM((structs * MAIN // GROUP, rows, GROUP * heads), BF16),
            pltpu.VMEM((GROUP * LANES, GROUP * heads), BF16),
            pltpu.VMEM((KEY_LANES, width), BF16),
            pltpu.VMEM((KEY_LANES, width), BF16),
            pltpu.VMEM((count // 2, rows, LANES), BF16),
            pltpu.VMEM((rows, group), F32),
            dma((structs,)),
            dma((len(shards),)),
            dma((count,)),
            dma((count,)),
            dma((len(shards), steps, count // 2)),
            dma((len(shards), steps, count // 2)),
            dma((2, steps, count // 2)),
            dma((2, steps, count // 2)),
            dma((2, spans - 1, 2)),
            dma((2, spans - 1, 2)),
            dma((len(shards),)),
            dma((samples,)),
            dma((1,)),
        ],
        compiler_params=pltpu.CompilerParams(
            vmem_limit_bytes=60 << 20, collective_id=2, has_side_effects=True
        ),
        name="front",
    )(struct_of, struct_len, act, cond, small, pair, *shards)


def middle_kernel(
    attn_ref, gate_ref, act_ref, cond_ref, cot_ref, full_ref,
    swish_w, linear_w, down_w, out_w, zero_w, scale_w, zero_two_w, shift_w,
    layer_ref, dgate_ref, dattn_ref, dmid_ref, dcond_ref, extra_ref, vector_ref,
    swish_g, linear_g, down_g, out_g, zero_g, scale_g, zero_two_g, shift_g,
):
    total, width = act_ref.shape
    samples, rows, _ = attn_ref.shape
    cond_width = cond_ref.shape[1]

    def whole(ref):
        return ref[...].reshape(-1, ref.shape[2])

    def store_grad(ref, left, right):
        size = ref.shape[1]
        step = 2 * size if size * 2 < left.shape[1] else size
        for first in range(0, left.shape[1], step):
            value = dot_tn(left[:, first : first + step], right).astype(BF16)
            for at in range(step // size):
                ref[first // size + at] = value[at * size : (at + 1) * size]

    cond = cond_ref[...]
    cond_normed, _ = norm_rows(cond.astype(F32))
    gain_two = full_ref[4:5, :cond_width]
    cond_second = (cond_normed * gain_two).astype(BF16)
    attn = jnp.concatenate([attn_ref[at].astype(F32) for at in range(samples)], axis=0)
    gate_sig = gate_ref[...]
    gated = (gate_sig * attn).astype(BF16)
    branch = dot_nn(gated, whole(out_w))
    zero_sig = sigmoid(dot_nn(cond, whole(zero_w)) + full_ref[3:4])
    middle = act_ref[...].astype(F32) + zero_sig * branch
    mid_normed, mid_inverse = norm_rows(middle)
    sig_second = sigmoid(dot_nn(cond_second, whole(scale_w)) + full_ref[5:6])
    adapted = (sig_second * mid_normed + dot_nn(cond_second, whole(shift_w))).astype(BF16)
    swish_pre = dot_nn(adapted, whole(swish_w))
    linear_pre = dot_nn(adapted, whole(linear_w))
    swish_sig = sigmoid(swish_pre)
    hidden = (swish_pre * swish_sig * linear_pre).astype(BF16)
    down_rows = dot_nn(hidden, whole(down_w))
    zero_sig_two = sigmoid(dot_nn(cond, whole(zero_two_w)) + full_ref[6:7])
    layer_ref[...] = (middle + zero_sig_two * down_rows).astype(BF16)

    upstream = cot_ref[...].astype(F32)
    d_down = (upstream * zero_sig_two).astype(BF16)
    d_zero_two = (upstream * down_rows * sigmoid_slope(zero_sig_two)).astype(BF16)
    store_grad(down_g, hidden, d_down)
    store_grad(zero_two_g, cond, d_zero_two)
    d_hidden = dot_nt(d_down, whole(down_w))
    d_swish = (d_hidden * linear_pre * swish_sig * (1.0 + swish_pre * (1.0 - swish_sig))).astype(BF16)
    d_linear = (d_hidden * swish_pre * swish_sig).astype(BF16)
    store_grad(swish_g, adapted, d_swish)
    store_grad(linear_g, adapted, d_linear)
    d_adapted = dot_nt(d_swish, whole(swish_w)) + dot_nt(d_linear, whole(linear_w))
    d_shift = d_adapted.astype(BF16)
    d_pre = (d_adapted * mid_normed * sigmoid_slope(sig_second)).astype(BF16)
    store_grad(scale_g, cond_second, d_pre)
    store_grad(shift_g, cond_second, d_shift)
    d_cond = dot_nt(d_shift, whole(shift_w)) + dot_nt(d_pre, whole(scale_w))
    dcond_ref[...] = d_cond * gain_two
    d_middle = upstream + norm_back(mid_normed, mid_inverse, d_adapted * sig_second)
    dmid_ref[...] = d_middle
    d_branch = (d_middle * zero_sig).astype(BF16)
    d_zero = (d_middle * branch * sigmoid_slope(zero_sig)).astype(BF16)
    store_grad(out_g, gated, d_branch)
    store_grad(zero_g, cond, d_zero)
    extra_ref[...] = dot_nt(d_zero, whole(zero_w)) + dot_nt(d_zero_two, whole(zero_two_w))
    d_gated = dot_nt(d_branch, whole(out_w))
    dgate_ref[...] = (d_gated * attn * sigmoid_slope(gate_sig)).astype(BF16)
    d_attn = d_gated * gate_sig
    for at in range(samples):
        dattn_ref[at] = d_attn[at * rows : (at + 1) * rows].astype(BF16)
    vector_ref[...] = jnp.zeros_like(vector_ref)
    vector_ref[3:4] = jnp.sum(d_zero.astype(F32), axis=0, keepdims=True)
    vector_ref[4:5, :cond_width] = jnp.sum(d_cond * cond_normed, axis=0, keepdims=True)
    vector_ref[5:6] = jnp.sum(d_pre.astype(F32), axis=0, keepdims=True)
    vector_ref[6:7] = jnp.sum(d_zero_two.astype(F32), axis=0, keepdims=True)


def middle_part(attended, gate_sig, act, cond, cotangent, full, weights):
    total, width = act.shape
    vmem = pl.BlockSpec(memory_space=pltpu.VMEM)
    return pl.pallas_call(
        middle_kernel,
        out_shape=(
            jax.ShapeDtypeStruct((total, width), BF16),
            jax.ShapeDtypeStruct((total, width), BF16),
            jax.ShapeDtypeStruct(attended.shape, BF16),
            jax.ShapeDtypeStruct((total, width), F32),
            jax.ShapeDtypeStruct(cond.shape, F32),
            jax.ShapeDtypeStruct(cond.shape, F32),
            jax.ShapeDtypeStruct(full.shape, F32),
        )
        + tuple(jax.ShapeDtypeStruct(weight.shape, BF16) for weight in weights),
        in_specs=[vmem] * 14,
        out_specs=[vmem] * 15,
        compiler_params=pltpu.CompilerParams(vmem_limit_bytes=62 << 20),
        name="middle",
    )(attended, gate_sig, act, cond, cotangent, full, *weights)


class Halving:
    def __init__(self, me, order, source, zones, send_sem, recv_sem):
        self.me, self.order, self.source, self.zones = me, order, source, zones
        self.send_sem, self.recv_sem = send_sem, recv_sem

    def copies(self, step):
        kept = flips(self.me, self.order[step + 1 :])
        found = []
        for at, spot in enumerate(kept):
            if step == 0:
                leaving = self.source.at[flip(spot, self.order[0])]
            else:
                leaving = self.zones[step - 1].at[2 * at + 1]
            found.append(
                send(
                    leaving, self.zones[step].at[at], self.send_sem.at[step, at],
                    self.recv_sem.at[step, at], dict(samp=flip(self.me, self.order[step])),
                )
            )
        return found

    def start(self, step):
        for copy in self.copies(step):
            copy.start()

    def finish(self, step):
        kept = flips(self.me, self.order[step + 1 :])
        zone = self.zones[step]
        for at, copy in enumerate(self.copies(step)):
            copy.wait_recv()

            def add(turn, carry, at=at):
                lines = pl.ds(pl.multiple_of(turn * 16, 16), 16)
                mine = self.source[kept[at], lines] if step == 0 else self.zones[step - 1][2 * at, lines]
                zone[at, lines] = (zone[at, lines].astype(F32) + mine.astype(F32)).astype(BF16)
                return carry

            lax.fori_loop(0, zone.shape[1] // 16, add, 0)

    def settle(self):
        for step in range(len(self.order)):
            for copy in self.copies(step):
                copy.wait_send()


def zone_shapes(shapes, count):
    zones = []
    for rows, columns in shapes:
        size = count // 2
        while size:
            zones.append(pltpu.VMEM((size, rows, columns), BF16))
            size //= 2
    return zones


def spans_of(shapes, columns, spans):
    lines = []
    for at, (rows, wide) in enumerate(shapes):
        for half in range(wide // columns):
            lines += [(at, row, half * columns) for row in range(0, rows, 8)]
    each = len(lines) // spans
    moves = []
    for piece in range(spans):
        row = 0
        for at, start, lane in lines[piece * each : (piece + 1) * each]:
            last = moves[-1] if moves else None
            if last and last[0] == piece and last[2] == at and last[4] == lane and last[3] + last[5] == start:
                moves[-1] = last[:5] + (last[5] + 8,)
            else:
                moves.append((piece, row, at, start, lane, 8))
            row += 8
    return (each * 8, moves)


def attend_back_kernel(
    late_shapes, struct_ref, q_ref, kv_ref, do_ref, prob_ref, *refs
):
    lates, refs = refs[: len(late_shapes)], refs[len(late_shapes) :]
    (dq_ref, dkv_ref, dpb_ref, late_out, *refs) = refs
    steps = 3
    late_zones, refs = refs[: steps * len(late_shapes)], refs[steps * len(late_shapes) :]
    (late_send, late_recv, *refs) = refs
    attend_back_body(
        late_shapes, struct_ref, q_ref, kv_ref, do_ref, prob_ref, lates, dq_ref, dkv_ref, dpb_ref, late_out,
        late_zones, late_send, late_recv, *refs
    )


def attend_back_body(
    late_shapes, struct_ref, q_ref, kv_ref, do_ref, prob_ref, lates, dq_ref, dkv_ref, dpb_ref, late_out,
    late_zones, late_send, late_recv,
    key_ref, value_ref, dq_acc, dk_acc, dv_acc, first_ref, tail_ref, part_ref, span_ref, pack_ref,
    got_zero, got_one, got_two, span_send, span_recv, pack_send, pack_recv,
):
    samples, rows, width = q_ref.shape
    count = pack_ref.shape[0]
    spans = kv_ref.shape[0]
    heads = width // HEAD_DIM
    block = rows * spans // count
    tail = block - MAIN
    structs = pack_ref.shape[1] // (heads // 2 + 1)
    main_rows = rows // block * MAIN
    keys = count * block
    group, windows = head_windows(width)
    scale = HEAD_DIM ** (-0.5)
    me = lax.axis_index("samp")
    my_span = lax.axis_index("head")
    orders = reduce_orders(count)
    others = [lax.rem(my_span + away, spans) for away in range(1, spans)]
    greet(
        [dict(samp=flip(me, bit)) for bit in sorted(orders[0])] + [dict(head=other) for other in others]
    )
    movers = [
        Halving(
            me, orders[at % 2], lates[at], late_zones[3 * at : 3 * at + 3], late_send.at[at], late_recv.at[at]
        )
        for at in range(len(lates))
    ]
    for mover in movers:
        mover.start(0)
    switch = tail_switch(count, heads, tail)
    key_ref[keys:] = jnp.zeros_like(key_ref[keys:])
    value_ref[keys:] = jnp.zeros_like(value_ref[keys:])

    def span_copy(place, sample, away):
        lanes = pl.ds(pl.multiple_of(place * group, LANES), group)
        return send(
            part_ref.at[others[away], :, sample, :, lanes],
            span_ref.at[away, :, sample, :, lanes],
            span_send.at[place, sample, away],
            span_recv.at[place, sample, away],
            dict(head=others[away]),
        )

    def one_group(place, carry):
        for sample in range(samples):
            for span in range(spans):
                for which, held in ((0, key_ref), (1, value_ref)):
                    held[span * main_rows : (span + 1) * main_rows] = kv_ref[
                        span, which, sample, :main_rows, pl.ds(pl.multiple_of(place * group, LANES), group)
                    ]
                    spot = count * MAIN + span * (rows - main_rows)
                    held[spot : spot + rows - main_rows] = kv_ref[
                        span, which, sample, main_rows:, pl.ds(pl.multiple_of(place * group, LANES), group)
                    ]
            dq_acc[...] = jnp.zeros_like(dq_acc)
            dk_acc[...] = jnp.zeros_like(dk_acc)
            dv_acc[...] = jnp.zeros_like(dv_acc)
            kept = [jnp.where(struct_ref[0] == slab, 1.0, 0.0).astype(BF16) for slab in range(structs)]
            added = [jnp.where(struct_ref[1] == slab, 1.0, 0.0).astype(BF16) for slab in range(structs)]
            even_scores = None
            for at, (start, span, offset) in enumerate(windows):
                lanes = pl.ds(pl.multiple_of(place * group + start, LANES), span)
                within = slice(start, start + span)
                mask = head_mask(span, offset)
                upstream = do_ref[sample, :, lanes]
                upstream = jnp.where(mask, upstream, jnp.zeros_like(upstream))
                query = q_ref[sample, :, lanes]
                query = jnp.where(mask, query, jnp.zeros_like(query))
                low = prob_ref[sample, place * len(windows) + at]
                weights = low.astype(F32)
                d_weights = dot_nt(upstream, value_ref[:, within])
                dv_acc[:, within] += dot_tn(low[:, :keys], upstream)
                cross = weights * d_weights
                delta = jnp.sum(cross, axis=1, keepdims=True)
                d_scores = (cross - weights * delta).astype(BF16)
                dq_acc[:, within] += jnp.where(mask, dot_nn(d_scores, key_ref[:, within]), 0.0)
                dk_acc[:, within] += dot_tn(d_scores[:, :keys], query)
                per_tile = LANES // (count * tail)
                turn = at % per_tile * count * tail
                rest = d_scores[:, count * MAIN :]
                rest = pltpu.roll(rest, turn, 1) if turn else rest
                spot = place * (len(windows) // per_tile) + at // per_tile
                if turn:
                    tail_ref[sample, spot] += rest
                else:
                    tail_ref[sample, spot] = rest
                if at % 2 == 0:
                    even_scores = d_scores
                    continue
                for pair in range(count // 2):
                    even = even_scores[:, pair * LANES : (pair + 1) * LANES]
                    odd = d_scores[:, pair * LANES : (pair + 1) * LANES]
                    low_tile = jnp.where(low_half(even), even, swap_halves(odd))
                    high_tile = jnp.where(low_half(even), swap_halves(even), odd)
                    for side, tile in ((0, low_tile), (1, high_tile)):
                        owner = 2 * pair + side
                        if sample == 0:
                            first_ref[at // 2, owner] = tile
                            continue
                        old = first_ref[at // 2, owner]
                        for slab in range(structs):
                            spot = slab * (heads // 2) + place * (len(windows) // 2) + at // 2
                            pack_ref[owner, spot] = old * kept[slab] + tile * added[slab]
            lanes = pl.ds(pl.multiple_of(place * group, LANES), group)
            dq_ref[sample, :, lanes] = (dq_acc[...] * scale).astype(BF16)
            for span in range(spans):
                spot = count * MAIN + span * (rows - main_rows)
                for which, total, factor in ((0, dk_acc, scale), (1, dv_acc, 1.0)):
                    part_ref[span, which, sample, :main_rows, lanes] = (
                        total[span * main_rows : (span + 1) * main_rows] * factor
                    ).astype(BF16)
                    part_ref[span, which, sample, main_rows:, lanes] = (
                        total[spot : spot + rows - main_rows] * factor
                    ).astype(BF16)
            for away in range(spans - 1):
                span_copy(place, sample, away).start()
        return carry

    for place in range(width // group):
        one_group(place, 0)
        for mover in movers:
            mover.finish(place)
            mover.start(place + 1)

    mixed = []
    for sample in range(samples):
        whole = jnp.concatenate([tail_ref[sample, at] for at in range(count // 2)], axis=1)
        mixed.append(dot_nt(whole, switch))
    for pair in range(count // 2):
        tiles = [part[:, pair * LANES : (pair + 1) * LANES] for part in mixed]
        for slab in range(structs):
            both = jnp.zeros_like(tiles[0])
            for sample in range(samples):
                both = both + jnp.where(struct_ref[sample] == slab, tiles[sample], 0.0)
            spot = structs * heads // 2 + slab
            pack_ref[2 * pair, spot] = jnp.where(low_half(both), both, 0.0).astype(BF16)
            pack_ref[2 * pair + 1, spot] = jnp.where(low_half(both), swap_halves(both), 0.0).astype(BF16)

    tiles = pack_ref.shape[1]
    halves = (pl.ds(0, tiles // 2), pl.ds(tiles // 2, tiles - tiles // 2))
    bounds = ((0, tiles // 2), (tiles // 2, tiles))
    landing = (got_zero, got_one, got_two)

    def stage_copies(step, half):
        order = orders[half]
        kept = flips(me, order[step + 1 :])
        return [
            send(
                pack_ref.at[flip(spot, order[step]), halves[half]],
                landing[step].at[at, halves[half]],
                pack_send.at[step, half, at],
                pack_recv.at[step, half, at],
                dict(samp=flip(me, order[step])),
            )
            for at, spot in enumerate(kept)
        ]

    flights = [[stage_copies(step, half) for half in range(2)] for step in range(len(orders[0]))]
    for half in range(2):
        for copy in flights[0][half]:
            copy.start()
    for step in range(len(orders[0])):
        for half in range(2):
            kept = flips(me, orders[half][step + 1 :])
            for at, spot in enumerate(kept):
                flights[step][half][at].wait_recv()

                def add(tile, carry, spot=spot, at=at, step=step):
                    pack_ref[spot, tile] = (
                        pack_ref[spot, tile].astype(F32) + landing[step][at, tile].astype(F32)
                    ).astype(BF16)
                    return carry

                lax.fori_loop(bounds[half][0], bounds[half][1], add, 0)
            if step + 1 < len(orders[0]):
                for copy in flights[step + 1][half]:
                    copy.start()
        if step == 0:
            for mover in movers:
                mover.finish(2)
            _, moves = spans_of(late_shapes, width, spans)
            for piece, row, at, start, lane, size in moves:
                late_out[piece, row : row + size] = movers[at].zones[2][
                    0, start : start + size, lane : lane + width
                ]

    def out(tile, carry):
        dpb_ref[tile] = pack_ref[me, tile]
        return carry

    lax.fori_loop(0, tiles, out, 0)

    for place in range(width // group):
        for sample in range(samples):
            for away in range(spans - 1):
                span_copy(place, sample, away).wait_recv()
    for which in range(2):
        for sample in range(samples):
            total = part_ref[my_span, which, sample].astype(F32)
            for away in range(spans - 1):
                total += span_ref[away, which, sample].astype(F32)
            dkv_ref[which, sample] = total.astype(BF16)
    for place in range(width // group):
        for sample in range(samples):
            for away in range(spans - 1):
                span_copy(place, sample, away).wait_send()
    for stage in flights:
        for half in stage:
            for copy in half:
                copy.wait_send()
    for mover in movers:
        mover.settle()


def attend_back(struct_of, structs, query, key_value, upstream, prob, lates, count):
    samples, rows, width = query.shape
    spans = key_value.shape[0]
    heads = width // HEAD_DIM
    group, windows = head_windows(width)
    keys = rows * spans
    tiles = structs * (heads // 2 + 1)
    steps = count.bit_length() - 1
    vmem = pl.BlockSpec(memory_space=pltpu.VMEM)
    smem = pl.BlockSpec(memory_space=pltpu.SMEM)
    late_shapes = [late.shape[1:] for late in lates]
    each, _ = spans_of(late_shapes, width, spans)
    dma = pltpu.SemaphoreType.DMA
    return pl.pallas_call(
        functools.partial(attend_back_kernel, late_shapes),
        out_shape=(
            jax.ShapeDtypeStruct((samples, rows, width), BF16),
            jax.ShapeDtypeStruct((2, samples, rows, width), BF16),
            jax.ShapeDtypeStruct((tiles, rows, LANES), BF16),
            jax.ShapeDtypeStruct((spans, each, width), BF16),
        ),
        in_specs=[smem] + [vmem] * (4 + len(lates)),
        out_specs=[vmem] * 4,
        scratch_shapes=zone_shapes(late_shapes, count)
        + [
            dma((len(lates), steps, count // 2)),
            dma((len(lates), steps, count // 2)),
            pltpu.VMEM((KEY_LANES, group), BF16),
            pltpu.VMEM((KEY_LANES, group), BF16),
            pltpu.VMEM((rows, group), F32),
            pltpu.VMEM((keys, group), F32),
            pltpu.VMEM((keys, group), F32),
            pltpu.VMEM((len(windows) // 2, count, rows, LANES), BF16),
            pltpu.VMEM((samples, count // 2, rows, LANES), BF16),
            pltpu.VMEM((spans, 2, samples, rows, width), BF16),
            pltpu.VMEM((spans - 1, 2, samples, rows, width), BF16),
            pltpu.VMEM((count, tiles, rows, LANES), BF16),
            pltpu.VMEM((count // 2, tiles, rows, LANES), BF16),
            pltpu.VMEM((count // 4, tiles, rows, LANES), BF16),
            pltpu.VMEM((count // 8, tiles, rows, LANES), BF16),
            pltpu.SemaphoreType.DMA((width // group, samples, spans - 1)),
            pltpu.SemaphoreType.DMA((width // group, samples, spans - 1)),
            pltpu.SemaphoreType.DMA((steps, 2, count // 2)),
            pltpu.SemaphoreType.DMA((steps, 2, count // 2)),
        ],
        compiler_params=pltpu.CompilerParams(
            vmem_limit_bytes=60 << 20, collective_id=1, has_side_effects=True
        ),
        name="attend_back",
    )(struct_of, query, key_value, upstream, prob, *lates)


def finish_kernel(
    early_shapes,
    act_ref, cond_ref, adapted_ref, sig_ref, full_ref, dq_ref, dkv_ref, dgate_ref, dmid_ref, dcond_ref,
    extra_ref, vector_ref, dpb_ref, late_ref, pair_ref, scale_w, shift_w, key_w, value_w, query_w, gate_w,
    *refs
):
    (ig_ref, cg_ref, pg_ref, small_out, early_all, late_all, *refs) = refs
    grads, refs = refs[: len(early_shapes)], refs[len(early_shapes) :]
    zones, refs = refs[: 3 * len(early_shapes)], refs[3 * len(early_shapes) :]
    (
        early_ref, early_got, late_got, small_ref, small_got, sum_ref, sum_got,
        pair_buf, lead_ref, lead_turned, spread_ref, block_ref, tail_block, weight_acc,
        pair_sem, block_sem, grad_send, grad_recv, late_send, late_recv, early_send, early_recv,
        small_send, small_recv, sum_send, sum_recv,
    ) = refs
    total, width = act_ref.shape
    count = grads[0].shape[0]
    spans = late_ref.shape[0]
    structs, block, rows, _ = pair_buf.shape
    samples = total // rows
    heads = width // HEAD_DIM
    tail = block - MAIN
    pieces = rows // block
    pairs = heads // 2
    me = lax.axis_index("samp")
    my_span = lax.axis_index("head")
    orders = reduce_orders(count)
    peers = flips(me, sorted(orders[0]))
    others = [lax.rem(my_span + away, spans) for away in range(1, spans)]

    loads = [
        pltpu.make_async_copy(pair_ref.at[struct], pair_buf.at[struct], pair_sem.at[struct])
        for struct in range(structs)
    ]
    for load in loads:
        load.start()
    greet([dict(samp=peer) for peer in peers[1:]] + [dict(head=other) for other in others])

    def span_scatter(source, got, sems):
        return [
            send(source.at[other], got.at[at], sems[0].at[0, at], sems[1].at[0, at], dict(head=other))
            for at, other in enumerate(others)
        ]

    def span_spread(whole, sems):
        return [
            send(whole.at[my_span], whole.at[my_span], sems[0].at[1, at], sems[1].at[1, at], dict(head=other))
            for at, other in enumerate(others)
        ]

    def span_add(source, got, whole):
        def add(turn, carry):
            lines = pl.ds(pl.multiple_of(turn * 8, 8), 8)
            summed = source[my_span, lines].astype(F32)
            for at in range(spans - 1):
                summed = summed + got[at, lines].astype(F32)
            whole[my_span, lines] = summed.astype(BF16)
            return carry

        lax.fori_loop(0, source.shape[1] // 8, add, 0)

    late_sems = (late_send, late_recv)
    early_sems = (early_send, early_recv)
    for copy in span_scatter(late_ref, late_got, late_sems):
        copy.start()

    adapted = adapted_ref[...]
    back = one_hot((rows, rows), lambda row: row)
    place = lax.broadcasted_iota(jnp.int32, (rows, rows), 1)
    row = lax.broadcasted_iota(jnp.int32, (rows, rows), 0)
    back = jnp.where(row == key_row_of(place, block, pieces), 1.0, 0.0).astype(BF16)
    d_query = jnp.concatenate([dq_ref[at].astype(F32) for at in range(samples)], axis=0).astype(BF16)
    d_key, d_value = [
        jnp.concatenate([dot_nn(back, dkv_ref[which, at]) for at in range(samples)], axis=0).astype(BF16)
        for which in range(2)
    ]
    d_gate = dgate_ref[...]

    def store_grad(at, left, right):
        size = grads[at].shape[1]
        value = dot_tn(left, right).astype(BF16)
        for owner in range(count):
            grads[at][owner] = value[owner * size : (owner + 1) * size]

    movers = [
        Halving(
            me, orders[at % 2], grads[at], zones[3 * at : 3 * at + 3], grad_send.at[at], grad_recv.at[at]
        )
        for at in range(len(grads))
    ]
    for at, upstream in ((2, d_key), (3, d_value), (4, d_query), (5, d_gate)):
        store_grad(at, adapted, upstream)
        movers[at].start(0)

    d_adapted = dot_nt(d_query, query_w[...].reshape(-1, width))
    d_adapted += dot_nt(d_key, key_w[...].reshape(-1, width))
    d_adapted += dot_nt(d_value, value_w[...].reshape(-1, width))
    d_adapted += dot_nt(d_gate, gate_w[...].reshape(-1, width))
    gain_one = full_ref[0:1, : cond_ref.shape[1]]
    act_normed, act_inverse = norm_rows(act_ref[...].astype(F32))
    cond_normed, cond_inverse = norm_rows(cond_ref[...].astype(F32))
    cond_first = (cond_normed * gain_one).astype(BF16)
    sig_first = sig_ref[...]
    d_shift = d_adapted.astype(BF16)
    d_pre = (d_adapted * act_normed * sigmoid_slope(sig_first)).astype(BF16)
    store_grad(0, cond_first, d_pre)
    store_grad(1, cond_first, d_shift)
    movers[0].start(0)
    movers[1].start(0)
    ig_ref[...] = dmid_ref[...] + norm_back(act_normed, act_inverse, d_adapted * sig_first)
    d_cond = dot_nt(d_shift, shift_w[...].reshape(-1, width)) + dot_nt(d_pre, scale_w[...].reshape(-1, width))
    cg_ref[...] = norm_back(cond_normed, cond_inverse, d_cond * gain_one + dcond_ref[...]) + extra_ref[...]
    small_ref[...] = vector_ref[...]
    small_ref[0:1, : cond_ref.shape[1]] = jnp.sum(d_cond * cond_normed, axis=0, keepdims=True)
    small_ref[1:2] = jnp.sum(d_pre.astype(F32), axis=0, keepdims=True)
    small_ref[2:3] = jnp.sum(d_query.astype(F32), axis=0, keepdims=True)

    project = full_ref[8:, :LANES]
    project = (project - jnp.mean(project, axis=1, keepdims=True)).astype(BF16)
    columns = columns_of(project)
    for at, part in enumerate(spread_heads(columns, GROUP)):
        spread_ref[at * LANES : (at + 1) * LANES] = part
    switch = pair_switch(heads)
    means = mean_pair()
    groups = MAIN // GROUP
    for struct in range(structs):
        whole = jnp.concatenate([dpb_ref[struct * pairs + at] for at in range(pairs)], axis=1)
        mixed = dot_nt(whole, switch).astype(BF16)
        for at in range(groups):
            lead_ref[struct * groups + at] = mixed[:, at * GROUP * heads : (at + 1) * GROUP * heads]
    turn_eye = one_hot((rows, rows), lambda line: line)
    weight_acc[...] = jnp.zeros_like(weight_acc)
    for load in loads:
        load.wait()

    def back_keys(struct, first, keys, lead, target):
        for at in range(keys // 2):
            key = first + 2 * at
            low = jnp.concatenate((pair_buf[struct, key], pair_buf[struct, key + 1]), axis=1)
            normed, inverse = norm_pair(low, means)
            upstream = dot_nt(lead, spread_ref[2 * at * LANES : (2 * at + 2) * LANES, : lead.shape[1]])
            cross = dot_nn((upstream * normed).astype(BF16), means)
            result = inverse * (upstream - normed * cross)
            target(2 * at, result[:, :LANES])
            target(2 * at + 1, result[:, LANES:])
            kept = normed.astype(BF16)
            for side in range(2):
                turned = lead_turned[(2 * at + side) * heads : (2 * at + side + 1) * heads]
                weight_acc[...] += dot_nn(turned, kept[:, side * LANES : (side + 1) * LANES])

    def block_copy(turn):
        slot = lax.rem(turn, 2)
        return pltpu.make_async_copy(
            block_ref.at[slot],
            pg_ref.at[lax.div(turn, groups), pl.ds(lax.rem(turn, groups) * GROUP, GROUP)],
            block_sem.at[slot],
        )

    def pair_group(turn, carry):
        @pl.when(turn >= 2)
        def _():
            block_copy(turn - 2).wait()

        slot = lax.rem(turn, 2)
        lead = lead_ref[turn]
        lead_turned[...] = dot_tn(lead, turn_eye).astype(BF16)

        def target(at, value):
            block_ref[slot, at] = value.astype(BF16)

        back_keys(lax.div(turn, groups), lax.rem(turn, groups) * GROUP, GROUP, lead, target)
        block_copy(turn).start()
        return carry

    turns = structs * groups
    cuts = [turns * at // 6 for at in range(7)]
    lax.fori_loop(cuts[0], cuts[1], pair_group, 0)
    for at in range(len(movers)):
        movers[at].finish(0)
        movers[at].start(1)
    for copy in span_scatter(late_ref, late_got, late_sems):
        copy.wait_recv()
    span_add(late_ref, late_got, late_all)
    for copy in span_spread(late_all, late_sems):
        copy.start()
    lax.fori_loop(cuts[1], cuts[3], pair_group, 0)
    for at in range(len(movers)):
        movers[at].finish(1)
        movers[at].start(2)
    lax.fori_loop(cuts[3], cuts[5], pair_group, 0)
    for at in range(len(movers)):
        movers[at].finish(2)
    _, moves = spans_of(early_shapes, width, spans)
    for piece, line, at, start, lane, size in moves:
        early_ref[piece, line : line + size] = movers[at].zones[2][0, start : start + size, lane : lane + width]
    for copy in span_scatter(early_ref, early_got, early_sems):
        copy.start()
    lax.fori_loop(cuts[5], cuts[6], pair_group, 0)
    for struct in range(structs):
        lead = dpb_ref[structs * pairs + struct]
        lead = lead[:, : tail * heads]
        lead_turned[: tail * heads] = dot_tn(lead, turn_eye).astype(BF16)

        def tail_target(at, value, struct=struct):
            tail_block[struct, at] = value.astype(BF16)

        back_keys(struct, MAIN, tail, lead, tail_target)
    tail_copies = [
        pltpu.make_async_copy(
            tail_block.at[struct], pg_ref.at[struct, pl.ds(MAIN, tail)], pair_sem.at[struct]
        )
        for struct in range(structs)
    ]
    for copy in tail_copies:
        copy.start()
    small_ref[8:, :LANES] = weight_acc[...]

    def small_copies(sending):
        return [
            send(
                small_ref, small_got.at[me if sending else peers[at]], small_send.at[at], small_recv.at[at],
                dict(samp=peers[at]),
            )
            for at in range(1, count)
        ]

    def sum_copies(sending):
        return [
            send(
                sum_ref, sum_got.at[my_span if sending else lax.rem(my_span + spans - 1 - at, spans)],
                sum_send.at[at], sum_recv.at[at], dict(head=other),
            )
            for at, other in enumerate(others)
        ]

    for copy in small_copies(True):
        copy.start()
    small_got[me] = small_ref[...]
    for copy in small_copies(False):
        copy.wait_recv()
    summed = small_got[0]
    for at in range(1, count):
        summed = summed + small_got[at]
    sum_ref[...] = summed
    for copy in sum_copies(True):
        copy.start()
    sum_got[my_span] = summed
    for copy in span_scatter(early_ref, early_got, early_sems):
        copy.wait_recv()
    span_add(early_ref, early_got, early_all)
    for copy in span_spread(early_all, early_sems):
        copy.start()
    for copy in span_spread(late_all, late_sems):
        copy.wait_recv()
    for copy in sum_copies(False):
        copy.wait_recv()
    summed = sum_got[0]
    for at in range(1, spans):
        summed = summed + sum_got[at]
    small_out[...] = summed
    for copy in span_spread(early_all, early_sems):
        copy.wait_recv()

    block_copy(turns - 2).wait()
    block_copy(turns - 1).wait()
    for copy in tail_copies:
        copy.wait()
    for mover in movers:
        mover.settle()
    for copies in (
        span_scatter(late_ref, late_got, late_sems), span_scatter(early_ref, early_got, early_sems),
        span_spread(late_all, late_sems), span_spread(early_all, early_sems),
        small_copies(True), sum_copies(True),
    ):
        for copy in copies:
            copy.wait_send()


def finish(
    act, cond, adapted, sig, full, d_query, d_key_value, d_gate, d_middle, d_cond, extra, vectors, packed,
    late, pair, weights,
):
    total, width = act.shape
    cond_width = cond.shape[1]
    spans, late_each, _ = late.shape
    count = weights[0].shape[0]
    structs, block, rows, _ = pair.shape
    heads = width // HEAD_DIM
    tail = block - MAIN
    early_shapes = [weight.shape[1:] for weight in weights]
    early_each, _ = spans_of(early_shapes, width, spans)
    steps = count.bit_length() - 1
    vmem = pl.BlockSpec(memory_space=pltpu.VMEM)
    far = pl.BlockSpec(memory_space=pl.ANY)
    dma = pltpu.SemaphoreType.DMA
    turns = structs * (MAIN // GROUP)
    return pl.pallas_call(
        functools.partial(finish_kernel, early_shapes),
        out_shape=(
            jax.ShapeDtypeStruct((total, width), F32),
            jax.ShapeDtypeStruct((total, cond_width), F32),
            jax.ShapeDtypeStruct(pair.shape, BF16),
            jax.ShapeDtypeStruct(full.shape, F32),
            jax.ShapeDtypeStruct((spans, early_each, width), BF16),
            jax.ShapeDtypeStruct((spans, late_each, width), BF16),
        ),
        in_specs=[vmem] * 14 + [far] + [vmem] * 6,
        out_specs=[vmem, vmem, far, vmem, vmem, vmem],
        scratch_shapes=[pltpu.VMEM(weight.shape, BF16) for weight in weights]
        + zone_shapes(early_shapes, count)
        + [
            pltpu.VMEM((spans, early_each, width), BF16),
            pltpu.VMEM((spans - 1, early_each, width), BF16),
            pltpu.VMEM((spans - 1, late_each, width), BF16),
            pltpu.VMEM(full.shape, F32),
            pltpu.VMEM((count,) + full.shape, F32),
            pltpu.VMEM(full.shape, F32),
            pltpu.VMEM((spans,) + full.shape, F32),
            pltpu.VMEM(pair.shape, BF16),
            pltpu.VMEM((turns, rows, GROUP * heads), BF16),
            pltpu.VMEM((GROUP * heads, rows), BF16),
            pltpu.VMEM((GROUP * LANES, GROUP * heads), BF16),
            pltpu.VMEM((2, GROUP, rows, LANES), BF16),
            pltpu.VMEM((structs, tail, rows, LANES), BF16),
            pltpu.VMEM((heads, LANES), F32),
            dma((structs,)),
            dma((2,)),
            dma((len(weights), steps, count // 2)),
            dma((len(weights), steps, count // 2)),
            dma((2, spans - 1)),
            dma((2, spans - 1)),
            dma((2, spans - 1)),
            dma((2, spans - 1)),
            dma((count,)),
            dma((count,)),
            dma((spans,)),
            dma((spans,)),
        ],
        compiler_params=pltpu.CompilerParams(
            vmem_limit_bytes=60 << 20, collective_id=3, has_side_effects=True
        ),
        name="finish",
    )(
        act, cond, adapted, sig, full, d_query, d_key_value, d_gate, d_middle, d_cond, extra, vectors, packed,
        late, pair, *weights
    )


def deliver_kernel(shapes, ig_in, cg_in, early_in, late_in, pair_in, ig_ref, cg_ref, pair_ref, *outs):
    pair_ref[...] = pair_in[...].astype(F32)

    @pl.when(pl.program_id(0) == 0)
    def _():
        ig_ref[...] = ig_in[...]
        cg_ref[...] = cg_in[...]
        spans, _, width = early_in.shape
        first = 0
        for part, source in zip(shapes, (early_in, late_in)):
            _, moves = spans_of(part, width, spans)
            for piece, line, at, start, lane, size in moves:
                outs[first + at][start : start + size, lane : lane + width] = source[
                    piece, line : line + size
                ].astype(F32)
            first += len(part)


def deliver(input_grad, cond_grad, early, late, pair_grad, shapes):
    structs, block, rows, channels = pair_grad.shape
    turn = block // 4

    def whole(shape):
        return pl.BlockSpec(tuple(shape), lambda at: (0,) * len(shape))

    tile = pl.BlockSpec((1, turn, rows, channels), lambda at: (at // 4, at % 4, 0, 0))
    flat = list(shapes[0]) + list(shapes[1])
    return pl.pallas_call(
        functools.partial(deliver_kernel, shapes),
        out_shape=(
            jax.ShapeDtypeStruct(input_grad.shape, F32),
            jax.ShapeDtypeStruct(cond_grad.shape, F32),
            jax.ShapeDtypeStruct(pair_grad.shape, F32),
        )
        + tuple(jax.ShapeDtypeStruct(shape, F32) for shape in flat),
        grid=(structs * 4,),
        in_specs=[whole(part.shape) for part in (input_grad, cond_grad, early, late)] + [tile],
        out_specs=[whole(input_grad.shape), whole(cond_grad.shape), tile] + [whole(shape) for shape in flat],
        compiler_params=pltpu.CompilerParams(vmem_limit_bytes=40 << 20),
        name="deliver",
    )(input_grad, cond_grad, early, late, pair_grad)


def pack_rows(pieces, columns):
    return jnp.concatenate([piece.reshape(-1, columns) for piece in pieces], axis=0)


def pack_small(pieces, columns):
    flat = jnp.concatenate([piece.reshape(-1) for piece in pieces])
    rows = -(-flat.shape[0] // columns)
    rows = -(-rows // 8) * 8
    return jnp.pad(flat, (0, rows * columns - flat.shape[0])).reshape(rows, columns)


def unpack_rows(gathered, shapes):
    whole, at = [], 0
    count, _, columns = gathered.shape
    for rows, cols in shapes:
        held = rows * cols // columns
        whole.append(gathered[:, at : at + held].reshape(count * rows, cols))
        at += held
    return whole


def unpack_small(gathered, shapes):
    whole, at = [], 0
    count = gathered.shape[0]
    flat = gathered.reshape(count, -1)
    for shape in shapes:
        size = 1
        for extent in shape:
            size *= extent
        whole.append(flat[:, at : at + size].reshape((count * shape[0],) + shape[1:]))
        at += size
    return whole


def plain_kernel(struct_ref, len_ref, q_ref, k_ref, v_ref, bias_ref, out_ref, prob_ref, acc_ref):
    sample = pl.program_id(0)
    group_at = pl.program_id(1)
    length = len_ref[struct_ref[sample]]
    keys = k_ref.shape[1]
    group, windows = head_windows(q_ref.shape[2])
    valid = lax.broadcasted_iota(jnp.int32, (1, keys), 1) < length
    acc_ref[...] = jnp.zeros_like(acc_ref)
    for at, (start, width, offset) in enumerate(windows):
        lanes = slice(start, start + width)
        mask = head_mask(width, offset)
        query = q_ref[0, :, lanes]
        query = jnp.where(mask, query, jnp.zeros_like(query))
        scores = dot_nt(query, k_ref[0, :, lanes]) * HEAD_DIM ** (-0.5) + bias_ref[
            0, at
        ].astype(F32)
        scores = jnp.where(valid, scores, NEG_BIG)
        weights = jnp.exp(scores - jnp.max(scores, axis=1, keepdims=True))
        weights = weights * (1.0 / jnp.sum(weights, axis=1, keepdims=True))
        weights = weights.astype(BF16)
        prob_ref[0, at] = weights
        mixed = dot_nn(weights, v_ref[0, :, lanes])
        acc_ref[:, lanes] += jnp.where(mask, mixed, 0.0)
    out_ref[0] = acc_ref[...].astype(BF16)


def plain(struct_of, struct_len, query, key, value, bias):
    samples, rows, width = query.shape
    keys = key.shape[1]
    heads = bias.shape[1]
    group, windows = head_windows(width)
    each = len(windows)
    return pl.pallas_call(
        plain_kernel,
        out_shape=(
            jax.ShapeDtypeStruct((samples, rows, width), BF16),
            jax.ShapeDtypeStruct((samples, heads, rows, keys), BF16),
        ),
        grid_spec=pltpu.PrefetchScalarGridSpec(
            num_scalar_prefetch=2,
            grid=(samples, heads // each),
            in_specs=[
                pl.BlockSpec((1, rows, group), lambda b, g, s, n: (b, 0, g)),
                pl.BlockSpec((1, keys, group), lambda b, g, s, n: (b, 0, g)),
                pl.BlockSpec((1, keys, group), lambda b, g, s, n: (b, 0, g)),
                pl.BlockSpec((1, each, rows, keys), lambda b, g, s, n: (s[b], g, 0, 0)),
            ],
            out_specs=[
                pl.BlockSpec((1, rows, group), lambda b, g, s, n: (b, 0, g)),
                pl.BlockSpec((1, each, rows, keys), lambda b, g, s, n: (b, g, 0, 0)),
            ],
            scratch_shapes=[pltpu.VMEM((rows, group), F32)],
        ),
        compiler_params=pltpu.CompilerParams(vmem_limit_bytes=48 << 20),
        name="plain",
    )(struct_of, struct_len, query, key, value, bias)


def plain_back_kernel(
    struct_ref, q_ref, k_ref, v_ref, do_ref, prob_ref, dq_ref, dk_ref, dv_ref, bias_ref,
    dq_acc, dk_acc, dv_acc, bias_acc,
):
    samples = q_ref.shape[0]
    structs = bias_ref.shape[0]
    group, windows = head_windows(q_ref.shape[2])
    scale = HEAD_DIM ** (-0.5)
    for sample in range(samples):
        struct = struct_ref[sample]
        dq_acc[...] = jnp.zeros_like(dq_acc)
        dk_acc[...] = jnp.zeros_like(dk_acc)
        dv_acc[...] = jnp.zeros_like(dv_acc)
        for at, (start, width, offset) in enumerate(windows):
            lanes = slice(start, start + width)
            mask = head_mask(width, offset)
            upstream = do_ref[sample, :, lanes]
            upstream = jnp.where(mask, upstream, jnp.zeros_like(upstream))
            query = q_ref[sample, :, lanes]
            query = jnp.where(mask, query, jnp.zeros_like(query))
            low = prob_ref[sample, at]
            weights = low.astype(F32)
            d_weights = dot_nt(upstream, v_ref[sample, :, lanes])
            dv_acc[:, lanes] += dot_tn(low, upstream)
            cross = weights * d_weights
            delta = jnp.sum(cross, axis=1, keepdims=True)
            d_scores = (cross - weights * delta).astype(BF16)
            dq_acc[:, lanes] += jnp.where(mask, dot_nn(d_scores, k_ref[sample, :, lanes]), 0.0)
            dk_acc[:, lanes] += dot_tn(d_scores, query)
            for slab in range(structs):
                part = jnp.where(struct == slab, 1.0, 0.0) * d_scores.astype(F32)
                if sample == 0:
                    bias_acc[slab, at] = part
                elif sample < samples - 1:
                    bias_acc[slab, at] += part
                else:
                    bias_ref[slab, at] = (bias_acc[slab, at] + part).astype(BF16)
        dq_ref[sample] = (dq_acc[...] * scale).astype(BF16)
        dk_ref[sample] = (dk_acc[...] * scale).astype(BF16)
        dv_ref[sample] = dv_acc[...].astype(BF16)


def plain_back(struct_of, structs, query, key, value, upstream, prob):
    samples, rows, width = query.shape
    keys = key.shape[1]
    heads = prob.shape[1]
    group, windows = head_windows(width)
    each = len(windows)
    return pl.pallas_call(
        plain_back_kernel,
        out_shape=(
            jax.ShapeDtypeStruct((samples, rows, width), BF16),
            jax.ShapeDtypeStruct((samples, keys, width), BF16),
            jax.ShapeDtypeStruct((samples, keys, width), BF16),
            jax.ShapeDtypeStruct((structs, heads, rows, keys), BF16),
        ),
        grid_spec=pltpu.PrefetchScalarGridSpec(
            num_scalar_prefetch=1,
            grid=(heads // each,),
            in_specs=[
                pl.BlockSpec((samples, rows, group), lambda g, s: (0, 0, g)),
                pl.BlockSpec((samples, keys, group), lambda g, s: (0, 0, g)),
                pl.BlockSpec((samples, keys, group), lambda g, s: (0, 0, g)),
                pl.BlockSpec((samples, rows, group), lambda g, s: (0, 0, g)),
                pl.BlockSpec((samples, each, rows, keys), lambda g, s: (0, g, 0, 0)),
            ],
            out_specs=[
                pl.BlockSpec((samples, rows, group), lambda g, s: (0, 0, g)),
                pl.BlockSpec((samples, keys, group), lambda g, s: (0, 0, g)),
                pl.BlockSpec((samples, keys, group), lambda g, s: (0, 0, g)),
                pl.BlockSpec((structs, each, rows, keys), lambda g, s: (0, g, 0, 0)),
            ],
            scratch_shapes=[
                pltpu.VMEM((rows, group), F32),
                pltpu.VMEM((keys, group), F32),
                pltpu.VMEM((keys, group), F32),
                pltpu.VMEM((structs, each, rows, keys), F32),
            ],
        ),
        compiler_params=pltpu.CompilerParams(vmem_limit_bytes=60 << 20),
        name="plain_back",
    )(struct_of, query, key, value, upstream, prob)


def plain_device(
    act, cond, pair, struct_of, struct_len,
    gain_first, scale_first, scale_bias_first, shift_first,
    query_weight, query_bias, key_weight, value_weight, gate_weight, output_weight,
    pair_weight, zero_first, zero_bias_first,
    gain_second, scale_second, scale_bias_second, shift_second,
    swish_weight, linear_weight, down_weight, zero_second, zero_bias_second,
    cotangent,
):
    samples, rows, width = act.shape
    cond_width = cond.shape[2]
    total = samples * rows
    structs = pair.shape[0]
    small = (
        gain_first, scale_bias_first, query_bias, zero_bias_first, gain_second,
        scale_bias_second, zero_bias_second, pair_weight,
    )
    early = (scale_first, shift_first, query_weight, key_weight, value_weight, gate_weight)
    late = (
        output_weight, zero_first, scale_second, shift_second, swish_weight, linear_weight,
        down_weight, zero_second,
    )
    small_all = lax.all_gather(pack_small(small, width), "samp", axis=0)
    early_all = lax.all_gather(pack_rows(early, width), "samp", axis=0)
    late_all = lax.all_gather(pack_rows(late, width), "samp", axis=0)
    (gain_one, bias_one, bias_query, bias_zero_one, gain_two, bias_two, bias_zero_two, pair_proj_w) = (
        unpack_small(small_all, [piece.shape for piece in small])
    )
    (w_scale, w_shift, w_query, w_key, w_value, w_gate) = unpack_rows(
        early_all, [piece.shape for piece in early]
    )
    (w_out, w_zero, w_scale_two, w_shift_two, w_swish, w_linear, w_down, w_zero_two) = unpack_rows(
        late_all, [piece.shape for piece in late]
    )

    pair_normed, pair_inverse = norm_rows(pair.astype(F32))
    pair_low = pair_normed.astype(BF16)
    pair_proj = jnp.einsum("sijc,ch->shij", pair_low, pair_proj_w, preferred_element_type=F32)
    bias_all = lax.all_gather(pair_proj.astype(BF16), "samp", axis=3, tiled=True)

    act_rows = act.reshape(total, width).astype(F32)
    cond_low = cond.reshape(total, cond_width)
    act_normed, act_inverse = norm_rows(act_rows)
    cond_normed, cond_inverse = norm_rows(cond_low.astype(F32))
    cond_first = (cond_normed * gain_one.astype(F32)).astype(BF16)
    sig_first = jax.nn.sigmoid(product(cond_first, w_scale) + bias_one.astype(F32))
    adapted = (sig_first * act_normed + product(cond_first, w_shift)).astype(BF16)
    key_rows = product(adapted, w_key).astype(BF16)
    value_rows = product(adapted, w_value).astype(BF16)
    query_rows = (product(adapted, w_query) + bias_query.astype(F32)).astype(BF16)
    gate_sig = jax.nn.sigmoid(product(adapted, w_gate))
    key_value = jnp.stack((key_rows, value_rows)).reshape(2, samples, rows, width)
    key_value = lax.all_gather(key_value, "head", axis=2, tiled=True)
    query_split = query_rows.reshape(samples, rows, width)
    attended, prob = plain(
        struct_of, struct_len, query_split, key_value[0], key_value[1], bias_all
    )
    attn_float = attended.reshape(total, width).astype(F32)

    gated_rows = (gate_sig * attn_float).astype(BF16)
    branch = product(gated_rows, w_out)
    zero_sig_first = jax.nn.sigmoid(product(cond_low, w_zero) + bias_zero_one.astype(F32))
    middle = act_rows + zero_sig_first * branch
    mid_normed, mid_inverse = norm_rows(middle)
    cond_second = (cond_normed * gain_two.astype(F32)).astype(BF16)
    sig_second = jax.nn.sigmoid(product(cond_second, w_scale_two) + bias_two.astype(F32))
    adapted_two = (sig_second * mid_normed + product(cond_second, w_shift_two)).astype(BF16)
    swish_pre = product(adapted_two, w_swish)
    linear_pre = product(adapted_two, w_linear)
    swish_sig = jax.nn.sigmoid(swish_pre)
    hidden = (swish_pre * swish_sig * linear_pre).astype(BF16)
    down_rows = product(hidden, w_down)
    zero_sig_second = jax.nn.sigmoid(product(cond_low, w_zero_two) + bias_zero_two.astype(F32))
    layer_out = (middle + zero_sig_second * down_rows).astype(BF16)

    upstream = cotangent.reshape(total, width).astype(F32)
    d_down = (upstream * zero_sig_second).astype(BF16)
    d_zero_second = (upstream * down_rows * sigmoid_slope(zero_sig_second)).astype(BF16)
    d_hidden = back_product(d_down, w_down)
    d_swish = (
        d_hidden * linear_pre * swish_sig * (1.0 + swish_pre * (1.0 - swish_sig))
    ).astype(BF16)
    d_linear = (d_hidden * swish_pre * swish_sig).astype(BF16)
    d_adapted_two = back_product(d_swish, w_swish) + back_product(d_linear, w_linear)
    d_shift_second = d_adapted_two.astype(BF16)
    d_pre_second = (d_adapted_two * mid_normed * sigmoid_slope(sig_second)).astype(BF16)
    d_cond_second = back_product(d_shift_second, w_shift_two) + back_product(
        d_pre_second, w_scale_two
    )
    d_middle = upstream + norm_back(mid_normed, mid_inverse, d_adapted_two * sig_second)
    d_branch = (d_middle * zero_sig_first).astype(BF16)
    d_zero_first = (d_middle * branch * sigmoid_slope(zero_sig_first)).astype(BF16)
    d_gated = back_product(d_branch, w_out)
    d_gate = (d_gated * attn_float * sigmoid_slope(gate_sig)).astype(BF16)
    d_attended = (d_gated * gate_sig).astype(BF16)

    late_grads = (
        outer_sum(gated_rows, d_branch),
        outer_sum(cond_low, d_zero_first),
        outer_sum(cond_second, d_pre_second),
        outer_sum(cond_second, d_shift_second),
        outer_sum(adapted_two, d_swish),
        outer_sum(adapted_two, d_linear),
        outer_sum(hidden, d_down),
        outer_sum(cond_low, d_zero_second),
    )

    d_query, d_key, d_value, bias_grad = plain_back(
        struct_of, structs, query_split, key_value[0], key_value[1],
        d_attended.reshape(samples, rows, width), prob,
    )
    d_key_value = lax.psum_scatter(
        jnp.stack((d_key, d_value)), "head", scatter_dimension=2, tiled=True
    )
    d_query = d_query.reshape(total, width)
    d_key = d_key_value[0].reshape(total, width)
    d_value = d_key_value[1].reshape(total, width)
    bias_summed = lax.psum_scatter(bias_grad, "samp", scatter_dimension=3, tiled=True)
    pair_weight_grad = jnp.einsum("sijc,shij->ch", pair_low, bias_summed, preferred_element_type=F32)
    pair_upstream = jnp.einsum(
        "shij,ch->sijc", bias_summed, pair_proj_w, preferred_element_type=F32
    )
    pair_grad = norm_back(pair_normed, pair_inverse, pair_upstream)
    d_adapted = (
        back_product(d_query, w_query)
        + back_product(d_key, w_key)
        + back_product(d_value, w_value)
        + back_product(d_gate, w_gate)
    )
    d_shift_first = d_adapted.astype(BF16)
    d_pre_first = (d_adapted * act_normed * sigmoid_slope(sig_first)).astype(BF16)
    d_cond_first = back_product(d_shift_first, w_shift) + back_product(d_pre_first, w_scale)
    input_grad = d_middle + norm_back(act_normed, act_inverse, d_adapted * sig_first)
    d_cond_normed = d_cond_first * gain_one.astype(F32) + d_cond_second * gain_two.astype(F32)
    cond_grad = (
        norm_back(cond_normed, cond_inverse, d_cond_normed)
        + back_product(d_zero_first, w_zero)
        + back_product(d_zero_second, w_zero_two)
    )
    early_grads = (
        outer_sum(cond_first, d_pre_first),
        outer_sum(cond_first, d_shift_first),
        outer_sum(adapted, d_query),
        outer_sum(adapted, d_key),
        outer_sum(adapted, d_value),
        outer_sum(adapted, d_gate),
    )
    small_grads = (
        jnp.sum(d_cond_first * cond_normed, axis=0),
        column_sum(d_pre_first),
        column_sum(d_query),
        column_sum(d_zero_first),
        jnp.sum(d_cond_second * cond_normed, axis=0),
        column_sum(d_pre_second),
        column_sum(d_zero_second),
        pair_weight_grad,
    )
    count = lax.axis_size("samp")

    def pack_grads(grads, shapes):
        pieces = [
            grad.astype(BF16).reshape(count, shape[0] * shape[1] // width, width)
            for grad, shape in zip(grads, shapes)
        ]
        return jnp.concatenate(pieces, axis=1)

    def reduce(packed):
        summed = lax.psum_scatter(packed, "samp", scatter_dimension=0, tiled=True)
        return lax.psum(summed[0], "head").astype(F32)

    late_sum = reduce(pack_grads(late_grads, [piece.shape for piece in late]))
    early_sum = reduce(pack_grads(early_grads, [piece.shape for piece in early]))
    small_flat = jnp.concatenate(
        [grad.astype(BF16).reshape(count, -1) for grad in small_grads], axis=1
    )
    small_sum = lax.psum(
        lax.psum_scatter(small_flat, "samp", scatter_dimension=0, tiled=True), "head"
    ).astype(F32)
    (g_out, g_zero, g_scale_two, g_shift_two, g_swish, g_linear, g_down, g_zero_two) = unpack_rows(
        late_sum[None], [piece.shape for piece in late]
    )
    (g_scale, g_shift, g_query, g_key, g_value, g_gate) = unpack_rows(
        early_sum[None], [piece.shape for piece in early]
    )
    (g_gain, g_bias, g_bias_query, g_bias_zero, g_gain_two, g_bias_two, g_bias_zero_two, g_pair) = (
        unpack_small(small_sum, [piece.shape for piece in small])
    )
    return (
        layer_out.reshape(act.shape), input_grad.reshape(act.shape), cond_grad.reshape(cond.shape),
        pair_grad, g_gain, g_scale, g_bias, g_shift, g_query, g_bias_query, g_key, g_value, g_gate,
        g_out, g_pair, g_zero, g_bias_zero, g_gain_two, g_scale_two, g_bias_two, g_shift_two,
        g_swish, g_linear, g_down, g_zero_two, g_bias_zero_two,
    )


def per_device(
    act, cond, pair, struct_of, struct_len,
    gain_first, scale_first, scale_bias_first, shift_first,
    query_weight, query_bias, key_weight, value_weight, gate_weight, output_weight,
    pair_weight, zero_first, zero_bias_first,
    gain_second, scale_second, scale_bias_second, shift_second,
    swish_weight, linear_weight, down_weight, zero_second, zero_bias_second,
    cotangent,
):
    samples, rows, width = act.shape
    cond_width = cond.shape[2]
    total = samples * rows
    count = lax.axis_size("samp")
    spans = lax.axis_size("head")
    heads = width // HEAD_DIM
    small = (
        gain_first, scale_bias_first, query_bias, zero_bias_first, gain_second,
        scale_bias_second, zero_bias_second,
    )
    early = (scale_first, shift_first, key_weight, value_weight, query_weight, gate_weight)
    late = (
        swish_weight, linear_weight, down_weight, output_weight, zero_first, scale_second, zero_second,
        shift_second,
    )
    mine_at = lax.axis_index("samp")
    mine = lax.broadcasted_iota(jnp.int32, (count, 1), 0) == mine_at

    def spread(piece, columns):
        held = jnp.where(mine, piece[None], jnp.zeros_like(piece[None])).reshape(1, -1)
        return jnp.pad(held, ((0, 0), (0, columns - held.shape[1])))

    turned = pair_weight.T
    held = jnp.where(mine.reshape(1, count, 1), turned[:, None], jnp.zeros_like(turned[:, None]))
    held = jnp.pad(held.reshape(heads, -1), ((0, 0), (0, width - LANES)))
    packed_small = jnp.concatenate(
        [spread(piece, width) for piece in small] + [jnp.zeros((1, width), BF16), held], axis=0
    )
    act_rows = act.reshape(total, width)
    cond_rows = cond.reshape(total, cond_width)
    pair_turned = pair.transpose(0, 2, 1, 3)
    (attended, prob, adapted, sig_first, gate_sig, query_split, key_value, full, *whole) = front(
        struct_of, struct_len, act_rows, cond_rows, packed_small, pair_turned, early + late, samples, count,
        spans,
    )
    (layer_out, d_gate, d_attended, d_middle, d_cond_two, extra, vectors, *late_parts) = middle_part(
        attended, gate_sig, act_rows, cond_rows, cotangent.reshape(total, width), full, whole[6:]
    )
    d_query, d_key_value, bias_packed, late_sum = attend_back(
        struct_of, pair.shape[0], query_split, key_value, d_attended, prob, late_parts, count
    )
    (input_grad, cond_grad, pair_grad, small_sum, early_sum, late_total) = finish(
        act_rows, cond_rows, adapted, sig_first, full, d_query, d_key_value, d_gate, d_middle, d_cond_two,
        extra, vectors, bias_packed, late_sum, pair_turned, whole[:6],
    )
    (input_grad, cond_grad, pair_grad, *weight_grads) = deliver(
        input_grad, cond_grad, early_sum, late_total, pair_grad,
        ([piece.shape for piece in early], [piece.shape for piece in late]),
    )
    (g_scale, g_shift, g_key, g_value, g_query, g_gate) = weight_grads[:6]
    (g_swish, g_linear, g_down, g_out, g_zero, g_scale_two, g_zero_two, g_shift_two) = weight_grads[6:]

    def own(row, size):
        return lax.dynamic_slice(small_sum, (row, mine_at * size), (1, size))[0]

    cond_share, share = cond_width // count, width // count
    channels = pair.shape[3] // count
    g_pair = lax.dynamic_slice(small_sum, (8, mine_at * channels), (heads, channels)).T
    return (
        layer_out.reshape(act.shape), input_grad.reshape(act.shape), cond_grad.reshape(cond.shape),
        pair_grad.transpose(0, 2, 1, 3), own(0, cond_share), g_scale, own(1, share), g_shift, g_query,
        own(2, share), g_key, g_value, g_gate, g_out, g_pair, g_zero, own(3, share), own(4, cond_share),
        g_scale_two, own(5, share), g_shift_two, g_swish, g_linear, g_down, g_zero_two, own(6, share),
    )


def fits(mesh, act, pair):
    samples, rows, width = act.shape
    count, spans = mesh.shape["samp"], mesh.shape["head"]
    block = pair.shape[2]
    tail = block - MAIN
    heads = width // HEAD_DIM
    return (
        count == 8
        and samples == 2
        and tail > 0
        and heads * tail == MAIN
        and rows % block == 0
        and rows * spans == block * count
        and rows % 8 == 0
        and block * count <= KEY_LANES
    )


def solution(mesh):
    tokens = P("samp", "head", None)
    pairs = P(None, "head", "samp", None)
    vector = P("samp")
    matrix = P("samp", None)
    weights = (
        vector, matrix, vector, matrix, matrix, vector, matrix, matrix, matrix, matrix, matrix,
        matrix, vector, vector, matrix, vector, matrix, matrix, matrix, matrix, matrix, vector,
    )
    def choose(*arrays):
        body = per_device if fits(mesh, arrays[0], arrays[2]) else plain_device
        return body(*arrays)

    return jax.shard_map(
        choose,
        mesh=mesh,
        in_specs=(tokens, tokens, pairs, vector, P()) + weights + (tokens,),
        out_specs=(tokens, tokens, tokens, pairs) + weights,
        check_vma=False,
    )
```

```python
import functools

import jax
import jax.numpy as jnp
from jax import lax
from jax.experimental import pallas as pl
from jax.experimental.pallas import tpu as pltpu
from jax.sharding import PartitionSpec as P

HEAD_DIM = 48
LANES = 128
MAIN = 64
KEY_LANES = 640
MESH = pl.DeviceIdType.MESH
EPSILON = 1e-05
NEG_BIG = -1000000000.0
F32 = jnp.float32
BF16 = jnp.bfloat16


def norm_rows(values):
    centered = values - jnp.mean(values, axis=-1, keepdims=True)
    variance = jnp.mean(centered * centered, axis=-1, keepdims=True)
    inverse = lax.rsqrt(variance + EPSILON)
    return (centered * inverse, inverse)


def norm_back(normed, inverse, upstream):
    mean_grad = jnp.mean(upstream, axis=-1, keepdims=True)
    mean_cross = jnp.mean(upstream * normed, axis=-1, keepdims=True)
    return inverse * (upstream - mean_grad - normed * mean_cross)


def product(left_side, right_side):
    return lax.dot_general(
        left_side, right_side, (((1,), (0,)), ((), ())), preferred_element_type=F32
    )


def back_product(upstream, right_side):
    return lax.dot_general(
        upstream, right_side, (((1,), (1,)), ((), ())), preferred_element_type=F32
    )


def outer_sum(left_side, upstream):
    return lax.dot_general(
        left_side, upstream, (((0,), (0,)), ((), ())), preferred_element_type=F32
    )


def column_sum(upstream):
    return jnp.sum(upstream.astype(F32), axis=0)


def sigmoid_slope(gate_sig):
    return gate_sig * (1.0 - gate_sig)


def head_windows(width):
    group = LANES * HEAD_DIM // 16
    group = min(group, width)
    windows = []
    for head in range(group // HEAD_DIM):
        first = head * HEAD_DIM
        last = first + HEAD_DIM - 1
        start = first // LANES * LANES
        stop = (last // LANES + 1) * LANES
        windows.append((start, stop - start, first - start))
    return (group, windows)


def head_mask(width, offset):
    lane = lax.broadcasted_iota(jnp.int32, (1, width), 1)
    return (lane >= offset) & (lane < offset + HEAD_DIM)


def dot_nt(left, right):
    return lax.dot_general(left, right, (((1,), (1,)), ((), ())), preferred_element_type=F32)


def dot_nn(left, right):
    return lax.dot_general(left, right, (((1,), (0,)), ((), ())), preferred_element_type=F32)


def dot_tn(left, right):
    return lax.dot_general(left, right, (((0,), (0,)), ((), ())), preferred_element_type=F32)


def tail_switch(count, heads, tail):
    lanes = count * heads * tail
    source = lax.broadcasted_iota(jnp.int32, (lanes, lanes), 0)
    target = lax.broadcasted_iota(jnp.int32, (lanes, lanes), 1)
    owner = source // (heads * tail)
    head = source % heads
    spot = head * (count * tail) + owner * tail + source // heads % tail
    return jnp.where(spot == target, 1.0, 0.0).astype(BF16)


def swap_halves(tile):
    return pltpu.roll(tile, MAIN, 1)


def low_half(tile):
    return lax.broadcasted_iota(jnp.int32, tile.shape, 1) < MAIN


def key_places(count, block):
    lane = lax.broadcasted_iota(jnp.int32, (1, KEY_LANES), 1)
    tail = block - MAIN
    spare = lane - count * MAIN
    main_at = lane + tail * (lane // MAIN)
    tail_at = block * (spare // tail) + MAIN + spare % tail
    past = jnp.where(spare < count * tail, tail_at, count * block)
    return jnp.where(spare < 0, main_at, past)


def flip(index, bit):
    return index + bit - 2 * bit * lax.rem(lax.div(index, bit), 2)


def flips(index, bits):
    spots = [index]
    for bit in bits:
        spots = spots + [flip(spot, bit) for spot in spots]
    return spots


def reduce_orders(count):
    bits = []
    bit = 2
    while bit < count:
        bits.append(bit)
        bit *= 2
    half = len(bits) // 2
    return ([1] + bits, [1] + bits[half:] + bits[:half])


def greet(partners):
    barrier = pltpu.get_barrier_semaphore()
    for partner in partners:
        pl.semaphore_signal(barrier, inc=1, device_id=partner, device_id_type=MESH)
    pl.semaphore_wait(barrier, len(partners))


def send(source, target, send_sem, recv_sem, device):
    return pltpu.make_async_remote_copy(
        src_ref=source, dst_ref=target, send_sem=send_sem, recv_sem=recv_sem,
        device_id=device, device_id_type=MESH,
    )


def sigmoid(values):
    return 1.0 / (1.0 + jnp.exp(-values))


def one_hot(shape, source_of):
    target = lax.broadcasted_iota(jnp.int32, shape, 0)
    source = lax.broadcasted_iota(jnp.int32, shape, 1)
    return jnp.where(source == source_of(target), 1.0, 0.0).astype(BF16)


def key_row_of(place, block, pieces):
    tail = block - MAIN
    main_at = place // MAIN * block + place % MAIN
    spare = place - pieces * MAIN
    tail_at = spare // tail * block + MAIN + spare % tail
    return jnp.where(place < pieces * MAIN, main_at, tail_at)


def pair_switch(heads):
    lanes = heads * MAIN
    source = lax.broadcasted_iota(jnp.int32, (lanes, lanes), 0)
    target = lax.broadcasted_iota(jnp.int32, (lanes, lanes), 1)
    return jnp.where(source % heads * MAIN + source // heads == target, 1.0, 0.0).astype(BF16)


def spread_heads(matrix, keys):
    channels, heads = matrix.shape
    one = lax.broadcasted_iota(jnp.int32, (heads, keys * heads), 0)
    two = lax.broadcasted_iota(jnp.int32, (heads, keys * heads), 1)
    repeat = dot_nn(matrix, jnp.where(two % heads == one, 1.0, 0.0).astype(BF16))
    owner = lax.broadcasted_iota(jnp.int32, (1, keys * heads), 1) // heads
    return [jnp.where(owner == key, repeat, 0.0).astype(BF16) for key in range(keys)]


def mean_pair():
    one = lax.broadcasted_iota(jnp.int32, (2 * LANES, 2 * LANES), 0) // LANES
    two = lax.broadcasted_iota(jnp.int32, (2 * LANES, 2 * LANES), 1) // LANES
    return jnp.where(one == two, 1.0 / LANES, 0.0).astype(BF16)


def norm_pair(low, means):
    centered = low.astype(F32) - dot_nn(low, means)
    variance = dot_nn((centered * centered).astype(BF16), means)
    inverse = lax.rsqrt(variance + EPSILON)
    return (centered * inverse, inverse)


GROUP = 16


def columns_of(project):
    size = project.shape[1]
    eye = one_hot((size, size), lambda row: row)
    return dot_nt(eye, project).astype(BF16)


def front_kernel(
    struct_ref, len_ref, act_ref, cond_ref, small_ref, pair_ref,
    *refs
):
    shards, refs = refs[:14], refs[14:]
    (out_ref, prob_out, adapted_ref, sig_ref, gate_ref, query_ref, kv_out, full_ref, *refs) = refs
    whole_outs, refs = refs[:14], refs[14:]
    (prob_ref, kv_ref, *refs) = refs
    wholes, refs = refs[:14], refs[14:]
    (scale_w, shift_w, key_w, value_w, query_w, gate_w) = wholes[:6]
    (
        small_all, pack_ref, pair_buf, lead_ref, spread_ref, keys_ref, values_ref, tail_ref, acc_ref,
        pair_sem, own_sem, small_send, small_recv, gather_send, gather_recv, pack_send, pack_recv,
        span_send, span_recv, whole_sem, prob_sem, kv_sem,
    ) = refs
    total, width = act_ref.shape
    samples, rows = out_ref.shape[0], out_ref.shape[1]
    count = pack_ref.shape[0]
    spans = kv_ref.shape[0]
    heads = width // HEAD_DIM
    structs = pair_ref.shape[0]
    block = pair_ref.shape[1]
    tail = block - MAIN
    pieces = rows // block
    main_rows = pieces * MAIN
    keys = count * block
    pairs = heads // 2
    group, windows = head_windows(width)
    me = lax.axis_index("samp")
    my_span = lax.axis_index("head")
    reduce_pair = reduce_orders(count)
    orders = [order[1:] + order[:1] for order in reduce_pair]
    bits = sorted(reduce_pair[0])
    steps = len(bits)
    peers = flips(me, bits)

    owns = [
        pltpu.make_async_copy(shard, whole.at[me], own_sem.at[at])
        for at, (shard, whole) in enumerate(zip(shards, wholes))
    ]
    for copy in owns:
        copy.start()

    loads = [
        pltpu.make_async_copy(pair_ref.at[struct], pair_buf.at[struct], pair_sem.at[struct])
        for struct in range(structs)
    ]
    for load in loads:
        load.start()
    whole_moves = [
        pltpu.make_async_copy(whole, out, whole_sem.at[at])
        for at, (whole, out) in enumerate(zip(wholes, whole_outs))
    ]
    prob_moves = [
        pltpu.make_async_copy(prob_ref.at[at], prob_out.at[at], prob_sem.at[at]) for at in range(samples)
    ]
    kv_move = pltpu.make_async_copy(kv_ref, kv_out, kv_sem.at[0])
    small_all[me] = small_ref[...]
    greet(
        [dict(samp=peer) for peer in peers[1:]]
        + [dict(head=lax.rem(my_span + away, spans)) for away in range(1, spans)]
    )
    for at in range(1, count):
        send(
            small_ref, small_all.at[me], small_send.at[at], small_recv.at[at], dict(samp=peers[at])
        ).start()

    def gather_copies(which, step, sending):
        order = orders[which % 2]
        held = flips(me, order[:step])
        copies = []
        for at, spot in enumerate(held):
            slot = spot if sending else flip(spot, order[step])
            copies.append(
                send(
                    shards[which] if at == 0 else wholes[which].at[slot], wholes[which].at[slot],
                    gather_send.at[which, step, at], gather_recv.at[which, step, at],
                    dict(samp=flip(me, order[step])),
                )
            )
        return copies

    def gather_start(pair_at, step):
        for which in (2 * pair_at, 2 * pair_at + 1):
            for copy in gather_copies(which, step, True):
                copy.start()

    def gather_wait(pair_at, step):
        for which in (2 * pair_at, 2 * pair_at + 1):
            for copy in gather_copies(which, step, False):
                copy.wait_recv()

    def late_start(step):
        for pair_at in range(3, 7):
            gather_start(pair_at, step)

    def late_out(pair_at):
        gather_wait(pair_at, 2)
        for which in (2 * pair_at, 2 * pair_at + 1):
            whole_moves[which].start()

    def late_wait(step):
        for pair_at in range(3, 7):
            gather_wait(pair_at, step)

    tiles = pack_ref.shape[1]
    halves = (pl.ds(0, tiles // 2), pl.ds(tiles // 2, tiles - tiles // 2))

    def pack_copies(half, step, sending):
        order = orders[half]
        copies = []
        for at, spot in enumerate(flips(me, order[:step])):
            slot = spot if sending else flip(spot, order[step])
            copies.append(
                send(
                    pack_ref.at[slot, halves[half]], pack_ref.at[slot, halves[half]],
                    pack_send.at[half, step, at], pack_recv.at[half, step, at],
                    dict(samp=flip(me, order[step])),
                )
            )
        return copies

    def pack_start(step):
        for half in range(2):
            for copy in pack_copies(half, step, True):
                copy.start()

    def pack_wait(step):
        for half in range(2):
            for copy in pack_copies(half, step, False):
                copy.wait_recv()

    gather_start(0, 0)
    gather_start(1, 0)

    for at in range(1, count):
        send(
            small_ref, small_all.at[peers[at]], small_send.at[at], small_recv.at[at], dict(samp=peers[at])
        ).wait_recv()
    full = small_all[0].astype(F32)
    for at in range(1, count):
        full = full + small_all[at].astype(F32)
    full_ref[...] = full
    for at, part in enumerate(spread_heads(columns_of(full[8:, :LANES].astype(BF16)), GROUP)):
        spread_ref[at * LANES : (at + 1) * LANES] = part
    means = mean_pair()
    order_switch = pair_switch(heads)
    groups = MAIN // GROUP
    for load in loads:
        load.wait()

    def project_keys(struct, first, number):
        total_lead = None
        for at in range(number // 2):
            key = first + 2 * at
            low = jnp.concatenate((pair_buf[struct, key], pair_buf[struct, key + 1]), axis=1)
            normed, _ = norm_pair(low, means)
            lead = dot_nn(
                normed.astype(BF16),
                spread_ref[2 * at * LANES : (2 * at + 2) * LANES, : number * heads],
            )
            total_lead = lead if total_lead is None else total_lead + lead
        return total_lead.astype(BF16)

    def pair_group(turn, carry):
        lead_ref[turn] = project_keys(lax.div(turn, groups), lax.rem(turn, groups) * GROUP, GROUP)
        return carry

    turns = structs * groups
    cuts = [turns * at // 6 for at in range(7)]
    gather_wait(0, 0)
    gather_start(0, 1)
    gather_wait(1, 0)
    gather_start(1, 1)
    gather_start(2, 0)
    lax.fori_loop(cuts[0], cuts[1], pair_group, 0)
    gather_wait(0, 1)
    gather_start(0, 2)
    lax.fori_loop(cuts[1], cuts[2], pair_group, 0)
    gather_wait(2, 0)
    gather_start(2, 1)
    late_start(0)
    lax.fori_loop(cuts[2], cuts[3], pair_group, 0)
    gather_wait(1, 1)
    gather_start(1, 2)

    gain_one = full[0:1, : cond_ref.shape[1]]
    act_normed, _ = norm_rows(act_ref[...].astype(F32))
    cond_normed, _ = norm_rows(cond_ref[...].astype(F32))
    cond_first = (cond_normed * gain_one).astype(BF16)
    for copy in owns[:6]:
        copy.wait()
    gather_wait(0, 2)
    scale = scale_w[...].reshape(-1, width)
    shift = shift_w[...].reshape(-1, width)
    sig_first = sigmoid(dot_nn(cond_first, scale) + full[1:2])
    adapted = sig_first * act_normed + dot_nn(cond_first, shift)
    sig_ref[...] = sig_first
    adapted_ref[...] = adapted.astype(BF16)
    reorder = one_hot((rows, rows), lambda row: key_row_of(row, block, pieces))
    gather_wait(1, 2)
    for which, whole in ((0, key_w), (1, value_w)):
        for sample in range(samples):
            ordered = dot_nn(
                reorder, adapted[sample * rows : (sample + 1) * rows].astype(BF16)
            ).astype(BF16)
            kv_ref[my_span, which, sample] = dot_nn(ordered, whole[...].reshape(-1, width)).astype(BF16)

    def span_move(way, step, which, sending):
        delta = 1 - 2 * way
        shard = my_span - delta * step if sending else my_span - delta * (step + 1)
        target = my_span + delta
        there = (shard >= 0) & (shard < spans)
        if sending:
            there = there & (target >= 0) & (target < spans)
        copy = send(
            kv_ref.at[shard, which], kv_ref.at[shard, which],
            span_send.at[way, step, which], span_recv.at[way, step, which],
            dict(head=target if sending else my_span - delta),
        )
        return there, copy

    def span_start(step, which):
        for way in range(2):
            there, copy = span_move(way, step, which, True)
            pl.when(there)(copy.start)

    def span_wait(step, which):
        for way in range(2):
            there, copy = span_move(way, step, which, False)
            pl.when(there)(copy.wait_recv)

    span_start(0, 0)
    lax.fori_loop(cuts[3], cuts[6], pair_group, 0)
    for struct in range(structs):
        whole = jnp.concatenate([lead_ref[struct * groups + at] for at in range(groups)], axis=1)
        mixed = dot_nn(whole, order_switch).astype(BF16)
        for at in range(pairs):
            pack_ref[me, struct * pairs + at] = mixed[:, at * LANES : (at + 1) * LANES]
        rest = project_keys(struct, MAIN, tail)
        blank = jnp.zeros((rows, LANES - tail * heads), BF16)
        pack_ref[me, structs * pairs + struct] = jnp.concatenate((rest, blank), axis=1)
    pack_start(0)
    span_wait(0, 0)
    span_start(1, 0)
    span_start(0, 1)
    gather_wait(2, 1)
    gather_start(2, 2)
    low = adapted.astype(BF16)
    gather_wait(2, 2)
    for move in whole_moves[:6]:
        move.start()
    query = dot_nn(low, query_w[...].reshape(-1, width)) + full[2:3]
    for sample in range(samples):
        query_ref[sample] = query[sample * rows : (sample + 1) * rows].astype(BF16)
    pack_wait(0)
    pack_start(1)
    gate_ref[...] = sigmoid(dot_nn(low, gate_w[...].reshape(-1, width)))
    late_wait(0)
    late_start(1)
    for step in range(1, spans - 1):
        span_wait(step, 0)
        if step + 1 < spans - 1:
            span_start(step + 1, 0)
        span_wait(step - 1, 1)
        span_start(step, 1)
    pack_wait(1)
    pack_start(2)

    switch = tail_switch(count, heads, tail)
    places = key_places(count, block)
    keys_ref[keys:] = jnp.zeros_like(keys_ref[keys:])
    values_ref[keys:] = jnp.zeros_like(values_ref[keys:])

    def gather_keys(sample, which, held):
        for span in range(spans):
            held[span * main_rows : (span + 1) * main_rows] = kv_ref[span, which, sample, :main_rows]
            spot = count * MAIN + span * (rows - main_rows)
            held[spot : spot + rows - main_rows] = kv_ref[span, which, sample, main_rows:]

    def one_sample(sample, carry):
        struct = struct_ref[sample]
        valid = places < len_ref[struct]
        gather_keys(sample, 0, keys_ref)
        tiles_of = []
        for pair in range(count // 2):
            even = pack_ref[2 * pair, structs * pairs + struct]
            odd = swap_halves(pack_ref[2 * pair + 1, structs * pairs + struct])
            tiles_of.append(jnp.where(low_half(even), even, odd))
        mixed = dot_nn(jnp.concatenate(tiles_of, axis=1), switch).astype(BF16)
        for at in range(count // 2):
            tail_ref[at] = mixed[:, at * LANES : (at + 1) * LANES]

        def one_group(place, carry):
            for at, (start, span, offset) in enumerate(windows):
                lanes = pl.ds(pl.multiple_of(place * group + start, LANES), span)
                mask = head_mask(span, offset)
                tile = struct * pairs + place * (len(windows) // 2) + at // 2
                bias = []
                for pair in range(count // 2):
                    even = pack_ref[2 * pair, tile]
                    odd = pack_ref[2 * pair + 1, tile]
                    if at % 2 == 0:
                        bias.append(jnp.where(low_half(even), even, swap_halves(odd)))
                    else:
                        bias.append(jnp.where(low_half(even), swap_halves(even), odd))
                per_tile = LANES // (count * tail)
                rest = tail_ref[place * (len(windows) // per_tile) + at // per_tile]
                turn = at % per_tile * count * tail
                bias.append(pltpu.roll(rest, LANES - turn, 1) if turn else rest)
                query = query_ref[sample, :, lanes]
                query = jnp.where(mask, query, jnp.zeros_like(query))
                scores = dot_nt(query, keys_ref[:, lanes]) * HEAD_DIM ** (-0.5) + jnp.concatenate(
                    bias, axis=1
                ).astype(F32)
                scores = jnp.where(valid, scores, NEG_BIG)
                weights = jnp.exp(scores - jnp.max(scores, axis=1, keepdims=True))
                weights = weights * (1.0 / jnp.sum(weights, axis=1, keepdims=True))
                prob_ref[sample, place * len(windows) + at] = weights.astype(BF16)
            return carry

        return lax.fori_loop(0, width // group, one_group, carry)

    def mix_sample(sample, carry):
        gather_keys(sample, 1, values_ref)

        def mix_group(place, carry):
            acc_ref[...] = jnp.zeros_like(acc_ref)
            for at, (start, span, offset) in enumerate(windows):
                lanes = pl.ds(pl.multiple_of(place * group + start, LANES), span)
                weights = prob_ref[sample, place * len(windows) + at]
                mixed = dot_nn(weights, values_ref[:, lanes])
                within = slice(start, start + span)
                acc_ref[:, within] += jnp.where(head_mask(span, offset), mixed, 0.0)
            out_ref[sample, :, pl.ds(pl.multiple_of(place * group, LANES), group)] = acc_ref[
                ...
            ].astype(BF16)
            return carry

        return lax.fori_loop(0, width // group, mix_group, carry)

    pack_wait(2)
    lax.fori_loop(0, samples // 2, one_sample, 0)
    for move in prob_moves[: samples // 2]:
        move.start()
    span_wait(spans - 2, 1)
    kv_move.start()
    lax.fori_loop(samples // 2, samples, one_sample, 0)
    for move in prob_moves[samples // 2 :]:
        move.start()
    for copy in owns[6:]:
        copy.wait()
    for pair_at in range(3, 7):
        gather_wait(pair_at, 1)
        gather_start(pair_at, 2)
        if pair_at == 3:
            lax.fori_loop(0, samples, mix_sample, 0)
        else:
            late_out(pair_at - 1)
    late_out(6)
    for move in whole_moves + prob_moves + [kv_move]:
        move.wait()

    for at in range(1, count):
        send(
            small_ref, small_all.at[me], small_send.at[at], small_recv.at[at], dict(samp=peers[at])
        ).wait_send()
    for which in range(len(wholes)):
        for step in range(steps):
            for copy in gather_copies(which, step, True):
                copy.wait_send()
    for half in range(2):
        for step in range(steps):
            for copy in pack_copies(half, step, True):
                copy.wait_send()
    for step in range(spans - 1):
        for which in range(2):
            for way in range(2):
                there, copy = span_move(way, step, which, True)
                pl.when(there)(copy.wait_send)


def front(struct_of, struct_len, act, cond, small, pair, shards, samples, count, spans):
    total, width = act.shape
    rows = total // samples
    structs, block = pair.shape[0], pair.shape[1]
    heads = width // HEAD_DIM
    group, windows = head_windows(width)
    tail = block - MAIN
    tiles = structs * (heads // 2 + 1)
    steps = count.bit_length() - 1
    vmem = pl.BlockSpec(memory_space=pltpu.VMEM)
    smem = pl.BlockSpec(memory_space=pltpu.SMEM)
    far = pl.BlockSpec(memory_space=pl.ANY)
    dma = pltpu.SemaphoreType.DMA
    return pl.pallas_call(
        front_kernel,
        out_shape=(
            jax.ShapeDtypeStruct((samples, rows, width), BF16),
            jax.ShapeDtypeStruct((samples, heads, rows, KEY_LANES), BF16),
            jax.ShapeDtypeStruct((total, width), BF16),
            jax.ShapeDtypeStruct((total, width), F32),
            jax.ShapeDtypeStruct((total, width), F32),
            jax.ShapeDtypeStruct((samples, rows, width), BF16),
            jax.ShapeDtypeStruct((spans, 2, samples, rows, width), BF16),
            jax.ShapeDtypeStruct(small.shape, F32),
        )
        + tuple(jax.ShapeDtypeStruct((count,) + shard.shape, BF16) for shard in shards),
        in_specs=[smem, smem, vmem, vmem, vmem] + [far] * 15,
        out_specs=[vmem, far] + [vmem] * 4 + [far, vmem] + [far] * 14,
        scratch_shapes=[
            pltpu.VMEM((samples, heads, rows, KEY_LANES), BF16),
            pltpu.VMEM((spans, 2, samples, rows, width), BF16),
        ]
        + [pltpu.VMEM((count,) + shard.shape, BF16) for shard in shards]
        + [
            pltpu.VMEM((count,) + small.shape, BF16),
            pltpu.VMEM((count, tiles, rows, LANES), BF16),
            pltpu.VMEM(pair.shape, BF16),
            pltpu.VMEM((structs * MAIN // GROUP, rows, GROUP * heads), BF16),
            pltpu.VMEM((GROUP * LANES, GROUP * heads), BF16),
            pltpu.VMEM((KEY_LANES, width), BF16),
            pltpu.VMEM((KEY_LANES, width), BF16),
            pltpu.VMEM((count // 2, rows, LANES), BF16),
            pltpu.VMEM((rows, group), F32),
            dma((structs,)),
            dma((len(shards),)),
            dma((count,)),
            dma((count,)),
            dma((len(shards), steps, count // 2)),
            dma((len(shards), steps, count // 2)),
            dma((2, steps, count // 2)),
            dma((2, steps, count // 2)),
            dma((2, spans - 1, 2)),
            dma((2, spans - 1, 2)),
            dma((len(shards),)),
            dma((samples,)),
            dma((1,)),
        ],
        compiler_params=pltpu.CompilerParams(
            vmem_limit_bytes=60 << 20, collective_id=2, has_side_effects=True
        ),
        name="front",
    )(struct_of, struct_len, act, cond, small, pair, *shards)


def middle_kernel(
    attn_ref, gate_ref, act_ref, cond_ref, cot_ref, full_ref, *refs
):
    sources, refs = refs[:8], refs[8:]
    outs, refs = refs[7:15], refs[:7] + refs[15:]
    in_sem, out_sem = refs[23:]
    loads = [
        pltpu.make_async_copy(source, held, in_sem.at[at])
        for at, (source, held) in enumerate(zip(sources, refs[7:15]))
    ]
    leaves = [
        pltpu.make_async_copy(held, out, out_sem.at[at]) for at, (held, out) in enumerate(zip(refs[15:23], outs))
    ]
    for at in (3, 4, 5, 7, 0, 1, 2, 6):
        loads[at].start()
    ready = {id(held): load for held, load in zip(refs[7:15], loads)}
    leaving = {id(held): leave for held, leave in zip(refs[15:23], leaves)}
    middle_body(ready, leaving, attn_ref, gate_ref, act_ref, cond_ref, cot_ref, full_ref, *refs[:23])
    for leave in leaves:
        leave.wait()


def middle_body(
    ready, leaving, attn_ref, gate_ref, act_ref, cond_ref, cot_ref, full_ref, layer_ref, dgate_ref, dattn_ref, dmid_ref, dcond_ref, extra_ref, vector_ref,
    swish_w, linear_w, down_w, out_w, zero_w, scale_w, zero_two_w, shift_w, swish_g, linear_g, down_g, out_g, zero_g, scale_g, zero_two_g, shift_g,
):
    total, width = act_ref.shape
    samples, rows, _ = attn_ref.shape
    cond_width = cond_ref.shape[1]

    def whole(ref):
        load = ready.pop(id(ref), None)
        if load is not None:
            load.wait()
        return ref[...].reshape(-1, ref.shape[2])

    def store_grad(ref, left, right):
        size = ref.shape[1]
        step = 2 * size if size * 2 < left.shape[1] else size
        for first in range(0, left.shape[1], step):
            value = dot_tn(left[:, first : first + step], right).astype(BF16)
            for at in range(step // size):
                ref[first // size + at] = value[at * size : (at + 1) * size]
        leaving[id(ref)].start()

    cond = cond_ref[...]
    cond_normed, _ = norm_rows(cond.astype(F32))
    gain_two = full_ref[4:5, :cond_width]
    cond_second = (cond_normed * gain_two).astype(BF16)
    attn = jnp.concatenate([attn_ref[at].astype(F32) for at in range(samples)], axis=0)
    gate_sig = gate_ref[...]
    gated = (gate_sig * attn).astype(BF16)
    branch = dot_nn(gated, whole(out_w))
    zero_sig = sigmoid(dot_nn(cond, whole(zero_w)) + full_ref[3:4])
    middle = act_ref[...].astype(F32) + zero_sig * branch
    mid_normed, mid_inverse = norm_rows(middle)
    sig_second = sigmoid(dot_nn(cond_second, whole(scale_w)) + full_ref[5:6])
    adapted = (sig_second * mid_normed + dot_nn(cond_second, whole(shift_w))).astype(BF16)
    swish_pre = dot_nn(adapted, whole(swish_w))
    linear_pre = dot_nn(adapted, whole(linear_w))
    swish_sig = sigmoid(swish_pre)
    hidden = (swish_pre * swish_sig * linear_pre).astype(BF16)
    down_rows = dot_nn(hidden, whole(down_w))
    zero_sig_two = sigmoid(dot_nn(cond, whole(zero_two_w)) + full_ref[6:7])
    layer_ref[...] = (middle + zero_sig_two * down_rows).astype(BF16)

    upstream = cot_ref[...].astype(F32)
    d_down = (upstream * zero_sig_two).astype(BF16)
    d_zero_two = (upstream * down_rows * sigmoid_slope(zero_sig_two)).astype(BF16)
    store_grad(down_g, hidden, d_down)
    store_grad(zero_two_g, cond, d_zero_two)
    d_hidden = dot_nt(d_down, whole(down_w))
    d_swish = (d_hidden * linear_pre * swish_sig * (1.0 + swish_pre * (1.0 - swish_sig))).astype(BF16)
    d_linear = (d_hidden * swish_pre * swish_sig).astype(BF16)
    store_grad(swish_g, adapted, d_swish)
    store_grad(linear_g, adapted, d_linear)
    d_adapted = dot_nt(d_swish, whole(swish_w)) + dot_nt(d_linear, whole(linear_w))
    d_shift = d_adapted.astype(BF16)
    d_pre = (d_adapted * mid_normed * sigmoid_slope(sig_second)).astype(BF16)
    store_grad(scale_g, cond_second, d_pre)
    store_grad(shift_g, cond_second, d_shift)
    d_cond = dot_nt(d_shift, whole(shift_w)) + dot_nt(d_pre, whole(scale_w))
    dcond_ref[...] = d_cond * gain_two
    d_middle = upstream + norm_back(mid_normed, mid_inverse, d_adapted * sig_second)
    dmid_ref[...] = d_middle
    d_branch = (d_middle * zero_sig).astype(BF16)
    d_zero = (d_middle * branch * sigmoid_slope(zero_sig)).astype(BF16)
    store_grad(out_g, gated, d_branch)
    store_grad(zero_g, cond, d_zero)
    extra_ref[...] = dot_nt(d_zero, whole(zero_w)) + dot_nt(d_zero_two, whole(zero_two_w))
    d_gated = dot_nt(d_branch, whole(out_w))
    dgate_ref[...] = (d_gated * attn * sigmoid_slope(gate_sig)).astype(BF16)
    d_attn = d_gated * gate_sig
    for at in range(samples):
        dattn_ref[at] = d_attn[at * rows : (at + 1) * rows].astype(BF16)
    vector_ref[...] = jnp.zeros_like(vector_ref)
    vector_ref[3:4] = jnp.sum(d_zero.astype(F32), axis=0, keepdims=True)
    vector_ref[4:5, :cond_width] = jnp.sum(d_cond * cond_normed, axis=0, keepdims=True)
    vector_ref[5:6] = jnp.sum(d_pre.astype(F32), axis=0, keepdims=True)
    vector_ref[6:7] = jnp.sum(d_zero_two.astype(F32), axis=0, keepdims=True)


def middle_part(attended, gate_sig, act, cond, cotangent, full, weights):
    total, width = act.shape
    vmem = pl.BlockSpec(memory_space=pltpu.VMEM)
    far = pl.BlockSpec(memory_space=pl.ANY)
    weights = list(weights)
    return pl.pallas_call(
        middle_kernel,
        out_shape=(
            jax.ShapeDtypeStruct((total, width), BF16),
            jax.ShapeDtypeStruct((total, width), BF16),
            jax.ShapeDtypeStruct(attended.shape, BF16),
            jax.ShapeDtypeStruct((total, width), F32),
            jax.ShapeDtypeStruct(cond.shape, F32),
            jax.ShapeDtypeStruct(cond.shape, F32),
            jax.ShapeDtypeStruct(full.shape, F32),
        )
        + tuple(jax.ShapeDtypeStruct(weight.shape, BF16) for weight in weights),
        in_specs=[vmem] * 6 + [far] * 8,
        out_specs=[vmem] * 7 + [far] * 8,
        scratch_shapes=[pltpu.VMEM(weight.shape, BF16) for weight in weights + weights]
        + [pltpu.SemaphoreType.DMA((8,)), pltpu.SemaphoreType.DMA((8,))],
        compiler_params=pltpu.CompilerParams(vmem_limit_bytes=62 << 20),
        name="middle",
    )(attended, gate_sig, act, cond, cotangent, full, *weights)


class Halving:
    def __init__(self, me, order, source, zones, send_sem, recv_sem, stay=None, stay_sem=None):
        self.me, self.order, self.source, self.zones = me, order, source, zones
        self.send_sem, self.recv_sem = send_sem, recv_sem
        self.stay, self.stay_sem = stay, stay_sem

    def stays(self):
        if self.stay is None:
            return []
        return [
            pltpu.make_async_copy(self.source.at[spot], self.stay.at[at], self.stay_sem.at[at])
            for at, spot in enumerate(flips(self.me, self.order[1:]))
        ]

    def copies(self, step):
        kept = flips(self.me, self.order[step + 1 :])
        found = []
        for at, spot in enumerate(kept):
            if step == 0:
                leaving = self.source.at[flip(spot, self.order[0])]
            else:
                leaving = self.zones[step - 1].at[2 * at + 1]
            found.append(
                send(
                    leaving, self.zones[step].at[at], self.send_sem.at[step, at],
                    self.recv_sem.at[step, at], dict(samp=flip(self.me, self.order[step])),
                )
            )
        return found

    def start(self, step):
        for copy in self.copies(step) + (self.stays() if step == 0 else []):
            copy.start()

    def first(self, at, spot, lines):
        return self.source[spot, lines] if self.stay is None else self.stay[at, lines]

    def finish(self, step):
        kept = flips(self.me, self.order[step + 1 :])
        zone = self.zones[step]
        if step == 0:
            for copy in self.stays():
                copy.wait()
        for at, copy in enumerate(self.copies(step)):
            copy.wait_recv()

            def add(turn, carry, at=at):
                lines = pl.ds(pl.multiple_of(turn * 16, 16), 16)
                mine = self.first(at, kept[at], lines) if step == 0 else self.zones[step - 1][2 * at, lines]
                zone[at, lines] = (zone[at, lines].astype(F32) + mine.astype(F32)).astype(BF16)
                return carry

            lax.fori_loop(0, zone.shape[1] // 16, add, 0)

    def settle(self):
        for step in range(len(self.order)):
            for copy in self.copies(step):
                copy.wait_send()


def zone_shapes(shapes, count):
    zones = []
    for rows, columns in shapes:
        size = count // 2
        while size:
            zones.append(pltpu.VMEM((size, rows, columns), BF16))
            size //= 2
    return zones


def spans_of(shapes, columns, spans):
    lines = []
    for at, (rows, wide) in enumerate(shapes):
        for half in range(wide // columns):
            lines += [(at, row, half * columns) for row in range(0, rows, 8)]
    each = len(lines) // spans
    moves = []
    for piece in range(spans):
        row = 0
        for at, start, lane in lines[piece * each : (piece + 1) * each]:
            last = moves[-1] if moves else None
            if last and last[0] == piece and last[2] == at and last[4] == lane and last[3] + last[5] == start:
                moves[-1] = last[:5] + (last[5] + 8,)
            else:
                moves.append((piece, row, at, start, lane, 8))
            row += 8
    return (each * 8, moves)


def attend_back_kernel(
    late_shapes, struct_ref, q_ref, kv_ref, do_ref, prob_ref, *refs
):
    lates, refs = refs[: len(late_shapes)], refs[len(late_shapes) :]
    (dq_ref, dkv_ref, dpb_ref, late_out, *refs) = refs
    steps = 3
    late_zones, refs = refs[: steps * len(late_shapes)], refs[steps * len(late_shapes) :]
    late_stay, refs = refs[: len(late_shapes)], refs[len(late_shapes) :]
    (late_send, late_recv, stay_sem, *refs) = refs
    attend_back_body(
        late_shapes, struct_ref, q_ref, kv_ref, do_ref, prob_ref, lates, dq_ref, dkv_ref, dpb_ref, late_out,
        late_zones, late_stay, late_send, late_recv, stay_sem, *refs
    )


def attend_back_body(
    late_shapes, struct_ref, q_ref, kv_ref, do_ref, prob_ref, lates, dq_ref, dkv_ref, dpb_ref, late_out,
    late_zones, late_stay, late_send, late_recv, stay_sem,
    key_ref, value_ref, dq_acc, dk_acc, dv_acc, first_ref, tail_ref, part_ref, span_ref, pack_ref,
    got_zero, got_one, got_two, span_send, span_recv, pack_send, pack_recv,
):
    samples, rows, width = q_ref.shape
    count = pack_ref.shape[0]
    spans = kv_ref.shape[0]
    heads = width // HEAD_DIM
    block = rows * spans // count
    tail = block - MAIN
    structs = pack_ref.shape[1] // (heads // 2 + 1)
    main_rows = rows // block * MAIN
    keys = count * block
    group, windows = head_windows(width)
    scale = HEAD_DIM ** (-0.5)
    me = lax.axis_index("samp")
    my_span = lax.axis_index("head")
    orders = reduce_orders(count)
    others = [lax.rem(my_span + away, spans) for away in range(1, spans)]
    greet(
        [dict(samp=flip(me, bit)) for bit in sorted(orders[0])] + [dict(head=other) for other in others]
    )
    movers = [
        Halving(
            me, orders[at % 2], lates[at], late_zones[3 * at : 3 * at + 3], late_send.at[at], late_recv.at[at],
            late_stay[at], stay_sem.at[at],
        )
        for at in range(len(lates))
    ]
    for mover in movers:
        mover.start(0)
    switch = tail_switch(count, heads, tail)
    key_ref[keys:] = jnp.zeros_like(key_ref[keys:])
    value_ref[keys:] = jnp.zeros_like(value_ref[keys:])

    def span_copy(place, sample, away):
        lanes = pl.ds(pl.multiple_of(place * group, LANES), group)
        return send(
            part_ref.at[others[away], :, sample, :, lanes],
            span_ref.at[away, :, sample, :, lanes],
            span_send.at[place, sample, away],
            span_recv.at[place, sample, away],
            dict(head=others[away]),
        )

    def one_group(place, carry):
        for sample in range(samples):
            for span in range(spans):
                for which, held in ((0, key_ref), (1, value_ref)):
                    held[span * main_rows : (span + 1) * main_rows] = kv_ref[
                        span, which, sample, :main_rows, pl.ds(pl.multiple_of(place * group, LANES), group)
                    ]
                    spot = count * MAIN + span * (rows - main_rows)
                    held[spot : spot + rows - main_rows] = kv_ref[
                        span, which, sample, main_rows:, pl.ds(pl.multiple_of(place * group, LANES), group)
                    ]
            dq_acc[...] = jnp.zeros_like(dq_acc)
            dk_acc[...] = jnp.zeros_like(dk_acc)
            dv_acc[...] = jnp.zeros_like(dv_acc)
            kept = [jnp.where(struct_ref[0] == slab, 1.0, 0.0).astype(BF16) for slab in range(structs)]
            added = [jnp.where(struct_ref[1] == slab, 1.0, 0.0).astype(BF16) for slab in range(structs)]
            even_scores = None
            for at, (start, span, offset) in enumerate(windows):
                lanes = pl.ds(pl.multiple_of(place * group + start, LANES), span)
                within = slice(start, start + span)
                mask = head_mask(span, offset)
                upstream = do_ref[sample, :, lanes]
                upstream = jnp.where(mask, upstream, jnp.zeros_like(upstream))
                query = q_ref[sample, :, lanes]
                query = jnp.where(mask, query, jnp.zeros_like(query))
                low = prob_ref[sample, place * len(windows) + at]
                weights = low.astype(F32)
                d_weights = dot_nt(upstream, value_ref[:, within])
                dv_acc[:, within] += dot_tn(low[:, :keys], upstream)
                cross = weights * d_weights
                delta = jnp.sum(cross, axis=1, keepdims=True)
                d_scores = (cross - weights * delta).astype(BF16)
                dq_acc[:, within] += jnp.where(mask, dot_nn(d_scores, key_ref[:, within]), 0.0)
                dk_acc[:, within] += dot_tn(d_scores[:, :keys], query)
                per_tile = LANES // (count * tail)
                turn = at % per_tile * count * tail
                rest = d_scores[:, count * MAIN :]
                rest = pltpu.roll(rest, turn, 1) if turn else rest
                spot = place * (len(windows) // per_tile) + at // per_tile
                if turn:
                    tail_ref[sample, spot] += rest
                else:
                    tail_ref[sample, spot] = rest
                if at % 2 == 0:
                    even_scores = d_scores
                    continue
                for pair in range(count // 2):
                    even = even_scores[:, pair * LANES : (pair + 1) * LANES]
                    odd = d_scores[:, pair * LANES : (pair + 1) * LANES]
                    low_tile = jnp.where(low_half(even), even, swap_halves(odd))
                    high_tile = jnp.where(low_half(even), swap_halves(even), odd)
                    for side, tile in ((0, low_tile), (1, high_tile)):
                        owner = 2 * pair + side
                        if sample == 0:
                            first_ref[at // 2, owner] = tile
                            continue
                        old = first_ref[at // 2, owner]
                        for slab in range(structs):
                            spot = slab * (heads // 2) + place * (len(windows) // 2) + at // 2
                            pack_ref[owner, spot] = old * kept[slab] + tile * added[slab]
            lanes = pl.ds(pl.multiple_of(place * group, LANES), group)
            dq_ref[sample, :, lanes] = (dq_acc[...] * scale).astype(BF16)
            for span in range(spans):
                spot = count * MAIN + span * (rows - main_rows)
                for which, total, factor in ((0, dk_acc, scale), (1, dv_acc, 1.0)):
                    part_ref[span, which, sample, :main_rows, lanes] = (
                        total[span * main_rows : (span + 1) * main_rows] * factor
                    ).astype(BF16)
                    part_ref[span, which, sample, main_rows:, lanes] = (
                        total[spot : spot + rows - main_rows] * factor
                    ).astype(BF16)
            for away in range(spans - 1):
                span_copy(place, sample, away).start()
            if sample == 0:

                @pl.when(place == 0)
                def _():
                    for mover in movers:
                        mover.finish(0)
                        mover.start(1)

        return carry

    lax.fori_loop(0, width // group, one_group, 0)

    mixed = []
    for sample in range(samples):
        whole = jnp.concatenate([tail_ref[sample, at] for at in range(count // 2)], axis=1)
        mixed.append(dot_nt(whole, switch))
    for pair in range(count // 2):
        tiles = [part[:, pair * LANES : (pair + 1) * LANES] for part in mixed]
        for slab in range(structs):
            both = jnp.zeros_like(tiles[0])
            for sample in range(samples):
                both = both + jnp.where(struct_ref[sample] == slab, tiles[sample], 0.0)
            spot = structs * heads // 2 + slab
            pack_ref[2 * pair, spot] = jnp.where(low_half(both), both, 0.0).astype(BF16)
            pack_ref[2 * pair + 1, spot] = jnp.where(low_half(both), swap_halves(both), 0.0).astype(BF16)

    tiles = pack_ref.shape[1]
    halves = (pl.ds(0, tiles // 2), pl.ds(tiles // 2, tiles - tiles // 2))
    bounds = ((0, tiles // 2), (tiles // 2, tiles))
    landing = (got_zero, got_one, got_two)

    def stage_copies(step, half):
        order = orders[half]
        kept = flips(me, order[step + 1 :])
        return [
            send(
                pack_ref.at[flip(spot, order[step]), halves[half]],
                landing[step].at[at, halves[half]],
                pack_send.at[step, half, at],
                pack_recv.at[step, half, at],
                dict(samp=flip(me, order[step])),
            )
            for at, spot in enumerate(kept)
        ]

    flights = [[stage_copies(step, half) for half in range(2)] for step in range(len(orders[0]))]
    for half in range(2):
        for copy in flights[0][half]:
            copy.start()
    for step in range(len(orders[0])):
        for half in range(2):
            kept = flips(me, orders[half][step + 1 :])
            for at, spot in enumerate(kept):
                flights[step][half][at].wait_recv()

                def add(tile, carry, spot=spot, at=at, step=step):
                    pack_ref[spot, tile] = (
                        pack_ref[spot, tile].astype(F32) + landing[step][at, tile].astype(F32)
                    ).astype(BF16)
                    return carry

                lax.fori_loop(bounds[half][0], bounds[half][1], add, 0)
            if step + 1 < len(orders[0]):
                for copy in flights[step + 1][half]:
                    copy.start()
        if step == 0:
            for mover in movers:
                mover.finish(1)
                mover.start(2)
        if step == 1:
            for mover in movers:
                mover.finish(2)
            _, moves = spans_of(late_shapes, width, spans)
            for piece, row, at, start, lane, size in moves:
                late_out[piece, row : row + size] = movers[at].zones[2][
                    0, start : start + size, lane : lane + width
                ]

    def out(tile, carry):
        dpb_ref[tile] = pack_ref[me, tile]
        return carry

    lax.fori_loop(0, tiles, out, 0)

    for place in range(width // group):
        for sample in range(samples):
            for away in range(spans - 1):
                span_copy(place, sample, away).wait_recv()
    for which in range(2):
        for sample in range(samples):
            total = part_ref[my_span, which, sample].astype(F32)
            for away in range(spans - 1):
                total += span_ref[away, which, sample].astype(F32)
            dkv_ref[which, sample] = total.astype(BF16)
    for place in range(width // group):
        for sample in range(samples):
            for away in range(spans - 1):
                span_copy(place, sample, away).wait_send()
    for stage in flights:
        for half in stage:
            for copy in half:
                copy.wait_send()
    for mover in movers:
        mover.settle()


def attend_back(struct_of, structs, query, key_value, upstream, prob, lates, count):
    samples, rows, width = query.shape
    spans = key_value.shape[0]
    heads = width // HEAD_DIM
    group, windows = head_windows(width)
    keys = rows * spans
    tiles = structs * (heads // 2 + 1)
    steps = count.bit_length() - 1
    vmem = pl.BlockSpec(memory_space=pltpu.VMEM)
    smem = pl.BlockSpec(memory_space=pltpu.SMEM)
    late_shapes = [late.shape[1:] for late in lates]
    each, _ = spans_of(late_shapes, width, spans)
    dma = pltpu.SemaphoreType.DMA
    return pl.pallas_call(
        functools.partial(attend_back_kernel, late_shapes),
        out_shape=(
            jax.ShapeDtypeStruct((samples, rows, width), BF16),
            jax.ShapeDtypeStruct((2, samples, rows, width), BF16),
            jax.ShapeDtypeStruct((tiles, rows, LANES), BF16),
            jax.ShapeDtypeStruct((spans, each, width), BF16),
        ),
        in_specs=[smem] + [vmem] * 4 + [pl.BlockSpec(memory_space=pl.ANY)] * len(lates),
        out_specs=[vmem] * 4,
        scratch_shapes=zone_shapes(late_shapes, count)
        + [pltpu.VMEM((count // 2,) + shape, BF16) for shape in late_shapes]
        + [
            dma((len(lates), steps, count // 2)),
            dma((len(lates), steps, count // 2)),
            dma((len(lates), count // 2)),
            pltpu.VMEM((KEY_LANES, group), BF16),
            pltpu.VMEM((KEY_LANES, group), BF16),
            pltpu.VMEM((rows, group), F32),
            pltpu.VMEM((keys, group), F32),
            pltpu.VMEM((keys, group), F32),
            pltpu.VMEM((len(windows) // 2, count, rows, LANES), BF16),
            pltpu.VMEM((samples, count // 2, rows, LANES), BF16),
            pltpu.VMEM((spans, 2, samples, rows, width), BF16),
            pltpu.VMEM((spans - 1, 2, samples, rows, width), BF16),
            pltpu.VMEM((count, tiles, rows, LANES), BF16),
            pltpu.VMEM((count // 2, tiles, rows, LANES), BF16),
            pltpu.VMEM((count // 4, tiles, rows, LANES), BF16),
            pltpu.VMEM((count // 8, tiles, rows, LANES), BF16),
            pltpu.SemaphoreType.DMA((width // group, samples, spans - 1)),
            pltpu.SemaphoreType.DMA((width // group, samples, spans - 1)),
            pltpu.SemaphoreType.DMA((steps, 2, count // 2)),
            pltpu.SemaphoreType.DMA((steps, 2, count // 2)),
        ],
        compiler_params=pltpu.CompilerParams(
            vmem_limit_bytes=60 << 20, collective_id=1, has_side_effects=True
        ),
        name="attend_back",
    )(struct_of, query, key_value, upstream, prob, *lates)


class ChainSum:
    def __init__(self, place, places, source, got, whole, send_sem, recv_sem):
        self.place, self.places, self.source, self.got, self.whole = place, places, source, got, whole
        self.send_sem, self.recv_sem = send_sem, recv_sem

    def ways(self):
        return ((0, 1, self.place), (1, -1, self.places - 1 - self.place))

    def owner(self, way, spot):
        return spot if way == 0 else self.places - 1 - spot

    def partial(self, way, delta, tick, leaving):
        return send(
            leaving, self.got.at[way, tick], self.send_sem.at[0, way, tick], self.recv_sem.at[0, way, tick],
            dict(head=self.place + delta),
        )

    def each_partial(self, tick, act):
        for way, delta, spot in self.ways():
            piece = self.places - 1 - tick + spot
            sends = (tick >= spot) & (piece > spot)

            @pl.when(sends & (spot == 0))
            def _(way=way, delta=delta, piece=piece):
                act(self.partial(way, delta, tick, self.source.at[self.owner(way, piece)]))

            if tick:

                @pl.when(sends & (spot > 0))
                def _(way=way, delta=delta):
                    act(self.partial(way, delta, tick, self.got.at[way, tick - 1]))

    def start(self, tick):
        self.each_partial(tick, lambda copy: copy.start())

    def add(self, target, spot, source):
        size = 24

        def step(turn, carry):
            lines = pl.ds(pl.multiple_of(turn * size, 8), size)
            target[spot + (lines,)] = (
                target[spot + (lines,)].astype(F32) + source(lines).astype(F32)
            ).astype(BF16)
            return carry

        lax.fori_loop(0, self.source.shape[1] // size, step, 0)

    def receive(self, tick):
        for way, delta, spot in self.ways():
            piece = self.places - 2 - tick + spot

            @pl.when((spot >= 1) & (tick >= spot - 1))
            def _(way=way, delta=delta, piece=piece):
                self.partial(way, delta, tick, self.got.at[way, tick]).wait_recv()
                if tick < self.places - 2:
                    mine = self.owner(way, piece)
                    self.add(self.got, (way, tick), lambda lines: self.source[mine, lines])

    def total(self):
        self.whole[self.place] = self.source[self.place]
        for way, delta, spot in self.ways():

            @pl.when(spot >= 1)
            def _(way=way):
                self.add(self.whole, (self.place,), lambda lines: self.got[way, self.places - 2, lines])

    def passing(self, way, delta, step, sending):
        piece = self.place - delta * step if sending else self.place - delta * (step + 1)
        target = self.place + delta
        there = (piece >= 0) & (piece < self.places)
        if sending:
            there = there & (target >= 0) & (target < self.places)
        copy = send(
            self.whole.at[piece], self.whole.at[piece], self.send_sem.at[1, way, step],
            self.recv_sem.at[1, way, step], dict(head=target if sending else self.place - delta),
        )
        return there, copy

    def spread_start(self, step):
        for way, delta, _ in self.ways():
            there, copy = self.passing(way, delta, step, True)
            pl.when(there)(copy.start)

    def spread_wait(self, step):
        for way, delta, _ in self.ways():
            there, copy = self.passing(way, delta, step, False)
            pl.when(there)(copy.wait_recv)

    def settle(self):
        for tick in range(self.places - 1):
            self.each_partial(tick, lambda copy: copy.wait_send())
            for way, delta, _ in self.ways():
                there, copy = self.passing(way, delta, tick, True)
                pl.when(there)(copy.wait_send)


def finish_kernel(
    early_shapes,
    act_ref, cond_ref, adapted_ref, sig_ref, full_ref, dq_ref, dkv_ref, dgate_ref, dmid_ref, dcond_ref,
    extra_ref, vector_ref, dpb_ref, late_ref, pair_ref, scale_w, shift_w, key_w, value_w, query_w, gate_w,
    *refs
):
    (ig_ref, cg_ref, pg_ref, small_out, early_all, late_all, *refs) = refs
    grads, refs = refs[: len(early_shapes)], refs[len(early_shapes) :]
    zones, refs = refs[: 3 * len(early_shapes)], refs[3 * len(early_shapes) :]
    (
        early_ref, early_got, late_got, small_ref, small_got, sum_ref, sum_got,
        pair_buf, lead_ref, lead_turned, spread_ref, block_ref, tail_block, weight_acc,
        pair_sem, block_sem, grad_send, grad_recv, late_send, late_recv, early_send, early_recv,
        small_send, small_recv, sum_send, sum_recv,
    ) = refs
    total, width = act_ref.shape
    count = grads[0].shape[0]
    spans = late_ref.shape[0]
    structs, block, rows, _ = pair_buf.shape
    samples = total // rows
    heads = width // HEAD_DIM
    tail = block - MAIN
    pieces = rows // block
    pairs = heads // 2
    me = lax.axis_index("samp")
    my_span = lax.axis_index("head")
    orders = reduce_orders(count)
    peers = flips(me, sorted(orders[0]))
    others = [lax.rem(my_span + away, spans) for away in range(1, spans)]

    loads = [
        pltpu.make_async_copy(pair_ref.at[struct], pair_buf.at[struct], pair_sem.at[struct])
        for struct in range(structs)
    ]
    for load in loads:
        load.start()
    greet([dict(samp=peer) for peer in peers[1:]] + [dict(head=other) for other in others])

    late_sum = ChainSum(my_span, spans, late_ref, late_got, late_all, late_send, late_recv)
    early_sum = ChainSum(my_span, spans, early_ref, early_got, early_all, early_send, early_recv)
    late_sum.start(0)

    adapted = adapted_ref[...]
    back = one_hot((rows, rows), lambda row: row)
    place = lax.broadcasted_iota(jnp.int32, (rows, rows), 1)
    row = lax.broadcasted_iota(jnp.int32, (rows, rows), 0)
    back = jnp.where(row == key_row_of(place, block, pieces), 1.0, 0.0).astype(BF16)
    d_query = jnp.concatenate([dq_ref[at].astype(F32) for at in range(samples)], axis=0).astype(BF16)
    d_key, d_value = [
        jnp.concatenate([dot_nn(back, dkv_ref[which, at]) for at in range(samples)], axis=0).astype(BF16)
        for which in range(2)
    ]
    d_gate = dgate_ref[...]

    def store_grad(at, left, right):
        size = grads[at].shape[1]
        value = dot_tn(left, right).astype(BF16)
        for owner in range(count):
            grads[at][owner] = value[owner * size : (owner + 1) * size]

    movers = [
        Halving(
            me, orders[at % 2], grads[at], zones[3 * at : 3 * at + 3], grad_send.at[at], grad_recv.at[at]
        )
        for at in range(len(grads))
    ]
    for at, upstream in ((2, d_key), (3, d_value), (4, d_query), (5, d_gate)):
        store_grad(at, adapted, upstream)
        movers[at].start(0)
    late_sum.receive(0)
    late_sum.start(1)
    for mover in movers[2:]:
        mover.finish(0)
        mover.start(1)

    d_adapted = dot_nt(d_query, query_w[...].reshape(-1, width))
    d_adapted += dot_nt(d_key, key_w[...].reshape(-1, width))
    d_adapted += dot_nt(d_value, value_w[...].reshape(-1, width))
    d_adapted += dot_nt(d_gate, gate_w[...].reshape(-1, width))
    gain_one = full_ref[0:1, : cond_ref.shape[1]]
    act_normed, act_inverse = norm_rows(act_ref[...].astype(F32))
    cond_normed, cond_inverse = norm_rows(cond_ref[...].astype(F32))
    cond_first = (cond_normed * gain_one).astype(BF16)
    sig_first = sig_ref[...]
    d_shift = d_adapted.astype(BF16)
    d_pre = (d_adapted * act_normed * sigmoid_slope(sig_first)).astype(BF16)
    store_grad(0, cond_first, d_pre)
    store_grad(1, cond_first, d_shift)
    movers[0].start(0)
    movers[1].start(0)
    for mover in movers[:2]:
        mover.finish(0)
        mover.start(1)
    late_sum.receive(1)
    late_sum.start(2)
    ig_ref[...] = dmid_ref[...] + norm_back(act_normed, act_inverse, d_adapted * sig_first)
    d_cond = dot_nt(d_shift, shift_w[...].reshape(-1, width)) + dot_nt(d_pre, scale_w[...].reshape(-1, width))
    cg_ref[...] = norm_back(cond_normed, cond_inverse, d_cond * gain_one + dcond_ref[...]) + extra_ref[...]
    small_ref[...] = vector_ref[...]
    small_ref[0:1, : cond_ref.shape[1]] = jnp.sum(d_cond * cond_normed, axis=0, keepdims=True)
    small_ref[1:2] = jnp.sum(d_pre.astype(F32), axis=0, keepdims=True)
    small_ref[2:3] = jnp.sum(d_query.astype(F32), axis=0, keepdims=True)

    project = full_ref[8:, :LANES]
    project = (project - jnp.mean(project, axis=1, keepdims=True)).astype(BF16)
    columns = columns_of(project)
    for at, part in enumerate(spread_heads(columns, GROUP)):
        spread_ref[at * LANES : (at + 1) * LANES] = part
    switch = pair_switch(heads)
    means = mean_pair()
    groups = MAIN // GROUP
    for struct in range(structs):
        whole = jnp.concatenate([dpb_ref[struct * pairs + at] for at in range(pairs)], axis=1)
        mixed = dot_nt(whole, switch).astype(BF16)
        for at in range(groups):
            lead_ref[struct * groups + at] = mixed[:, at * GROUP * heads : (at + 1) * GROUP * heads]
    turn_eye = one_hot((rows, rows), lambda line: line)
    weight_acc[...] = jnp.zeros_like(weight_acc)
    for load in loads:
        load.wait()

    def back_keys(struct, first, keys, lead, target):
        for at in range(keys // 2):
            key = first + 2 * at
            low = jnp.concatenate((pair_buf[struct, key], pair_buf[struct, key + 1]), axis=1)
            normed, inverse = norm_pair(low, means)
            upstream = dot_nt(lead, spread_ref[2 * at * LANES : (2 * at + 2) * LANES, : lead.shape[1]])
            cross = dot_nn((upstream * normed).astype(BF16), means)
            result = inverse * (upstream - normed * cross)
            target(2 * at, result[:, :LANES])
            target(2 * at + 1, result[:, LANES:])
            kept = normed.astype(BF16)
            for side in range(2):
                turned = lead_turned[(2 * at + side) * heads : (2 * at + side + 1) * heads]
                weight_acc[...] += dot_nn(turned, kept[:, side * LANES : (side + 1) * LANES])

    def block_copy(turn):
        slot = lax.rem(turn, 2)
        return pltpu.make_async_copy(
            block_ref.at[slot],
            pg_ref.at[lax.div(turn, groups), pl.ds(lax.rem(turn, groups) * GROUP, GROUP)],
            block_sem.at[slot],
        )

    def pair_group(turn, carry):
        @pl.when(turn >= 2)
        def _():
            block_copy(turn - 2).wait()

        slot = lax.rem(turn, 2)
        lead = lead_ref[turn]
        lead_turned[...] = dot_tn(lead, turn_eye).astype(BF16)

        def target(at, value):
            block_ref[slot, at] = value.astype(BF16)

        back_keys(lax.div(turn, groups), lax.rem(turn, groups) * GROUP, GROUP, lead, target)
        block_copy(turn).start()
        return carry

    turns = structs * groups
    late_sum.receive(2)
    late_sum.total()
    late_sum.spread_start(0)

    def stage(number):
        for mover in movers[2:] + movers[:2]:
            mover.finish(number)
            if number < 2:
                mover.start(number + 1)

    def lead_sum():
        stage(2)
        _, moves = spans_of(early_shapes, width, spans)
        for piece, line, at, start, lane, size in moves:
            early_ref[piece, line : line + size] = movers[at].zones[2][
                0, start : start + size, lane : lane + width
            ]
        early_sum.start(0)

    def early_turn(tick):
        early_sum.receive(tick)
        early_sum.start(tick + 1)

    def late_turn(step):
        late_sum.spread_wait(step)
        late_sum.spread_start(step + 1)

    events = {
        1: lambda: stage(1),
        2: lambda: late_turn(0),
        5: lead_sum,
        6: lambda: late_turn(1),
        8: lambda: early_turn(0),
        10: lambda: early_turn(1),
    }

    def pair_turn(turn, carry):
        pair_group(turn, carry)
        for at, event in events.items():
            pl.when(turn == at)(event)
        return carry

    lax.fori_loop(0, turns, pair_turn, 0)
    late_sum.spread_wait(2)
    early_sum.receive(2)
    early_sum.total()
    early_sum.spread_start(0)
    for struct in range(structs):
        lead = dpb_ref[structs * pairs + struct]
        lead = lead[:, : tail * heads]
        lead_turned[: tail * heads] = dot_tn(lead, turn_eye).astype(BF16)

        def tail_target(at, value, struct=struct):
            tail_block[struct, at] = value.astype(BF16)

        back_keys(struct, MAIN, tail, lead, tail_target)
    tail_copies = [
        pltpu.make_async_copy(
            tail_block.at[struct], pg_ref.at[struct, pl.ds(MAIN, tail)], pair_sem.at[struct]
        )
        for struct in range(structs)
    ]
    for copy in tail_copies:
        copy.start()
    small_ref[8:, :LANES] = weight_acc[...]
    early_sum.spread_wait(0)
    early_sum.spread_start(1)

    def small_copies(sending):
        return [
            send(
                small_ref, small_got.at[me if sending else peers[at]], small_send.at[at], small_recv.at[at],
                dict(samp=peers[at]),
            )
            for at in range(1, count)
        ]

    def sum_copies(sending):
        return [
            send(
                sum_ref, sum_got.at[my_span if sending else lax.rem(my_span + spans - 1 - at, spans)],
                sum_send.at[at], sum_recv.at[at], dict(head=other),
            )
            for at, other in enumerate(others)
        ]

    for copy in small_copies(True):
        copy.start()
    small_got[me] = small_ref[...]
    for copy in small_copies(False):
        copy.wait_recv()
    summed = small_got[0]
    for at in range(1, count):
        summed = summed + small_got[at]
    sum_ref[...] = summed
    for copy in sum_copies(True):
        copy.start()
    sum_got[my_span] = summed
    early_sum.spread_wait(1)
    early_sum.spread_start(2)
    for copy in sum_copies(False):
        copy.wait_recv()
    summed = sum_got[0]
    for at in range(1, spans):
        summed = summed + sum_got[at]
    small_out[...] = summed
    early_sum.spread_wait(2)

    block_copy(turns - 2).wait()
    block_copy(turns - 1).wait()
    for copy in tail_copies:
        copy.wait()
    for mover in movers:
        mover.settle()
    late_sum.settle()
    early_sum.settle()
    for copy in small_copies(True) + sum_copies(True):
        copy.wait_send()


def finish(
    act, cond, adapted, sig, full, d_query, d_key_value, d_gate, d_middle, d_cond, extra, vectors, packed,
    late, pair, weights,
):
    total, width = act.shape
    cond_width = cond.shape[1]
    spans, late_each, _ = late.shape
    count = weights[0].shape[0]
    structs, block, rows, _ = pair.shape
    heads = width // HEAD_DIM
    tail = block - MAIN
    early_shapes = [weight.shape[1:] for weight in weights]
    early_each, _ = spans_of(early_shapes, width, spans)
    steps = count.bit_length() - 1
    vmem = pl.BlockSpec(memory_space=pltpu.VMEM)
    far = pl.BlockSpec(memory_space=pl.ANY)
    dma = pltpu.SemaphoreType.DMA
    turns = structs * (MAIN // GROUP)
    return pl.pallas_call(
        functools.partial(finish_kernel, early_shapes),
        out_shape=(
            jax.ShapeDtypeStruct((total, width), F32),
            jax.ShapeDtypeStruct((total, cond_width), F32),
            jax.ShapeDtypeStruct(pair.shape, BF16),
            jax.ShapeDtypeStruct(full.shape, F32),
            jax.ShapeDtypeStruct((spans, early_each, width), BF16),
            jax.ShapeDtypeStruct((spans, late_each, width), BF16),
        ),
        in_specs=[vmem] * 14 + [far] + [vmem] * 6,
        out_specs=[vmem, vmem, far, vmem, vmem, vmem],
        scratch_shapes=[pltpu.VMEM(weight.shape, BF16) for weight in weights]
        + zone_shapes(early_shapes, count)
        + [
            pltpu.VMEM((spans, early_each, width), BF16),
            pltpu.VMEM((2, spans - 1, early_each, width), BF16),
            pltpu.VMEM((2, spans - 1, late_each, width), BF16),
            pltpu.VMEM(full.shape, F32),
            pltpu.VMEM((count,) + full.shape, F32),
            pltpu.VMEM(full.shape, F32),
            pltpu.VMEM((spans,) + full.shape, F32),
            pltpu.VMEM(pair.shape, BF16),
            pltpu.VMEM((turns, rows, GROUP * heads), BF16),
            pltpu.VMEM((GROUP * heads, rows), BF16),
            pltpu.VMEM((GROUP * LANES, GROUP * heads), BF16),
            pltpu.VMEM((2, GROUP, rows, LANES), BF16),
            pltpu.VMEM((structs, tail, rows, LANES), BF16),
            pltpu.VMEM((heads, LANES), F32),
            dma((structs,)),
            dma((2,)),
            dma((len(weights), steps, count // 2)),
            dma((len(weights), steps, count // 2)),
            dma((2, 2, spans - 1)),
            dma((2, 2, spans - 1)),
            dma((2, 2, spans - 1)),
            dma((2, 2, spans - 1)),
            dma((count,)),
            dma((count,)),
            dma((spans,)),
            dma((spans,)),
        ],
        compiler_params=pltpu.CompilerParams(
            vmem_limit_bytes=60 << 20, collective_id=3, has_side_effects=True
        ),
        name="finish",
    )(
        act, cond, adapted, sig, full, d_query, d_key_value, d_gate, d_middle, d_cond, extra, vectors, packed,
        late, pair, *weights
    )


def deliver_kernel(shapes, ig_in, cg_in, early_in, late_in, pair_in, ig_out, cg_out, pair_ref, *refs):
    number = len(shapes[0]) + len(shapes[1])
    outs, held = refs[:number], refs[number : 2 * number]
    sems = refs[2 * number]
    moves = [pltpu.make_async_copy(ig_in, ig_out, sems.at[0]), pltpu.make_async_copy(cg_in, cg_out, sems.at[1])]
    moves += [
        pltpu.make_async_copy(part, out, sems.at[2 + at]) for at, (part, out) in enumerate(zip(held, outs))
    ]
    pair_ref[...] = pair_in[...].astype(F32)

    @pl.when(pl.program_id(0) == 0)
    def _():
        spans, _, width = early_in.shape
        first = 0
        for part, source in zip(shapes, (early_in, late_in)):
            _, places = spans_of(part, width, spans)
            for piece, line, at, start, lane, size in places:
                held[first + at][start : start + size, lane : lane + width] = source[
                    piece, line : line + size
                ].astype(F32)
            first += len(part)
        for move in moves:
            move.start()

    @pl.when(pl.program_id(0) == pl.num_programs(0) - 1)
    def _():
        for move in moves:
            move.wait()


def deliver(input_grad, cond_grad, early, late, pair_grad, shapes):
    structs, block, rows, channels = pair_grad.shape
    turn = block // 4

    def whole(shape):
        return pl.BlockSpec(tuple(shape), lambda at: (0,) * len(shape), pipeline_mode=pl.Buffered(1))

    far = pl.BlockSpec(memory_space=pl.ANY)
    tile = pl.BlockSpec((1, turn, rows, channels), lambda at: (at // 4, at % 4, 0, 0))
    flat = list(shapes[0]) + list(shapes[1])
    return pl.pallas_call(
        functools.partial(deliver_kernel, shapes),
        out_shape=(
            jax.ShapeDtypeStruct(input_grad.shape, F32),
            jax.ShapeDtypeStruct(cond_grad.shape, F32),
            jax.ShapeDtypeStruct(pair_grad.shape, F32),
        )
        + tuple(jax.ShapeDtypeStruct(shape, F32) for shape in flat),
        grid=(structs * 4,),
        in_specs=[whole(part.shape) for part in (input_grad, cond_grad, early, late)] + [tile],
        out_specs=[far, far, tile] + [far] * len(flat),
        scratch_shapes=[pltpu.VMEM(shape, F32) for shape in flat] + [pltpu.SemaphoreType.DMA((2 + len(flat),))],
        compiler_params=pltpu.CompilerParams(vmem_limit_bytes=62 << 20),
        name="deliver",
    )(input_grad, cond_grad, early, late, pair_grad)


def plain_kernel(struct_ref, len_ref, q_ref, k_ref, v_ref, bias_ref, out_ref, prob_ref, acc_ref):
    sample = pl.program_id(0)
    group_at = pl.program_id(1)
    length = len_ref[struct_ref[sample]]
    keys = k_ref.shape[1]
    group, windows = head_windows(q_ref.shape[2])
    valid = lax.broadcasted_iota(jnp.int32, (1, keys), 1) < length
    acc_ref[...] = jnp.zeros_like(acc_ref)
    for at, (start, width, offset) in enumerate(windows):
        lanes = slice(start, start + width)
        mask = head_mask(width, offset)
        query = q_ref[0, :, lanes]
        query = jnp.where(mask, query, jnp.zeros_like(query))
        scores = dot_nt(query, k_ref[0, :, lanes]) * HEAD_DIM ** (-0.5) + bias_ref[
            0, at
        ].astype(F32)
        scores = jnp.where(valid, scores, NEG_BIG)
        weights = jnp.exp(scores - jnp.max(scores, axis=1, keepdims=True))
        weights = weights * (1.0 / jnp.sum(weights, axis=1, keepdims=True))
        weights = weights.astype(BF16)
        prob_ref[0, at] = weights
        mixed = dot_nn(weights, v_ref[0, :, lanes])
        acc_ref[:, lanes] += jnp.where(mask, mixed, 0.0)
    out_ref[0] = acc_ref[...].astype(BF16)


def plain(struct_of, struct_len, query, key, value, bias):
    samples, rows, width = query.shape
    keys = key.shape[1]
    heads = bias.shape[1]
    group, windows = head_windows(width)
    each = len(windows)
    return pl.pallas_call(
        plain_kernel,
        out_shape=(
            jax.ShapeDtypeStruct((samples, rows, width), BF16),
            jax.ShapeDtypeStruct((samples, heads, rows, keys), BF16),
        ),
        grid_spec=pltpu.PrefetchScalarGridSpec(
            num_scalar_prefetch=2,
            grid=(samples, heads // each),
            in_specs=[
                pl.BlockSpec((1, rows, group), lambda b, g, s, n: (b, 0, g)),
                pl.BlockSpec((1, keys, group), lambda b, g, s, n: (b, 0, g)),
                pl.BlockSpec((1, keys, group), lambda b, g, s, n: (b, 0, g)),
                pl.BlockSpec((1, each, rows, keys), lambda b, g, s, n: (s[b], g, 0, 0)),
            ],
            out_specs=[
                pl.BlockSpec((1, rows, group), lambda b, g, s, n: (b, 0, g)),
                pl.BlockSpec((1, each, rows, keys), lambda b, g, s, n: (b, g, 0, 0)),
            ],
            scratch_shapes=[pltpu.VMEM((rows, group), F32)],
        ),
        compiler_params=pltpu.CompilerParams(vmem_limit_bytes=48 << 20),
        name="plain",
    )(struct_of, struct_len, query, key, value, bias)


def plain_back_kernel(
    struct_ref, q_ref, k_ref, v_ref, do_ref, prob_ref, dq_ref, dk_ref, dv_ref, bias_ref,
    dq_acc, dk_acc, dv_acc, bias_acc,
):
    samples = q_ref.shape[0]
    structs = bias_ref.shape[0]
    group, windows = head_windows(q_ref.shape[2])
    scale = HEAD_DIM ** (-0.5)
    for sample in range(samples):
        struct = struct_ref[sample]
        dq_acc[...] = jnp.zeros_like(dq_acc)
        dk_acc[...] = jnp.zeros_like(dk_acc)
        dv_acc[...] = jnp.zeros_like(dv_acc)
        for at, (start, width, offset) in enumerate(windows):
            lanes = slice(start, start + width)
            mask = head_mask(width, offset)
            upstream = do_ref[sample, :, lanes]
            upstream = jnp.where(mask, upstream, jnp.zeros_like(upstream))
            query = q_ref[sample, :, lanes]
            query = jnp.where(mask, query, jnp.zeros_like(query))
            low = prob_ref[sample, at]
            weights = low.astype(F32)
            d_weights = dot_nt(upstream, v_ref[sample, :, lanes])
            dv_acc[:, lanes] += dot_tn(low, upstream)
            cross = weights * d_weights
            delta = jnp.sum(cross, axis=1, keepdims=True)
            d_scores = (cross - weights * delta).astype(BF16)
            dq_acc[:, lanes] += jnp.where(mask, dot_nn(d_scores, k_ref[sample, :, lanes]), 0.0)
            dk_acc[:, lanes] += dot_tn(d_scores, query)
            for slab in range(structs):
                part = jnp.where(struct == slab, 1.0, 0.0) * d_scores.astype(F32)
                if sample == 0:
                    bias_acc[slab, at] = part
                elif sample < samples - 1:
                    bias_acc[slab, at] += part
                else:
                    bias_ref[slab, at] = (bias_acc[slab, at] + part).astype(BF16)
        dq_ref[sample] = (dq_acc[...] * scale).astype(BF16)
        dk_ref[sample] = (dk_acc[...] * scale).astype(BF16)
        dv_ref[sample] = dv_acc[...].astype(BF16)


def plain_back(struct_of, structs, query, key, value, upstream, prob):
    samples, rows, width = query.shape
    keys = key.shape[1]
    heads = prob.shape[1]
    group, windows = head_windows(width)
    each = len(windows)
    return pl.pallas_call(
        plain_back_kernel,
        out_shape=(
            jax.ShapeDtypeStruct((samples, rows, width), BF16),
            jax.ShapeDtypeStruct((samples, keys, width), BF16),
            jax.ShapeDtypeStruct((samples, keys, width), BF16),
            jax.ShapeDtypeStruct((structs, heads, rows, keys), BF16),
        ),
        grid_spec=pltpu.PrefetchScalarGridSpec(
            num_scalar_prefetch=1,
            grid=(heads // each,),
            in_specs=[
                pl.BlockSpec((samples, rows, group), lambda g, s: (0, 0, g)),
                pl.BlockSpec((samples, keys, group), lambda g, s: (0, 0, g)),
                pl.BlockSpec((samples, keys, group), lambda g, s: (0, 0, g)),
                pl.BlockSpec((samples, rows, group), lambda g, s: (0, 0, g)),
                pl.BlockSpec((samples, each, rows, keys), lambda g, s: (0, g, 0, 0)),
            ],
            out_specs=[
                pl.BlockSpec((samples, rows, group), lambda g, s: (0, 0, g)),
                pl.BlockSpec((samples, keys, group), lambda g, s: (0, 0, g)),
                pl.BlockSpec((samples, keys, group), lambda g, s: (0, 0, g)),
                pl.BlockSpec((structs, each, rows, keys), lambda g, s: (0, g, 0, 0)),
            ],
            scratch_shapes=[
                pltpu.VMEM((rows, group), F32),
                pltpu.VMEM((keys, group), F32),
                pltpu.VMEM((keys, group), F32),
                pltpu.VMEM((structs, each, rows, keys), F32),
            ],
        ),
        compiler_params=pltpu.CompilerParams(vmem_limit_bytes=60 << 20),
        name="plain_back",
    )(struct_of, query, key, value, upstream, prob)


def pack_rows(pieces, columns):
    return jnp.concatenate([piece.reshape(-1, columns) for piece in pieces], axis=0)


def pack_small(pieces, columns):
    flat = jnp.concatenate([piece.reshape(-1) for piece in pieces])
    rows = -(-flat.shape[0] // columns)
    rows = -(-rows // 8) * 8
    return jnp.pad(flat, (0, rows * columns - flat.shape[0])).reshape(rows, columns)


def unpack_rows(gathered, shapes):
    whole, at = [], 0
    count, _, columns = gathered.shape
    for rows, cols in shapes:
        held = rows * cols // columns
        whole.append(gathered[:, at : at + held].reshape(count * rows, cols))
        at += held
    return whole


def unpack_small(gathered, shapes):
    whole, at = [], 0
    count = gathered.shape[0]
    flat = gathered.reshape(count, -1)
    for shape in shapes:
        size = 1
        for extent in shape:
            size *= extent
        whole.append(flat[:, at : at + size].reshape((count * shape[0],) + shape[1:]))
        at += size
    return whole


def plain_device(
    act, cond, pair, struct_of, struct_len,
    gain_first, scale_first, scale_bias_first, shift_first,
    query_weight, query_bias, key_weight, value_weight, gate_weight, output_weight,
    pair_weight, zero_first, zero_bias_first,
    gain_second, scale_second, scale_bias_second, shift_second,
    swish_weight, linear_weight, down_weight, zero_second, zero_bias_second,
    cotangent,
):
    samples, rows, width = act.shape
    cond_width = cond.shape[2]
    total = samples * rows
    structs = pair.shape[0]
    small = (
        gain_first, scale_bias_first, query_bias, zero_bias_first, gain_second,
        scale_bias_second, zero_bias_second, pair_weight,
    )
    early = (scale_first, shift_first, query_weight, key_weight, value_weight, gate_weight)
    late = (
        output_weight, zero_first, scale_second, shift_second, swish_weight, linear_weight,
        down_weight, zero_second,
    )
    small_all = lax.all_gather(pack_small(small, width), "samp", axis=0)
    early_all = lax.all_gather(pack_rows(early, width), "samp", axis=0)
    late_all = lax.all_gather(pack_rows(late, width), "samp", axis=0)
    (gain_one, bias_one, bias_query, bias_zero_one, gain_two, bias_two, bias_zero_two, pair_proj_w) = (
        unpack_small(small_all, [piece.shape for piece in small])
    )
    (w_scale, w_shift, w_query, w_key, w_value, w_gate) = unpack_rows(
        early_all, [piece.shape for piece in early]
    )
    (w_out, w_zero, w_scale_two, w_shift_two, w_swish, w_linear, w_down, w_zero_two) = unpack_rows(
        late_all, [piece.shape for piece in late]
    )

    pair_normed, pair_inverse = norm_rows(pair.astype(F32))
    pair_low = pair_normed.astype(BF16)
    pair_proj = jnp.einsum("sijc,ch->shij", pair_low, pair_proj_w, preferred_element_type=F32)
    bias_all = lax.all_gather(pair_proj.astype(BF16), "samp", axis=3, tiled=True)

    act_rows = act.reshape(total, width).astype(F32)
    cond_low = cond.reshape(total, cond_width)
    act_normed, act_inverse = norm_rows(act_rows)
    cond_normed, cond_inverse = norm_rows(cond_low.astype(F32))
    cond_first = (cond_normed * gain_one.astype(F32)).astype(BF16)
    sig_first = jax.nn.sigmoid(product(cond_first, w_scale) + bias_one.astype(F32))
    adapted = (sig_first * act_normed + product(cond_first, w_shift)).astype(BF16)
    key_rows = product(adapted, w_key).astype(BF16)
    value_rows = product(adapted, w_value).astype(BF16)
    query_rows = (product(adapted, w_query) + bias_query.astype(F32)).astype(BF16)
    gate_sig = jax.nn.sigmoid(product(adapted, w_gate))
    key_value = jnp.stack((key_rows, value_rows)).reshape(2, samples, rows, width)
    key_value = lax.all_gather(key_value, "head", axis=2, tiled=True)
    query_split = query_rows.reshape(samples, rows, width)
    attended, prob = plain(
        struct_of, struct_len, query_split, key_value[0], key_value[1], bias_all
    )
    attn_float = attended.reshape(total, width).astype(F32)

    gated_rows = (gate_sig * attn_float).astype(BF16)
    branch = product(gated_rows, w_out)
    zero_sig_first = jax.nn.sigmoid(product(cond_low, w_zero) + bias_zero_one.astype(F32))
    middle = act_rows + zero_sig_first * branch
    mid_normed, mid_inverse = norm_rows(middle)
    cond_second = (cond_normed * gain_two.astype(F32)).astype(BF16)
    sig_second = jax.nn.sigmoid(product(cond_second, w_scale_two) + bias_two.astype(F32))
    adapted_two = (sig_second * mid_normed + product(cond_second, w_shift_two)).astype(BF16)
    swish_pre = product(adapted_two, w_swish)
    linear_pre = product(adapted_two, w_linear)
    swish_sig = jax.nn.sigmoid(swish_pre)
    hidden = (swish_pre * swish_sig * linear_pre).astype(BF16)
    down_rows = product(hidden, w_down)
    zero_sig_second = jax.nn.sigmoid(product(cond_low, w_zero_two) + bias_zero_two.astype(F32))
    layer_out = (middle + zero_sig_second * down_rows).astype(BF16)

    upstream = cotangent.reshape(total, width).astype(F32)
    d_down = (upstream * zero_sig_second).astype(BF16)
    d_zero_second = (upstream * down_rows * sigmoid_slope(zero_sig_second)).astype(BF16)
    d_hidden = back_product(d_down, w_down)
    d_swish = (
        d_hidden * linear_pre * swish_sig * (1.0 + swish_pre * (1.0 - swish_sig))
    ).astype(BF16)
    d_linear = (d_hidden * swish_pre * swish_sig).astype(BF16)
    d_adapted_two = back_product(d_swish, w_swish) + back_product(d_linear, w_linear)
    d_shift_second = d_adapted_two.astype(BF16)
    d_pre_second = (d_adapted_two * mid_normed * sigmoid_slope(sig_second)).astype(BF16)
    d_cond_second = back_product(d_shift_second, w_shift_two) + back_product(
        d_pre_second, w_scale_two
    )
    d_middle = upstream + norm_back(mid_normed, mid_inverse, d_adapted_two * sig_second)
    d_branch = (d_middle * zero_sig_first).astype(BF16)
    d_zero_first = (d_middle * branch * sigmoid_slope(zero_sig_first)).astype(BF16)
    d_gated = back_product(d_branch, w_out)
    d_gate = (d_gated * attn_float * sigmoid_slope(gate_sig)).astype(BF16)
    d_attended = (d_gated * gate_sig).astype(BF16)

    late_grads = (
        outer_sum(gated_rows, d_branch),
        outer_sum(cond_low, d_zero_first),
        outer_sum(cond_second, d_pre_second),
        outer_sum(cond_second, d_shift_second),
        outer_sum(adapted_two, d_swish),
        outer_sum(adapted_two, d_linear),
        outer_sum(hidden, d_down),
        outer_sum(cond_low, d_zero_second),
    )

    d_query, d_key, d_value, bias_grad = plain_back(
        struct_of, structs, query_split, key_value[0], key_value[1],
        d_attended.reshape(samples, rows, width), prob,
    )
    d_key_value = lax.psum_scatter(
        jnp.stack((d_key, d_value)), "head", scatter_dimension=2, tiled=True
    )
    d_query = d_query.reshape(total, width)
    d_key = d_key_value[0].reshape(total, width)
    d_value = d_key_value[1].reshape(total, width)
    bias_summed = lax.psum_scatter(bias_grad, "samp", scatter_dimension=3, tiled=True)
    pair_weight_grad = jnp.einsum("sijc,shij->ch", pair_low, bias_summed, preferred_element_type=F32)
    pair_upstream = jnp.einsum(
        "shij,ch->sijc", bias_summed, pair_proj_w, preferred_element_type=F32
    )
    pair_grad = norm_back(pair_normed, pair_inverse, pair_upstream)
    d_adapted = (
        back_product(d_query, w_query)
        + back_product(d_key, w_key)
        + back_product(d_value, w_value)
        + back_product(d_gate, w_gate)
    )
    d_shift_first = d_adapted.astype(BF16)
    d_pre_first = (d_adapted * act_normed * sigmoid_slope(sig_first)).astype(BF16)
    d_cond_first = back_product(d_shift_first, w_shift) + back_product(d_pre_first, w_scale)
    input_grad = d_middle + norm_back(act_normed, act_inverse, d_adapted * sig_first)
    d_cond_normed = d_cond_first * gain_one.astype(F32) + d_cond_second * gain_two.astype(F32)
    cond_grad = (
        norm_back(cond_normed, cond_inverse, d_cond_normed)
        + back_product(d_zero_first, w_zero)
        + back_product(d_zero_second, w_zero_two)
    )
    early_grads = (
        outer_sum(cond_first, d_pre_first),
        outer_sum(cond_first, d_shift_first),
        outer_sum(adapted, d_query),
        outer_sum(adapted, d_key),
        outer_sum(adapted, d_value),
        outer_sum(adapted, d_gate),
    )
    small_grads = (
        jnp.sum(d_cond_first * cond_normed, axis=0),
        column_sum(d_pre_first),
        column_sum(d_query),
        column_sum(d_zero_first),
        jnp.sum(d_cond_second * cond_normed, axis=0),
        column_sum(d_pre_second),
        column_sum(d_zero_second),
        pair_weight_grad,
    )
    count = lax.axis_size("samp")

    def pack_grads(grads, shapes):
        pieces = [
            grad.astype(BF16).reshape(count, shape[0] * shape[1] // width, width)
            for grad, shape in zip(grads, shapes)
        ]
        return jnp.concatenate(pieces, axis=1)

    def reduce(packed):
        summed = lax.psum_scatter(packed, "samp", scatter_dimension=0, tiled=True)
        return lax.psum(summed[0], "head").astype(F32)

    late_sum = reduce(pack_grads(late_grads, [piece.shape for piece in late]))
    early_sum = reduce(pack_grads(early_grads, [piece.shape for piece in early]))
    small_flat = jnp.concatenate(
        [grad.astype(BF16).reshape(count, -1) for grad in small_grads], axis=1
    )
    small_sum = lax.psum(
        lax.psum_scatter(small_flat, "samp", scatter_dimension=0, tiled=True), "head"
    ).astype(F32)
    (g_out, g_zero, g_scale_two, g_shift_two, g_swish, g_linear, g_down, g_zero_two) = unpack_rows(
        late_sum[None], [piece.shape for piece in late]
    )
    (g_scale, g_shift, g_query, g_key, g_value, g_gate) = unpack_rows(
        early_sum[None], [piece.shape for piece in early]
    )
    (g_gain, g_bias, g_bias_query, g_bias_zero, g_gain_two, g_bias_two, g_bias_zero_two, g_pair) = (
        unpack_small(small_sum, [piece.shape for piece in small])
    )
    return (
        layer_out.reshape(act.shape), input_grad.reshape(act.shape), cond_grad.reshape(cond.shape),
        pair_grad, g_gain, g_scale, g_bias, g_shift, g_query, g_bias_query, g_key, g_value, g_gate,
        g_out, g_pair, g_zero, g_bias_zero, g_gain_two, g_scale_two, g_bias_two, g_shift_two,
        g_swish, g_linear, g_down, g_zero_two, g_bias_zero_two,
    )


def per_device(
    act, cond, pair, struct_of, struct_len,
    gain_first, scale_first, scale_bias_first, shift_first,
    query_weight, query_bias, key_weight, value_weight, gate_weight, output_weight,
    pair_weight, zero_first, zero_bias_first,
    gain_second, scale_second, scale_bias_second, shift_second,
    swish_weight, linear_weight, down_weight, zero_second, zero_bias_second,
    cotangent,
):
    samples, rows, width = act.shape
    cond_width = cond.shape[2]
    total = samples * rows
    count = lax.axis_size("samp")
    spans = lax.axis_size("head")
    heads = width // HEAD_DIM
    small = (
        gain_first, scale_bias_first, query_bias, zero_bias_first, gain_second,
        scale_bias_second, zero_bias_second,
    )
    early = (scale_first, shift_first, key_weight, value_weight, query_weight, gate_weight)
    late = (
        swish_weight, linear_weight, down_weight, output_weight, zero_first, scale_second, zero_second,
        shift_second,
    )
    mine_at = lax.axis_index("samp")
    mine = lax.broadcasted_iota(jnp.int32, (count, 1), 0) == mine_at

    def spread(piece, columns):
        held = jnp.where(mine, piece[None], jnp.zeros_like(piece[None])).reshape(1, -1)
        return jnp.pad(held, ((0, 0), (0, columns - held.shape[1])))

    turned = pair_weight.T
    held = jnp.where(mine.reshape(1, count, 1), turned[:, None], jnp.zeros_like(turned[:, None]))
    held = jnp.pad(held.reshape(heads, -1), ((0, 0), (0, width - LANES)))
    packed_small = jnp.concatenate(
        [spread(piece, width) for piece in small] + [jnp.zeros((1, width), BF16), held], axis=0
    )
    act_rows = act.reshape(total, width)
    cond_rows = cond.reshape(total, cond_width)
    pair_turned = pair.transpose(0, 2, 1, 3)
    (attended, prob, adapted, sig_first, gate_sig, query_split, key_value, full, *whole) = front(
        struct_of, struct_len, act_rows, cond_rows, packed_small, pair_turned, early + late, samples, count,
        spans,
    )
    (layer_out, d_gate, d_attended, d_middle, d_cond_two, extra, vectors, *late_parts) = middle_part(
        attended, gate_sig, act_rows, cond_rows, cotangent.reshape(total, width), full, whole[6:]
    )
    d_query, d_key_value, bias_packed, late_sum = attend_back(
        struct_of, pair.shape[0], query_split, key_value, d_attended, prob, late_parts, count
    )
    (input_grad, cond_grad, pair_grad, small_sum, early_sum, late_total) = finish(
        act_rows, cond_rows, adapted, sig_first, full, d_query, d_key_value, d_gate, d_middle, d_cond_two,
        extra, vectors, bias_packed, late_sum, pair_turned, whole[:6],
    )
    (input_grad, cond_grad, pair_grad, *weight_grads) = deliver(
        input_grad, cond_grad, early_sum, late_total, pair_grad,
        ([piece.shape for piece in early], [piece.shape for piece in late]),
    )
    (g_scale, g_shift, g_key, g_value, g_query, g_gate) = weight_grads[:6]
    (g_swish, g_linear, g_down, g_out, g_zero, g_scale_two, g_zero_two, g_shift_two) = weight_grads[6:]

    def own(row, size):
        return lax.dynamic_slice(small_sum, (row, mine_at * size), (1, size))[0]

    cond_share, share = cond_width // count, width // count
    channels = pair.shape[3] // count
    g_pair = lax.dynamic_slice(small_sum, (8, mine_at * channels), (heads, channels)).T
    return (
        layer_out.reshape(act.shape), input_grad.reshape(act.shape), cond_grad.reshape(cond.shape),
        pair_grad.transpose(0, 2, 1, 3), own(0, cond_share), g_scale, own(1, share), g_shift, g_query,
        own(2, share), g_key, g_value, g_gate, g_out, g_pair, g_zero, own(3, share), own(4, cond_share),
        g_scale_two, own(5, share), g_shift_two, g_swish, g_linear, g_down, g_zero_two, own(6, share),
    )


def fits(mesh, act, pair):
    samples, rows, width = act.shape
    count, spans = mesh.shape["samp"], mesh.shape["head"]
    block = pair.shape[2]
    tail = block - MAIN
    heads = width // HEAD_DIM
    return (
        count == 8
        and samples == 2
        and tail > 0
        and heads * tail == MAIN
        and rows % block == 0
        and rows * spans == block * count
        and rows % 8 == 0
        and block * count <= KEY_LANES
    )


def solution(mesh):
    tokens = P("samp", "head", None)
    pairs = P(None, "head", "samp", None)
    vector = P("samp")
    matrix = P("samp", None)
    weights = (
        vector, matrix, vector, matrix, matrix, vector, matrix, matrix, matrix, matrix, matrix,
        matrix, vector, vector, matrix, vector, matrix, matrix, matrix, matrix, matrix, vector,
    )
    def choose(*arrays):
        body = per_device if fits(mesh, arrays[0], arrays[2]) else plain_device
        return body(*arrays)

    return jax.shard_map(
        choose,
        mesh=mesh,
        in_specs=(tokens, tokens, pairs, vector, P()) + weights + (tokens,),
        out_specs=(tokens, tokens, tokens, pairs) + weights,
        check_vma=False,
    )
```

```python
import functools

import jax
import jax.numpy as jnp
from jax import lax
from jax.experimental import pallas as pl
from jax.experimental.pallas import tpu as pltpu
from jax.sharding import PartitionSpec as P

HEAD_DIM = 48
LANES = 128
MAIN = 64
KEY_LANES = 640
MESH = pl.DeviceIdType.MESH
EPSILON = 1e-05
NEG_BIG = -1000000000.0
F32 = jnp.float32
BF16 = jnp.bfloat16


def norm_rows(values):
    centered = values - jnp.mean(values, axis=-1, keepdims=True)
    variance = jnp.mean(centered * centered, axis=-1, keepdims=True)
    inverse = lax.rsqrt(variance + EPSILON)
    return (centered * inverse, inverse)


def norm_back(normed, inverse, upstream):
    mean_grad = jnp.mean(upstream, axis=-1, keepdims=True)
    mean_cross = jnp.mean(upstream * normed, axis=-1, keepdims=True)
    return inverse * (upstream - mean_grad - normed * mean_cross)


def product(left_side, right_side):
    return lax.dot_general(
        left_side, right_side, (((1,), (0,)), ((), ())), preferred_element_type=F32
    )


def back_product(upstream, right_side):
    return lax.dot_general(
        upstream, right_side, (((1,), (1,)), ((), ())), preferred_element_type=F32
    )


def outer_sum(left_side, upstream):
    return lax.dot_general(
        left_side, upstream, (((0,), (0,)), ((), ())), preferred_element_type=F32
    )


def column_sum(upstream):
    return jnp.sum(upstream.astype(F32), axis=0)


def sigmoid_slope(gate_sig):
    return gate_sig * (1.0 - gate_sig)


def head_windows(width):
    group = LANES * HEAD_DIM // 16
    group = min(group, width)
    windows = []
    for head in range(group // HEAD_DIM):
        first = head * HEAD_DIM
        last = first + HEAD_DIM - 1
        start = first // LANES * LANES
        stop = (last // LANES + 1) * LANES
        windows.append((start, stop - start, first - start))
    return (group, windows)


def head_mask(width, offset):
    lane = lax.broadcasted_iota(jnp.int32, (1, width), 1)
    return (lane >= offset) & (lane < offset + HEAD_DIM)


def dot_nt(left, right):
    return lax.dot_general(left, right, (((1,), (1,)), ((), ())), preferred_element_type=F32)


def dot_nn(left, right):
    return lax.dot_general(left, right, (((1,), (0,)), ((), ())), preferred_element_type=F32)


def dot_tn(left, right):
    return lax.dot_general(left, right, (((0,), (0,)), ((), ())), preferred_element_type=F32)


def tail_switch(count, heads, tail):
    lanes = count * heads * tail
    source = lax.broadcasted_iota(jnp.int32, (lanes, lanes), 0)
    target = lax.broadcasted_iota(jnp.int32, (lanes, lanes), 1)
    owner = source // (heads * tail)
    head = source % heads
    spot = head * (count * tail) + owner * tail + source // heads % tail
    return jnp.where(spot == target, 1.0, 0.0).astype(BF16)


def swap_halves(tile):
    return pltpu.roll(tile, MAIN, 1)


def low_half(tile):
    return lax.broadcasted_iota(jnp.int32, tile.shape, 1) < MAIN


def key_places(count, block):
    lane = lax.broadcasted_iota(jnp.int32, (1, KEY_LANES), 1)
    tail = block - MAIN
    spare = lane - count * MAIN
    main_at = lane + tail * (lane // MAIN)
    tail_at = block * (spare // tail) + MAIN + spare % tail
    past = jnp.where(spare < count * tail, tail_at, count * block)
    return jnp.where(spare < 0, main_at, past)


def flip(index, bit):
    return index + bit - 2 * bit * lax.rem(lax.div(index, bit), 2)


def flips(index, bits):
    spots = [index]
    for bit in bits:
        spots = spots + [flip(spot, bit) for spot in spots]
    return spots


def reduce_orders(count):
    bits = []
    bit = 2
    while bit < count:
        bits.append(bit)
        bit *= 2
    half = len(bits) // 2
    return ([1] + bits, [1] + bits[half:] + bits[:half])


def greet(partners):
    barrier = pltpu.get_barrier_semaphore()
    for partner in partners:
        pl.semaphore_signal(barrier, inc=1, device_id=partner, device_id_type=MESH)
    pl.semaphore_wait(barrier, len(partners))


def send(source, target, send_sem, recv_sem, device):
    return pltpu.make_async_remote_copy(
        src_ref=source, dst_ref=target, send_sem=send_sem, recv_sem=recv_sem,
        device_id=device, device_id_type=MESH,
    )


def sigmoid(values):
    return 1.0 / (1.0 + jnp.exp(-values))


def one_hot(shape, source_of):
    target = lax.broadcasted_iota(jnp.int32, shape, 0)
    source = lax.broadcasted_iota(jnp.int32, shape, 1)
    return jnp.where(source == source_of(target), 1.0, 0.0).astype(BF16)


def key_row_of(place, block, pieces):
    tail = block - MAIN
    main_at = place // MAIN * block + place % MAIN
    spare = place - pieces * MAIN
    tail_at = spare // tail * block + MAIN + spare % tail
    return jnp.where(place < pieces * MAIN, main_at, tail_at)


def pair_switch(heads):
    lanes = heads * MAIN
    source = lax.broadcasted_iota(jnp.int32, (lanes, lanes), 0)
    target = lax.broadcasted_iota(jnp.int32, (lanes, lanes), 1)
    return jnp.where(source % heads * MAIN + source // heads == target, 1.0, 0.0).astype(BF16)


def spread_heads(matrix, keys):
    channels, heads = matrix.shape
    one = lax.broadcasted_iota(jnp.int32, (heads, keys * heads), 0)
    two = lax.broadcasted_iota(jnp.int32, (heads, keys * heads), 1)
    repeat = dot_nn(matrix, jnp.where(two % heads == one, 1.0, 0.0).astype(BF16))
    owner = lax.broadcasted_iota(jnp.int32, (1, keys * heads), 1) // heads
    return [jnp.where(owner == key, repeat, 0.0).astype(BF16) for key in range(keys)]


def mean_pair():
    one = lax.broadcasted_iota(jnp.int32, (2 * LANES, 2 * LANES), 0) // LANES
    two = lax.broadcasted_iota(jnp.int32, (2 * LANES, 2 * LANES), 1) // LANES
    return jnp.where(one == two, 1.0 / LANES, 0.0).astype(BF16)


def norm_pair(low, means):
    centered = low.astype(F32) - dot_nn(low, means)
    variance = dot_nn((centered * centered).astype(BF16), means)
    inverse = lax.rsqrt(variance + EPSILON)
    return (centered * inverse, inverse)


GROUP = 16


def columns_of(project):
    size = project.shape[1]
    eye = one_hot((size, size), lambda row: row)
    return dot_nt(eye, project).astype(BF16)


def front_kernel(
    struct_ref, len_ref, act_ref, cond_ref, small_ref, pair_ref,
    *refs
):
    shards, refs = refs[:14], refs[14:]
    (out_ref, prob_out, adapted_ref, sig_ref, gate_ref, query_ref, kv_out, full_ref, *refs) = refs
    whole_outs, refs = refs[:14], refs[14:]
    (prob_ref, kv_ref, *refs) = refs
    wholes, refs = refs[:14], refs[14:]
    (scale_w, shift_w, key_w, value_w, query_w, gate_w) = wholes[:6]
    (
        small_all, pack_ref, pair_buf, lead_ref, spread_ref, keys_ref, values_ref, tail_ref, acc_ref,
        pair_sem, own_sem, small_send, small_recv, gather_send, gather_recv, pack_send, pack_recv,
        span_send, span_recv, whole_sem, prob_sem, kv_sem,
    ) = refs
    total, width = act_ref.shape
    samples, rows = out_ref.shape[0], out_ref.shape[1]
    count = pack_ref.shape[0]
    spans = kv_ref.shape[0]
    heads = width // HEAD_DIM
    structs = pair_ref.shape[0]
    block = pair_ref.shape[1]
    tail = block - MAIN
    pieces = rows // block
    main_rows = pieces * MAIN
    keys = count * block
    pairs = heads // 2
    group, windows = head_windows(width)
    me = lax.axis_index("samp")
    my_span = lax.axis_index("head")
    reduce_pair = reduce_orders(count)
    orders = [order[1:] + order[:1] for order in reduce_pair]
    bits = sorted(reduce_pair[0])
    steps = len(bits)
    peers = flips(me, bits)

    owns = [
        pltpu.make_async_copy(shard, whole.at[me], own_sem.at[at])
        for at, (shard, whole) in enumerate(zip(shards, wholes))
    ]
    for copy in owns:
        copy.start()

    loads = [
        pltpu.make_async_copy(pair_ref.at[struct], pair_buf.at[struct], pair_sem.at[struct])
        for struct in range(structs)
    ]
    for load in loads:
        load.start()
    whole_moves = [
        pltpu.make_async_copy(whole, out, whole_sem.at[at])
        for at, (whole, out) in enumerate(zip(wholes, whole_outs))
    ]
    prob_moves = [
        pltpu.make_async_copy(prob_ref.at[at], prob_out.at[at], prob_sem.at[at]) for at in range(samples)
    ]
    kv_move = pltpu.make_async_copy(kv_ref, kv_out, kv_sem.at[0])
    small_all[me] = small_ref[...]
    greet(
        [dict(samp=peer) for peer in peers[1:]]
        + [dict(head=lax.rem(my_span + away, spans)) for away in range(1, spans)]
    )
    for at in range(1, count):
        send(
            small_ref, small_all.at[me], small_send.at[at], small_recv.at[at], dict(samp=peers[at])
        ).start()

    def gather_copies(which, step, sending):
        order = orders[which % 2]
        held = flips(me, order[:step])
        copies = []
        for at, spot in enumerate(held):
            slot = spot if sending else flip(spot, order[step])
            copies.append(
                send(
                    shards[which] if at == 0 else wholes[which].at[slot], wholes[which].at[slot],
                    gather_send.at[which, step, at], gather_recv.at[which, step, at],
                    dict(samp=flip(me, order[step])),
                )
            )
        return copies

    def gather_start(pair_at, step):
        for which in (2 * pair_at, 2 * pair_at + 1):
            for copy in gather_copies(which, step, True):
                copy.start()

    def gather_wait(pair_at, step):
        for which in (2 * pair_at, 2 * pair_at + 1):
            for copy in gather_copies(which, step, False):
                copy.wait_recv()

    def late_start(step):
        for pair_at in range(3, 7):
            gather_start(pair_at, step)

    def late_out(pair_at):
        gather_wait(pair_at, 2)
        for which in (2 * pair_at, 2 * pair_at + 1):
            whole_moves[which].start()

    def late_wait(step):
        for pair_at in range(3, 7):
            gather_wait(pair_at, step)

    tiles = pack_ref.shape[1]
    halves = (pl.ds(0, tiles // 2), pl.ds(tiles // 2, tiles - tiles // 2))

    def pack_copies(half, step, sending):
        order = orders[half]
        copies = []
        for at, spot in enumerate(flips(me, order[:step])):
            slot = spot if sending else flip(spot, order[step])
            copies.append(
                send(
                    pack_ref.at[slot, halves[half]], pack_ref.at[slot, halves[half]],
                    pack_send.at[half, step, at], pack_recv.at[half, step, at],
                    dict(samp=flip(me, order[step])),
                )
            )
        return copies

    def pack_start(step):
        for half in range(2):
            for copy in pack_copies(half, step, True):
                copy.start()

    def pack_wait(step):
        for half in range(2):
            for copy in pack_copies(half, step, False):
                copy.wait_recv()

    gather_start(0, 0)
    gather_start(1, 0)

    for at in range(1, count):
        send(
            small_ref, small_all.at[peers[at]], small_send.at[at], small_recv.at[at], dict(samp=peers[at])
        ).wait_recv()
    share, cond_share = width // count, cond_ref.shape[1] // count
    channels = LANES // count
    blocks = [small_all[at].astype(F32) for at in range(count)]
    wide = jnp.concatenate([part[:8, :share] for part in blocks], axis=1)
    narrow = jnp.concatenate([part[:8, :cond_share] for part in blocks], axis=1)
    narrow = jnp.concatenate((narrow, jnp.zeros((8, width - narrow.shape[1]), F32)), axis=1)
    line = lax.broadcasted_iota(jnp.int32, (8, width), 0)
    turned = jnp.concatenate([part[8:, :channels] for part in blocks], axis=1)
    turned = jnp.concatenate((turned, jnp.zeros((heads, width - LANES), F32)), axis=1)
    full = jnp.concatenate((jnp.where((line == 0) | (line == 4), narrow, wide), turned), axis=0)
    full_ref[...] = full
    for at, part in enumerate(spread_heads(columns_of(full[8:, :LANES].astype(BF16)), GROUP)):
        spread_ref[at * LANES : (at + 1) * LANES] = part
    means = mean_pair()
    order_switch = pair_switch(heads)
    groups = MAIN // GROUP
    for load in loads:
        load.wait()

    def project_keys(struct, first, number):
        total_lead = None
        for at in range(number // 2):
            key = first + 2 * at
            low = jnp.concatenate((pair_buf[struct, key], pair_buf[struct, key + 1]), axis=1)
            normed, _ = norm_pair(low, means)
            lead = dot_nn(
                normed.astype(BF16),
                spread_ref[2 * at * LANES : (2 * at + 2) * LANES, : number * heads],
            )
            total_lead = lead if total_lead is None else total_lead + lead
        return total_lead.astype(BF16)

    def pair_group(turn, carry):
        lead_ref[turn] = project_keys(lax.div(turn, groups), lax.rem(turn, groups) * GROUP, GROUP)
        return carry

    turns = structs * groups
    cuts = [turns * at // 6 for at in range(7)]
    gather_wait(0, 0)
    gather_start(0, 1)
    gather_wait(1, 0)
    gather_start(1, 1)
    gather_start(2, 0)
    lax.fori_loop(cuts[0], cuts[1], pair_group, 0)
    gather_wait(0, 1)
    gather_start(0, 2)
    lax.fori_loop(cuts[1], cuts[2], pair_group, 0)
    gather_wait(2, 0)
    gather_start(2, 1)
    late_start(0)
    lax.fori_loop(cuts[2], cuts[3], pair_group, 0)
    gather_wait(1, 1)
    gather_start(1, 2)

    gain_one = full[0:1, : cond_ref.shape[1]]
    act_normed, _ = norm_rows(act_ref[...].astype(F32))
    cond_normed, _ = norm_rows(cond_ref[...].astype(F32))
    cond_first = (cond_normed * gain_one).astype(BF16)
    for copy in owns[:6]:
        copy.wait()
    gather_wait(0, 2)
    scale = scale_w[...].reshape(-1, width)
    shift = shift_w[...].reshape(-1, width)
    sig_first = sigmoid(dot_nn(cond_first, scale) + full[1:2])
    adapted = sig_first * act_normed + dot_nn(cond_first, shift)
    sig_ref[...] = sig_first
    adapted_ref[...] = adapted.astype(BF16)
    reorder = one_hot((rows, rows), lambda row: key_row_of(row, block, pieces))
    gather_wait(1, 2)
    for which, whole in ((0, key_w), (1, value_w)):
        for sample in range(samples):
            ordered = dot_nn(
                reorder, adapted[sample * rows : (sample + 1) * rows].astype(BF16)
            ).astype(BF16)
            kv_ref[my_span, which, sample] = dot_nn(ordered, whole[...].reshape(-1, width)).astype(BF16)

    def span_move(way, step, which, sending):
        delta = 1 - 2 * way
        shard = my_span - delta * step if sending else my_span - delta * (step + 1)
        target = my_span + delta
        there = (shard >= 0) & (shard < spans)
        if sending:
            there = there & (target >= 0) & (target < spans)
        copy = send(
            kv_ref.at[shard, which], kv_ref.at[shard, which],
            span_send.at[way, step, which], span_recv.at[way, step, which],
            dict(head=target if sending else my_span - delta),
        )
        return there, copy

    def span_start(step, which):
        for way in range(2):
            there, copy = span_move(way, step, which, True)
            pl.when(there)(copy.start)

    def span_wait(step, which):
        for way in range(2):
            there, copy = span_move(way, step, which, False)
            pl.when(there)(copy.wait_recv)

    span_start(0, 0)
    lax.fori_loop(cuts[3], cuts[6], pair_group, 0)
    for struct in range(structs):
        whole = jnp.concatenate([lead_ref[struct * groups + at] for at in range(groups)], axis=1)
        mixed = dot_nn(whole, order_switch).astype(BF16)
        for at in range(pairs):
            pack_ref[me, struct * pairs + at] = mixed[:, at * LANES : (at + 1) * LANES]
        rest = project_keys(struct, MAIN, tail)
        blank = jnp.zeros((rows, LANES - tail * heads), BF16)
        pack_ref[me, structs * pairs + struct] = jnp.concatenate((rest, blank), axis=1)
    pack_start(0)
    span_wait(0, 0)
    span_start(1, 0)
    span_start(0, 1)
    gather_wait(2, 1)
    gather_start(2, 2)
    low = adapted.astype(BF16)
    gather_wait(2, 2)
    for move in whole_moves[:6]:
        move.start()
    query = dot_nn(low, query_w[...].reshape(-1, width)) + full[2:3]
    for sample in range(samples):
        query_ref[sample] = query[sample * rows : (sample + 1) * rows].astype(BF16)
    pack_wait(0)
    pack_start(1)
    gate_ref[...] = sigmoid(dot_nn(low, gate_w[...].reshape(-1, width)))
    late_wait(0)
    late_start(1)
    for step in range(1, spans - 1):
        span_wait(step, 0)
        if step + 1 < spans - 1:
            span_start(step + 1, 0)
        span_wait(step - 1, 1)
        span_start(step, 1)
    pack_wait(1)
    pack_start(2)

    switch = tail_switch(count, heads, tail)
    places = key_places(count, block)
    keys_ref[keys:] = jnp.zeros_like(keys_ref[keys:])
    values_ref[keys:] = jnp.zeros_like(values_ref[keys:])

    def gather_keys(sample, which, held):
        for span in range(spans):
            held[span * main_rows : (span + 1) * main_rows] = kv_ref[span, which, sample, :main_rows]
            spot = count * MAIN + span * (rows - main_rows)
            held[spot : spot + rows - main_rows] = kv_ref[span, which, sample, main_rows:]

    def one_sample(sample, carry):
        struct = struct_ref[sample]
        valid = places < len_ref[struct]
        gather_keys(sample, 0, keys_ref)
        tiles_of = []
        for pair in range(count // 2):
            even = pack_ref[2 * pair, structs * pairs + struct]
            odd = swap_halves(pack_ref[2 * pair + 1, structs * pairs + struct])
            tiles_of.append(jnp.where(low_half(even), even, odd))
        mixed = dot_nn(jnp.concatenate(tiles_of, axis=1), switch).astype(BF16)
        for at in range(count // 2):
            tail_ref[at] = mixed[:, at * LANES : (at + 1) * LANES]

        def one_group(place, carry):
            for at, (start, span, offset) in enumerate(windows):
                lanes = pl.ds(pl.multiple_of(place * group + start, LANES), span)
                mask = head_mask(span, offset)
                tile = struct * pairs + place * (len(windows) // 2) + at // 2
                bias = []
                for pair in range(count // 2):
                    even = pack_ref[2 * pair, tile]
                    odd = pack_ref[2 * pair + 1, tile]
                    if at % 2 == 0:
                        bias.append(jnp.where(low_half(even), even, swap_halves(odd)))
                    else:
                        bias.append(jnp.where(low_half(even), swap_halves(even), odd))
                per_tile = LANES // (count * tail)
                rest = tail_ref[place * (len(windows) // per_tile) + at // per_tile]
                turn = at % per_tile * count * tail
                bias.append(pltpu.roll(rest, LANES - turn, 1) if turn else rest)
                query = query_ref[sample, :, lanes]
                query = jnp.where(mask, query, jnp.zeros_like(query))
                scores = dot_nt(query, keys_ref[:, lanes]) * HEAD_DIM ** (-0.5) + jnp.concatenate(
                    bias, axis=1
                ).astype(F32)
                scores = jnp.where(valid, scores, NEG_BIG)
                weights = jnp.exp(scores - jnp.max(scores, axis=1, keepdims=True))
                weights = weights * (1.0 / jnp.sum(weights, axis=1, keepdims=True))
                prob_ref[sample, place * len(windows) + at] = weights.astype(BF16)
            return carry

        return lax.fori_loop(0, width // group, one_group, carry)

    def mix_sample(sample, carry):
        gather_keys(sample, 1, values_ref)

        def mix_group(place, carry):
            acc_ref[...] = jnp.zeros_like(acc_ref)
            for at, (start, span, offset) in enumerate(windows):
                lanes = pl.ds(pl.multiple_of(place * group + start, LANES), span)
                weights = prob_ref[sample, place * len(windows) + at]
                mixed = dot_nn(weights, values_ref[:, lanes])
                within = slice(start, start + span)
                acc_ref[:, within] += jnp.where(head_mask(span, offset), mixed, 0.0)
            out_ref[sample, :, pl.ds(pl.multiple_of(place * group, LANES), group)] = acc_ref[
                ...
            ].astype(BF16)
            return carry

        return lax.fori_loop(0, width // group, mix_group, carry)

    pack_wait(2)
    lax.fori_loop(0, samples // 2, one_sample, 0)
    for move in prob_moves[: samples // 2]:
        move.start()
    span_wait(spans - 2, 1)
    kv_move.start()
    lax.fori_loop(samples // 2, samples, one_sample, 0)
    for move in prob_moves[samples // 2 :]:
        move.start()
    for copy in owns[6:]:
        copy.wait()
    for pair_at in range(3, 7):
        gather_wait(pair_at, 1)
        gather_start(pair_at, 2)
        if pair_at == 3:
            lax.fori_loop(0, samples, mix_sample, 0)
        else:
            late_out(pair_at - 1)
    late_out(6)
    for move in whole_moves + prob_moves + [kv_move]:
        move.wait()

    for at in range(1, count):
        send(
            small_ref, small_all.at[me], small_send.at[at], small_recv.at[at], dict(samp=peers[at])
        ).wait_send()
    for which in range(len(wholes)):
        for step in range(steps):
            for copy in gather_copies(which, step, True):
                copy.wait_send()
    for half in range(2):
        for step in range(steps):
            for copy in pack_copies(half, step, True):
                copy.wait_send()
    for step in range(spans - 1):
        for which in range(2):
            for way in range(2):
                there, copy = span_move(way, step, which, True)
                pl.when(there)(copy.wait_send)


def front(struct_of, struct_len, act, cond, small, pair, shards, samples, count, spans):
    total, width = act.shape
    rows = total // samples
    structs, block = pair.shape[0], pair.shape[1]
    heads = width // HEAD_DIM
    group, windows = head_windows(width)
    tail = block - MAIN
    tiles = structs * (heads // 2 + 1)
    steps = count.bit_length() - 1
    vmem = pl.BlockSpec(memory_space=pltpu.VMEM)
    smem = pl.BlockSpec(memory_space=pltpu.SMEM)
    far = pl.BlockSpec(memory_space=pl.ANY)
    dma = pltpu.SemaphoreType.DMA
    return pl.pallas_call(
        front_kernel,
        out_shape=(
            jax.ShapeDtypeStruct((samples, rows, width), BF16),
            jax.ShapeDtypeStruct((samples, heads, rows, KEY_LANES), BF16),
            jax.ShapeDtypeStruct((total, width), BF16),
            jax.ShapeDtypeStruct((total, width), F32),
            jax.ShapeDtypeStruct((total, width), F32),
            jax.ShapeDtypeStruct((samples, rows, width), BF16),
            jax.ShapeDtypeStruct((spans, 2, samples, rows, width), BF16),
            jax.ShapeDtypeStruct((small.shape[0], width), F32),
        )
        + tuple(jax.ShapeDtypeStruct((count,) + shard.shape, BF16) for shard in shards),
        in_specs=[smem, smem, vmem, vmem, vmem] + [far] * 15,
        out_specs=[vmem, far] + [vmem] * 4 + [far, vmem] + [far] * 14,
        scratch_shapes=[
            pltpu.VMEM((samples, heads, rows, KEY_LANES), BF16),
            pltpu.VMEM((spans, 2, samples, rows, width), BF16),
        ]
        + [pltpu.VMEM((count,) + shard.shape, BF16) for shard in shards]
        + [
            pltpu.VMEM((count,) + small.shape, BF16),
            pltpu.VMEM((count, tiles, rows, LANES), BF16),
            pltpu.VMEM(pair.shape, BF16),
            pltpu.VMEM((structs * MAIN // GROUP, rows, GROUP * heads), BF16),
            pltpu.VMEM((GROUP * LANES, GROUP * heads), BF16),
            pltpu.VMEM((KEY_LANES, width), BF16),
            pltpu.VMEM((KEY_LANES, width), BF16),
            pltpu.VMEM((count // 2, rows, LANES), BF16),
            pltpu.VMEM((rows, group), F32),
            dma((structs,)),
            dma((len(shards),)),
            dma((count,)),
            dma((count,)),
            dma((len(shards), steps, count // 2)),
            dma((len(shards), steps, count // 2)),
            dma((2, steps, count // 2)),
            dma((2, steps, count // 2)),
            dma((2, spans - 1, 2)),
            dma((2, spans - 1, 2)),
            dma((len(shards),)),
            dma((samples,)),
            dma((1,)),
        ],
        compiler_params=pltpu.CompilerParams(
            vmem_limit_bytes=60 << 20, collective_id=2, has_side_effects=True
        ),
        name="front",
    )(struct_of, struct_len, act, cond, small, pair, *shards)


def middle_kernel(
    attn_ref, gate_ref, act_ref, cond_ref, cot_ref, full_ref, *refs
):
    sources, refs = refs[:8], refs[8:]
    outs, refs = refs[7:15], refs[:7] + refs[15:]
    in_sem, out_sem = refs[23:]
    loads = [
        pltpu.make_async_copy(source, held, in_sem.at[at])
        for at, (source, held) in enumerate(zip(sources, refs[7:15]))
    ]
    leaves = [
        pltpu.make_async_copy(held, out, out_sem.at[at]) for at, (held, out) in enumerate(zip(refs[15:23], outs))
    ]
    for at in (3, 4, 5, 7, 0, 1, 2, 6):
        loads[at].start()
    ready = {id(held): load for held, load in zip(refs[7:15], loads)}
    leaving = {id(held): leave for held, leave in zip(refs[15:23], leaves)}
    middle_body(ready, leaving, attn_ref, gate_ref, act_ref, cond_ref, cot_ref, full_ref, *refs[:23])
    for leave in leaves:
        leave.wait()


def middle_body(
    ready, leaving, attn_ref, gate_ref, act_ref, cond_ref, cot_ref, full_ref, layer_ref, dgate_ref, dattn_ref, dmid_ref, dcond_ref, extra_ref, vector_ref,
    swish_w, linear_w, down_w, out_w, zero_w, scale_w, zero_two_w, shift_w, swish_g, linear_g, down_g, out_g, zero_g, scale_g, zero_two_g, shift_g,
):
    total, width = act_ref.shape
    samples, rows, _ = attn_ref.shape
    cond_width = cond_ref.shape[1]

    def whole(ref):
        load = ready.pop(id(ref), None)
        if load is not None:
            load.wait()
        return ref[...].reshape(-1, ref.shape[2])

    def store_grad(ref, left, right):
        size = ref.shape[1]
        step = 2 * size if size * 2 < left.shape[1] else size
        for first in range(0, left.shape[1], step):
            value = dot_tn(left[:, first : first + step], right).astype(BF16)
            for at in range(step // size):
                ref[first // size + at] = value[at * size : (at + 1) * size]
        leaving[id(ref)].start()

    cond = cond_ref[...]
    cond_normed, _ = norm_rows(cond.astype(F32))
    gain_two = full_ref[4:5, :cond_width]
    cond_second = (cond_normed * gain_two).astype(BF16)
    attn = jnp.concatenate([attn_ref[at].astype(F32) for at in range(samples)], axis=0)
    gate_sig = gate_ref[...]
    gated = (gate_sig * attn).astype(BF16)
    branch = dot_nn(gated, whole(out_w))
    zero_sig = sigmoid(dot_nn(cond, whole(zero_w)) + full_ref[3:4])
    middle = act_ref[...].astype(F32) + zero_sig * branch
    mid_normed, mid_inverse = norm_rows(middle)
    sig_second = sigmoid(dot_nn(cond_second, whole(scale_w)) + full_ref[5:6])
    adapted = (sig_second * mid_normed + dot_nn(cond_second, whole(shift_w))).astype(BF16)
    swish_pre = dot_nn(adapted, whole(swish_w))
    linear_pre = dot_nn(adapted, whole(linear_w))
    swish_sig = sigmoid(swish_pre)
    hidden = (swish_pre * swish_sig * linear_pre).astype(BF16)
    down_rows = dot_nn(hidden, whole(down_w))
    zero_sig_two = sigmoid(dot_nn(cond, whole(zero_two_w)) + full_ref[6:7])
    layer_ref[...] = (middle + zero_sig_two * down_rows).astype(BF16)

    upstream = cot_ref[...].astype(F32)
    d_down = (upstream * zero_sig_two).astype(BF16)
    d_zero_two = (upstream * down_rows * sigmoid_slope(zero_sig_two)).astype(BF16)
    store_grad(down_g, hidden, d_down)
    store_grad(zero_two_g, cond, d_zero_two)
    d_hidden = dot_nt(d_down, whole(down_w))
    d_swish = (d_hidden * linear_pre * swish_sig * (1.0 + swish_pre * (1.0 - swish_sig))).astype(BF16)
    d_linear = (d_hidden * swish_pre * swish_sig).astype(BF16)
    store_grad(swish_g, adapted, d_swish)
    store_grad(linear_g, adapted, d_linear)
    d_adapted = dot_nt(d_swish, whole(swish_w)) + dot_nt(d_linear, whole(linear_w))
    d_shift = d_adapted.astype(BF16)
    d_pre = (d_adapted * mid_normed * sigmoid_slope(sig_second)).astype(BF16)
    store_grad(scale_g, cond_second, d_pre)
    store_grad(shift_g, cond_second, d_shift)
    d_cond = dot_nt(d_shift, whole(shift_w)) + dot_nt(d_pre, whole(scale_w))
    dcond_ref[...] = d_cond * gain_two
    d_middle = upstream + norm_back(mid_normed, mid_inverse, d_adapted * sig_second)
    dmid_ref[...] = d_middle
    d_branch = (d_middle * zero_sig).astype(BF16)
    d_zero = (d_middle * branch * sigmoid_slope(zero_sig)).astype(BF16)
    store_grad(out_g, gated, d_branch)
    store_grad(zero_g, cond, d_zero)
    extra_ref[...] = dot_nt(d_zero, whole(zero_w)) + dot_nt(d_zero_two, whole(zero_two_w))
    d_gated = dot_nt(d_branch, whole(out_w))
    dgate_ref[...] = (d_gated * attn * sigmoid_slope(gate_sig)).astype(BF16)
    d_attn = d_gated * gate_sig
    for at in range(samples):
        dattn_ref[at] = d_attn[at * rows : (at + 1) * rows].astype(BF16)
    vector_ref[...] = jnp.zeros_like(vector_ref)
    vector_ref[3:4] = jnp.sum(d_zero.astype(F32), axis=0, keepdims=True)
    vector_ref[4:5, :cond_width] = jnp.sum(d_cond * cond_normed, axis=0, keepdims=True)
    vector_ref[5:6] = jnp.sum(d_pre.astype(F32), axis=0, keepdims=True)
    vector_ref[6:7] = jnp.sum(d_zero_two.astype(F32), axis=0, keepdims=True)


def middle_part(attended, gate_sig, act, cond, cotangent, full, weights):
    total, width = act.shape
    vmem = pl.BlockSpec(memory_space=pltpu.VMEM)
    far = pl.BlockSpec(memory_space=pl.ANY)
    weights = list(weights)
    return pl.pallas_call(
        middle_kernel,
        out_shape=(
            jax.ShapeDtypeStruct((total, width), BF16),
            jax.ShapeDtypeStruct((total, width), BF16),
            jax.ShapeDtypeStruct(attended.shape, BF16),
            jax.ShapeDtypeStruct((total, width), F32),
            jax.ShapeDtypeStruct(cond.shape, F32),
            jax.ShapeDtypeStruct(cond.shape, F32),
            jax.ShapeDtypeStruct(full.shape, F32),
        )
        + tuple(jax.ShapeDtypeStruct(weight.shape, BF16) for weight in weights),
        in_specs=[vmem] * 6 + [far] * 8,
        out_specs=[vmem] * 7 + [far] * 8,
        scratch_shapes=[pltpu.VMEM(weight.shape, BF16) for weight in weights + weights]
        + [pltpu.SemaphoreType.DMA((8,)), pltpu.SemaphoreType.DMA((8,))],
        compiler_params=pltpu.CompilerParams(vmem_limit_bytes=62 << 20),
        name="middle",
    )(attended, gate_sig, act, cond, cotangent, full, *weights)


class Halving:
    def __init__(self, me, order, source, zones, send_sem, recv_sem, stay=None, stay_sem=None):
        self.me, self.order, self.source, self.zones = me, order, source, zones
        self.send_sem, self.recv_sem = send_sem, recv_sem
        self.stay, self.stay_sem = stay, stay_sem

    def stays(self):
        if self.stay is None:
            return []
        return [
            pltpu.make_async_copy(self.source.at[spot], self.stay.at[at], self.stay_sem.at[at])
            for at, spot in enumerate(flips(self.me, self.order[1:]))
        ]

    def copies(self, step):
        kept = flips(self.me, self.order[step + 1 :])
        found = []
        for at, spot in enumerate(kept):
            if step == 0:
                leaving = self.source.at[flip(spot, self.order[0])]
            else:
                leaving = self.zones[step - 1].at[2 * at + 1]
            found.append(
                send(
                    leaving, self.zones[step].at[at], self.send_sem.at[step, at],
                    self.recv_sem.at[step, at], dict(samp=flip(self.me, self.order[step])),
                )
            )
        return found

    def start(self, step):
        for copy in self.copies(step) + (self.stays() if step == 0 else []):
            copy.start()

    def first(self, at, spot, lines):
        return self.source[spot, lines] if self.stay is None else self.stay[at, lines]

    def finish(self, step):
        kept = flips(self.me, self.order[step + 1 :])
        zone = self.zones[step]
        if step == 0:
            for copy in self.stays():
                copy.wait()
        for at, copy in enumerate(self.copies(step)):
            copy.wait_recv()

            def add(turn, carry, at=at):
                lines = pl.ds(pl.multiple_of(turn * 16, 16), 16)
                mine = self.first(at, kept[at], lines) if step == 0 else self.zones[step - 1][2 * at, lines]
                zone[at, lines] = (zone[at, lines].astype(F32) + mine.astype(F32)).astype(BF16)
                return carry

            lax.fori_loop(0, zone.shape[1] // 16, add, 0)

    def settle(self):
        for step in range(len(self.order)):
            for copy in self.copies(step):
                copy.wait_send()


def zone_shapes(shapes, count):
    zones = []
    for rows, columns in shapes:
        size = count // 2
        while size:
            zones.append(pltpu.VMEM((size, rows, columns), BF16))
            size //= 2
    return zones


def spans_of(shapes, columns, spans):
    lines = []
    for at, (rows, wide) in enumerate(shapes):
        for half in range(wide // columns):
            lines += [(at, row, half * columns) for row in range(0, rows, 8)]
    each = len(lines) // spans
    moves = []
    for piece in range(spans):
        row = 0
        for at, start, lane in lines[piece * each : (piece + 1) * each]:
            last = moves[-1] if moves else None
            if last and last[0] == piece and last[2] == at and last[4] == lane and last[3] + last[5] == start:
                moves[-1] = last[:5] + (last[5] + 8,)
            else:
                moves.append((piece, row, at, start, lane, 8))
            row += 8
    return (each * 8, moves)


def attend_back_kernel(
    late_shapes, struct_ref, q_ref, kv_ref, do_ref, prob_in, *refs
):
    lates, refs = refs[: len(late_shapes)], refs[len(late_shapes) :]
    (dq_ref, dkv_ref, dpb_ref, late_out, *refs) = refs
    steps = 3
    late_zones, refs = refs[: steps * len(late_shapes)], refs[steps * len(late_shapes) :]
    late_stay, refs = refs[: len(late_shapes)], refs[len(late_shapes) :]
    (late_send, late_recv, stay_sem, prob_ref, prob_sem, *refs) = refs
    each = prob_ref.shape[1] // 2

    def prob_copy(sample, place):
        heads_of = pl.ds(place * each, each)
        return pltpu.make_async_copy(
            prob_in.at[sample, heads_of], prob_ref.at[sample, heads_of], prob_sem.at[sample, place]
        )

    for place in range(2):
        for sample in range(prob_ref.shape[0]):
            prob_copy(sample, place).start()
    attend_back_body(
        prob_copy,
        late_shapes, struct_ref, q_ref, kv_ref, do_ref, prob_ref, lates, dq_ref, dkv_ref, dpb_ref, late_out,
        late_zones, late_stay, late_send, late_recv, stay_sem, *refs
    )


def attend_back_body(
    prob_copy, late_shapes, struct_ref, q_ref, kv_ref, do_ref, prob_ref, lates, dq_ref, dkv_ref, dpb_ref, late_out,
    late_zones, late_stay, late_send, late_recv, stay_sem,
    key_ref, value_ref, dq_acc, dk_acc, dv_acc, first_ref, tail_ref, part_ref, span_ref, pack_ref,
    got_zero, got_one, got_two, span_send, span_recv, pack_send, pack_recv,
):
    samples, rows, width = q_ref.shape
    count = pack_ref.shape[0]
    spans = kv_ref.shape[0]
    heads = width // HEAD_DIM
    block = rows * spans // count
    tail = block - MAIN
    structs = pack_ref.shape[1] // (heads // 2 + 1)
    main_rows = rows // block * MAIN
    keys = count * block
    group, windows = head_windows(width)
    scale = HEAD_DIM ** (-0.5)
    me = lax.axis_index("samp")
    my_span = lax.axis_index("head")
    orders = reduce_orders(count)
    others = [lax.rem(my_span + away, spans) for away in range(1, spans)]
    greet(
        [dict(samp=flip(me, bit)) for bit in sorted(orders[0])] + [dict(head=other) for other in others]
    )
    movers = [
        Halving(
            me, orders[at % 2], lates[at], late_zones[3 * at : 3 * at + 3], late_send.at[at], late_recv.at[at],
            late_stay[at], stay_sem.at[at],
        )
        for at in range(len(lates))
    ]
    for mover in movers:
        mover.start(0)
    switch = tail_switch(count, heads, tail)
    key_ref[keys:] = jnp.zeros_like(key_ref[keys:])
    value_ref[keys:] = jnp.zeros_like(value_ref[keys:])

    def span_copy(place, sample, away):
        lanes = pl.ds(pl.multiple_of(place * group, LANES), group)
        return send(
            part_ref.at[others[away], :, sample, :, lanes],
            span_ref.at[away, :, sample, :, lanes],
            span_send.at[place, sample, away],
            span_recv.at[place, sample, away],
            dict(head=others[away]),
        )

    def one_group(place, carry):
        for sample in range(samples):
            prob_copy(sample, place).wait()
            for span in range(spans):
                for which, held in ((0, key_ref), (1, value_ref)):
                    held[span * main_rows : (span + 1) * main_rows] = kv_ref[
                        span, which, sample, :main_rows, pl.ds(pl.multiple_of(place * group, LANES), group)
                    ]
                    spot = count * MAIN + span * (rows - main_rows)
                    held[spot : spot + rows - main_rows] = kv_ref[
                        span, which, sample, main_rows:, pl.ds(pl.multiple_of(place * group, LANES), group)
                    ]
            dq_acc[...] = jnp.zeros_like(dq_acc)
            dk_acc[...] = jnp.zeros_like(dk_acc)
            dv_acc[...] = jnp.zeros_like(dv_acc)
            kept = [jnp.where(struct_ref[0] == slab, 1.0, 0.0).astype(BF16) for slab in range(structs)]
            added = [jnp.where(struct_ref[1] == slab, 1.0, 0.0).astype(BF16) for slab in range(structs)]
            even_scores = None
            for at, (start, span, offset) in enumerate(windows):
                lanes = pl.ds(pl.multiple_of(place * group + start, LANES), span)
                within = slice(start, start + span)
                mask = head_mask(span, offset)
                upstream = do_ref[sample, :, lanes]
                upstream = jnp.where(mask, upstream, jnp.zeros_like(upstream))
                query = q_ref[sample, :, lanes]
                query = jnp.where(mask, query, jnp.zeros_like(query))
                low = prob_ref[sample, place * len(windows) + at]
                weights = low.astype(F32)
                d_weights = dot_nt(upstream, value_ref[:, within])
                dv_acc[:, within] += dot_tn(low[:, :keys], upstream)
                cross = weights * d_weights
                delta = jnp.sum(cross, axis=1, keepdims=True)
                d_scores = (cross - weights * delta).astype(BF16)
                dq_acc[:, within] += jnp.where(mask, dot_nn(d_scores, key_ref[:, within]), 0.0)
                dk_acc[:, within] += dot_tn(d_scores[:, :keys], query)
                per_tile = LANES // (count * tail)
                turn = at % per_tile * count * tail
                rest = d_scores[:, count * MAIN :]
                rest = pltpu.roll(rest, turn, 1) if turn else rest
                spot = place * (len(windows) // per_tile) + at // per_tile
                if turn:
                    tail_ref[sample, spot] += rest
                else:
                    tail_ref[sample, spot] = rest
                if at % 2 == 0:
                    even_scores = d_scores
                    continue
                for pair in range(count // 2):
                    even = even_scores[:, pair * LANES : (pair + 1) * LANES]
                    odd = d_scores[:, pair * LANES : (pair + 1) * LANES]
                    low_tile = jnp.where(low_half(even), even, swap_halves(odd))
                    high_tile = jnp.where(low_half(even), swap_halves(even), odd)
                    for side, tile in ((0, low_tile), (1, high_tile)):
                        owner = 2 * pair + side
                        if sample == 0:
                            first_ref[at // 2, owner] = tile
                            continue
                        old = first_ref[at // 2, owner]
                        for slab in range(structs):
                            spot = slab * (heads // 2) + place * (len(windows) // 2) + at // 2
                            pack_ref[owner, spot] = old * kept[slab] + tile * added[slab]
            lanes = pl.ds(pl.multiple_of(place * group, LANES), group)
            dq_ref[sample, :, lanes] = (dq_acc[...] * scale).astype(BF16)
            for span in range(spans):
                spot = count * MAIN + span * (rows - main_rows)
                for which, total, factor in ((0, dk_acc, scale), (1, dv_acc, 1.0)):
                    part_ref[span, which, sample, :main_rows, lanes] = (
                        total[span * main_rows : (span + 1) * main_rows] * factor
                    ).astype(BF16)
                    part_ref[span, which, sample, main_rows:, lanes] = (
                        total[spot : spot + rows - main_rows] * factor
                    ).astype(BF16)
            for away in range(spans - 1):
                span_copy(place, sample, away).start()
            if sample == 0:

                @pl.when(place == 0)
                def _():
                    for mover in movers:
                        mover.finish(0)
                        mover.start(1)

        return carry

    lax.fori_loop(0, width // group, one_group, 0)

    mixed = []
    for sample in range(samples):
        whole = jnp.concatenate([tail_ref[sample, at] for at in range(count // 2)], axis=1)
        mixed.append(dot_nt(whole, switch))
    for pair in range(count // 2):
        tiles = [part[:, pair * LANES : (pair + 1) * LANES] for part in mixed]
        for slab in range(structs):
            both = jnp.zeros_like(tiles[0])
            for sample in range(samples):
                both = both + jnp.where(struct_ref[sample] == slab, tiles[sample], 0.0)
            spot = structs * heads // 2 + slab
            pack_ref[2 * pair, spot] = jnp.where(low_half(both), both, 0.0).astype(BF16)
            pack_ref[2 * pair + 1, spot] = jnp.where(low_half(both), swap_halves(both), 0.0).astype(BF16)

    tiles = pack_ref.shape[1]
    halves = (pl.ds(0, tiles // 2), pl.ds(tiles // 2, tiles - tiles // 2))
    bounds = ((0, tiles // 2), (tiles // 2, tiles))
    landing = (got_zero, got_one, got_two)

    def stage_copies(step, half):
        order = orders[half]
        kept = flips(me, order[step + 1 :])
        return [
            send(
                pack_ref.at[flip(spot, order[step]), halves[half]],
                landing[step].at[at, halves[half]],
                pack_send.at[step, half, at],
                pack_recv.at[step, half, at],
                dict(samp=flip(me, order[step])),
            )
            for at, spot in enumerate(kept)
        ]

    flights = [[stage_copies(step, half) for half in range(2)] for step in range(len(orders[0]))]
    for half in range(2):
        for copy in flights[0][half]:
            copy.start()
    for step in range(len(orders[0])):
        for half in range(2):
            kept = flips(me, orders[half][step + 1 :])
            for at, spot in enumerate(kept):
                flights[step][half][at].wait_recv()

                def add(tile, carry, spot=spot, at=at, step=step):
                    pack_ref[spot, tile] = (
                        pack_ref[spot, tile].astype(F32) + landing[step][at, tile].astype(F32)
                    ).astype(BF16)
                    return carry

                lax.fori_loop(bounds[half][0], bounds[half][1], add, 0)
            if step + 1 < len(orders[0]):
                for copy in flights[step + 1][half]:
                    copy.start()
        if step == 0:
            for mover in movers:
                mover.finish(1)
                mover.start(2)
        if step == 1:
            for mover in movers:
                mover.finish(2)
            _, moves = spans_of(late_shapes, width, spans)
            for piece, row, at, start, lane, size in moves:
                late_out[piece, row : row + size] = movers[at].zones[2][
                    0, start : start + size, lane : lane + width
                ]

    def out(tile, carry):
        dpb_ref[tile] = pack_ref[me, tile]
        return carry

    lax.fori_loop(0, tiles, out, 0)

    for place in range(width // group):
        for sample in range(samples):
            for away in range(spans - 1):
                span_copy(place, sample, away).wait_recv()
    for which in range(2):
        for sample in range(samples):
            total = part_ref[my_span, which, sample].astype(F32)
            for away in range(spans - 1):
                total += span_ref[away, which, sample].astype(F32)
            dkv_ref[which, sample] = total.astype(BF16)
    for place in range(width // group):
        for sample in range(samples):
            for away in range(spans - 1):
                span_copy(place, sample, away).wait_send()
    for stage in flights:
        for half in stage:
            for copy in half:
                copy.wait_send()
    for mover in movers:
        mover.settle()


def attend_back(struct_of, structs, query, key_value, upstream, prob, lates, count):
    samples, rows, width = query.shape
    spans = key_value.shape[0]
    heads = width // HEAD_DIM
    group, windows = head_windows(width)
    keys = rows * spans
    tiles = structs * (heads // 2 + 1)
    steps = count.bit_length() - 1
    vmem = pl.BlockSpec(memory_space=pltpu.VMEM)
    smem = pl.BlockSpec(memory_space=pltpu.SMEM)
    late_shapes = [late.shape[1:] for late in lates]
    each, _ = spans_of(late_shapes, width, spans)
    dma = pltpu.SemaphoreType.DMA
    return pl.pallas_call(
        functools.partial(attend_back_kernel, late_shapes),
        out_shape=(
            jax.ShapeDtypeStruct((samples, rows, width), BF16),
            jax.ShapeDtypeStruct((2, samples, rows, width), BF16),
            jax.ShapeDtypeStruct((tiles, rows, LANES), BF16),
            jax.ShapeDtypeStruct((spans, each, width), BF16),
        ),
        in_specs=[smem] + [vmem] * 3 + [pl.BlockSpec(memory_space=pl.ANY)] * (1 + len(lates)),
        out_specs=[vmem] * 4,
        scratch_shapes=zone_shapes(late_shapes, count)
        + [pltpu.VMEM((count // 2,) + shape, BF16) for shape in late_shapes]
        + [
            dma((len(lates), steps, count // 2)),
            dma((len(lates), steps, count // 2)),
            dma((len(lates), count // 2)),
            pltpu.VMEM(prob.shape, BF16),
            dma((samples, 2)),
            pltpu.VMEM((KEY_LANES, group), BF16),
            pltpu.VMEM((KEY_LANES, group), BF16),
            pltpu.VMEM((rows, group), F32),
            pltpu.VMEM((keys, group), F32),
            pltpu.VMEM((keys, group), F32),
            pltpu.VMEM((len(windows) // 2, count, rows, LANES), BF16),
            pltpu.VMEM((samples, count // 2, rows, LANES), BF16),
            pltpu.VMEM((spans, 2, samples, rows, width), BF16),
            pltpu.VMEM((spans - 1, 2, samples, rows, width), BF16),
            pltpu.VMEM((count, tiles, rows, LANES), BF16),
            pltpu.VMEM((count // 2, tiles, rows, LANES), BF16),
            pltpu.VMEM((count // 4, tiles, rows, LANES), BF16),
            pltpu.VMEM((count // 8, tiles, rows, LANES), BF16),
            pltpu.SemaphoreType.DMA((width // group, samples, spans - 1)),
            pltpu.SemaphoreType.DMA((width // group, samples, spans - 1)),
            pltpu.SemaphoreType.DMA((steps, 2, count // 2)),
            pltpu.SemaphoreType.DMA((steps, 2, count // 2)),
        ],
        compiler_params=pltpu.CompilerParams(
            vmem_limit_bytes=60 << 20, collective_id=1, has_side_effects=True
        ),
        name="attend_back",
    )(struct_of, query, key_value, upstream, prob, *lates)


class ChainSum:
    def __init__(self, place, places, source, got, whole, send_sem, recv_sem):
        self.place, self.places, self.source, self.got, self.whole = place, places, source, got, whole
        self.send_sem, self.recv_sem = send_sem, recv_sem

    def ways(self):
        return ((0, 1, self.place), (1, -1, self.places - 1 - self.place))

    def owner(self, way, spot):
        return spot if way == 0 else self.places - 1 - spot

    def partial(self, way, delta, tick, leaving):
        return send(
            leaving, self.got.at[way, tick], self.send_sem.at[0, way, tick], self.recv_sem.at[0, way, tick],
            dict(head=self.place + delta),
        )

    def each_partial(self, tick, act):
        for way, delta, spot in self.ways():
            piece = self.places - 1 - tick + spot
            sends = (tick >= spot) & (piece > spot)

            @pl.when(sends & (spot == 0))
            def _(way=way, delta=delta, piece=piece):
                act(self.partial(way, delta, tick, self.source.at[self.owner(way, piece)]))

            if tick:

                @pl.when(sends & (spot > 0))
                def _(way=way, delta=delta):
                    act(self.partial(way, delta, tick, self.got.at[way, tick - 1]))

    def start(self, tick):
        self.each_partial(tick, lambda copy: copy.start())

    def add(self, target, spot, source):
        size = 24

        def step(turn, carry):
            lines = pl.ds(pl.multiple_of(turn * size, 8), size)
            target[spot + (lines,)] = (
                target[spot + (lines,)].astype(F32) + source(lines).astype(F32)
            ).astype(BF16)
            return carry

        lax.fori_loop(0, self.source.shape[1] // size, step, 0)

    def receive(self, tick):
        for way, delta, spot in self.ways():
            piece = self.places - 2 - tick + spot

            @pl.when((spot >= 1) & (tick >= spot - 1))
            def _(way=way, delta=delta, piece=piece):
                self.partial(way, delta, tick, self.got.at[way, tick]).wait_recv()
                if tick < self.places - 2:
                    mine = self.owner(way, piece)
                    self.add(self.got, (way, tick), lambda lines: self.source[mine, lines])

    def total(self):
        self.whole[self.place] = self.source[self.place]
        for way, delta, spot in self.ways():

            @pl.when(spot >= 1)
            def _(way=way):
                self.add(self.whole, (self.place,), lambda lines: self.got[way, self.places - 2, lines])

    def passing(self, way, delta, step, sending):
        piece = self.place - delta * step if sending else self.place - delta * (step + 1)
        target = self.place + delta
        there = (piece >= 0) & (piece < self.places)
        if sending:
            there = there & (target >= 0) & (target < self.places)
        copy = send(
            self.whole.at[piece], self.whole.at[piece], self.send_sem.at[1, way, step],
            self.recv_sem.at[1, way, step], dict(head=target if sending else self.place - delta),
        )
        return there, copy

    def spread_start(self, step):
        for way, delta, _ in self.ways():
            there, copy = self.passing(way, delta, step, True)
            pl.when(there)(copy.start)

    def spread_wait(self, step):
        for way, delta, _ in self.ways():
            there, copy = self.passing(way, delta, step, False)
            pl.when(there)(copy.wait_recv)

    def settle(self):
        for tick in range(self.places - 1):
            self.each_partial(tick, lambda copy: copy.wait_send())
            for way, delta, _ in self.ways():
                there, copy = self.passing(way, delta, tick, True)
                pl.when(there)(copy.wait_send)


def finish_kernel(
    early_shapes,
    act_ref, cond_ref, adapted_ref, sig_ref, full_ref, dq_ref, dkv_ref, dgate_ref, dmid_ref, dcond_ref,
    extra_ref, vector_ref, dpb_ref, late_ref, pair_ref, *refs
):
    weights_in, refs = refs[:6], refs[6:]
    (ig_ref, cg_ref, pg_ref, small_out, early_all, late_all, *refs) = refs
    grads, refs = refs[: len(early_shapes)], refs[len(early_shapes) :]
    zones, refs = refs[: 3 * len(early_shapes)], refs[3 * len(early_shapes) :]
    (
        early_ref, early_got, late_got, small_ref, small_got, sum_ref, sum_got,
        pair_buf, lead_ref, lead_turned, spread_ref, block_ref, tail_block, weight_acc,
        pair_sem, block_sem, grad_send, grad_recv, late_send, late_recv, early_send, early_recv,
        small_send, small_recv, sum_send, sum_recv, weight_sem, *weights_here
    ) = refs
    (scale_w, shift_w, key_w, value_w, query_w, gate_w) = weights_here
    weight_loads = [
        pltpu.make_async_copy(source, held, weight_sem.at[at])
        for at, (source, held) in enumerate(zip(weights_in, weights_here))
    ]
    total, width = act_ref.shape
    count = grads[0].shape[0]
    spans = late_ref.shape[0]
    structs, block, rows, _ = pair_buf.shape
    samples = total // rows
    heads = width // HEAD_DIM
    tail = block - MAIN
    pieces = rows // block
    pairs = heads // 2
    me = lax.axis_index("samp")
    my_span = lax.axis_index("head")
    orders = reduce_orders(count)
    peers = flips(me, sorted(orders[0]))
    others = [lax.rem(my_span + away, spans) for away in range(1, spans)]

    loads = [
        pltpu.make_async_copy(pair_ref.at[struct], pair_buf.at[struct], pair_sem.at[struct])
        for struct in range(structs)
    ]
    for load in weight_loads + loads:
        load.start()
    greet([dict(samp=peer) for peer in peers[1:]] + [dict(head=other) for other in others])

    late_sum = ChainSum(my_span, spans, late_ref, late_got, late_all, late_send, late_recv)
    early_sum = ChainSum(my_span, spans, early_ref, early_got, early_all, early_send, early_recv)
    late_sum.start(0)

    adapted = adapted_ref[...]
    back = one_hot((rows, rows), lambda row: row)
    place = lax.broadcasted_iota(jnp.int32, (rows, rows), 1)
    row = lax.broadcasted_iota(jnp.int32, (rows, rows), 0)
    back = jnp.where(row == key_row_of(place, block, pieces), 1.0, 0.0).astype(BF16)
    d_query = jnp.concatenate([dq_ref[at].astype(F32) for at in range(samples)], axis=0).astype(BF16)
    d_key, d_value = [
        jnp.concatenate([dot_nn(back, dkv_ref[which, at]) for at in range(samples)], axis=0).astype(BF16)
        for which in range(2)
    ]
    d_gate = dgate_ref[...]

    def store_grad(at, left, right):
        size = grads[at].shape[1]
        value = dot_tn(left, right).astype(BF16)
        for owner in range(count):
            grads[at][owner] = value[owner * size : (owner + 1) * size]

    movers = [
        Halving(
            me, orders[at % 2], grads[at], zones[3 * at : 3 * at + 3], grad_send.at[at], grad_recv.at[at]
        )
        for at in range(len(grads))
    ]
    for at, upstream in ((2, d_key), (3, d_value), (4, d_query), (5, d_gate)):
        store_grad(at, adapted, upstream)
        movers[at].start(0)
    late_sum.receive(0)
    late_sum.start(1)
    for mover in movers[2:]:
        mover.finish(0)
        mover.start(1)

    for load in weight_loads:
        load.wait()
    d_adapted = dot_nt(d_query, query_w[...].reshape(-1, width))
    d_adapted += dot_nt(d_key, key_w[...].reshape(-1, width))
    d_adapted += dot_nt(d_value, value_w[...].reshape(-1, width))
    d_adapted += dot_nt(d_gate, gate_w[...].reshape(-1, width))
    gain_one = full_ref[0:1, : cond_ref.shape[1]]
    act_normed, act_inverse = norm_rows(act_ref[...].astype(F32))
    cond_normed, cond_inverse = norm_rows(cond_ref[...].astype(F32))
    cond_first = (cond_normed * gain_one).astype(BF16)
    sig_first = sig_ref[...]
    d_shift = d_adapted.astype(BF16)
    d_pre = (d_adapted * act_normed * sigmoid_slope(sig_first)).astype(BF16)
    store_grad(0, cond_first, d_pre)
    store_grad(1, cond_first, d_shift)
    movers[0].start(0)
    movers[1].start(0)
    for mover in movers[:2]:
        mover.finish(0)
        mover.start(1)
    late_sum.receive(1)
    late_sum.start(2)
    ig_ref[...] = dmid_ref[...] + norm_back(act_normed, act_inverse, d_adapted * sig_first)
    d_cond = dot_nt(d_shift, shift_w[...].reshape(-1, width)) + dot_nt(d_pre, scale_w[...].reshape(-1, width))
    cg_ref[...] = norm_back(cond_normed, cond_inverse, d_cond * gain_one + dcond_ref[...]) + extra_ref[...]
    small_ref[...] = vector_ref[...]
    small_ref[0:1, : cond_ref.shape[1]] = jnp.sum(d_cond * cond_normed, axis=0, keepdims=True)
    small_ref[1:2] = jnp.sum(d_pre.astype(F32), axis=0, keepdims=True)
    small_ref[2:3] = jnp.sum(d_query.astype(F32), axis=0, keepdims=True)

    project = full_ref[8:, :LANES]
    project = (project - jnp.mean(project, axis=1, keepdims=True)).astype(BF16)
    columns = columns_of(project)
    for at, part in enumerate(spread_heads(columns, GROUP)):
        spread_ref[at * LANES : (at + 1) * LANES] = part
    switch = pair_switch(heads)
    means = mean_pair()
    groups = MAIN // GROUP
    for struct in range(structs):
        whole = jnp.concatenate([dpb_ref[struct * pairs + at] for at in range(pairs)], axis=1)
        mixed = dot_nt(whole, switch).astype(BF16)
        for at in range(groups):
            lead_ref[struct * groups + at] = mixed[:, at * GROUP * heads : (at + 1) * GROUP * heads]
    turn_eye = one_hot((rows, rows), lambda line: line)
    weight_acc[...] = jnp.zeros_like(weight_acc)
    for load in loads:
        load.wait()

    def back_keys(struct, first, keys, lead, target):
        for at in range(keys // 2):
            key = first + 2 * at
            low = jnp.concatenate((pair_buf[struct, key], pair_buf[struct, key + 1]), axis=1)
            normed, inverse = norm_pair(low, means)
            upstream = dot_nt(lead, spread_ref[2 * at * LANES : (2 * at + 2) * LANES, : lead.shape[1]])
            cross = dot_nn((upstream * normed).astype(BF16), means)
            result = inverse * (upstream - normed * cross)
            target(2 * at, result[:, :LANES])
            target(2 * at + 1, result[:, LANES:])
            kept = normed.astype(BF16)
            for side in range(2):
                turned = lead_turned[(2 * at + side) * heads : (2 * at + side + 1) * heads]
                weight_acc[...] += dot_nn(turned, kept[:, side * LANES : (side + 1) * LANES])

    def block_copy(turn):
        slot = lax.rem(turn, 2)
        return pltpu.make_async_copy(
            block_ref.at[slot],
            pg_ref.at[lax.div(turn, groups), pl.ds(lax.rem(turn, groups) * GROUP, GROUP)],
            block_sem.at[slot],
        )

    def pair_group(turn, carry):
        @pl.when(turn >= 2)
        def _():
            block_copy(turn - 2).wait()

        slot = lax.rem(turn, 2)
        lead = lead_ref[turn]
        lead_turned[...] = dot_tn(lead, turn_eye).astype(BF16)

        def target(at, value):
            block_ref[slot, at] = value.astype(BF16)

        back_keys(lax.div(turn, groups), lax.rem(turn, groups) * GROUP, GROUP, lead, target)
        block_copy(turn).start()
        return carry

    turns = structs * groups
    late_sum.receive(2)
    late_sum.total()
    late_sum.spread_start(0)

    def stage(number):
        for mover in movers[2:] + movers[:2]:
            mover.finish(number)
            if number < 2:
                mover.start(number + 1)

    def lead_sum():
        stage(2)
        _, moves = spans_of(early_shapes, width, spans)
        for piece, line, at, start, lane, size in moves:
            early_ref[piece, line : line + size] = movers[at].zones[2][
                0, start : start + size, lane : lane + width
            ]
        early_sum.start(0)

    def early_turn(tick):
        early_sum.receive(tick)
        early_sum.start(tick + 1)

    def late_turn(step):
        late_sum.spread_wait(step)
        late_sum.spread_start(step + 1)

    events = {
        1: lambda: stage(1),
        2: lambda: late_turn(0),
        5: lead_sum,
        6: lambda: late_turn(1),
        8: lambda: early_turn(0),
        10: lambda: early_turn(1),
    }

    def pair_turn(turn, carry):
        pair_group(turn, carry)
        for at, event in events.items():
            pl.when(turn == at)(event)
        return carry

    lax.fori_loop(0, turns, pair_turn, 0)
    late_sum.spread_wait(2)
    early_sum.receive(2)
    early_sum.total()
    early_sum.spread_start(0)
    for struct in range(structs):
        lead = dpb_ref[structs * pairs + struct]
        lead = lead[:, : tail * heads]
        lead_turned[: tail * heads] = dot_tn(lead, turn_eye).astype(BF16)

        def tail_target(at, value, struct=struct):
            tail_block[struct, at] = value.astype(BF16)

        back_keys(struct, MAIN, tail, lead, tail_target)
    tail_copies = [
        pltpu.make_async_copy(
            tail_block.at[struct], pg_ref.at[struct, pl.ds(MAIN, tail)], pair_sem.at[struct]
        )
        for struct in range(structs)
    ]
    for copy in tail_copies:
        copy.start()
    small_ref[8:, :LANES] = weight_acc[...]
    early_sum.spread_wait(0)
    early_sum.spread_start(1)

    def small_copies(sending):
        return [
            send(
                small_ref, small_got.at[me if sending else peers[at]], small_send.at[at], small_recv.at[at],
                dict(samp=peers[at]),
            )
            for at in range(1, count)
        ]

    def sum_copies(sending):
        return [
            send(
                sum_ref, sum_got.at[my_span if sending else lax.rem(my_span + spans - 1 - at, spans)],
                sum_send.at[at], sum_recv.at[at], dict(head=other),
            )
            for at, other in enumerate(others)
        ]

    for copy in small_copies(True):
        copy.start()
    small_got[me] = small_ref[...]
    for copy in small_copies(False):
        copy.wait_recv()
    summed = small_got[0]
    for at in range(1, count):
        summed = summed + small_got[at]
    sum_ref[...] = summed
    for copy in sum_copies(True):
        copy.start()
    sum_got[my_span] = summed
    early_sum.spread_wait(1)
    early_sum.spread_start(2)
    for copy in sum_copies(False):
        copy.wait_recv()
    summed = sum_got[0]
    for at in range(1, spans):
        summed = summed + sum_got[at]
    share, cond_share = width // count, cond_ref.shape[1] // count
    channels = LANES // count

    def own(rows_of, size):
        part = jnp.where(me == 0, rows_of[:, :size], 0.0)
        for at in range(1, count):
            part = part + jnp.where(me == at, rows_of[:, at * size : (at + 1) * size], 0.0)
        return jnp.concatenate((part, jnp.zeros((part.shape[0], LANES - size), F32)), axis=1)

    line = lax.broadcasted_iota(jnp.int32, (8, LANES), 0)
    vectors_own = jnp.where((line == 0) | (line == 4), own(summed[:8], cond_share), own(summed[:8], share))
    small_out[...] = jnp.concatenate((vectors_own, own(summed[8:], channels)), axis=0)
    early_sum.spread_wait(2)

    block_copy(turns - 2).wait()
    block_copy(turns - 1).wait()
    for copy in tail_copies:
        copy.wait()
    for mover in movers:
        mover.settle()
    late_sum.settle()
    early_sum.settle()
    for copy in small_copies(True) + sum_copies(True):
        copy.wait_send()


def finish(
    act, cond, adapted, sig, full, d_query, d_key_value, d_gate, d_middle, d_cond, extra, vectors, packed,
    late, pair, weights,
):
    total, width = act.shape
    cond_width = cond.shape[1]
    spans, late_each, _ = late.shape
    count = weights[0].shape[0]
    structs, block, rows, _ = pair.shape
    heads = width // HEAD_DIM
    tail = block - MAIN
    early_shapes = [weight.shape[1:] for weight in weights]
    early_each, _ = spans_of(early_shapes, width, spans)
    steps = count.bit_length() - 1
    vmem = pl.BlockSpec(memory_space=pltpu.VMEM)
    far = pl.BlockSpec(memory_space=pl.ANY)
    dma = pltpu.SemaphoreType.DMA
    turns = structs * (MAIN // GROUP)
    return pl.pallas_call(
        functools.partial(finish_kernel, early_shapes),
        out_shape=(
            jax.ShapeDtypeStruct((total, width), F32),
            jax.ShapeDtypeStruct((total, cond_width), F32),
            jax.ShapeDtypeStruct(pair.shape, BF16),
            jax.ShapeDtypeStruct((full.shape[0], LANES), F32),
            jax.ShapeDtypeStruct((spans, early_each, width), BF16),
            jax.ShapeDtypeStruct((spans, late_each, width), BF16),
        ),
        in_specs=[vmem] * 14 + [far] * 7,
        out_specs=[vmem, vmem, far, vmem, vmem, vmem],
        scratch_shapes=[pltpu.VMEM(weight.shape, BF16) for weight in weights]
        + zone_shapes(early_shapes, count)
        + [
            pltpu.VMEM((spans, early_each, width), BF16),
            pltpu.VMEM((2, spans - 1, early_each, width), BF16),
            pltpu.VMEM((2, spans - 1, late_each, width), BF16),
            pltpu.VMEM(full.shape, F32),
            pltpu.VMEM((count,) + full.shape, F32),
            pltpu.VMEM(full.shape, F32),
            pltpu.VMEM((spans,) + full.shape, F32),
            pltpu.VMEM(pair.shape, BF16),
            pltpu.VMEM((turns, rows, GROUP * heads), BF16),
            pltpu.VMEM((GROUP * heads, rows), BF16),
            pltpu.VMEM((GROUP * LANES, GROUP * heads), BF16),
            pltpu.VMEM((2, GROUP, rows, LANES), BF16),
            pltpu.VMEM((structs, tail, rows, LANES), BF16),
            pltpu.VMEM((heads, LANES), F32),
            dma((structs,)),
            dma((2,)),
            dma((len(weights), steps, count // 2)),
            dma((len(weights), steps, count // 2)),
            dma((2, 2, spans - 1)),
            dma((2, 2, spans - 1)),
            dma((2, 2, spans - 1)),
            dma((2, 2, spans - 1)),
            dma((count,)),
            dma((count,)),
            dma((spans,)),
            dma((spans,)),
            dma((len(weights),)),
        ]
        + [pltpu.VMEM(weight.shape, BF16) for weight in weights],
        compiler_params=pltpu.CompilerParams(
            vmem_limit_bytes=60 << 20, collective_id=3, has_side_effects=True
        ),
        name="finish",
    )(
        act, cond, adapted, sig, full, d_query, d_key_value, d_gate, d_middle, d_cond, extra, vectors, packed,
        late, pair, *weights
    )


def deliver_kernel(shapes, ig_in, cg_in, early_in, late_in, pair_in, ig_out, cg_out, pair_ref, *refs):
    number = len(shapes[0]) + len(shapes[1])
    outs, held = refs[:number], refs[number : 2 * number]
    sems = refs[2 * number]
    moves = [pltpu.make_async_copy(ig_in, ig_out, sems.at[0]), pltpu.make_async_copy(cg_in, cg_out, sems.at[1])]
    moves += [
        pltpu.make_async_copy(part, out, sems.at[2 + at]) for at, (part, out) in enumerate(zip(held, outs))
    ]
    pair_ref[...] = pair_in[...].astype(F32)

    @pl.when(pl.program_id(0) == 0)
    def _():
        spans, _, width = early_in.shape
        first = 0
        for part, source in zip(shapes, (early_in, late_in)):
            _, places = spans_of(part, width, spans)
            for piece, line, at, start, lane, size in places:
                held[first + at][start : start + size, lane : lane + width] = source[
                    piece, line : line + size
                ].astype(F32)
            first += len(part)
        for move in moves:
            move.start()

    @pl.when(pl.program_id(0) == pl.num_programs(0) - 1)
    def _():
        for move in moves:
            move.wait()


def deliver(input_grad, cond_grad, early, late, pair_grad, shapes):
    structs, block, rows, channels = pair_grad.shape
    turn = block // 4

    def whole(shape):
        return pl.BlockSpec(tuple(shape), lambda at: (0,) * len(shape), pipeline_mode=pl.Buffered(1))

    far = pl.BlockSpec(memory_space=pl.ANY)
    tile = pl.BlockSpec((1, turn, rows, channels), lambda at: (at // 4, at % 4, 0, 0))
    flat = list(shapes[0]) + list(shapes[1])
    return pl.pallas_call(
        functools.partial(deliver_kernel, shapes),
        out_shape=(
            jax.ShapeDtypeStruct(input_grad.shape, F32),
            jax.ShapeDtypeStruct(cond_grad.shape, F32),
            jax.ShapeDtypeStruct(pair_grad.shape, F32),
        )
        + tuple(jax.ShapeDtypeStruct(shape, F32) for shape in flat),
        grid=(structs * 4,),
        in_specs=[whole(part.shape) for part in (input_grad, cond_grad, early, late)] + [tile],
        out_specs=[far, far, tile] + [far] * len(flat),
        scratch_shapes=[pltpu.VMEM(shape, F32) for shape in flat] + [pltpu.SemaphoreType.DMA((2 + len(flat),))],
        compiler_params=pltpu.CompilerParams(vmem_limit_bytes=62 << 20),
        name="deliver",
    )(input_grad, cond_grad, early, late, pair_grad)


def plain_kernel(struct_ref, len_ref, q_ref, k_ref, v_ref, bias_ref, out_ref, prob_ref, acc_ref):
    sample = pl.program_id(0)
    group_at = pl.program_id(1)
    length = len_ref[struct_ref[sample]]
    keys = k_ref.shape[1]
    group, windows = head_windows(q_ref.shape[2])
    valid = lax.broadcasted_iota(jnp.int32, (1, keys), 1) < length
    acc_ref[...] = jnp.zeros_like(acc_ref)
    for at, (start, width, offset) in enumerate(windows):
        lanes = slice(start, start + width)
        mask = head_mask(width, offset)
        query = q_ref[0, :, lanes]
        query = jnp.where(mask, query, jnp.zeros_like(query))
        scores = dot_nt(query, k_ref[0, :, lanes]) * HEAD_DIM ** (-0.5) + bias_ref[
            0, at
        ].astype(F32)
        scores = jnp.where(valid, scores, NEG_BIG)
        weights = jnp.exp(scores - jnp.max(scores, axis=1, keepdims=True))
        weights = weights * (1.0 / jnp.sum(weights, axis=1, keepdims=True))
        weights = weights.astype(BF16)
        prob_ref[0, at] = weights
        mixed = dot_nn(weights, v_ref[0, :, lanes])
        acc_ref[:, lanes] += jnp.where(mask, mixed, 0.0)
    out_ref[0] = acc_ref[...].astype(BF16)


def plain(struct_of, struct_len, query, key, value, bias):
    samples, rows, width = query.shape
    keys = key.shape[1]
    heads = bias.shape[1]
    group, windows = head_windows(width)
    each = len(windows)
    return pl.pallas_call(
        plain_kernel,
        out_shape=(
            jax.ShapeDtypeStruct((samples, rows, width), BF16),
            jax.ShapeDtypeStruct((samples, heads, rows, keys), BF16),
        ),
        grid_spec=pltpu.PrefetchScalarGridSpec(
            num_scalar_prefetch=2,
            grid=(samples, heads // each),
            in_specs=[
                pl.BlockSpec((1, rows, group), lambda b, g, s, n: (b, 0, g)),
                pl.BlockSpec((1, keys, group), lambda b, g, s, n: (b, 0, g)),
                pl.BlockSpec((1, keys, group), lambda b, g, s, n: (b, 0, g)),
                pl.BlockSpec((1, each, rows, keys), lambda b, g, s, n: (s[b], g, 0, 0)),
            ],
            out_specs=[
                pl.BlockSpec((1, rows, group), lambda b, g, s, n: (b, 0, g)),
                pl.BlockSpec((1, each, rows, keys), lambda b, g, s, n: (b, g, 0, 0)),
            ],
            scratch_shapes=[pltpu.VMEM((rows, group), F32)],
        ),
        compiler_params=pltpu.CompilerParams(vmem_limit_bytes=48 << 20),
        name="plain",
    )(struct_of, struct_len, query, key, value, bias)


def plain_back_kernel(
    struct_ref, q_ref, k_ref, v_ref, do_ref, prob_ref, dq_ref, dk_ref, dv_ref, bias_ref,
    dq_acc, dk_acc, dv_acc, bias_acc,
):
    samples = q_ref.shape[0]
    structs = bias_ref.shape[0]
    group, windows = head_windows(q_ref.shape[2])
    scale = HEAD_DIM ** (-0.5)
    for sample in range(samples):
        struct = struct_ref[sample]
        dq_acc[...] = jnp.zeros_like(dq_acc)
        dk_acc[...] = jnp.zeros_like(dk_acc)
        dv_acc[...] = jnp.zeros_like(dv_acc)
        for at, (start, width, offset) in enumerate(windows):
            lanes = slice(start, start + width)
            mask = head_mask(width, offset)
            upstream = do_ref[sample, :, lanes]
            upstream = jnp.where(mask, upstream, jnp.zeros_like(upstream))
            query = q_ref[sample, :, lanes]
            query = jnp.where(mask, query, jnp.zeros_like(query))
            low = prob_ref[sample, at]
            weights = low.astype(F32)
            d_weights = dot_nt(upstream, v_ref[sample, :, lanes])
            dv_acc[:, lanes] += dot_tn(low, upstream)
            cross = weights * d_weights
            delta = jnp.sum(cross, axis=1, keepdims=True)
            d_scores = (cross - weights * delta).astype(BF16)
            dq_acc[:, lanes] += jnp.where(mask, dot_nn(d_scores, k_ref[sample, :, lanes]), 0.0)
            dk_acc[:, lanes] += dot_tn(d_scores, query)
            for slab in range(structs):
                part = jnp.where(struct == slab, 1.0, 0.0) * d_scores.astype(F32)
                if sample == 0:
                    bias_acc[slab, at] = part
                elif sample < samples - 1:
                    bias_acc[slab, at] += part
                else:
                    bias_ref[slab, at] = (bias_acc[slab, at] + part).astype(BF16)
        dq_ref[sample] = (dq_acc[...] * scale).astype(BF16)
        dk_ref[sample] = (dk_acc[...] * scale).astype(BF16)
        dv_ref[sample] = dv_acc[...].astype(BF16)


def plain_back(struct_of, structs, query, key, value, upstream, prob):
    samples, rows, width = query.shape
    keys = key.shape[1]
    heads = prob.shape[1]
    group, windows = head_windows(width)
    each = len(windows)
    return pl.pallas_call(
        plain_back_kernel,
        out_shape=(
            jax.ShapeDtypeStruct((samples, rows, width), BF16),
            jax.ShapeDtypeStruct((samples, keys, width), BF16),
            jax.ShapeDtypeStruct((samples, keys, width), BF16),
            jax.ShapeDtypeStruct((structs, heads, rows, keys), BF16),
        ),
        grid_spec=pltpu.PrefetchScalarGridSpec(
            num_scalar_prefetch=1,
            grid=(heads // each,),
            in_specs=[
                pl.BlockSpec((samples, rows, group), lambda g, s: (0, 0, g)),
                pl.BlockSpec((samples, keys, group), lambda g, s: (0, 0, g)),
                pl.BlockSpec((samples, keys, group), lambda g, s: (0, 0, g)),
                pl.BlockSpec((samples, rows, group), lambda g, s: (0, 0, g)),
                pl.BlockSpec((samples, each, rows, keys), lambda g, s: (0, g, 0, 0)),
            ],
            out_specs=[
                pl.BlockSpec((samples, rows, group), lambda g, s: (0, 0, g)),
                pl.BlockSpec((samples, keys, group), lambda g, s: (0, 0, g)),
                pl.BlockSpec((samples, keys, group), lambda g, s: (0, 0, g)),
                pl.BlockSpec((structs, each, rows, keys), lambda g, s: (0, g, 0, 0)),
            ],
            scratch_shapes=[
                pltpu.VMEM((rows, group), F32),
                pltpu.VMEM((keys, group), F32),
                pltpu.VMEM((keys, group), F32),
                pltpu.VMEM((structs, each, rows, keys), F32),
            ],
        ),
        compiler_params=pltpu.CompilerParams(vmem_limit_bytes=60 << 20),
        name="plain_back",
    )(struct_of, query, key, value, upstream, prob)


def pack_rows(pieces, columns):
    return jnp.concatenate([piece.reshape(-1, columns) for piece in pieces], axis=0)


def pack_small(pieces, columns):
    flat = jnp.concatenate([piece.reshape(-1) for piece in pieces])
    rows = -(-flat.shape[0] // columns)
    rows = -(-rows // 8) * 8
    return jnp.pad(flat, (0, rows * columns - flat.shape[0])).reshape(rows, columns)


def unpack_rows(gathered, shapes):
    whole, at = [], 0
    count, _, columns = gathered.shape
    for rows, cols in shapes:
        held = rows * cols // columns
        whole.append(gathered[:, at : at + held].reshape(count * rows, cols))
        at += held
    return whole


def unpack_small(gathered, shapes):
    whole, at = [], 0
    count = gathered.shape[0]
    flat = gathered.reshape(count, -1)
    for shape in shapes:
        size = 1
        for extent in shape:
            size *= extent
        whole.append(flat[:, at : at + size].reshape((count * shape[0],) + shape[1:]))
        at += size
    return whole


def plain_device(
    act, cond, pair, struct_of, struct_len,
    gain_first, scale_first, scale_bias_first, shift_first,
    query_weight, query_bias, key_weight, value_weight, gate_weight, output_weight,
    pair_weight, zero_first, zero_bias_first,
    gain_second, scale_second, scale_bias_second, shift_second,
    swish_weight, linear_weight, down_weight, zero_second, zero_bias_second,
    cotangent,
):
    samples, rows, width = act.shape
    cond_width = cond.shape[2]
    total = samples * rows
    structs = pair.shape[0]
    small = (
        gain_first, scale_bias_first, query_bias, zero_bias_first, gain_second,
        scale_bias_second, zero_bias_second, pair_weight,
    )
    early = (scale_first, shift_first, query_weight, key_weight, value_weight, gate_weight)
    late = (
        output_weight, zero_first, scale_second, shift_second, swish_weight, linear_weight,
        down_weight, zero_second,
    )
    small_all = lax.all_gather(pack_small(small, width), "samp", axis=0)
    early_all = lax.all_gather(pack_rows(early, width), "samp", axis=0)
    late_all = lax.all_gather(pack_rows(late, width), "samp", axis=0)
    (gain_one, bias_one, bias_query, bias_zero_one, gain_two, bias_two, bias_zero_two, pair_proj_w) = (
        unpack_small(small_all, [piece.shape for piece in small])
    )
    (w_scale, w_shift, w_query, w_key, w_value, w_gate) = unpack_rows(
        early_all, [piece.shape for piece in early]
    )
    (w_out, w_zero, w_scale_two, w_shift_two, w_swish, w_linear, w_down, w_zero_two) = unpack_rows(
        late_all, [piece.shape for piece in late]
    )

    pair_normed, pair_inverse = norm_rows(pair.astype(F32))
    pair_low = pair_normed.astype(BF16)
    pair_proj = jnp.einsum("sijc,ch->shij", pair_low, pair_proj_w, preferred_element_type=F32)
    bias_all = lax.all_gather(pair_proj.astype(BF16), "samp", axis=3, tiled=True)

    act_rows = act.reshape(total, width).astype(F32)
    cond_low = cond.reshape(total, cond_width)
    act_normed, act_inverse = norm_rows(act_rows)
    cond_normed, cond_inverse = norm_rows(cond_low.astype(F32))
    cond_first = (cond_normed * gain_one.astype(F32)).astype(BF16)
    sig_first = jax.nn.sigmoid(product(cond_first, w_scale) + bias_one.astype(F32))
    adapted = (sig_first * act_normed + product(cond_first, w_shift)).astype(BF16)
    key_rows = product(adapted, w_key).astype(BF16)
    value_rows = product(adapted, w_value).astype(BF16)
    query_rows = (product(adapted, w_query) + bias_query.astype(F32)).astype(BF16)
    gate_sig = jax.nn.sigmoid(product(adapted, w_gate))
    key_value = jnp.stack((key_rows, value_rows)).reshape(2, samples, rows, width)
    key_value = lax.all_gather(key_value, "head", axis=2, tiled=True)
    query_split = query_rows.reshape(samples, rows, width)
    attended, prob = plain(
        struct_of, struct_len, query_split, key_value[0], key_value[1], bias_all
    )
    attn_float = attended.reshape(total, width).astype(F32)

    gated_rows = (gate_sig * attn_float).astype(BF16)
    branch = product(gated_rows, w_out)
    zero_sig_first = jax.nn.sigmoid(product(cond_low, w_zero) + bias_zero_one.astype(F32))
    middle = act_rows + zero_sig_first * branch
    mid_normed, mid_inverse = norm_rows(middle)
    cond_second = (cond_normed * gain_two.astype(F32)).astype(BF16)
    sig_second = jax.nn.sigmoid(product(cond_second, w_scale_two) + bias_two.astype(F32))
    adapted_two = (sig_second * mid_normed + product(cond_second, w_shift_two)).astype(BF16)
    swish_pre = product(adapted_two, w_swish)
    linear_pre = product(adapted_two, w_linear)
    swish_sig = jax.nn.sigmoid(swish_pre)
    hidden = (swish_pre * swish_sig * linear_pre).astype(BF16)
    down_rows = product(hidden, w_down)
    zero_sig_second = jax.nn.sigmoid(product(cond_low, w_zero_two) + bias_zero_two.astype(F32))
    layer_out = (middle + zero_sig_second * down_rows).astype(BF16)

    upstream = cotangent.reshape(total, width).astype(F32)
    d_down = (upstream * zero_sig_second).astype(BF16)
    d_zero_second = (upstream * down_rows * sigmoid_slope(zero_sig_second)).astype(BF16)
    d_hidden = back_product(d_down, w_down)
    d_swish = (
        d_hidden * linear_pre * swish_sig * (1.0 + swish_pre * (1.0 - swish_sig))
    ).astype(BF16)
    d_linear = (d_hidden * swish_pre * swish_sig).astype(BF16)
    d_adapted_two = back_product(d_swish, w_swish) + back_product(d_linear, w_linear)
    d_shift_second = d_adapted_two.astype(BF16)
    d_pre_second = (d_adapted_two * mid_normed * sigmoid_slope(sig_second)).astype(BF16)
    d_cond_second = back_product(d_shift_second, w_shift_two) + back_product(
        d_pre_second, w_scale_two
    )
    d_middle = upstream + norm_back(mid_normed, mid_inverse, d_adapted_two * sig_second)
    d_branch = (d_middle * zero_sig_first).astype(BF16)
    d_zero_first = (d_middle * branch * sigmoid_slope(zero_sig_first)).astype(BF16)
    d_gated = back_product(d_branch, w_out)
    d_gate = (d_gated * attn_float * sigmoid_slope(gate_sig)).astype(BF16)
    d_attended = (d_gated * gate_sig).astype(BF16)

    late_grads = (
        outer_sum(gated_rows, d_branch),
        outer_sum(cond_low, d_zero_first),
        outer_sum(cond_second, d_pre_second),
        outer_sum(cond_second, d_shift_second),
        outer_sum(adapted_two, d_swish),
        outer_sum(adapted_two, d_linear),
        outer_sum(hidden, d_down),
        outer_sum(cond_low, d_zero_second),
    )

    d_query, d_key, d_value, bias_grad = plain_back(
        struct_of, structs, query_split, key_value[0], key_value[1],
        d_attended.reshape(samples, rows, width), prob,
    )
    d_key_value = lax.psum_scatter(
        jnp.stack((d_key, d_value)), "head", scatter_dimension=2, tiled=True
    )
    d_query = d_query.reshape(total, width)
    d_key = d_key_value[0].reshape(total, width)
    d_value = d_key_value[1].reshape(total, width)
    bias_summed = lax.psum_scatter(bias_grad, "samp", scatter_dimension=3, tiled=True)
    pair_weight_grad = jnp.einsum("sijc,shij->ch", pair_low, bias_summed, preferred_element_type=F32)
    pair_upstream = jnp.einsum(
        "shij,ch->sijc", bias_summed, pair_proj_w, preferred_element_type=F32
    )
    pair_grad = norm_back(pair_normed, pair_inverse, pair_upstream)
    d_adapted = (
        back_product(d_query, w_query)
        + back_product(d_key, w_key)
        + back_product(d_value, w_value)
        + back_product(d_gate, w_gate)
    )
    d_shift_first = d_adapted.astype(BF16)
    d_pre_first = (d_adapted * act_normed * sigmoid_slope(sig_first)).astype(BF16)
    d_cond_first = back_product(d_shift_first, w_shift) + back_product(d_pre_first, w_scale)
    input_grad = d_middle + norm_back(act_normed, act_inverse, d_adapted * sig_first)
    d_cond_normed = d_cond_first * gain_one.astype(F32) + d_cond_second * gain_two.astype(F32)
    cond_grad = (
        norm_back(cond_normed, cond_inverse, d_cond_normed)
        + back_product(d_zero_first, w_zero)
        + back_product(d_zero_second, w_zero_two)
    )
    early_grads = (
        outer_sum(cond_first, d_pre_first),
        outer_sum(cond_first, d_shift_first),
        outer_sum(adapted, d_query),
        outer_sum(adapted, d_key),
        outer_sum(adapted, d_value),
        outer_sum(adapted, d_gate),
    )
    small_grads = (
        jnp.sum(d_cond_first * cond_normed, axis=0),
        column_sum(d_pre_first),
        column_sum(d_query),
        column_sum(d_zero_first),
        jnp.sum(d_cond_second * cond_normed, axis=0),
        column_sum(d_pre_second),
        column_sum(d_zero_second),
        pair_weight_grad,
    )
    count = lax.axis_size("samp")

    def pack_grads(grads, shapes):
        pieces = [
            grad.astype(BF16).reshape(count, shape[0] * shape[1] // width, width)
            for grad, shape in zip(grads, shapes)
        ]
        return jnp.concatenate(pieces, axis=1)

    def reduce(packed):
        summed = lax.psum_scatter(packed, "samp", scatter_dimension=0, tiled=True)
        return lax.psum(summed[0], "head").astype(F32)

    late_sum = reduce(pack_grads(late_grads, [piece.shape for piece in late]))
    early_sum = reduce(pack_grads(early_grads, [piece.shape for piece in early]))
    small_flat = jnp.concatenate(
        [grad.astype(BF16).reshape(count, -1) for grad in small_grads], axis=1
    )
    small_sum = lax.psum(
        lax.psum_scatter(small_flat, "samp", scatter_dimension=0, tiled=True), "head"
    ).astype(F32)
    (g_out, g_zero, g_scale_two, g_shift_two, g_swish, g_linear, g_down, g_zero_two) = unpack_rows(
        late_sum[None], [piece.shape for piece in late]
    )
    (g_scale, g_shift, g_query, g_key, g_value, g_gate) = unpack_rows(
        early_sum[None], [piece.shape for piece in early]
    )
    (g_gain, g_bias, g_bias_query, g_bias_zero, g_gain_two, g_bias_two, g_bias_zero_two, g_pair) = (
        unpack_small(small_sum, [piece.shape for piece in small])
    )
    return (
        layer_out.reshape(act.shape), input_grad.reshape(act.shape), cond_grad.reshape(cond.shape),
        pair_grad, g_gain, g_scale, g_bias, g_shift, g_query, g_bias_query, g_key, g_value, g_gate,
        g_out, g_pair, g_zero, g_bias_zero, g_gain_two, g_scale_two, g_bias_two, g_shift_two,
        g_swish, g_linear, g_down, g_zero_two, g_bias_zero_two,
    )


def per_device(
    act, cond, pair, struct_of, struct_len,
    gain_first, scale_first, scale_bias_first, shift_first,
    query_weight, query_bias, key_weight, value_weight, gate_weight, output_weight,
    pair_weight, zero_first, zero_bias_first,
    gain_second, scale_second, scale_bias_second, shift_second,
    swish_weight, linear_weight, down_weight, zero_second, zero_bias_second,
    cotangent,
):
    samples, rows, width = act.shape
    cond_width = cond.shape[2]
    total = samples * rows
    count = lax.axis_size("samp")
    spans = lax.axis_size("head")
    heads = width // HEAD_DIM
    small = (
        gain_first, scale_bias_first, query_bias, zero_bias_first, gain_second,
        scale_bias_second, zero_bias_second,
    )
    early = (scale_first, shift_first, key_weight, value_weight, query_weight, gate_weight)
    late = (
        swish_weight, linear_weight, down_weight, output_weight, zero_first, scale_second, zero_second,
        shift_second,
    )
    packed_small = jnp.concatenate(
        [jnp.pad(piece, (0, LANES - piece.shape[0]))[None] for piece in small]
        + [jnp.zeros((1, LANES), BF16), jnp.pad(pair_weight.T, ((0, 0), (0, LANES - pair_weight.shape[0])))],
        axis=0,
    )
    act_rows = act.reshape(total, width)
    cond_rows = cond.reshape(total, cond_width)
    pair_turned = pair.transpose(0, 2, 1, 3)
    (attended, prob, adapted, sig_first, gate_sig, query_split, key_value, full, *whole) = front(
        struct_of, struct_len, act_rows, cond_rows, packed_small, pair_turned, early + late, samples, count,
        spans,
    )
    (layer_out, d_gate, d_attended, d_middle, d_cond_two, extra, vectors, *late_parts) = middle_part(
        attended, gate_sig, act_rows, cond_rows, cotangent.reshape(total, width), full, whole[6:]
    )
    d_query, d_key_value, bias_packed, late_sum = attend_back(
        struct_of, pair.shape[0], query_split, key_value, d_attended, prob, late_parts, count
    )
    (input_grad, cond_grad, pair_grad, small_sum, early_sum, late_total) = finish(
        act_rows, cond_rows, adapted, sig_first, full, d_query, d_key_value, d_gate, d_middle, d_cond_two,
        extra, vectors, bias_packed, late_sum, pair_turned, whole[:6],
    )
    (input_grad, cond_grad, pair_grad, *weight_grads) = deliver(
        input_grad, cond_grad, early_sum, late_total, pair_grad,
        ([piece.shape for piece in early], [piece.shape for piece in late]),
    )
    (g_scale, g_shift, g_key, g_value, g_query, g_gate) = weight_grads[:6]
    (g_swish, g_linear, g_down, g_out, g_zero, g_scale_two, g_zero_two, g_shift_two) = weight_grads[6:]

    def own(row, size):
        return small_sum[row, :size]

    cond_share, share = cond_width // count, width // count
    g_pair = small_sum[8:, : pair_weight.shape[0]].T
    return (
        layer_out.reshape(act.shape), input_grad.reshape(act.shape), cond_grad.reshape(cond.shape),
        pair_grad.transpose(0, 2, 1, 3), own(0, cond_share), g_scale, own(1, share), g_shift, g_query,
        own(2, share), g_key, g_value, g_gate, g_out, g_pair, g_zero, own(3, share), own(4, cond_share),
        g_scale_two, own(5, share), g_shift_two, g_swish, g_linear, g_down, g_zero_two, own(6, share),
    )


def fits(mesh, act, pair):
    samples, rows, width = act.shape
    count, spans = mesh.shape["samp"], mesh.shape["head"]
    block = pair.shape[2]
    tail = block - MAIN
    heads = width // HEAD_DIM
    return (
        count == 8
        and samples == 2
        and tail > 0
        and heads * tail == MAIN
        and rows % block == 0
        and rows * spans == block * count
        and rows % 8 == 0
        and block * count <= KEY_LANES
    )


def solution(mesh):
    tokens = P("samp", "head", None)
    pairs = P(None, "head", "samp", None)
    vector = P("samp")
    matrix = P("samp", None)
    weights = (
        vector, matrix, vector, matrix, matrix, vector, matrix, matrix, matrix, matrix, matrix,
        matrix, vector, vector, matrix, vector, matrix, matrix, matrix, matrix, matrix, vector,
    )
    def choose(*arrays):
        body = per_device if fits(mesh, arrays[0], arrays[2]) else plain_device
        return body(*arrays)

    return jax.shard_map(
        choose,
        mesh=mesh,
        in_specs=(tokens, tokens, pairs, vector, P()) + weights + (tokens,),
        out_specs=(tokens, tokens, tokens, pairs) + weights,
        check_vma=False,
    )
```

```python
import functools

import jax
import jax.numpy as jnp
from jax import lax
from jax.experimental import pallas as pl
from jax.experimental.pallas import tpu as pltpu
from jax.sharding import PartitionSpec as P

HEAD_DIM = 48
LANES = 128
MAIN = 64
KEY_LANES = 640
MESH = pl.DeviceIdType.MESH
EPSILON = 1e-05
NEG_BIG = -1000000000.0
F32 = jnp.float32
BF16 = jnp.bfloat16


def norm_rows(values):
    centered = values - jnp.mean(values, axis=-1, keepdims=True)
    variance = jnp.mean(centered * centered, axis=-1, keepdims=True)
    inverse = lax.rsqrt(variance + EPSILON)
    return (centered * inverse, inverse)


def norm_back(normed, inverse, upstream):
    mean_grad = jnp.mean(upstream, axis=-1, keepdims=True)
    mean_cross = jnp.mean(upstream * normed, axis=-1, keepdims=True)
    return inverse * (upstream - mean_grad - normed * mean_cross)


def product(left_side, right_side):
    return lax.dot_general(
        left_side, right_side, (((1,), (0,)), ((), ())), preferred_element_type=F32
    )


def back_product(upstream, right_side):
    return lax.dot_general(
        upstream, right_side, (((1,), (1,)), ((), ())), preferred_element_type=F32
    )


def outer_sum(left_side, upstream):
    return lax.dot_general(
        left_side, upstream, (((0,), (0,)), ((), ())), preferred_element_type=F32
    )


def column_sum(upstream):
    return jnp.sum(upstream.astype(F32), axis=0)


def sigmoid_slope(gate_sig):
    return gate_sig * (1.0 - gate_sig)


def head_windows(width):
    group = LANES * HEAD_DIM // 16
    group = min(group, width)
    windows = []
    for head in range(group // HEAD_DIM):
        first = head * HEAD_DIM
        last = first + HEAD_DIM - 1
        start = first // LANES * LANES
        stop = (last // LANES + 1) * LANES
        windows.append((start, stop - start, first - start))
    return (group, windows)


def head_mask(width, offset):
    lane = lax.broadcasted_iota(jnp.int32, (1, width), 1)
    return (lane >= offset) & (lane < offset + HEAD_DIM)


def dot_nt(left, right):
    return lax.dot_general(left, right, (((1,), (1,)), ((), ())), preferred_element_type=F32)


def dot_nn(left, right):
    return lax.dot_general(left, right, (((1,), (0,)), ((), ())), preferred_element_type=F32)


def dot_tn(left, right):
    return lax.dot_general(left, right, (((0,), (0,)), ((), ())), preferred_element_type=F32)


def tail_switch(count, heads, tail):
    lanes = count * heads * tail
    source = lax.broadcasted_iota(jnp.int32, (lanes, lanes), 0)
    target = lax.broadcasted_iota(jnp.int32, (lanes, lanes), 1)
    owner = source // (heads * tail)
    head = source % heads
    spot = head * (count * tail) + owner * tail + source // heads % tail
    return jnp.where(spot == target, 1.0, 0.0).astype(BF16)


def swap_halves(tile):
    return pltpu.roll(tile, MAIN, 1)


def low_half(tile):
    return lax.broadcasted_iota(jnp.int32, tile.shape, 1) < MAIN


def key_places(count, block):
    lane = lax.broadcasted_iota(jnp.int32, (1, KEY_LANES), 1)
    tail = block - MAIN
    spare = lane - count * MAIN
    main_at = lane + tail * (lane // MAIN)
    tail_at = block * (spare // tail) + MAIN + spare % tail
    past = jnp.where(spare < count * tail, tail_at, count * block)
    return jnp.where(spare < 0, main_at, past)


def flip(index, bit):
    return index + bit - 2 * bit * lax.rem(lax.div(index, bit), 2)


def flips(index, bits):
    spots = [index]
    for bit in bits:
        spots = spots + [flip(spot, bit) for spot in spots]
    return spots


def reduce_orders(count):
    bits = []
    bit = 2
    while bit < count:
        bits.append(bit)
        bit *= 2
    half = len(bits) // 2
    return ([1] + bits, [1] + bits[half:] + bits[:half])


def greet(partners):
    barrier = pltpu.get_barrier_semaphore()
    for partner in partners:
        pl.semaphore_signal(barrier, inc=1, device_id=partner, device_id_type=MESH)
    pl.semaphore_wait(barrier, len(partners))


def send(source, target, send_sem, recv_sem, device):
    return pltpu.make_async_remote_copy(
        src_ref=source, dst_ref=target, send_sem=send_sem, recv_sem=recv_sem,
        device_id=device, device_id_type=MESH,
    )


def sigmoid(values):
    return 1.0 / (1.0 + jnp.exp(-values))


def one_hot(shape, source_of):
    target = lax.broadcasted_iota(jnp.int32, shape, 0)
    source = lax.broadcasted_iota(jnp.int32, shape, 1)
    return jnp.where(source == source_of(target), 1.0, 0.0).astype(BF16)


def key_row_of(place, block, pieces):
    tail = block - MAIN
    main_at = place // MAIN * block + place % MAIN
    spare = place - pieces * MAIN
    tail_at = spare // tail * block + MAIN + spare % tail
    return jnp.where(place < pieces * MAIN, main_at, tail_at)


def pair_switch(heads):
    lanes = heads * MAIN
    source = lax.broadcasted_iota(jnp.int32, (lanes, lanes), 0)
    target = lax.broadcasted_iota(jnp.int32, (lanes, lanes), 1)
    return jnp.where(source % heads * MAIN + source // heads == target, 1.0, 0.0).astype(BF16)


def spread_heads(matrix, keys):
    channels, heads = matrix.shape
    one = lax.broadcasted_iota(jnp.int32, (heads, keys * heads), 0)
    two = lax.broadcasted_iota(jnp.int32, (heads, keys * heads), 1)
    repeat = dot_nn(matrix, jnp.where(two % heads == one, 1.0, 0.0).astype(BF16))
    owner = lax.broadcasted_iota(jnp.int32, (1, keys * heads), 1) // heads
    return [jnp.where(owner == key, repeat, 0.0).astype(BF16) for key in range(keys)]


def mean_pair():
    one = lax.broadcasted_iota(jnp.int32, (2 * LANES, 2 * LANES), 0) // LANES
    two = lax.broadcasted_iota(jnp.int32, (2 * LANES, 2 * LANES), 1) // LANES
    return jnp.where(one == two, 1.0 / LANES, 0.0).astype(BF16)


def norm_pair(low, means):
    centered = low.astype(F32) - dot_nn(low, means)
    variance = dot_nn((centered * centered).astype(BF16), means)
    inverse = lax.rsqrt(variance + EPSILON)
    return (centered * inverse, inverse)


GROUP = 16


def columns_of(project):
    size = project.shape[1]
    eye = one_hot((size, size), lambda row: row)
    return dot_nt(eye, project).astype(BF16)


def front_kernel(
    struct_ref, len_ref, act_ref, cond_ref, small_ref, pair_ref,
    *refs
):
    shards, refs = refs[:14], refs[14:]
    (out_ref, prob_out, adapted_ref, sig_ref, gate_ref, query_ref, kv_out, full_ref, *refs) = refs
    whole_outs, refs = refs[:14], refs[14:]
    (prob_ref, kv_ref, *refs) = refs
    wholes, refs = refs[:14], refs[14:]
    (scale_w, shift_w, key_w, value_w, query_w, gate_w) = wholes[:6]
    (
        small_all, pack_ref, pair_buf, lead_ref, spread_ref, keys_ref, values_ref, tail_ref, acc_ref,
        pair_sem, own_sem, small_send, small_recv, gather_send, gather_recv, pack_send, pack_recv,
        span_send, span_recv, whole_sem, prob_sem, kv_sem,
    ) = refs
    total, width = act_ref.shape
    samples, rows = out_ref.shape[0], out_ref.shape[1]
    count = pack_ref.shape[0]
    spans = kv_ref.shape[0]
    heads = width // HEAD_DIM
    structs = pair_ref.shape[0]
    block = pair_ref.shape[1]
    tail = block - MAIN
    pieces = rows // block
    main_rows = pieces * MAIN
    keys = count * block
    pairs = heads // 2
    group, windows = head_windows(width)
    me = lax.axis_index("samp")
    my_span = lax.axis_index("head")
    reduce_pair = reduce_orders(count)
    orders = [order[1:] + order[:1] for order in reduce_pair]
    bits = sorted(reduce_pair[0])
    steps = len(bits)
    peers = flips(me, bits)

    owns = [
        pltpu.make_async_copy(shard, whole.at[me], own_sem.at[at])
        for at, (shard, whole) in enumerate(zip(shards, wholes))
    ]
    for copy in owns:
        copy.start()

    loads = [
        pltpu.make_async_copy(pair_ref.at[struct], pair_buf.at[struct], pair_sem.at[struct])
        for struct in range(structs)
    ]
    for load in loads:
        load.start()
    whole_moves = [
        pltpu.make_async_copy(whole, out, whole_sem.at[at])
        for at, (whole, out) in enumerate(zip(wholes, whole_outs))
    ]
    prob_moves = [
        pltpu.make_async_copy(prob_ref.at[at], prob_out.at[at], prob_sem.at[at]) for at in range(samples)
    ]
    kv_move = pltpu.make_async_copy(kv_ref, kv_out, kv_sem.at[0])
    small_all[me] = small_ref[...]
    greet(
        [dict(samp=peer) for peer in peers[1:]]
        + [dict(head=lax.rem(my_span + away, spans)) for away in range(1, spans)]
    )
    for at in range(1, count):
        send(
            small_ref, small_all.at[me], small_send.at[at], small_recv.at[at], dict(samp=peers[at])
        ).start()

    def gather_copies(which, step, sending):
        order = orders[which % 2]
        held = flips(me, order[:step])
        copies = []
        for at, spot in enumerate(held):
            slot = spot if sending else flip(spot, order[step])
            copies.append(
                send(
                    shards[which] if at == 0 else wholes[which].at[slot], wholes[which].at[slot],
                    gather_send.at[which, step, at], gather_recv.at[which, step, at],
                    dict(samp=flip(me, order[step])),
                )
            )
        return copies

    def gather_start(pair_at, step):
        for which in (2 * pair_at, 2 * pair_at + 1):
            for copy in gather_copies(which, step, True):
                copy.start()

    def gather_wait(pair_at, step):
        for which in (2 * pair_at, 2 * pair_at + 1):
            for copy in gather_copies(which, step, False):
                copy.wait_recv()

    def late_start(step):
        for pair_at in range(3, 7):
            gather_start(pair_at, step)

    def late_out(pair_at):
        gather_wait(pair_at, 2)
        for which in (2 * pair_at, 2 * pair_at + 1):
            whole_moves[which].start()

    def late_wait(step):
        for pair_at in range(3, 7):
            gather_wait(pair_at, step)

    tiles = pack_ref.shape[1]
    halves = (pl.ds(0, tiles // 2), pl.ds(tiles // 2, tiles - tiles // 2))

    def pack_copies(half, step, sending):
        order = orders[half]
        copies = []
        for at, spot in enumerate(flips(me, order[:step])):
            slot = spot if sending else flip(spot, order[step])
            copies.append(
                send(
                    pack_ref.at[slot, halves[half]], pack_ref.at[slot, halves[half]],
                    pack_send.at[half, step, at], pack_recv.at[half, step, at],
                    dict(samp=flip(me, order[step])),
                )
            )
        return copies

    def pack_start(step):
        for half in range(2):
            for copy in pack_copies(half, step, True):
                copy.start()

    def pack_wait(step):
        for half in range(2):
            for copy in pack_copies(half, step, False):
                copy.wait_recv()

    gather_start(0, 0)
    gather_start(1, 0)

    for at in range(1, count):
        send(
            small_ref, small_all.at[peers[at]], small_send.at[at], small_recv.at[at], dict(samp=peers[at])
        ).wait_recv()
    share, cond_share = width // count, cond_ref.shape[1] // count
    channels = LANES // count
    blocks = [small_all[at].astype(F32) for at in range(count)]
    wide = jnp.concatenate([part[:8, :share] for part in blocks], axis=1)
    narrow = jnp.concatenate([part[:8, :cond_share] for part in blocks], axis=1)
    narrow = jnp.concatenate((narrow, jnp.zeros((8, width - narrow.shape[1]), F32)), axis=1)
    line = lax.broadcasted_iota(jnp.int32, (8, width), 0)
    turned = jnp.concatenate([part[8:, :channels] for part in blocks], axis=1)
    turned = jnp.concatenate((turned, jnp.zeros((heads, width - LANES), F32)), axis=1)
    full = jnp.concatenate((jnp.where((line == 0) | (line == 4), narrow, wide), turned), axis=0)
    full_ref[...] = full
    for at, part in enumerate(spread_heads(columns_of(full[8:, :LANES].astype(BF16)), GROUP)):
        spread_ref[at * LANES : (at + 1) * LANES] = part
    means = mean_pair()
    order_switch = pair_switch(heads)
    groups = MAIN // GROUP
    for load in loads:
        load.wait()

    def project_keys(struct, first, number):
        total_lead = None
        for at in range(number // 2):
            key = first + 2 * at
            low = jnp.concatenate((pair_buf[struct, key], pair_buf[struct, key + 1]), axis=1)
            normed, _ = norm_pair(low, means)
            lead = dot_nn(
                normed.astype(BF16),
                spread_ref[2 * at * LANES : (2 * at + 2) * LANES, : number * heads],
            )
            total_lead = lead if total_lead is None else total_lead + lead
        return total_lead.astype(BF16)

    def pair_group(turn, carry):
        lead_ref[turn] = project_keys(lax.div(turn, groups), lax.rem(turn, groups) * GROUP, GROUP)
        return carry

    turns = structs * groups
    cuts = [turns * at // 6 for at in range(7)]
    gather_wait(0, 0)
    gather_start(0, 1)
    gather_wait(1, 0)
    gather_start(1, 1)
    gather_start(2, 0)
    lax.fori_loop(cuts[0], cuts[1], pair_group, 0)
    gather_wait(0, 1)
    gather_start(0, 2)
    lax.fori_loop(cuts[1], cuts[2], pair_group, 0)
    gather_wait(2, 0)
    gather_start(2, 1)
    late_start(0)
    lax.fori_loop(cuts[2], cuts[3], pair_group, 0)
    gather_wait(1, 1)
    gather_start(1, 2)

    gain_one = full[0:1, : cond_ref.shape[1]]
    act_normed, _ = norm_rows(act_ref[...].astype(F32))
    cond_normed, _ = norm_rows(cond_ref[...].astype(F32))
    cond_first = (cond_normed * gain_one).astype(BF16)
    for copy in owns[:6]:
        copy.wait()
    gather_wait(0, 2)
    scale = scale_w[...].reshape(-1, width)
    shift = shift_w[...].reshape(-1, width)
    sig_first = sigmoid(dot_nn(cond_first, scale) + full[1:2])
    adapted = sig_first * act_normed + dot_nn(cond_first, shift)
    sig_ref[...] = sig_first
    adapted_ref[...] = adapted.astype(BF16)
    reorder = one_hot((rows, rows), lambda row: key_row_of(row, block, pieces))
    gather_wait(1, 2)
    for which, whole in ((0, key_w), (1, value_w)):
        for sample in range(samples):
            ordered = dot_nn(
                reorder, adapted[sample * rows : (sample + 1) * rows].astype(BF16)
            ).astype(BF16)
            kv_ref[my_span, which, sample] = dot_nn(ordered, whole[...].reshape(-1, width)).astype(BF16)

    def span_move(way, step, which, sending):
        delta = 1 - 2 * way
        shard = my_span - delta * step if sending else my_span - delta * (step + 1)
        target = my_span + delta
        there = (shard >= 0) & (shard < spans)
        if sending:
            there = there & (target >= 0) & (target < spans)
        copy = send(
            kv_ref.at[shard, which], kv_ref.at[shard, which],
            span_send.at[way, step, which], span_recv.at[way, step, which],
            dict(head=target if sending else my_span - delta),
        )
        return there, copy

    def span_start(step, which):
        for way in range(2):
            there, copy = span_move(way, step, which, True)
            pl.when(there)(copy.start)

    def span_wait(step, which):
        for way in range(2):
            there, copy = span_move(way, step, which, False)
            pl.when(there)(copy.wait_recv)

    span_start(0, 0)
    lax.fori_loop(cuts[3], cuts[6], pair_group, 0)
    for struct in range(structs):
        whole = jnp.concatenate([lead_ref[struct * groups + at] for at in range(groups)], axis=1)
        mixed = dot_nn(whole, order_switch).astype(BF16)
        for at in range(pairs):
            pack_ref[me, struct * pairs + at] = mixed[:, at * LANES : (at + 1) * LANES]
        rest = project_keys(struct, MAIN, tail)
        blank = jnp.zeros((rows, LANES - tail * heads), BF16)
        pack_ref[me, structs * pairs + struct] = jnp.concatenate((rest, blank), axis=1)
    pack_start(0)
    span_wait(0, 0)
    span_start(1, 0)
    span_start(0, 1)
    gather_wait(2, 1)
    gather_start(2, 2)
    low = adapted.astype(BF16)
    gather_wait(2, 2)
    for move in whole_moves[:6]:
        move.start()
    query = dot_nn(low, query_w[...].reshape(-1, width)) + full[2:3]
    for sample in range(samples):
        query_ref[sample] = query[sample * rows : (sample + 1) * rows].astype(BF16)
    pack_wait(0)
    pack_start(1)
    gate_ref[...] = sigmoid(dot_nn(low, gate_w[...].reshape(-1, width)))
    late_wait(0)
    late_start(1)
    for step in range(1, spans - 1):
        span_wait(step, 0)
        if step + 1 < spans - 1:
            span_start(step + 1, 0)
        span_wait(step - 1, 1)
        span_start(step, 1)
    pack_wait(1)
    pack_start(2)

    switch = tail_switch(count, heads, tail)
    places = key_places(count, block)
    keys_ref[keys:] = jnp.zeros_like(keys_ref[keys:])
    values_ref[keys:] = jnp.zeros_like(values_ref[keys:])

    def gather_keys(sample, which, held):
        for span in range(spans):
            held[span * main_rows : (span + 1) * main_rows] = kv_ref[span, which, sample, :main_rows]
            spot = count * MAIN + span * (rows - main_rows)
            held[spot : spot + rows - main_rows] = kv_ref[span, which, sample, main_rows:]

    def one_sample(sample, carry):
        struct = struct_ref[sample]
        valid = places < len_ref[struct]
        gather_keys(sample, 0, keys_ref)
        tiles_of = []
        for pair in range(count // 2):
            even = pack_ref[2 * pair, structs * pairs + struct]
            odd = swap_halves(pack_ref[2 * pair + 1, structs * pairs + struct])
            tiles_of.append(jnp.where(low_half(even), even, odd))
        mixed = dot_nn(jnp.concatenate(tiles_of, axis=1), switch).astype(BF16)
        for at in range(count // 2):
            tail_ref[at] = mixed[:, at * LANES : (at + 1) * LANES]

        def one_group(place, carry):
            for at, (start, span, offset) in enumerate(windows):
                lanes = pl.ds(pl.multiple_of(place * group + start, LANES), span)
                mask = head_mask(span, offset)
                tile = struct * pairs + place * (len(windows) // 2) + at // 2
                bias = []
                for pair in range(count // 2):
                    even = pack_ref[2 * pair, tile]
                    odd = pack_ref[2 * pair + 1, tile]
                    if at % 2 == 0:
                        bias.append(jnp.where(low_half(even), even, swap_halves(odd)))
                    else:
                        bias.append(jnp.where(low_half(even), swap_halves(even), odd))
                per_tile = LANES // (count * tail)
                rest = tail_ref[place * (len(windows) // per_tile) + at // per_tile]
                turn = at % per_tile * count * tail
                bias.append(pltpu.roll(rest, LANES - turn, 1) if turn else rest)
                query = query_ref[sample, :, lanes]
                query = jnp.where(mask, query, jnp.zeros_like(query))
                scores = dot_nt(query, keys_ref[:, lanes]) * HEAD_DIM ** (-0.5) + jnp.concatenate(
                    bias, axis=1
                ).astype(F32)
                scores = jnp.where(valid, scores, NEG_BIG)
                weights = jnp.exp(scores - jnp.max(scores, axis=1, keepdims=True))
                weights = weights * (1.0 / jnp.sum(weights, axis=1, keepdims=True))
                prob_ref[sample, place * len(windows) + at] = weights.astype(BF16)
            return carry

        return lax.fori_loop(0, width // group, one_group, carry)

    def mix_sample(sample, carry):
        gather_keys(sample, 1, values_ref)

        def mix_group(place, carry):
            acc_ref[...] = jnp.zeros_like(acc_ref)
            for at, (start, span, offset) in enumerate(windows):
                lanes = pl.ds(pl.multiple_of(place * group + start, LANES), span)
                weights = prob_ref[sample, place * len(windows) + at]
                mixed = dot_nn(weights, values_ref[:, lanes])
                within = slice(start, start + span)
                acc_ref[:, within] += jnp.where(head_mask(span, offset), mixed, 0.0)
            out_ref[sample, :, pl.ds(pl.multiple_of(place * group, LANES), group)] = acc_ref[
                ...
            ].astype(BF16)
            return carry

        return lax.fori_loop(0, width // group, mix_group, carry)

    pack_wait(2)
    lax.fori_loop(0, samples // 2, one_sample, 0)
    for move in prob_moves[: samples // 2]:
        move.start()
    span_wait(spans - 2, 1)
    kv_move.start()
    lax.fori_loop(samples // 2, samples, one_sample, 0)
    for move in prob_moves[samples // 2 :]:
        move.start()
    for copy in owns[6:]:
        copy.wait()
    for pair_at in range(3, 7):
        gather_wait(pair_at, 1)
        gather_start(pair_at, 2)
        if pair_at == 3:
            lax.fori_loop(0, samples, mix_sample, 0)
        else:
            late_out(pair_at - 1)
    late_out(6)
    for move in whole_moves + prob_moves + [kv_move]:
        move.wait()

    for at in range(1, count):
        send(
            small_ref, small_all.at[me], small_send.at[at], small_recv.at[at], dict(samp=peers[at])
        ).wait_send()
    for which in range(len(wholes)):
        for step in range(steps):
            for copy in gather_copies(which, step, True):
                copy.wait_send()
    for half in range(2):
        for step in range(steps):
            for copy in pack_copies(half, step, True):
                copy.wait_send()
    for step in range(spans - 1):
        for which in range(2):
            for way in range(2):
                there, copy = span_move(way, step, which, True)
                pl.when(there)(copy.wait_send)


def front(struct_of, struct_len, act, cond, small, pair, shards, samples, count, spans):
    total, width = act.shape
    rows = total // samples
    structs, block = pair.shape[0], pair.shape[1]
    heads = width // HEAD_DIM
    group, windows = head_windows(width)
    tail = block - MAIN
    tiles = structs * (heads // 2 + 1)
    steps = count.bit_length() - 1
    vmem = pl.BlockSpec(memory_space=pltpu.VMEM)
    smem = pl.BlockSpec(memory_space=pltpu.SMEM)
    far = pl.BlockSpec(memory_space=pl.ANY)
    dma = pltpu.SemaphoreType.DMA
    return pl.pallas_call(
        front_kernel,
        out_shape=(
            jax.ShapeDtypeStruct((samples, rows, width), BF16),
            jax.ShapeDtypeStruct((samples, heads, rows, KEY_LANES), BF16),
            jax.ShapeDtypeStruct((total, width), BF16),
            jax.ShapeDtypeStruct((total, width), F32),
            jax.ShapeDtypeStruct((total, width), F32),
            jax.ShapeDtypeStruct((samples, rows, width), BF16),
            jax.ShapeDtypeStruct((spans, 2, samples, rows, width), BF16),
            jax.ShapeDtypeStruct((small.shape[0], width), F32),
        )
        + tuple(jax.ShapeDtypeStruct((count,) + shard.shape, BF16) for shard in shards),
        in_specs=[smem, smem, vmem, vmem, vmem] + [far] * 15,
        out_specs=[vmem, far] + [vmem] * 4 + [far, vmem] + [far] * 14,
        scratch_shapes=[
            pltpu.VMEM((samples, heads, rows, KEY_LANES), BF16),
            pltpu.VMEM((spans, 2, samples, rows, width), BF16),
        ]
        + [pltpu.VMEM((count,) + shard.shape, BF16) for shard in shards]
        + [
            pltpu.VMEM((count,) + small.shape, BF16),
            pltpu.VMEM((count, tiles, rows, LANES), BF16),
            pltpu.VMEM(pair.shape, BF16),
            pltpu.VMEM((structs * MAIN // GROUP, rows, GROUP * heads), BF16),
            pltpu.VMEM((GROUP * LANES, GROUP * heads), BF16),
            pltpu.VMEM((KEY_LANES, width), BF16),
            pltpu.VMEM((KEY_LANES, width), BF16),
            pltpu.VMEM((count // 2, rows, LANES), BF16),
            pltpu.VMEM((rows, group), F32),
            dma((structs,)),
            dma((len(shards),)),
            dma((count,)),
            dma((count,)),
            dma((len(shards), steps, count // 2)),
            dma((len(shards), steps, count // 2)),
            dma((2, steps, count // 2)),
            dma((2, steps, count // 2)),
            dma((2, spans - 1, 2)),
            dma((2, spans - 1, 2)),
            dma((len(shards),)),
            dma((samples,)),
            dma((1,)),
        ],
        compiler_params=pltpu.CompilerParams(
            vmem_limit_bytes=60 << 20, collective_id=2, has_side_effects=True
        ),
        name="front",
    )(struct_of, struct_len, act, cond, small, pair, *shards)


def middle_kernel(
    attn_ref, gate_ref, act_ref, cond_ref, cot_ref, full_ref, *refs
):
    sources, refs = refs[:8], refs[8:]
    outs, refs = refs[7:15], refs[:7] + refs[15:]
    in_sem, out_sem = refs[23:]
    loads = [
        pltpu.make_async_copy(source, held, in_sem.at[at])
        for at, (source, held) in enumerate(zip(sources, refs[7:15]))
    ]
    leaves = [
        pltpu.make_async_copy(held, out, out_sem.at[at]) for at, (held, out) in enumerate(zip(refs[15:23], outs))
    ]
    for at in (3, 4, 5, 7, 0, 1, 2, 6):
        loads[at].start()
    ready = {id(held): load for held, load in zip(refs[7:15], loads)}
    leaving = {id(held): leave for held, leave in zip(refs[15:23], leaves)}
    middle_body(ready, leaving, attn_ref, gate_ref, act_ref, cond_ref, cot_ref, full_ref, *refs[:23])
    for leave in leaves:
        leave.wait()


def middle_body(
    ready, leaving, attn_ref, gate_ref, act_ref, cond_ref, cot_ref, full_ref, layer_ref, dgate_ref, dattn_ref, dmid_ref, dcond_ref, extra_ref, vector_ref,
    swish_w, linear_w, down_w, out_w, zero_w, scale_w, zero_two_w, shift_w, swish_g, linear_g, down_g, out_g, zero_g, scale_g, zero_two_g, shift_g,
):
    total, width = act_ref.shape
    samples, rows, _ = attn_ref.shape
    cond_width = cond_ref.shape[1]

    def whole(ref):
        load = ready.pop(id(ref), None)
        if load is not None:
            load.wait()
        return ref[...].reshape(-1, ref.shape[2])

    def store_grad(ref, left, right):
        size = ref.shape[1]
        step = 2 * size if size * 2 < left.shape[1] else size
        for first in range(0, left.shape[1], step):
            value = dot_tn(left[:, first : first + step], right).astype(BF16)
            for at in range(step // size):
                ref[first // size + at] = value[at * size : (at + 1) * size]
        leaving[id(ref)].start()

    cond = cond_ref[...]
    cond_normed, _ = norm_rows(cond.astype(F32))
    gain_two = full_ref[4:5, :cond_width]
    cond_second = (cond_normed * gain_two).astype(BF16)
    attn = jnp.concatenate([attn_ref[at].astype(F32) for at in range(samples)], axis=0)
    gate_sig = gate_ref[...]
    gated = (gate_sig * attn).astype(BF16)
    branch = dot_nn(gated, whole(out_w))
    zero_sig = sigmoid(dot_nn(cond, whole(zero_w)) + full_ref[3:4])
    middle = act_ref[...].astype(F32) + zero_sig * branch
    mid_normed, mid_inverse = norm_rows(middle)
    sig_second = sigmoid(dot_nn(cond_second, whole(scale_w)) + full_ref[5:6])
    adapted = (sig_second * mid_normed + dot_nn(cond_second, whole(shift_w))).astype(BF16)
    swish_pre = dot_nn(adapted, whole(swish_w))
    linear_pre = dot_nn(adapted, whole(linear_w))
    swish_sig = sigmoid(swish_pre)
    hidden = (swish_pre * swish_sig * linear_pre).astype(BF16)
    down_rows = dot_nn(hidden, whole(down_w))
    zero_sig_two = sigmoid(dot_nn(cond, whole(zero_two_w)) + full_ref[6:7])
    layer_ref[...] = (middle + zero_sig_two * down_rows).astype(BF16)

    upstream = cot_ref[...].astype(F32)
    d_down = (upstream * zero_sig_two).astype(BF16)
    d_zero_two = (upstream * down_rows * sigmoid_slope(zero_sig_two)).astype(BF16)
    store_grad(down_g, hidden, d_down)
    store_grad(zero_two_g, cond, d_zero_two)
    d_hidden = dot_nt(d_down, whole(down_w))
    d_swish = (d_hidden * linear_pre * swish_sig * (1.0 + swish_pre * (1.0 - swish_sig))).astype(BF16)
    d_linear = (d_hidden * swish_pre * swish_sig).astype(BF16)
    store_grad(swish_g, adapted, d_swish)
    store_grad(linear_g, adapted, d_linear)
    d_adapted = dot_nt(d_swish, whole(swish_w)) + dot_nt(d_linear, whole(linear_w))
    d_shift = d_adapted.astype(BF16)
    d_pre = (d_adapted * mid_normed * sigmoid_slope(sig_second)).astype(BF16)
    store_grad(scale_g, cond_second, d_pre)
    store_grad(shift_g, cond_second, d_shift)
    d_cond = dot_nt(d_shift, whole(shift_w)) + dot_nt(d_pre, whole(scale_w))
    dcond_ref[...] = d_cond * gain_two
    d_middle = upstream + norm_back(mid_normed, mid_inverse, d_adapted * sig_second)
    dmid_ref[...] = d_middle
    d_branch = (d_middle * zero_sig).astype(BF16)
    d_zero = (d_middle * branch * sigmoid_slope(zero_sig)).astype(BF16)
    store_grad(out_g, gated, d_branch)
    store_grad(zero_g, cond, d_zero)
    extra_ref[...] = dot_nt(d_zero, whole(zero_w)) + dot_nt(d_zero_two, whole(zero_two_w))
    d_gated = dot_nt(d_branch, whole(out_w))
    dgate_ref[...] = (d_gated * attn * sigmoid_slope(gate_sig)).astype(BF16)
    d_attn = d_gated * gate_sig
    for at in range(samples):
        dattn_ref[at] = d_attn[at * rows : (at + 1) * rows].astype(BF16)
    vector_ref[...] = jnp.zeros_like(vector_ref)
    vector_ref[3:4] = jnp.sum(d_zero.astype(F32), axis=0, keepdims=True)
    vector_ref[4:5, :cond_width] = jnp.sum(d_cond * cond_normed, axis=0, keepdims=True)
    vector_ref[5:6] = jnp.sum(d_pre.astype(F32), axis=0, keepdims=True)
    vector_ref[6:7] = jnp.sum(d_zero_two.astype(F32), axis=0, keepdims=True)


def middle_part(attended, gate_sig, act, cond, cotangent, full, weights):
    total, width = act.shape
    vmem = pl.BlockSpec(memory_space=pltpu.VMEM)
    far = pl.BlockSpec(memory_space=pl.ANY)
    weights = list(weights)
    return pl.pallas_call(
        middle_kernel,
        out_shape=(
            jax.ShapeDtypeStruct((total, width), BF16),
            jax.ShapeDtypeStruct((total, width), BF16),
            jax.ShapeDtypeStruct(attended.shape, BF16),
            jax.ShapeDtypeStruct((total, width), F32),
            jax.ShapeDtypeStruct(cond.shape, F32),
            jax.ShapeDtypeStruct(cond.shape, F32),
            jax.ShapeDtypeStruct(full.shape, F32),
        )
        + tuple(jax.ShapeDtypeStruct(weight.shape, BF16) for weight in weights),
        in_specs=[vmem] * 6 + [far] * 8,
        out_specs=[vmem] * 7 + [far] * 8,
        scratch_shapes=[pltpu.VMEM(weight.shape, BF16) for weight in weights + weights]
        + [pltpu.SemaphoreType.DMA((8,)), pltpu.SemaphoreType.DMA((8,))],
        compiler_params=pltpu.CompilerParams(vmem_limit_bytes=62 << 20),
        name="middle",
    )(attended, gate_sig, act, cond, cotangent, full, *weights)


class Halving:
    def __init__(self, me, order, source, zones, send_sem, recv_sem, stay=None, stay_sem=None):
        self.me, self.order, self.source, self.zones = me, order, source, zones
        self.send_sem, self.recv_sem = send_sem, recv_sem
        self.stay, self.stay_sem = stay, stay_sem

    def stays(self):
        if self.stay is None:
            return []
        return [
            pltpu.make_async_copy(self.source.at[spot], self.stay.at[at], self.stay_sem.at[at])
            for at, spot in enumerate(flips(self.me, self.order[1:]))
        ]

    def copies(self, step):
        kept = flips(self.me, self.order[step + 1 :])
        found = []
        for at, spot in enumerate(kept):
            if step == 0:
                leaving = self.source.at[flip(spot, self.order[0])]
            else:
                leaving = self.zones[step - 1].at[2 * at + 1]
            found.append(
                send(
                    leaving, self.zones[step].at[at], self.send_sem.at[step, at],
                    self.recv_sem.at[step, at], dict(samp=flip(self.me, self.order[step])),
                )
            )
        return found

    def start(self, step):
        for copy in self.copies(step) + (self.stays() if step == 0 else []):
            copy.start()

    def first(self, at, spot, lines):
        return self.source[spot, lines] if self.stay is None else self.stay[at, lines]

    def finish(self, step):
        kept = flips(self.me, self.order[step + 1 :])
        zone = self.zones[step]
        if step == 0:
            for copy in self.stays():
                copy.wait()
        for at, copy in enumerate(self.copies(step)):
            copy.wait_recv()

            def add(turn, carry, at=at):
                lines = pl.ds(pl.multiple_of(turn * 16, 16), 16)
                mine = self.first(at, kept[at], lines) if step == 0 else self.zones[step - 1][2 * at, lines]
                zone[at, lines] = (zone[at, lines].astype(F32) + mine.astype(F32)).astype(BF16)
                return carry

            lax.fori_loop(0, zone.shape[1] // 16, add, 0)

    def settle(self):
        for step in range(len(self.order)):
            for copy in self.copies(step):
                copy.wait_send()


def zone_shapes(shapes, count):
    zones = []
    for rows, columns in shapes:
        size = count // 2
        while size:
            zones.append(pltpu.VMEM((size, rows, columns), BF16))
            size //= 2
    return zones


def spans_of(shapes, columns, spans):
    lines = []
    for at, (rows, wide) in enumerate(shapes):
        for half in range(wide // columns):
            lines += [(at, row, half * columns) for row in range(0, rows, 8)]
    each = len(lines) // spans
    moves = []
    for piece in range(spans):
        row = 0
        for at, start, lane in lines[piece * each : (piece + 1) * each]:
            last = moves[-1] if moves else None
            if last and last[0] == piece and last[2] == at and last[4] == lane and last[3] + last[5] == start:
                moves[-1] = last[:5] + (last[5] + 8,)
            else:
                moves.append((piece, row, at, start, lane, 8))
            row += 8
    return (each * 8, moves)


def attend_back_kernel(
    late_shapes, struct_ref, q_ref, kv_ref, do_ref, prob_in, *refs
):
    lates, refs = refs[: len(late_shapes)], refs[len(late_shapes) :]
    (dq_ref, dkv_ref, dpb_ref, late_out, *refs) = refs
    steps = 3
    late_zones, refs = refs[: steps * len(late_shapes)], refs[steps * len(late_shapes) :]
    late_stay, refs = refs[: len(late_shapes)], refs[len(late_shapes) :]
    (late_send, late_recv, stay_sem, prob_ref, prob_sem, *refs) = refs
    each = prob_ref.shape[1] // 2

    def prob_copy(sample, place):
        heads_of = pl.ds(place * each, each)
        return pltpu.make_async_copy(
            prob_in.at[sample, heads_of], prob_ref.at[sample, heads_of], prob_sem.at[sample, place]
        )

    for place in range(2):
        for sample in range(prob_ref.shape[0]):
            prob_copy(sample, place).start()
    attend_back_body(
        prob_copy,
        late_shapes, struct_ref, q_ref, kv_ref, do_ref, prob_ref, lates, dq_ref, dkv_ref, dpb_ref, late_out,
        late_zones, late_stay, late_send, late_recv, stay_sem, *refs
    )


def attend_back_body(
    prob_copy, late_shapes, struct_ref, q_ref, kv_ref, do_ref, prob_ref, lates, dq_ref, dkv_ref, dpb_ref, late_out,
    late_zones, late_stay, late_send, late_recv, stay_sem,
    key_ref, value_ref, dq_acc, dk_acc, dv_acc, first_ref, tail_ref, part_ref, span_ref, pack_ref,
    got_zero, got_one, got_two, span_send, span_recv, pack_send, pack_recv,
):
    samples, rows, width = q_ref.shape
    count = pack_ref.shape[0]
    spans = kv_ref.shape[0]
    heads = width // HEAD_DIM
    block = rows * spans // count
    tail = block - MAIN
    structs = pack_ref.shape[1] // (heads // 2 + 1)
    main_rows = rows // block * MAIN
    keys = count * block
    group, windows = head_windows(width)
    scale = HEAD_DIM ** (-0.5)
    me = lax.axis_index("samp")
    my_span = lax.axis_index("head")
    orders = reduce_orders(count)
    others = [lax.rem(my_span + away, spans) for away in range(1, spans)]
    greet(
        [dict(samp=flip(me, bit)) for bit in sorted(orders[0])] + [dict(head=other) for other in others]
    )
    movers = [
        Halving(
            me, orders[at % 2], lates[at], late_zones[3 * at : 3 * at + 3], late_send.at[at], late_recv.at[at],
            late_stay[at], stay_sem.at[at],
        )
        for at in range(len(lates))
    ]
    for mover in movers:
        mover.start(0)
    switch = tail_switch(count, heads, tail)
    key_ref[keys:] = jnp.zeros_like(key_ref[keys:])
    value_ref[keys:] = jnp.zeros_like(value_ref[keys:])

    def span_copy(place, sample, away):
        lanes = pl.ds(pl.multiple_of(place * group, LANES), group)
        return send(
            part_ref.at[others[away], :, sample, :, lanes],
            span_ref.at[away, :, sample, :, lanes],
            span_send.at[place, sample, away],
            span_recv.at[place, sample, away],
            dict(head=others[away]),
        )

    def one_group(place, carry):
        for sample in range(samples):
            prob_copy(sample, place).wait()
            for span in range(spans):
                for which, held in ((0, key_ref), (1, value_ref)):
                    held[span * main_rows : (span + 1) * main_rows] = kv_ref[
                        span, which, sample, :main_rows, pl.ds(pl.multiple_of(place * group, LANES), group)
                    ]
                    spot = count * MAIN + span * (rows - main_rows)
                    held[spot : spot + rows - main_rows] = kv_ref[
                        span, which, sample, main_rows:, pl.ds(pl.multiple_of(place * group, LANES), group)
                    ]
            dq_acc[...] = jnp.zeros_like(dq_acc)
            dk_acc[...] = jnp.zeros_like(dk_acc)
            dv_acc[...] = jnp.zeros_like(dv_acc)
            kept = [jnp.where(struct_ref[0] == slab, 1.0, 0.0).astype(BF16) for slab in range(structs)]
            added = [jnp.where(struct_ref[1] == slab, 1.0, 0.0).astype(BF16) for slab in range(structs)]
            even_scores = None
            for at, (start, span, offset) in enumerate(windows):
                lanes = pl.ds(pl.multiple_of(place * group + start, LANES), span)
                within = slice(start, start + span)
                mask = head_mask(span, offset)
                upstream = do_ref[sample, :, lanes]
                upstream = jnp.where(mask, upstream, jnp.zeros_like(upstream))
                query = q_ref[sample, :, lanes]
                query = jnp.where(mask, query, jnp.zeros_like(query))
                low = prob_ref[sample, place * len(windows) + at]
                weights = low.astype(F32)
                d_weights = dot_nt(upstream, value_ref[:, within])
                dv_acc[:, within] += dot_tn(low[:, :keys], upstream)
                cross = weights * d_weights
                delta = jnp.sum(cross, axis=1, keepdims=True)
                d_scores = (cross - weights * delta).astype(BF16)
                dq_acc[:, within] += jnp.where(mask, dot_nn(d_scores, key_ref[:, within]), 0.0)
                dk_acc[:, within] += dot_tn(d_scores[:, :keys], query)
                per_tile = LANES // (count * tail)
                turn = at % per_tile * count * tail
                rest = d_scores[:, count * MAIN :]
                rest = pltpu.roll(rest, turn, 1) if turn else rest
                spot = place * (len(windows) // per_tile) + at // per_tile
                if turn:
                    tail_ref[sample, spot] += rest
                else:
                    tail_ref[sample, spot] = rest
                if at % 2 == 0:
                    even_scores = d_scores
                    continue
                for pair in range(count // 2):
                    even = even_scores[:, pair * LANES : (pair + 1) * LANES]
                    odd = d_scores[:, pair * LANES : (pair + 1) * LANES]
                    low_tile = jnp.where(low_half(even), even, swap_halves(odd))
                    high_tile = jnp.where(low_half(even), swap_halves(even), odd)
                    for side, tile in ((0, low_tile), (1, high_tile)):
                        owner = 2 * pair + side
                        if sample == 0:
                            first_ref[at // 2, owner] = tile
                            continue
                        old = first_ref[at // 2, owner]
                        for slab in range(structs):
                            spot = slab * (heads // 2) + place * (len(windows) // 2) + at // 2
                            pack_ref[owner, spot] = old * kept[slab] + tile * added[slab]
            lanes = pl.ds(pl.multiple_of(place * group, LANES), group)
            dq_ref[sample, :, lanes] = (dq_acc[...] * scale).astype(BF16)
            for span in range(spans):
                spot = count * MAIN + span * (rows - main_rows)
                for which, total, factor in ((0, dk_acc, scale), (1, dv_acc, 1.0)):
                    part_ref[span, which, sample, :main_rows, lanes] = (
                        total[span * main_rows : (span + 1) * main_rows] * factor
                    ).astype(BF16)
                    part_ref[span, which, sample, main_rows:, lanes] = (
                        total[spot : spot + rows - main_rows] * factor
                    ).astype(BF16)
            for away in range(spans - 1):
                span_copy(place, sample, away).start()
            if sample == 0:

                @pl.when(place == 0)
                def _():
                    for mover in movers:
                        mover.finish(0)
                        mover.start(1)

        return carry

    lax.fori_loop(0, width // group, one_group, 0)

    mixed = []
    for sample in range(samples):
        whole = jnp.concatenate([tail_ref[sample, at] for at in range(count // 2)], axis=1)
        mixed.append(dot_nt(whole, switch))
    for pair in range(count // 2):
        tiles = [part[:, pair * LANES : (pair + 1) * LANES] for part in mixed]
        for slab in range(structs):
            both = jnp.zeros_like(tiles[0])
            for sample in range(samples):
                both = both + jnp.where(struct_ref[sample] == slab, tiles[sample], 0.0)
            spot = structs * heads // 2 + slab
            pack_ref[2 * pair, spot] = jnp.where(low_half(both), both, 0.0).astype(BF16)
            pack_ref[2 * pair + 1, spot] = jnp.where(low_half(both), swap_halves(both), 0.0).astype(BF16)

    tiles = pack_ref.shape[1]
    halves = (pl.ds(0, tiles // 2), pl.ds(tiles // 2, tiles - tiles // 2))
    bounds = ((0, tiles // 2), (tiles // 2, tiles))
    landing = (got_zero, got_one, got_two)

    def stage_copies(step, half):
        order = orders[half]
        kept = flips(me, order[step + 1 :])
        return [
            send(
                pack_ref.at[flip(spot, order[step]), halves[half]],
                landing[step].at[at, halves[half]],
                pack_send.at[step, half, at],
                pack_recv.at[step, half, at],
                dict(samp=flip(me, order[step])),
            )
            for at, spot in enumerate(kept)
        ]

    flights = [[stage_copies(step, half) for half in range(2)] for step in range(len(orders[0]))]
    for half in range(2):
        for copy in flights[0][half]:
            copy.start()
    for step in range(len(orders[0])):
        for half in range(2):
            kept = flips(me, orders[half][step + 1 :])
            for at, spot in enumerate(kept):
                flights[step][half][at].wait_recv()

                def add(tile, carry, spot=spot, at=at, step=step):
                    pack_ref[spot, tile] = (
                        pack_ref[spot, tile].astype(F32) + landing[step][at, tile].astype(F32)
                    ).astype(BF16)
                    return carry

                lax.fori_loop(bounds[half][0], bounds[half][1], add, 0)
            if step + 1 < len(orders[0]):
                for copy in flights[step + 1][half]:
                    copy.start()
        if step == 0:
            for mover in movers:
                mover.finish(1)
                mover.start(2)
        if step == 1:
            for mover in movers:
                mover.finish(2)
            _, moves = spans_of(late_shapes, width, spans)
            for piece, row, at, start, lane, size in moves:
                late_out[piece, row : row + size] = movers[at].zones[2][
                    0, start : start + size, lane : lane + width
                ]

    def out(tile, carry):
        dpb_ref[tile] = pack_ref[me, tile]
        return carry

    lax.fori_loop(0, tiles, out, 0)

    for place in range(width // group):
        for sample in range(samples):
            for away in range(spans - 1):
                span_copy(place, sample, away).wait_recv()
    for which in range(2):
        for sample in range(samples):
            total = part_ref[my_span, which, sample].astype(F32)
            for away in range(spans - 1):
                total += span_ref[away, which, sample].astype(F32)
            dkv_ref[which, sample] = total.astype(BF16)
    for place in range(width // group):
        for sample in range(samples):
            for away in range(spans - 1):
                span_copy(place, sample, away).wait_send()
    for stage in flights:
        for half in stage:
            for copy in half:
                copy.wait_send()
    for mover in movers:
        mover.settle()


def attend_back(struct_of, structs, query, key_value, upstream, prob, lates, count):
    samples, rows, width = query.shape
    spans = key_value.shape[0]
    heads = width // HEAD_DIM
    group, windows = head_windows(width)
    keys = rows * spans
    tiles = structs * (heads // 2 + 1)
    steps = count.bit_length() - 1
    vmem = pl.BlockSpec(memory_space=pltpu.VMEM)
    smem = pl.BlockSpec(memory_space=pltpu.SMEM)
    late_shapes = [late.shape[1:] for late in lates]
    each, _ = spans_of(late_shapes, width, spans)
    dma = pltpu.SemaphoreType.DMA
    return pl.pallas_call(
        functools.partial(attend_back_kernel, late_shapes),
        out_shape=(
            jax.ShapeDtypeStruct((samples, rows, width), BF16),
            jax.ShapeDtypeStruct((2, samples, rows, width), BF16),
            jax.ShapeDtypeStruct((tiles, rows, LANES), BF16),
            jax.ShapeDtypeStruct((spans, each, width), BF16),
        ),
        in_specs=[smem] + [vmem] * 3 + [pl.BlockSpec(memory_space=pl.ANY)] * (1 + len(lates)),
        out_specs=[vmem] * 4,
        scratch_shapes=zone_shapes(late_shapes, count)
        + [pltpu.VMEM((count // 2,) + shape, BF16) for shape in late_shapes]
        + [
            dma((len(lates), steps, count // 2)),
            dma((len(lates), steps, count // 2)),
            dma((len(lates), count // 2)),
            pltpu.VMEM(prob.shape, BF16),
            dma((samples, 2)),
            pltpu.VMEM((KEY_LANES, group), BF16),
            pltpu.VMEM((KEY_LANES, group), BF16),
            pltpu.VMEM((rows, group), F32),
            pltpu.VMEM((keys, group), F32),
            pltpu.VMEM((keys, group), F32),
            pltpu.VMEM((len(windows) // 2, count, rows, LANES), BF16),
            pltpu.VMEM((samples, count // 2, rows, LANES), BF16),
            pltpu.VMEM((spans, 2, samples, rows, width), BF16),
            pltpu.VMEM((spans - 1, 2, samples, rows, width), BF16),
            pltpu.VMEM((count, tiles, rows, LANES), BF16),
            pltpu.VMEM((count // 2, tiles, rows, LANES), BF16),
            pltpu.VMEM((count // 4, tiles, rows, LANES), BF16),
            pltpu.VMEM((count // 8, tiles, rows, LANES), BF16),
            pltpu.SemaphoreType.DMA((width // group, samples, spans - 1)),
            pltpu.SemaphoreType.DMA((width // group, samples, spans - 1)),
            pltpu.SemaphoreType.DMA((steps, 2, count // 2)),
            pltpu.SemaphoreType.DMA((steps, 2, count // 2)),
        ],
        compiler_params=pltpu.CompilerParams(
            vmem_limit_bytes=60 << 20, collective_id=1, has_side_effects=True
        ),
        name="attend_back",
    )(struct_of, query, key_value, upstream, prob, *lates)


class ChainSum:
    def __init__(self, place, places, source, got, whole, send_sem, recv_sem):
        self.place, self.places, self.source, self.got, self.whole = place, places, source, got, whole
        self.send_sem, self.recv_sem = send_sem, recv_sem

    def ways(self):
        return ((0, 1, self.place), (1, -1, self.places - 1 - self.place))

    def owner(self, way, spot):
        return spot if way == 0 else self.places - 1 - spot

    def partial(self, way, delta, tick, leaving):
        return send(
            leaving, self.got.at[way, tick], self.send_sem.at[0, way, tick], self.recv_sem.at[0, way, tick],
            dict(head=self.place + delta),
        )

    def each_partial(self, tick, act):
        for way, delta, spot in self.ways():
            piece = self.places - 1 - tick + spot
            sends = (tick >= spot) & (piece > spot)

            @pl.when(sends & (spot == 0))
            def _(way=way, delta=delta, piece=piece):
                act(self.partial(way, delta, tick, self.source.at[self.owner(way, piece)]))

            if tick:

                @pl.when(sends & (spot > 0))
                def _(way=way, delta=delta):
                    act(self.partial(way, delta, tick, self.got.at[way, tick - 1]))

    def start(self, tick):
        self.each_partial(tick, lambda copy: copy.start())

    def add(self, target, spot, source):
        size = 24

        def step(turn, carry):
            lines = pl.ds(pl.multiple_of(turn * size, 8), size)
            target[spot + (lines,)] = (
                target[spot + (lines,)].astype(F32) + source(lines).astype(F32)
            ).astype(BF16)
            return carry

        lax.fori_loop(0, self.source.shape[1] // size, step, 0)

    def receive(self, tick):
        for way, delta, spot in self.ways():
            piece = self.places - 2 - tick + spot

            @pl.when((spot >= 1) & (tick >= spot - 1))
            def _(way=way, delta=delta, piece=piece):
                self.partial(way, delta, tick, self.got.at[way, tick]).wait_recv()
                if tick < self.places - 2:
                    mine = self.owner(way, piece)
                    self.add(self.got, (way, tick), lambda lines: self.source[mine, lines])

    def total(self):
        self.whole[self.place] = self.source[self.place]
        for way, delta, spot in self.ways():

            @pl.when(spot >= 1)
            def _(way=way):
                self.add(self.whole, (self.place,), lambda lines: self.got[way, self.places - 2, lines])

    def passing(self, way, delta, step, sending):
        piece = self.place - delta * step if sending else self.place - delta * (step + 1)
        target = self.place + delta
        there = (piece >= 0) & (piece < self.places)
        if sending:
            there = there & (target >= 0) & (target < self.places)
        copy = send(
            self.whole.at[piece], self.whole.at[piece], self.send_sem.at[1, way, step],
            self.recv_sem.at[1, way, step], dict(head=target if sending else self.place - delta),
        )
        return there, copy

    def spread_start(self, step):
        for way, delta, _ in self.ways():
            there, copy = self.passing(way, delta, step, True)
            pl.when(there)(copy.start)

    def spread_wait(self, step):
        for way, delta, _ in self.ways():
            there, copy = self.passing(way, delta, step, False)
            pl.when(there)(copy.wait_recv)

    def settle(self):
        for tick in range(self.places - 1):
            self.each_partial(tick, lambda copy: copy.wait_send())
            for way, delta, _ in self.ways():
                there, copy = self.passing(way, delta, tick, True)
                pl.when(there)(copy.wait_send)


def finish_kernel(
    early_shapes,
    act_ref, cond_ref, adapted_ref, sig_ref, full_ref, dq_ref, dkv_ref, dgate_ref, dmid_ref, dcond_ref,
    extra_ref, vector_ref, dpb_ref, late_ref, pair_ref, *refs
):
    weights_in, refs = refs[:6], refs[6:]
    (ig_ref, cg_ref, pg_ref, small_out, early_all, late_all, *refs) = refs
    grads, refs = refs[: len(early_shapes)], refs[len(early_shapes) :]
    zones, refs = refs[: 3 * len(early_shapes)], refs[3 * len(early_shapes) :]
    (
        early_ref, early_got, late_got, small_ref, small_got, sum_ref, sum_got,
        pair_buf, lead_ref, lead_turned, spread_ref, block_ref, tail_block, weight_acc,
        pair_sem, block_sem, grad_send, grad_recv, late_send, late_recv, early_send, early_recv,
        small_send, small_recv, sum_send, sum_recv, weight_sem, *weights_here
    ) = refs
    (scale_w, shift_w, key_w, value_w, query_w, gate_w) = weights_here
    weight_loads = [
        pltpu.make_async_copy(source, held, weight_sem.at[at])
        for at, (source, held) in enumerate(zip(weights_in, weights_here))
    ]
    total, width = act_ref.shape
    count = grads[0].shape[0]
    spans = late_ref.shape[0]
    structs, block, rows, _ = pair_buf.shape
    samples = total // rows
    heads = width // HEAD_DIM
    tail = block - MAIN
    pieces = rows // block
    pairs = heads // 2
    me = lax.axis_index("samp")
    my_span = lax.axis_index("head")
    orders = reduce_orders(count)
    peers = flips(me, sorted(orders[0]))
    others = [lax.rem(my_span + away, spans) for away in range(1, spans)]

    loads = [
        pltpu.make_async_copy(pair_ref.at[struct], pair_buf.at[struct], pair_sem.at[struct])
        for struct in range(structs)
    ]
    for load in weight_loads + loads:
        load.start()
    greet([dict(samp=peer) for peer in peers[1:]] + [dict(head=other) for other in others])

    late_sum = ChainSum(my_span, spans, late_ref, late_got, late_all, late_send, late_recv)
    early_sum = ChainSum(my_span, spans, early_ref, early_got, early_all, early_send, early_recv)
    late_sum.start(0)

    adapted = adapted_ref[...]
    back = one_hot((rows, rows), lambda row: row)
    place = lax.broadcasted_iota(jnp.int32, (rows, rows), 1)
    row = lax.broadcasted_iota(jnp.int32, (rows, rows), 0)
    back = jnp.where(row == key_row_of(place, block, pieces), 1.0, 0.0).astype(BF16)
    d_query = jnp.concatenate([dq_ref[at].astype(F32) for at in range(samples)], axis=0).astype(BF16)
    d_key, d_value = [
        jnp.concatenate([dot_nn(back, dkv_ref[which, at]) for at in range(samples)], axis=0).astype(BF16)
        for which in range(2)
    ]
    d_gate = dgate_ref[...]

    def store_grad(at, left, right):
        size = grads[at].shape[1]
        value = dot_tn(left, right).astype(BF16)
        for owner in range(count):
            grads[at][owner] = value[owner * size : (owner + 1) * size]

    movers = [
        Halving(
            me, orders[at % 2], grads[at], zones[3 * at : 3 * at + 3], grad_send.at[at], grad_recv.at[at]
        )
        for at in range(len(grads))
    ]
    for at, upstream in ((2, d_key), (3, d_value), (4, d_query), (5, d_gate)):
        store_grad(at, adapted, upstream)
        movers[at].start(0)
    late_sum.receive(0)
    late_sum.start(1)
    for mover in movers[2:]:
        mover.finish(0)
        mover.start(1)

    for load in weight_loads:
        load.wait()
    d_adapted = dot_nt(d_query, query_w[...].reshape(-1, width))
    d_adapted += dot_nt(d_key, key_w[...].reshape(-1, width))
    d_adapted += dot_nt(d_value, value_w[...].reshape(-1, width))
    d_adapted += dot_nt(d_gate, gate_w[...].reshape(-1, width))
    gain_one = full_ref[0:1, : cond_ref.shape[1]]
    act_normed, act_inverse = norm_rows(act_ref[...].astype(F32))
    cond_normed, cond_inverse = norm_rows(cond_ref[...].astype(F32))
    cond_first = (cond_normed * gain_one).astype(BF16)
    sig_first = sig_ref[...]
    d_shift = d_adapted.astype(BF16)
    d_pre = (d_adapted * act_normed * sigmoid_slope(sig_first)).astype(BF16)
    store_grad(0, cond_first, d_pre)
    store_grad(1, cond_first, d_shift)
    movers[0].start(0)
    movers[1].start(0)
    for mover in movers[:2]:
        mover.finish(0)
        mover.start(1)
    late_sum.receive(1)
    late_sum.start(2)
    ig_ref[...] = dmid_ref[...] + norm_back(act_normed, act_inverse, d_adapted * sig_first)
    d_cond = dot_nt(d_shift, shift_w[...].reshape(-1, width)) + dot_nt(d_pre, scale_w[...].reshape(-1, width))
    cg_ref[...] = norm_back(cond_normed, cond_inverse, d_cond * gain_one + dcond_ref[...]) + extra_ref[...]
    small_ref[...] = vector_ref[...]
    small_ref[0:1, : cond_ref.shape[1]] = jnp.sum(d_cond * cond_normed, axis=0, keepdims=True)
    small_ref[1:2] = jnp.sum(d_pre.astype(F32), axis=0, keepdims=True)
    small_ref[2:3] = jnp.sum(d_query.astype(F32), axis=0, keepdims=True)

    project = full_ref[8:, :LANES]
    project = (project - jnp.mean(project, axis=1, keepdims=True)).astype(BF16)
    columns = columns_of(project)
    for at, part in enumerate(spread_heads(columns, GROUP)):
        spread_ref[at * LANES : (at + 1) * LANES] = part
    switch = pair_switch(heads)
    means = mean_pair()
    groups = MAIN // GROUP
    for struct in range(structs):
        whole = jnp.concatenate([dpb_ref[struct * pairs + at] for at in range(pairs)], axis=1)
        mixed = dot_nt(whole, switch).astype(BF16)
        for at in range(groups):
            lead_ref[struct * groups + at] = mixed[:, at * GROUP * heads : (at + 1) * GROUP * heads]
    turn_eye = one_hot((rows, rows), lambda line: line)
    weight_acc[...] = jnp.zeros_like(weight_acc)
    for load in loads:
        load.wait()

    def back_keys(struct, first, keys, lead, target):
        for at in range(keys // 2):
            key = first + 2 * at
            low = jnp.concatenate((pair_buf[struct, key], pair_buf[struct, key + 1]), axis=1)
            normed, inverse = norm_pair(low, means)
            upstream = dot_nt(lead, spread_ref[2 * at * LANES : (2 * at + 2) * LANES, : lead.shape[1]])
            cross = dot_nn((upstream * normed).astype(BF16), means)
            result = inverse * (upstream - normed * cross)
            target(2 * at, result[:, :LANES])
            target(2 * at + 1, result[:, LANES:])
            kept = normed.astype(BF16)
            for side in range(2):
                turned = lead_turned[(2 * at + side) * heads : (2 * at + side + 1) * heads]
                weight_acc[...] += dot_nn(turned, kept[:, side * LANES : (side + 1) * LANES])

    def block_copy(turn):
        slot = lax.rem(turn, 2)
        return pltpu.make_async_copy(
            block_ref.at[slot],
            pg_ref.at[lax.div(turn, groups), pl.ds(lax.rem(turn, groups) * GROUP, GROUP)],
            block_sem.at[slot],
        )

    def pair_group(turn, carry):
        @pl.when(turn >= 2)
        def _():
            block_copy(turn - 2).wait()

        slot = lax.rem(turn, 2)
        lead = lead_ref[turn]
        lead_turned[...] = dot_tn(lead, turn_eye).astype(BF16)

        def target(at, value):
            block_ref[slot, at] = value.astype(BF16)

        back_keys(lax.div(turn, groups), lax.rem(turn, groups) * GROUP, GROUP, lead, target)
        block_copy(turn).start()
        return carry

    turns = structs * groups
    late_sum.receive(2)
    late_sum.total()
    late_sum.spread_start(0)

    def stage(number):
        for mover in movers[2:] + movers[:2]:
            mover.finish(number)
            if number < 2:
                mover.start(number + 1)

    def lead_sum():
        stage(2)
        _, moves = spans_of(early_shapes, width, spans)
        for piece, line, at, start, lane, size in moves:
            early_ref[piece, line : line + size] = movers[at].zones[2][
                0, start : start + size, lane : lane + width
            ]
        early_sum.start(0)

    def early_turn(tick):
        early_sum.receive(tick)
        early_sum.start(tick + 1)

    def late_turn(step):
        late_sum.spread_wait(step)
        late_sum.spread_start(step + 1)

    events = {
        1: lambda: stage(1),
        2: lambda: late_turn(0),
        5: lead_sum,
        6: lambda: late_turn(1),
        8: lambda: early_turn(0),
        10: lambda: early_turn(1),
    }

    def pair_turn(turn, carry):
        pair_group(turn, carry)
        for at, event in events.items():
            pl.when(turn == at)(event)
        return carry

    lax.fori_loop(0, turns, pair_turn, 0)
    late_sum.spread_wait(2)
    early_sum.receive(2)
    early_sum.total()
    early_sum.spread_start(0)
    for struct in range(structs):
        lead = dpb_ref[structs * pairs + struct]
        lead = lead[:, : tail * heads]
        lead_turned[: tail * heads] = dot_tn(lead, turn_eye).astype(BF16)

        def tail_target(at, value, struct=struct):
            tail_block[struct, at] = value.astype(BF16)

        back_keys(struct, MAIN, tail, lead, tail_target)
    tail_copies = [
        pltpu.make_async_copy(
            tail_block.at[struct], pg_ref.at[struct, pl.ds(MAIN, tail)], pair_sem.at[struct]
        )
        for struct in range(structs)
    ]
    for copy in tail_copies:
        copy.start()
    small_ref[8:, :LANES] = weight_acc[...]
    early_sum.spread_wait(0)
    early_sum.spread_start(1)

    def small_copies(sending):
        return [
            send(
                small_ref, small_got.at[me if sending else peers[at]], small_send.at[at], small_recv.at[at],
                dict(samp=peers[at]),
            )
            for at in range(1, count)
        ]

    def sum_copies(sending):
        return [
            send(
                sum_ref, sum_got.at[my_span if sending else lax.rem(my_span + spans - 1 - at, spans)],
                sum_send.at[at], sum_recv.at[at], dict(head=other),
            )
            for at, other in enumerate(others)
        ]

    for copy in small_copies(True):
        copy.start()
    small_got[me] = small_ref[...]
    for copy in small_copies(False):
        copy.wait_recv()
    summed = small_got[0]
    for at in range(1, count):
        summed = summed + small_got[at]
    sum_ref[...] = summed
    for copy in sum_copies(True):
        copy.start()
    sum_got[my_span] = summed
    early_sum.spread_wait(1)
    early_sum.spread_start(2)
    for copy in sum_copies(False):
        copy.wait_recv()
    summed = sum_got[0]
    for at in range(1, spans):
        summed = summed + sum_got[at]
    share, cond_share = width // count, cond_ref.shape[1] // count
    channels = LANES // count

    def own(rows_of, size):
        part = jnp.where(me == 0, rows_of[:, :size], 0.0)
        for at in range(1, count):
            part = part + jnp.where(me == at, rows_of[:, at * size : (at + 1) * size], 0.0)
        return jnp.concatenate((part, jnp.zeros((part.shape[0], LANES - size), F32)), axis=1)

    line = lax.broadcasted_iota(jnp.int32, (8, LANES), 0)
    vectors_own = jnp.where((line == 0) | (line == 4), own(summed[:8], cond_share), own(summed[:8], share))
    small_out[...] = jnp.concatenate((vectors_own, own(summed[8:], channels)), axis=0)
    early_sum.spread_wait(2)

    block_copy(turns - 2).wait()
    block_copy(turns - 1).wait()
    for copy in tail_copies:
        copy.wait()
    for mover in movers:
        mover.settle()
    late_sum.settle()
    early_sum.settle()
    for copy in small_copies(True) + sum_copies(True):
        copy.wait_send()


def finish(
    act, cond, adapted, sig, full, d_query, d_key_value, d_gate, d_middle, d_cond, extra, vectors, packed,
    late, pair, weights,
):
    total, width = act.shape
    cond_width = cond.shape[1]
    spans, late_each, _ = late.shape
    count = weights[0].shape[0]
    structs, block, rows, _ = pair.shape
    heads = width // HEAD_DIM
    tail = block - MAIN
    early_shapes = [weight.shape[1:] for weight in weights]
    early_each, _ = spans_of(early_shapes, width, spans)
    steps = count.bit_length() - 1
    vmem = pl.BlockSpec(memory_space=pltpu.VMEM)
    far = pl.BlockSpec(memory_space=pl.ANY)
    dma = pltpu.SemaphoreType.DMA
    turns = structs * (MAIN // GROUP)
    return pl.pallas_call(
        functools.partial(finish_kernel, early_shapes),
        out_shape=(
            jax.ShapeDtypeStruct((total, width), F32),
            jax.ShapeDtypeStruct((total, cond_width), F32),
            jax.ShapeDtypeStruct(pair.shape, BF16),
            jax.ShapeDtypeStruct((full.shape[0], LANES), F32),
            jax.ShapeDtypeStruct((spans, early_each, width), BF16),
            jax.ShapeDtypeStruct((spans, late_each, width), BF16),
        ),
        in_specs=[vmem] * 14 + [far] * 7,
        out_specs=[vmem, vmem, far, vmem, vmem, vmem],
        scratch_shapes=[pltpu.VMEM(weight.shape, BF16) for weight in weights]
        + zone_shapes(early_shapes, count)
        + [
            pltpu.VMEM((spans, early_each, width), BF16),
            pltpu.VMEM((2, spans - 1, early_each, width), BF16),
            pltpu.VMEM((2, spans - 1, late_each, width), BF16),
            pltpu.VMEM(full.shape, F32),
            pltpu.VMEM((count,) + full.shape, F32),
            pltpu.VMEM(full.shape, F32),
            pltpu.VMEM((spans,) + full.shape, F32),
            pltpu.VMEM(pair.shape, BF16),
            pltpu.VMEM((turns, rows, GROUP * heads), BF16),
            pltpu.VMEM((GROUP * heads, rows), BF16),
            pltpu.VMEM((GROUP * LANES, GROUP * heads), BF16),
            pltpu.VMEM((2, GROUP, rows, LANES), BF16),
            pltpu.VMEM((structs, tail, rows, LANES), BF16),
            pltpu.VMEM((heads, LANES), F32),
            dma((structs,)),
            dma((2,)),
            dma((len(weights), steps, count // 2)),
            dma((len(weights), steps, count // 2)),
            dma((2, 2, spans - 1)),
            dma((2, 2, spans - 1)),
            dma((2, 2, spans - 1)),
            dma((2, 2, spans - 1)),
            dma((count,)),
            dma((count,)),
            dma((spans,)),
            dma((spans,)),
            dma((len(weights),)),
        ]
        + [pltpu.VMEM(weight.shape, BF16) for weight in weights],
        compiler_params=pltpu.CompilerParams(
            vmem_limit_bytes=60 << 20, collective_id=3, has_side_effects=True
        ),
        name="finish",
    )(
        act, cond, adapted, sig, full, d_query, d_key_value, d_gate, d_middle, d_cond, extra, vectors, packed,
        late, pair, *weights
    )


def deliver_kernel(shapes, ig_in, cg_in, early_in, late_in, pair_in, ig_out, cg_out, pair_ref, *refs):
    number = len(shapes[0]) + len(shapes[1])
    outs, held = refs[:number], refs[number : 2 * number]
    sems = refs[2 * number]
    moves = [pltpu.make_async_copy(ig_in, ig_out, sems.at[0]), pltpu.make_async_copy(cg_in, cg_out, sems.at[1])]
    moves += [
        pltpu.make_async_copy(part, out, sems.at[2 + at]) for at, (part, out) in enumerate(zip(held, outs))
    ]
    pair_ref[...] = pair_in[...].astype(F32)

    @pl.when(pl.program_id(0) == 0)
    def _():
        spans, _, width = early_in.shape
        first = 0
        for part, source in zip(shapes, (early_in, late_in)):
            _, places = spans_of(part, width, spans)
            for piece, line, at, start, lane, size in places:
                held[first + at][start : start + size, lane : lane + width] = source[
                    piece, line : line + size
                ].astype(F32)
            first += len(part)
        for move in moves:
            move.start()

    @pl.when(pl.program_id(0) == pl.num_programs(0) - 1)
    def _():
        for move in moves:
            move.wait()


def deliver(input_grad, cond_grad, early, late, pair_grad, shapes):
    structs, block, rows, channels = pair_grad.shape
    turn = block // 2

    def whole(shape):
        return pl.BlockSpec(tuple(shape), lambda at: (0,) * len(shape), pipeline_mode=pl.Buffered(1))

    far = pl.BlockSpec(memory_space=pl.ANY)
    tile = pl.BlockSpec((1, turn, rows, channels), lambda at: (at // 2, at % 2, 0, 0))
    flat = list(shapes[0]) + list(shapes[1])
    return pl.pallas_call(
        functools.partial(deliver_kernel, shapes),
        out_shape=(
            jax.ShapeDtypeStruct(input_grad.shape, F32),
            jax.ShapeDtypeStruct(cond_grad.shape, F32),
            jax.ShapeDtypeStruct(pair_grad.shape, F32),
        )
        + tuple(jax.ShapeDtypeStruct(shape, F32) for shape in flat),
        grid=(structs * 2,),
        in_specs=[whole(part.shape) for part in (input_grad, cond_grad, early, late)] + [tile],
        out_specs=[far, far, tile] + [far] * len(flat),
        scratch_shapes=[pltpu.VMEM(shape, F32) for shape in flat] + [pltpu.SemaphoreType.DMA((2 + len(flat),))],
        compiler_params=pltpu.CompilerParams(vmem_limit_bytes=62 << 20),
        name="deliver",
    )(input_grad, cond_grad, early, late, pair_grad)


def plain_kernel(struct_ref, len_ref, q_ref, k_ref, v_ref, bias_ref, out_ref, prob_ref, acc_ref):
    sample = pl.program_id(0)
    group_at = pl.program_id(1)
    length = len_ref[struct_ref[sample]]
    keys = k_ref.shape[1]
    group, windows = head_windows(q_ref.shape[2])
    valid = lax.broadcasted_iota(jnp.int32, (1, keys), 1) < length
    acc_ref[...] = jnp.zeros_like(acc_ref)
    for at, (start, width, offset) in enumerate(windows):
        lanes = slice(start, start + width)
        mask = head_mask(width, offset)
        query = q_ref[0, :, lanes]
        query = jnp.where(mask, query, jnp.zeros_like(query))
        scores = dot_nt(query, k_ref[0, :, lanes]) * HEAD_DIM ** (-0.5) + bias_ref[
            0, at
        ].astype(F32)
        scores = jnp.where(valid, scores, NEG_BIG)
        weights = jnp.exp(scores - jnp.max(scores, axis=1, keepdims=True))
        weights = weights * (1.0 / jnp.sum(weights, axis=1, keepdims=True))
        weights = weights.astype(BF16)
        prob_ref[0, at] = weights
        mixed = dot_nn(weights, v_ref[0, :, lanes])
        acc_ref[:, lanes] += jnp.where(mask, mixed, 0.0)
    out_ref[0] = acc_ref[...].astype(BF16)


def plain(struct_of, struct_len, query, key, value, bias):
    samples, rows, width = query.shape
    keys = key.shape[1]
    heads = bias.shape[1]
    group, windows = head_windows(width)
    each = len(windows)
    return pl.pallas_call(
        plain_kernel,
        out_shape=(
            jax.ShapeDtypeStruct((samples, rows, width), BF16),
            jax.ShapeDtypeStruct((samples, heads, rows, keys), BF16),
        ),
        grid_spec=pltpu.PrefetchScalarGridSpec(
            num_scalar_prefetch=2,
            grid=(samples, heads // each),
            in_specs=[
                pl.BlockSpec((1, rows, group), lambda b, g, s, n: (b, 0, g)),
                pl.BlockSpec((1, keys, group), lambda b, g, s, n: (b, 0, g)),
                pl.BlockSpec((1, keys, group), lambda b, g, s, n: (b, 0, g)),
                pl.BlockSpec((1, each, rows, keys), lambda b, g, s, n: (s[b], g, 0, 0)),
            ],
            out_specs=[
                pl.BlockSpec((1, rows, group), lambda b, g, s, n: (b, 0, g)),
                pl.BlockSpec((1, each, rows, keys), lambda b, g, s, n: (b, g, 0, 0)),
            ],
            scratch_shapes=[pltpu.VMEM((rows, group), F32)],
        ),
        compiler_params=pltpu.CompilerParams(vmem_limit_bytes=48 << 20),
        name="plain",
    )(struct_of, struct_len, query, key, value, bias)


def plain_back_kernel(
    struct_ref, q_ref, k_ref, v_ref, do_ref, prob_ref, dq_ref, dk_ref, dv_ref, bias_ref,
    dq_acc, dk_acc, dv_acc, bias_acc,
):
    samples = q_ref.shape[0]
    structs = bias_ref.shape[0]
    group, windows = head_windows(q_ref.shape[2])
    scale = HEAD_DIM ** (-0.5)
    for sample in range(samples):
        struct = struct_ref[sample]
        dq_acc[...] = jnp.zeros_like(dq_acc)
        dk_acc[...] = jnp.zeros_like(dk_acc)
        dv_acc[...] = jnp.zeros_like(dv_acc)
        for at, (start, width, offset) in enumerate(windows):
            lanes = slice(start, start + width)
            mask = head_mask(width, offset)
            upstream = do_ref[sample, :, lanes]
            upstream = jnp.where(mask, upstream, jnp.zeros_like(upstream))
            query = q_ref[sample, :, lanes]
            query = jnp.where(mask, query, jnp.zeros_like(query))
            low = prob_ref[sample, at]
            weights = low.astype(F32)
            d_weights = dot_nt(upstream, v_ref[sample, :, lanes])
            dv_acc[:, lanes] += dot_tn(low, upstream)
            cross = weights * d_weights
            delta = jnp.sum(cross, axis=1, keepdims=True)
            d_scores = (cross - weights * delta).astype(BF16)
            dq_acc[:, lanes] += jnp.where(mask, dot_nn(d_scores, k_ref[sample, :, lanes]), 0.0)
            dk_acc[:, lanes] += dot_tn(d_scores, query)
            for slab in range(structs):
                part = jnp.where(struct == slab, 1.0, 0.0) * d_scores.astype(F32)
                if sample == 0:
                    bias_acc[slab, at] = part
                elif sample < samples - 1:
                    bias_acc[slab, at] += part
                else:
                    bias_ref[slab, at] = (bias_acc[slab, at] + part).astype(BF16)
        dq_ref[sample] = (dq_acc[...] * scale).astype(BF16)
        dk_ref[sample] = (dk_acc[...] * scale).astype(BF16)
        dv_ref[sample] = dv_acc[...].astype(BF16)


def plain_back(struct_of, structs, query, key, value, upstream, prob):
    samples, rows, width = query.shape
    keys = key.shape[1]
    heads = prob.shape[1]
    group, windows = head_windows(width)
    each = len(windows)
    return pl.pallas_call(
        plain_back_kernel,
        out_shape=(
            jax.ShapeDtypeStruct((samples, rows, width), BF16),
            jax.ShapeDtypeStruct((samples, keys, width), BF16),
            jax.ShapeDtypeStruct((samples, keys, width), BF16),
            jax.ShapeDtypeStruct((structs, heads, rows, keys), BF16),
        ),
        grid_spec=pltpu.PrefetchScalarGridSpec(
            num_scalar_prefetch=1,
            grid=(heads // each,),
            in_specs=[
                pl.BlockSpec((samples, rows, group), lambda g, s: (0, 0, g)),
                pl.BlockSpec((samples, keys, group), lambda g, s: (0, 0, g)),
                pl.BlockSpec((samples, keys, group), lambda g, s: (0, 0, g)),
                pl.BlockSpec((samples, rows, group), lambda g, s: (0, 0, g)),
                pl.BlockSpec((samples, each, rows, keys), lambda g, s: (0, g, 0, 0)),
            ],
            out_specs=[
                pl.BlockSpec((samples, rows, group), lambda g, s: (0, 0, g)),
                pl.BlockSpec((samples, keys, group), lambda g, s: (0, 0, g)),
                pl.BlockSpec((samples, keys, group), lambda g, s: (0, 0, g)),
                pl.BlockSpec((structs, each, rows, keys), lambda g, s: (0, g, 0, 0)),
            ],
            scratch_shapes=[
                pltpu.VMEM((rows, group), F32),
                pltpu.VMEM((keys, group), F32),
                pltpu.VMEM((keys, group), F32),
                pltpu.VMEM((structs, each, rows, keys), F32),
            ],
        ),
        compiler_params=pltpu.CompilerParams(vmem_limit_bytes=60 << 20),
        name="plain_back",
    )(struct_of, query, key, value, upstream, prob)


def pack_rows(pieces, columns):
    return jnp.concatenate([piece.reshape(-1, columns) for piece in pieces], axis=0)


def pack_small(pieces, columns):
    flat = jnp.concatenate([piece.reshape(-1) for piece in pieces])
    rows = -(-flat.shape[0] // columns)
    rows = -(-rows // 8) * 8
    return jnp.pad(flat, (0, rows * columns - flat.shape[0])).reshape(rows, columns)


def unpack_rows(gathered, shapes):
    whole, at = [], 0
    count, _, columns = gathered.shape
    for rows, cols in shapes:
        held = rows * cols // columns
        whole.append(gathered[:, at : at + held].reshape(count * rows, cols))
        at += held
    return whole


def unpack_small(gathered, shapes):
    whole, at = [], 0
    count = gathered.shape[0]
    flat = gathered.reshape(count, -1)
    for shape in shapes:
        size = 1
        for extent in shape:
            size *= extent
        whole.append(flat[:, at : at + size].reshape((count * shape[0],) + shape[1:]))
        at += size
    return whole


def plain_device(
    act, cond, pair, struct_of, struct_len,
    gain_first, scale_first, scale_bias_first, shift_first,
    query_weight, query_bias, key_weight, value_weight, gate_weight, output_weight,
    pair_weight, zero_first, zero_bias_first,
    gain_second, scale_second, scale_bias_second, shift_second,
    swish_weight, linear_weight, down_weight, zero_second, zero_bias_second,
    cotangent,
):
    samples, rows, width = act.shape
    cond_width = cond.shape[2]
    total = samples * rows
    structs = pair.shape[0]
    small = (
        gain_first, scale_bias_first, query_bias, zero_bias_first, gain_second,
        scale_bias_second, zero_bias_second, pair_weight,
    )
    early = (scale_first, shift_first, query_weight, key_weight, value_weight, gate_weight)
    late = (
        output_weight, zero_first, scale_second, shift_second, swish_weight, linear_weight,
        down_weight, zero_second,
    )
    small_all = lax.all_gather(pack_small(small, width), "samp", axis=0)
    early_all = lax.all_gather(pack_rows(early, width), "samp", axis=0)
    late_all = lax.all_gather(pack_rows(late, width), "samp", axis=0)
    (gain_one, bias_one, bias_query, bias_zero_one, gain_two, bias_two, bias_zero_two, pair_proj_w) = (
        unpack_small(small_all, [piece.shape for piece in small])
    )
    (w_scale, w_shift, w_query, w_key, w_value, w_gate) = unpack_rows(
        early_all, [piece.shape for piece in early]
    )
    (w_out, w_zero, w_scale_two, w_shift_two, w_swish, w_linear, w_down, w_zero_two) = unpack_rows(
        late_all, [piece.shape for piece in late]
    )

    pair_normed, pair_inverse = norm_rows(pair.astype(F32))
    pair_low = pair_normed.astype(BF16)
    pair_proj = jnp.einsum("sijc,ch->shij", pair_low, pair_proj_w, preferred_element_type=F32)
    bias_all = lax.all_gather(pair_proj.astype(BF16), "samp", axis=3, tiled=True)

    act_rows = act.reshape(total, width).astype(F32)
    cond_low = cond.reshape(total, cond_width)
    act_normed, act_inverse = norm_rows(act_rows)
    cond_normed, cond_inverse = norm_rows(cond_low.astype(F32))
    cond_first = (cond_normed * gain_one.astype(F32)).astype(BF16)
    sig_first = jax.nn.sigmoid(product(cond_first, w_scale) + bias_one.astype(F32))
    adapted = (sig_first * act_normed + product(cond_first, w_shift)).astype(BF16)
    key_rows = product(adapted, w_key).astype(BF16)
    value_rows = product(adapted, w_value).astype(BF16)
    query_rows = (product(adapted, w_query) + bias_query.astype(F32)).astype(BF16)
    gate_sig = jax.nn.sigmoid(product(adapted, w_gate))
    key_value = jnp.stack((key_rows, value_rows)).reshape(2, samples, rows, width)
    key_value = lax.all_gather(key_value, "head", axis=2, tiled=True)
    query_split = query_rows.reshape(samples, rows, width)
    attended, prob = plain(
        struct_of, struct_len, query_split, key_value[0], key_value[1], bias_all
    )
    attn_float = attended.reshape(total, width).astype(F32)

    gated_rows = (gate_sig * attn_float).astype(BF16)
    branch = product(gated_rows, w_out)
    zero_sig_first = jax.nn.sigmoid(product(cond_low, w_zero) + bias_zero_one.astype(F32))
    middle = act_rows + zero_sig_first * branch
    mid_normed, mid_inverse = norm_rows(middle)
    cond_second = (cond_normed * gain_two.astype(F32)).astype(BF16)
    sig_second = jax.nn.sigmoid(product(cond_second, w_scale_two) + bias_two.astype(F32))
    adapted_two = (sig_second * mid_normed + product(cond_second, w_shift_two)).astype(BF16)
    swish_pre = product(adapted_two, w_swish)
    linear_pre = product(adapted_two, w_linear)
    swish_sig = jax.nn.sigmoid(swish_pre)
    hidden = (swish_pre * swish_sig * linear_pre).astype(BF16)
    down_rows = product(hidden, w_down)
    zero_sig_second = jax.nn.sigmoid(product(cond_low, w_zero_two) + bias_zero_two.astype(F32))
    layer_out = (middle + zero_sig_second * down_rows).astype(BF16)

    upstream = cotangent.reshape(total, width).astype(F32)
    d_down = (upstream * zero_sig_second).astype(BF16)
    d_zero_second = (upstream * down_rows * sigmoid_slope(zero_sig_second)).astype(BF16)
    d_hidden = back_product(d_down, w_down)
    d_swish = (
        d_hidden * linear_pre * swish_sig * (1.0 + swish_pre * (1.0 - swish_sig))
    ).astype(BF16)
    d_linear = (d_hidden * swish_pre * swish_sig).astype(BF16)
    d_adapted_two = back_product(d_swish, w_swish) + back_product(d_linear, w_linear)
    d_shift_second = d_adapted_two.astype(BF16)
    d_pre_second = (d_adapted_two * mid_normed * sigmoid_slope(sig_second)).astype(BF16)
    d_cond_second = back_product(d_shift_second, w_shift_two) + back_product(
        d_pre_second, w_scale_two
    )
    d_middle = upstream + norm_back(mid_normed, mid_inverse, d_adapted_two * sig_second)
    d_branch = (d_middle * zero_sig_first).astype(BF16)
    d_zero_first = (d_middle * branch * sigmoid_slope(zero_sig_first)).astype(BF16)
    d_gated = back_product(d_branch, w_out)
    d_gate = (d_gated * attn_float * sigmoid_slope(gate_sig)).astype(BF16)
    d_attended = (d_gated * gate_sig).astype(BF16)

    late_grads = (
        outer_sum(gated_rows, d_branch),
        outer_sum(cond_low, d_zero_first),
        outer_sum(cond_second, d_pre_second),
        outer_sum(cond_second, d_shift_second),
        outer_sum(adapted_two, d_swish),
        outer_sum(adapted_two, d_linear),
        outer_sum(hidden, d_down),
        outer_sum(cond_low, d_zero_second),
    )

    d_query, d_key, d_value, bias_grad = plain_back(
        struct_of, structs, query_split, key_value[0], key_value[1],
        d_attended.reshape(samples, rows, width), prob,
    )
    d_key_value = lax.psum_scatter(
        jnp.stack((d_key, d_value)), "head", scatter_dimension=2, tiled=True
    )
    d_query = d_query.reshape(total, width)
    d_key = d_key_value[0].reshape(total, width)
    d_value = d_key_value[1].reshape(total, width)
    bias_summed = lax.psum_scatter(bias_grad, "samp", scatter_dimension=3, tiled=True)
    pair_weight_grad = jnp.einsum("sijc,shij->ch", pair_low, bias_summed, preferred_element_type=F32)
    pair_upstream = jnp.einsum(
        "shij,ch->sijc", bias_summed, pair_proj_w, preferred_element_type=F32
    )
    pair_grad = norm_back(pair_normed, pair_inverse, pair_upstream)
    d_adapted = (
        back_product(d_query, w_query)
        + back_product(d_key, w_key)
        + back_product(d_value, w_value)
        + back_product(d_gate, w_gate)
    )
    d_shift_first = d_adapted.astype(BF16)
    d_pre_first = (d_adapted * act_normed * sigmoid_slope(sig_first)).astype(BF16)
    d_cond_first = back_product(d_shift_first, w_shift) + back_product(d_pre_first, w_scale)
    input_grad = d_middle + norm_back(act_normed, act_inverse, d_adapted * sig_first)
    d_cond_normed = d_cond_first * gain_one.astype(F32) + d_cond_second * gain_two.astype(F32)
    cond_grad = (
        norm_back(cond_normed, cond_inverse, d_cond_normed)
        + back_product(d_zero_first, w_zero)
        + back_product(d_zero_second, w_zero_two)
    )
    early_grads = (
        outer_sum(cond_first, d_pre_first),
        outer_sum(cond_first, d_shift_first),
        outer_sum(adapted, d_query),
        outer_sum(adapted, d_key),
        outer_sum(adapted, d_value),
        outer_sum(adapted, d_gate),
    )
    small_grads = (
        jnp.sum(d_cond_first * cond_normed, axis=0),
        column_sum(d_pre_first),
        column_sum(d_query),
        column_sum(d_zero_first),
        jnp.sum(d_cond_second * cond_normed, axis=0),
        column_sum(d_pre_second),
        column_sum(d_zero_second),
        pair_weight_grad,
    )
    count = lax.axis_size("samp")

    def pack_grads(grads, shapes):
        pieces = [
            grad.astype(BF16).reshape(count, shape[0] * shape[1] // width, width)
            for grad, shape in zip(grads, shapes)
        ]
        return jnp.concatenate(pieces, axis=1)

    def reduce(packed):
        summed = lax.psum_scatter(packed, "samp", scatter_dimension=0, tiled=True)
        return lax.psum(summed[0], "head").astype(F32)

    late_sum = reduce(pack_grads(late_grads, [piece.shape for piece in late]))
    early_sum = reduce(pack_grads(early_grads, [piece.shape for piece in early]))
    small_flat = jnp.concatenate(
        [grad.astype(BF16).reshape(count, -1) for grad in small_grads], axis=1
    )
    small_sum = lax.psum(
        lax.psum_scatter(small_flat, "samp", scatter_dimension=0, tiled=True), "head"
    ).astype(F32)
    (g_out, g_zero, g_scale_two, g_shift_two, g_swish, g_linear, g_down, g_zero_two) = unpack_rows(
        late_sum[None], [piece.shape for piece in late]
    )
    (g_scale, g_shift, g_query, g_key, g_value, g_gate) = unpack_rows(
        early_sum[None], [piece.shape for piece in early]
    )
    (g_gain, g_bias, g_bias_query, g_bias_zero, g_gain_two, g_bias_two, g_bias_zero_two, g_pair) = (
        unpack_small(small_sum, [piece.shape for piece in small])
    )
    return (
        layer_out.reshape(act.shape), input_grad.reshape(act.shape), cond_grad.reshape(cond.shape),
        pair_grad, g_gain, g_scale, g_bias, g_shift, g_query, g_bias_query, g_key, g_value, g_gate,
        g_out, g_pair, g_zero, g_bias_zero, g_gain_two, g_scale_two, g_bias_two, g_shift_two,
        g_swish, g_linear, g_down, g_zero_two, g_bias_zero_two,
    )


def per_device(
    act, cond, pair, struct_of, struct_len,
    gain_first, scale_first, scale_bias_first, shift_first,
    query_weight, query_bias, key_weight, value_weight, gate_weight, output_weight,
    pair_weight, zero_first, zero_bias_first,
    gain_second, scale_second, scale_bias_second, shift_second,
    swish_weight, linear_weight, down_weight, zero_second, zero_bias_second,
    cotangent,
):
    samples, rows, width = act.shape
    cond_width = cond.shape[2]
    total = samples * rows
    count = lax.axis_size("samp")
    spans = lax.axis_size("head")
    heads = width // HEAD_DIM
    small = (
        gain_first, scale_bias_first, query_bias, zero_bias_first, gain_second,
        scale_bias_second, zero_bias_second,
    )
    early = (scale_first, shift_first, key_weight, value_weight, query_weight, gate_weight)
    late = (
        swish_weight, linear_weight, down_weight, output_weight, zero_first, scale_second, zero_second,
        shift_second,
    )
    packed_small = jnp.concatenate(
        [jnp.pad(piece, (0, LANES - piece.shape[0]))[None] for piece in small]
        + [jnp.zeros((1, LANES), BF16), jnp.pad(pair_weight.T, ((0, 0), (0, LANES - pair_weight.shape[0])))],
        axis=0,
    )
    act_rows = act.reshape(total, width)
    cond_rows = cond.reshape(total, cond_width)
    pair_turned = pair.transpose(0, 2, 1, 3)
    (attended, prob, adapted, sig_first, gate_sig, query_split, key_value, full, *whole) = front(
        struct_of, struct_len, act_rows, cond_rows, packed_small, pair_turned, early + late, samples, count,
        spans,
    )
    (layer_out, d_gate, d_attended, d_middle, d_cond_two, extra, vectors, *late_parts) = middle_part(
        attended, gate_sig, act_rows, cond_rows, cotangent.reshape(total, width), full, whole[6:]
    )
    d_query, d_key_value, bias_packed, late_sum = attend_back(
        struct_of, pair.shape[0], query_split, key_value, d_attended, prob, late_parts, count
    )
    (input_grad, cond_grad, pair_grad, small_sum, early_sum, late_total) = finish(
        act_rows, cond_rows, adapted, sig_first, full, d_query, d_key_value, d_gate, d_middle, d_cond_two,
        extra, vectors, bias_packed, late_sum, pair_turned, whole[:6],
    )
    (input_grad, cond_grad, pair_grad, *weight_grads) = deliver(
        input_grad, cond_grad, early_sum, late_total, pair_grad,
        ([piece.shape for piece in early], [piece.shape for piece in late]),
    )
    (g_scale, g_shift, g_key, g_value, g_query, g_gate) = weight_grads[:6]
    (g_swish, g_linear, g_down, g_out, g_zero, g_scale_two, g_zero_two, g_shift_two) = weight_grads[6:]

    def own(row, size):
        return small_sum[row, :size]

    cond_share, share = cond_width // count, width // count
    g_pair = small_sum[8:, : pair_weight.shape[0]].T
    return (
        layer_out.reshape(act.shape), input_grad.reshape(act.shape), cond_grad.reshape(cond.shape),
        pair_grad.transpose(0, 2, 1, 3), own(0, cond_share), g_scale, own(1, share), g_shift, g_query,
        own(2, share), g_key, g_value, g_gate, g_out, g_pair, g_zero, own(3, share), own(4, cond_share),
        g_scale_two, own(5, share), g_shift_two, g_swish, g_linear, g_down, g_zero_two, own(6, share),
    )


def fits(mesh, act, pair):
    samples, rows, width = act.shape
    count, spans = mesh.shape["samp"], mesh.shape["head"]
    block = pair.shape[2]
    tail = block - MAIN
    heads = width // HEAD_DIM
    return (
        count == 8
        and samples == 2
        and tail > 0
        and heads * tail == MAIN
        and rows % block == 0
        and rows * spans == block * count
        and rows % 8 == 0
        and block * count <= KEY_LANES
    )


def solution(mesh):
    tokens = P("samp", "head", None)
    pairs = P(None, "head", "samp", None)
    vector = P("samp")
    matrix = P("samp", None)
    weights = (
        vector, matrix, vector, matrix, matrix, vector, matrix, matrix, matrix, matrix, matrix,
        matrix, vector, vector, matrix, vector, matrix, matrix, matrix, matrix, matrix, vector,
    )
    def choose(*arrays):
        body = per_device if fits(mesh, arrays[0], arrays[2]) else plain_device
        return body(*arrays)

    return jax.shard_map(
        choose,
        mesh=mesh,
        in_specs=(tokens, tokens, pairs, vector, P()) + weights + (tokens,),
        out_specs=(tokens, tokens, tokens, pairs) + weights,
        check_vma=False,
    )
```
